32 devices in a mesh: dp: 8 (over z, x), sp: 4 (over y, core).
Axes of the slice: x: 2, y: 2, z: 4, core: 2. Of those that a mesh axis runs over, the one named last changes fastest.
Arguments:
- tokens: bfloat16 [8192, 768], P(('dp', 'sp')), may hold values from -6 to 6
- segment_ids: int32 [8, 1024], P('dp'), may hold values from 0 to 3, never falling along the last dimension, each value on 1 to 512 neighbouring positions
- masked_rows: int32 [2432], P(('dp', 'sp')), may hold values from 0 to 255, as said below
- replacement: bfloat16 [2432, 768], P(('dp', 'sp')), may hold values from -6 to 6
- cotangent: float32 [2432, 768], P(('dp', 'sp')), may hold values from -6 to 6
- w_qkv: bfloat16 [768, 2304], replicated, may hold values from -0.21875 to 0.21875
- w_out_attn: bfloat16 [768, 768], replicated, may hold values from -0.875 to 0.875
- w_in_ff: bfloat16 [768, 6144], replicated, may hold values from -0.21875 to 0.21875
- w_out_ff: bfloat16 [3072, 768], replicated, may hold values from -0.109375 to 0.109375
- gain_one: float32 [768], replicated, may hold values from 0.1 to 1.9
- shift_one: float32 [768], replicated, may hold values from -3 to 3
- gain_two: float32 [768], replicated, may hold values from 0.1 to 1.9
- shift_two: float32 [768], replicated, may hold values from -3 to 3
Outputs:
- layer_out: bfloat16 [8192, 768], P(('dp', 'sp'))
- grad_tokens: float32 [8192, 768], P(('dp', 'sp'))
- grad_replacement: float32 [2432, 768], P(('dp', 'sp'))
- grad_qkv: float32 [768, 2304], P('dp')
- grad_out_attn: float32 [768, 768], P('dp')
- grad_in_ff: float32 [768, 6144], P('dp')
- grad_out_ff: float32 [3072, 768], P('dp')
- grad_gain_one: float32 [768], replicated
- grad_shift_one: float32 [768], replicated
- grad_gain_two: float32 [768], replicated
- grad_shift_two: float32 [768], replicated
The draws below stay inside these ranges and needn't reach their ends.
Inputs may be any that keep to these rules, and one draw needn't show every extreme that they name: `masked_rows`: within each device's block of 76 entries the rows are distinct and increasing.
All inputs are finite; a program needn't handle non-finite values.
Results may differ from the reference program's by a relative error of at most 0.017.
Values may be sent and summed in bfloat16 or wider, within the bound.
No kernel may reach another device: no remote copies, remote signals or barrier semaphores. Data moves between devices by JAX's collectives and lax.ppermute only.
A program may use at most 128 MiB of HBM per device.

```python
import math
import jax
import jax.numpy as jnp
import numpy as np
from jax import lax

D = 768
HEADS = 12
HEAD_DIM = 64
FF = 3072
TOK_DEV = 256
SEGS = 4
GROUP_TOK = 1024
MAX_LEN = 512
MASK_DEV = 76
TOKENS = 8192
MASKED = 2432
N_DP = 8
N_SP = 4


def draw_masked_rows(key, part):
    keys = jax.random.split(key, MASKED // MASK_DEV)

    def one_device(sub):
        order = jax.random.permutation(sub, TOK_DEV)[:MASK_DEV]
        return jnp.sort(order)
    return jax.vmap(one_device)(keys).reshape(MASKED).astype(jnp.int32)


def strengthened(values, rng, source, target, blocks, factor):
    owner, partner = [(jnp.arange(values.shape[position]) // (values.shape[position] // blocks)).reshape([-1 if axis == position else 1 for axis in range(values.ndim)]) for position in (source, target)]
    chosen = jax.random.permutation(rng, blocks)[partner]
    strong = (owner == chosen) | (owner == (partner + blocks // 2) % blocks)
    return jnp.where(strong, factor * values, values)


def block_scale(stream_key, shape, shards, least, top_value):
    loudness = 1.0
    for axis_at, parts in shards:
        heights = jax.random.uniform(jax.random.fold_in(jax.random.fold_in(stream_key, 6), axis_at), (parts,), jnp.float32, least / len(shards), top_value / len(shards))
        loudness = loudness * jnp.repeat(jnp.exp(heights), shape[axis_at] // parts).reshape((-1,) + (1,) * (len(shape) - 1 - axis_at))
    return loudness


def profile(number_of, total, reach, slope):
    portions = [(1 << 20) // math.isqrt(rank ** slope) + 1 for rank in range(2, number_of + 1)]
    surplus, holding = total - reach - (number_of - 1), [1] * (number_of - 1)
    while surplus > 0:
        candidates = [i for i in range(number_of - 1) if holding[i] < reach]
        mass, budget = sum([portions[i] for i in candidates]), surplus
        for i in candidates:
            addition = min(reach - holding[i], max(1, budget * portions[i] // mass), surplus)
            holding[i] = holding[i] + addition
            surplus = surplus - addition
    return np.array([reach] + holding)


def ragged_sizes(rng, amount, total, limit, slope):
    if amount == 2:
        one = jax.random.randint(rng, (), max(1, total - limit), min(limit, total - 1) + 1)
        return jnp.stack([one, total - one])
    sizes = jnp.asarray(profile(amount, total, limit, slope), jnp.int32)
    twos = (amount - 1) // 2
    source_of, sink = sizes[1:1 + 2 * twos:2], sizes[2:2 + 2 * twos:2]
    margin = jnp.minimum(source_of - 1, limit - sink)
    shifted = jax.random.randint(jax.random.fold_in(rng, 1), (twos,), 0, 1 << 20) % (margin + 1)
    sizes = sizes.at[1:1 + 2 * twos:2].set(source_of - shifted).at[2:2 + 2 * twos:2].set(sink + shifted)
    return sizes[jax.random.permutation(jax.random.fold_in(rng, 2), amount)]


def scatter_about(rng, extent, scale, most, cuts=(), kind=jnp.bfloat16):
    loudness = block_scale(rng, extent, cuts, -0.22, 0.18) if cuts else 1.0
    entries = jax.random.normal(rng, extent, jnp.float32) * scale * loudness
    return jnp.minimum(jnp.maximum(entries, -most), most).astype(kind)


def gaussian_with(own_key, dims, scale, most, pieces, heavy, kind=jnp.bfloat16):
    values = scale * jax.random.normal(own_key, dims, jnp.float32)
    if pieces:
        values = values * block_scale(own_key, dims, pieces, -0.22, 0.18)
    return jnp.clip(strengthened(values, jax.random.fold_in(own_key, 3), *heavy), -most, most).astype(kind)


def setup_inputs(seed: int = 0) -> dict:
    key_list = jax.random.split(jax.random.key(seed), 14)
    tokens = gaussian_with(key_list[0], (TOKENS, D), 1.0, 6.0, ((0, 32),), (0, 1, 32, 2.75))
    segment_ids = jax.vmap(lambda own: jnp.searchsorted(jnp.cumsum(ragged_sizes(own, SEGS, GROUP_TOK, MAX_LEN, 0)), jnp.arange(GROUP_TOK), side="right"))(jax.random.split(key_list[1], N_DP)).reshape((N_DP, GROUP_TOK)).astype(jnp.int32)
    masked_rows = draw_masked_rows(jax.random.fold_in(key_list[13], 71), 0)
    replacement = scatter_about(key_list[3], (MASKED, D), 1.0, 6.0, ((0, 32),))
    cotangent = scatter_about(key_list[4], (MASKED, D), 1.0, 6.0, ((0, 32),), jnp.float32)
    w_qkv = scatter_about(key_list[5], (D, 3 * D), D ** -0.5, 0.21875)
    w_out_attn = scatter_about(key_list[6], (D, D), (D // 16) ** -0.5, 0.875)
    w_in_ff = scatter_about(key_list[7], (D, 2 * FF), D ** -0.5, 0.21875)
    w_out_ff = scatter_about(key_list[8], (FF, D), FF ** -0.5, 0.109375)
    gain_one = jnp.clip(1.0 + 0.18 * jax.random.normal(key_list[9], (D,), jnp.float32), 0.1, 1.9)
    shift_one = scatter_about(key_list[10], (D,), 0.5, 3.0, (), jnp.float32)
    gain_two = jnp.clip(1.0 + 0.18 * jax.random.normal(key_list[11], (D,), jnp.float32), 0.1, 1.9)
    shift_two = scatter_about(key_list[12], (D,), 0.5, 3.0, (), jnp.float32)
    return dict(tokens=tokens, segment_ids=segment_ids, masked_rows=masked_rows, replacement=replacement, cotangent=cotangent, w_qkv=w_qkv, w_out_attn=w_out_attn, w_in_ff=w_in_ff, w_out_ff=w_out_ff, gain_one=gain_one, shift_one=shift_one, gain_two=gain_two, shift_two=shift_two)


@jax.custom_vjp
def low(v):
    return lax.optimization_barrier(v.astype(jnp.bfloat16)).astype(jnp.float32)

@jax.custom_vjp
def low_back(v):
    return v

def low_keep(v):
    return (low(v), None)

def low_pass(kept, grad):
    return (grad,)

def back_keep(v):
    return (v, None)

def back_low(kept, grad):
    return (low(grad),)
low.defvjp(low_keep, low_pass)
low_back.defvjp(back_keep, back_low)
norm_epsilon = 1e-05
masked_score = -1e+30

def alibi_slopes(head_count):
    nearest = 2 ** int(math.floor(math.log2(head_count)))
    base_list = [2.0 ** (-8.0 * (index + 1) / nearest) for index in range(nearest)]
    extra_list = [2.0 ** (-8.0 * (2 * index + 1) / (2 * nearest)) for index in range(head_count - nearest)]
    return jnp.array(base_list + extra_list, dtype=jnp.float32)

def normalize(value, gain, shift):
    center = value - lax.optimization_barrier(jnp.mean(value, axis=-1, keepdims=True))
    spread = lax.optimization_barrier(jnp.mean(center * center, axis=-1, keepdims=True))
    return center * lax.rsqrt(spread + norm_epsilon) * gain + shift

def attend_block(query_blk, keys, values, seg_q, seg_k, pos_q, pos_k, slopes, scale):
    scores = jnp.einsum('qhd,khd->hqk', query_blk, keys, precision=lax.Precision.HIGHEST) * scale
    distance = jnp.abs(pos_q[:, None] - pos_k[None, :]).astype(jnp.float32)
    scores = scores - slopes[:, None, None] * distance[None]
    scores = jnp.where((seg_q[:, None] == seg_k[None, :])[None], scores, masked_score)
    scores = low_back(scores)
    probs = low(jax.nn.softmax(scores, axis=-1))
    return jnp.einsum('hqk,khd->qhd', probs, values, precision=lax.Precision.HIGHEST)

def attention(query, keys, values, seg):
    group_tok = query.shape[0]
    block = min(512, group_tok)
    count = group_tok // block
    positions = jnp.arange(group_tok, dtype=jnp.int32)
    slopes = alibi_slopes(HEADS)
    scale = HEAD_DIM ** (-0.5)

    def one_block(item):
        return attend_block(item[0], keys, values, item[1], seg, item[2], positions, slopes, scale)
    outs = lax.map(jax.checkpoint(one_block), (query.reshape(count, block, HEADS, HEAD_DIM), seg.reshape(count, block), positions.reshape(count, block)))
    return outs.reshape(group_tok, HEADS * HEAD_DIM)

def layer(tok_in, repl_in, w_qkv, w_out_attn, w_in_ff, w_out_ff, gain_one, shift_one, gain_two, shift_two, seg, rows):
    group_tok = tok_in.shape[0]
    start = tok_in.at[rows].set(repl_in)
    qkv = low_back(low(jnp.dot(start, w_qkv, precision=lax.Precision.HIGHEST)))
    qkv = qkv.reshape(group_tok, 3, HEADS, HEAD_DIM)
    attn = attention(qkv[:, 0], qkv[:, 1], qkv[:, 2], seg)
    attn = low_back(low(attn))
    proj = low_back(jnp.dot(attn, w_out_attn, precision=lax.Precision.HIGHEST))
    first = normalize(start + proj, gain_one, shift_one)
    mixed = low_back(jnp.dot(low(first), w_in_ff, precision=lax.Precision.HIGHEST))
    hidden = low(jax.nn.gelu(mixed[:, :FF], approximate=False) * mixed[:, FF:])
    branch = low_back(jnp.dot(hidden, w_out_ff, precision=lax.Precision.HIGHEST))
    return normalize(first + branch, gain_two, shift_two)

def reference(tokens, segment_ids, masked_rows, replacement, cotangent, w_qkv, w_out_attn, w_in_ff, w_out_ff, gain_one, shift_one, gain_two, shift_two):
    groups = segment_ids.shape[0]
    group_tok = segment_ids.shape[1]
    width = tokens.shape[1]
    per_dev = group_tok // N_SP
    mask_group = masked_rows.shape[0] // groups
    mask_dev = mask_group // N_SP
    tok = tokens.astype(jnp.float32).reshape(groups, group_tok, width)
    repl = replacement.astype(jnp.float32).reshape(groups, mask_group, width)
    cot = cotangent.astype(jnp.float32).reshape(groups, mask_group, width)
    offsets = jnp.arange(mask_group, dtype=jnp.int32) // mask_dev * per_dev
    rows = masked_rows.reshape(groups, mask_group).astype(jnp.int32) + offsets[None, :]
    params = (w_qkv.astype(jnp.float32), w_out_attn.astype(jnp.float32), w_in_ff.astype(jnp.float32), w_out_ff.astype(jnp.float32), gain_one, shift_one, gain_two, shift_two)
    zeros = tuple((jnp.zeros_like(p) for p in params))

    def one_group(carry, item):
        tok_g, repl_g, cot_g, seg_g, rows_g = item

        def forward(tok_in, repl_in, *weights):
            return layer(tok_in, repl_in, *weights, seg_g, rows_g)
        out, pullback = jax.vjp(forward, tok_g, repl_g, *params)
        grad_out = jnp.zeros_like(out).at[rows_g].add(cot_g)
        grads = pullback(grad_out)
        new_carry = tuple((c + g for c, g in zip(carry, grads[2:])))
        return (new_carry, (out.astype(jnp.bfloat16), grads[0], grads[1]))
    sums, (outs, grad_tok, grad_rep) = lax.scan(one_group, zeros, (tok, repl, cot, segment_ids, rows))
    layer_out = outs.reshape(groups * group_tok, width)
    grad_tokens = grad_tok.reshape(groups * group_tok, width)
    grad_replacement = grad_rep.reshape(groups * mask_group, width)
    return (layer_out, grad_tokens, grad_replacement, sums[0], sums[1], sums[2], sums[3], sums[4], sums[5], sums[6], sums[7])
```

```python
import math

import jax
import jax.numpy as jnp
from jax import lax
from jax.sharding import PartitionSpec as P

HEADS = 12
norm_epsilon = 1e-05
masked_score = -1e30
F32 = jnp.float32
BF16 = jnp.bfloat16


def alibi_slopes(head_count):
    nearest = 2 ** int(math.floor(math.log2(head_count)))
    base_list = [2.0 ** (-8.0 * (index + 1) / nearest) for index in range(nearest)]
    extra_list = [
        2.0 ** (-8.0 * (2 * index + 1) / (2 * nearest)) for index in range(head_count - nearest)
    ]
    return jnp.array(base_list + extra_list, dtype=F32)


def normalize(value, gain, shift):
    center = value - jnp.mean(value, axis=-1, keepdims=True)
    spread = jnp.mean(center * center, axis=-1, keepdims=True)
    return center * lax.rsqrt(spread + norm_epsilon) * gain + shift


def gated_unit(gate, up_half):
    return jax.nn.gelu(gate, approximate=False) * up_half


def dot(a, b):
    return jnp.dot(a, b, preferred_element_type=F32)


def dot_nt(a, b):
    return lax.dot_general(a, b, (((1,), (1,)), ((), ())), preferred_element_type=F32)


def dot_tn(a, b):
    return lax.dot_general(a, b, (((0,), (0,)), ((), ())), preferred_element_type=F32)


def flip(value, axis, bits):
    count = lax.axis_size(axis)
    return lax.ppermute(value, axis, [(index, index ^ bits) for index in range(count)])


def gather_blocks(value):
    far = flip(value, "sp", 2)
    near = flip(value, "sp", 1)
    cross = flip(far, "sp", 1)
    return [value, near, far, cross]


def exchange_blocks(blocks):
    far = flip(jnp.stack([blocks[2], blocks[3]]), "sp", 2)
    near = flip(blocks[1], "sp", 1)
    cross = flip(far[1], "sp", 1)
    return [blocks[0], near, far[0], cross]


def pick(value, index):
    return lax.dynamic_index_in_dim(value, index, 0, keepdims=False)


def natural_order(blocks, rank):
    stacked = jnp.stack(blocks)
    return [pick(stacked, rank ^ index) for index in range(len(blocks))]


def split_sum(value):
    high = value.astype(BF16)
    low = (value - high.astype(F32)).astype(BF16)
    return jnp.concatenate([high, low], axis=0)


def join_sum(pair):
    half = pair.shape[0] // 2
    return pair[:half].astype(F32) + pair[half:].astype(F32)


def reduce_rows(grad):
    count = lax.axis_size("dp")
    if count != 8:
        return lax.psum_scatter(grad, "dp", scatter_dimension=0, tiled=True)
    place = lax.axis_index("dp")
    outer, inner = place // 2, place % 2
    view = grad.reshape(4, 2, grad.shape[0] // 8, grad.shape[1])
    keep = lax.dynamic_index_in_dim(view, inner, 1, keepdims=False)
    send = lax.dynamic_index_in_dim(view, 1 - inner, 1, keepdims=False).astype(BF16)
    came = flip(send, "dp", 1)
    total = pick(keep, outer).astype(F32) + pick(came, outer).astype(F32)
    for step in (1, 2, 3):
        part = pick(keep, outer ^ step).astype(F32) + pick(came, outer ^ step).astype(F32)
        total = total + flip(part.astype(BF16), "dp", 2 * step).astype(F32)
    return total


def reduce_quarter_rows(pieces, sums):
    count = lax.axis_size("dp")
    rank = lax.axis_index("sp")
    if count != 8:
        moves = []
        for place in range(count):
            for quarter in range(4):
                target = quarter * (count // 4) + place // 4
                moves.append((place * 4 + quarter, target * 4 + place % 4))
        results = []
        for grad in pieces:
            shard = lax.psum_scatter(grad, "dp", scatter_dimension=0, tiled=True)
            results.append(lax.ppermute(shard, ("dp", "sp"), moves))
        return results, lax.psum(sums, "dp")
    place = lax.axis_index("dp")
    outer, inner = place // 2, place % 2
    width = pieces[0].shape[1]
    sizes = [grad.shape[0] // 8 for grad in pieces]
    packed = jnp.concatenate(
        [grad.reshape(2, 4, size, width) for grad, size in zip(pieces, sizes)], axis=2
    ).astype(BF16)
    each = packed.shape[2]
    keep = pick(packed, inner)
    send = pick(packed, 1 - inner).reshape(4 * each, width)
    came = flip(jnp.concatenate([send, split_sum(sums)], axis=0), "dp", 1)
    sums = sums + join_sum(came[4 * each :])
    came = came[: 4 * each].reshape(4, each, width)
    total = 0.0
    for step in range(4):
        moves = []
        for z in range(4):
            for x in range(2):
                for quarter in range(4):
                    moves.append(((z * 2 + x) * 4 + quarter, (quarter * 2 + x) * 4 + (z ^ step)))
        part = pick(keep, outer ^ step).astype(F32) + pick(came, outer ^ step).astype(F32)
        part = jnp.concatenate([part.astype(BF16), split_sum(sums)], axis=0)
        part = lax.ppermute(part, ("dp", "sp"), moves)
        part = jnp.concatenate([part[:each].astype(F32), join_sum(part[each:])], axis=0)
        total = total + part
    results = []
    first = 0
    for size in sizes:
        results.append(total[first : first + size])
        first += size
    return results, total[each:]


def local(
    tokens,
    segment_ids,
    masked_rows,
    replacement,
    cotangent,
    w_qkv,
    w_out_attn,
    w_in_ff,
    w_out_ff,
    gain_one,
    shift_one,
    gain_two,
    shift_two,
):
    rows_dev, width = tokens.shape
    ranks = lax.axis_size("sp")
    rank = lax.axis_index("sp")
    heads_local = HEADS // ranks
    head_dim = width // HEADS
    local_width = heads_local * head_dim
    hidden_width = w_out_ff.shape[0]
    hidden_local = hidden_width // ranks
    scale = head_dim ** (-0.5)
    group_tok = rows_dev * ranks
    order = rank ^ jnp.arange(ranks, dtype=jnp.int32)

    seg = segment_ids[0].reshape(ranks, rows_dev)[order].reshape(group_tok)
    positions = jnp.arange(group_tok, dtype=jnp.int32).reshape(ranks, rows_dev)[order]
    positions = positions.reshape(group_tok)
    slopes = lax.dynamic_slice_in_dim(alibi_slopes(HEADS), rank * heads_local, heads_local, 0)

    w_qkv_rel = w_qkv.reshape(width, 3, ranks, local_width).transpose(2, 0, 1, 3)[order]
    w_qkv_rel = w_qkv_rel.reshape(ranks, width, 3 * local_width)
    w_out_rel = w_out_attn.reshape(ranks, local_width, width)[order]
    w_gate = lax.dynamic_slice_in_dim(w_in_ff, rank * hidden_local, hidden_local, 1)
    w_up = lax.dynamic_slice_in_dim(w_in_ff, hidden_width + rank * hidden_local, hidden_local, 1)
    w_in_loc = jnp.concatenate([w_gate, w_up], axis=1)
    w_down = lax.dynamic_slice_in_dim(w_out_ff, rank * hidden_local, hidden_local, 0)

    select = jnp.arange(rows_dev, dtype=jnp.int32)[:, None] == masked_rows[None, :]
    hit = jnp.any(select, axis=1, keepdims=True)
    placed = dot(select.astype(BF16), replacement)
    select = select.astype(F32)
    start_low = jnp.where(hit, placed.astype(BF16), tokens)
    start = start_low.astype(F32)
    start_all = jnp.concatenate(gather_blocks(start_low), axis=0)

    qkv = dot(start_all, w_qkv_rel[0]).astype(BF16).reshape(group_tok, 3, heads_local, head_dim)
    query, keys, values = qkv[:, 0], qkv[:, 1], qkv[:, 2]
    raw = jnp.einsum("qhd,khd->hqk", query, keys, preferred_element_type=F32) * scale
    distance = jnp.abs(positions[:, None] - positions[None, :]).astype(F32)
    raw = raw - slopes[:, None, None] * distance[None]
    scores = jnp.where((seg[:, None] == seg[None, :])[None], raw, masked_score)
    peak = jnp.max(scores, axis=-1, keepdims=True)
    weights = jnp.exp(scores - peak)
    total = jnp.sum(weights, axis=-1, keepdims=True)
    probs = (weights / total).astype(BF16)
    logsum = peak + jnp.log(total)
    attn_heads = jnp.einsum("hqk,khd->qhd", probs, values, preferred_element_type=F32)
    attn_heads = attn_heads.astype(BF16).reshape(group_tok, local_width)
    parts = exchange_blocks(list(attn_heads.reshape(ranks, rows_dev, local_width)))
    attn_low = jnp.concatenate(parts, axis=1)

    proj = dot(attn_low, w_out_rel.reshape(width, width))
    first_norm, pull_one = jax.vjp(normalize, start + proj, gain_one, shift_one)
    first_low = first_norm.astype(BF16)
    first_all = jnp.concatenate(gather_blocks(first_low), axis=0)
    mixed = dot(first_low, w_in_ff)
    hidden, pull_gate = jax.vjp(gated_unit, mixed[:, :hidden_width], mixed[:, hidden_width:])
    branch = dot(hidden.astype(BF16), w_out_ff)
    result, pull_two = jax.vjp(normalize, first_norm + branch, gain_two, shift_two)
    layer_out = result.astype(BF16)
    grad_result = jnp.dot(select, cotangent, precision=lax.Precision.HIGHEST)
    d_second, d_gain_two, d_shift_two = pull_two(grad_result)
    d_branch = d_second.astype(BF16)
    d_branch_all = jnp.concatenate(gather_blocks(d_branch), axis=0)
    d_hidden = dot_nt(d_branch, w_out_ff)
    d_gate, d_up = pull_gate(d_hidden)
    d_mixed = jnp.concatenate([d_gate, d_up], axis=1).astype(BF16)
    d_first = d_second + dot_nt(d_mixed, w_in_ff)
    d_sum_one, d_gain_one, d_shift_one = pull_one(d_first)
    d_proj = d_sum_one.astype(BF16)

    norm_sums = jnp.stack([d_gain_one, d_shift_one, d_gain_two, d_shift_two])
    sent = jnp.concatenate([d_proj, split_sum(norm_sums)], axis=0)
    blocks = gather_blocks(sent)
    norm_sums = norm_sums
    for block in blocks[1:]:
        norm_sums = norm_sums + join_sum(block[rows_dev:])
    d_proj_all = jnp.concatenate([block[:rows_dev] for block in blocks], axis=0)

    mixed_q = dot(first_all, w_in_loc)
    hidden_q, pull_q = jax.vjp(gated_unit, mixed_q[:, :hidden_local], mixed_q[:, hidden_local:])
    g_out_ff = dot_tn(hidden_q.astype(BF16), d_branch_all)
    d_gate_q, d_up_q = pull_q(dot_nt(d_branch_all, w_down))
    d_mixed_q = jnp.concatenate([d_gate_q, d_up_q], axis=1).astype(BF16)
    g_in_ff = dot_tn(first_all, d_mixed_q)
    share_in_ff = reduce_rows(g_in_ff.astype(BF16))

    g_out_attn = dot_tn(attn_heads, d_proj_all)
    (share_out_ff, share_out_attn), norm_sums = reduce_quarter_rows(
        [g_out_ff, g_out_attn], norm_sums
    )

    d_attn = dot_nt(d_proj_all, w_out_rel[0]).astype(BF16)
    d_attn = d_attn.reshape(group_tok, heads_local, head_dim)
    probs = jnp.exp(scores - logsum)
    d_probs = jnp.einsum("qhd,khd->hqk", d_attn, values, preferred_element_type=F32)
    delta = jnp.sum(probs * d_probs, axis=-1, keepdims=True)
    d_scores = (probs * (d_probs - delta)).astype(BF16)
    d_query = jnp.einsum("hqk,khd->qhd", d_scores, keys, preferred_element_type=F32) * scale
    d_keys = jnp.einsum("hqk,qhd->khd", d_scores, query, preferred_element_type=F32) * scale
    d_values = jnp.einsum("hqk,qhd->khd", probs.astype(BF16), d_attn, preferred_element_type=F32)
    d_qkv = jnp.stack([d_query, d_keys, d_values], axis=1).astype(BF16)
    d_qkv = d_qkv.reshape(group_tok, 3 * local_width)
    g_qkv = dot_tn(start_all, d_qkv)
    share_qkv = reduce_rows(g_qkv.astype(BF16))

    parts = exchange_blocks(list(d_qkv.reshape(ranks, rows_dev, 3 * local_width)))
    d_start = d_sum_one
    for index in range(ranks):
        d_start = d_start + dot_nt(parts[index], w_qkv_rel[index])
    grad_tokens = jnp.where(hit, 0.0, d_start)
    grad_replacement = jnp.einsum("tm,tc->mc", select, d_start, precision=lax.Precision.HIGHEST)

    def columns(share, halves):
        blocks = natural_order(gather_blocks(share.astype(BF16)), rank)
        each = share.shape[1] // halves
        parts = [block[:, i * each : (i + 1) * each] for i in range(halves) for block in blocks]
        return jnp.concatenate(parts, axis=1).astype(F32)

    def rows(share):
        blocks = natural_order(gather_blocks(share.astype(BF16)), rank)
        return jnp.concatenate(blocks, axis=0).astype(F32)

    return (
        layer_out,
        grad_tokens,
        grad_replacement,
        columns(share_qkv, 3),
        rows(share_out_attn),
        columns(share_in_ff, 2),
        rows(share_out_ff),
        norm_sums[0],
        norm_sums[1],
        norm_sums[2],
        norm_sums[3],
    )


def solution(mesh):
    return jax.shard_map(
        local,
        mesh=mesh,
        in_specs=(
            P(("dp", "sp"), None),
            P("dp", None),
            P(("dp", "sp")),
            P(("dp", "sp"), None),
            P(("dp", "sp"), None),
            P(),
            P(),
            P(),
            P(),
            P(),
            P(),
            P(),
            P(),
        ),
        out_specs=(
            P(("dp", "sp"), None),
            P(("dp", "sp"), None),
            P(("dp", "sp"), None),
            P("dp", None),
            P("dp", None),
            P("dp", None),
            P("dp", None),
            P(),
            P(),
            P(),
            P(),
        ),
        check_vma=False,
    )
```

```python
import functools
import math

import jax
import jax.numpy as jnp
from jax import lax
from jax.experimental import pallas as pl
from jax.experimental.pallas import tpu as pltpu
from jax.sharding import PartitionSpec as P

HEADS = 12
RANKS = 4
EPSILON = 1e-05
FAR = 1e30
F32 = jnp.float32
BF16 = jnp.bfloat16
VM = pl.BlockSpec(memory_space=pltpu.VMEM)
SM = pl.BlockSpec(memory_space=pltpu.SMEM)


def shape(dims, kind):
    return jax.ShapeDtypeStruct(dims, kind)


def scratch(dims, kind):
    return pltpu.VMEM(dims, kind)


def params(mebibytes):
    return pltpu.CompilerParams(vmem_limit_bytes=mebibytes << 20)


def alibi_slopes(head_count):
    nearest = 2 ** int(math.floor(math.log2(head_count)))
    base_list = [2.0 ** (-8.0 * (index + 1) / nearest) for index in range(nearest)]
    extra_list = [
        2.0 ** (-8.0 * (2 * index + 1) / (2 * nearest)) for index in range(head_count - nearest)
    ]
    return jnp.array(base_list + extra_list, dtype=F32)


def dot(a, b):
    return jnp.dot(a, b, preferred_element_type=F32)


def dot_nt(a, b):
    return lax.dot_general(a, b, (((1,), (1,)), ((), ())), preferred_element_type=F32)


def dot_tn(a, b):
    return lax.dot_general(a, b, (((0,), (0,)), ((), ())), preferred_element_type=F32)


def exact_dot(a, b):
    return jnp.dot(a, b, precision=lax.Precision.HIGHEST, preferred_element_type=F32)


def standardize(value):
    center = value - jnp.mean(value, axis=-1, keepdims=True)
    spread = jnp.mean(center * center, axis=-1, keepdims=True)
    inverse = lax.rsqrt(spread + EPSILON)
    return center * inverse, inverse


def standardize_back(grad, unit, inverse):
    mean = jnp.mean(grad, axis=-1, keepdims=True)
    return inverse * (grad - mean - unit * jnp.mean(grad * unit, axis=-1, keepdims=True))


def gelu_pair(x):
    cdf = 0.5 * (1.0 + lax.erf(x * math.sqrt(0.5)))
    pdf = jnp.exp(-0.5 * x * x) * (1.0 / math.sqrt(2.0 * math.pi))
    return x * cdf, cdf + x * pdf


def pair_active(info, rank, first, second, rows):
    one, two = rank ^ first, rank ^ second
    low, high = jnp.minimum(one, two), jnp.maximum(one, two)
    return jnp.logical_or(one == two, info[low * rows + rows] == info[high * rows + 1])


def pair_distance(seg_rows, rank, keys_at, query_at, rows):
    key_pos, query_pos = (rank ^ keys_at) * rows, (rank ^ query_at) * rows
    down = lax.broadcasted_iota(jnp.int32, (rows, rows), 0)
    across = lax.broadcasted_iota(jnp.int32, (rows, rows), 1)
    gap = jnp.abs(down - across + (key_pos - query_pos)).astype(F32)
    seg_q = seg_rows[:, pl.ds(pl.multiple_of(query_pos, rows), rows)]
    seg_k = seg_rows[:, pl.ds(pl.multiple_of(key_pos, rows), rows)]
    seg_k = jnp.transpose(jnp.broadcast_to(seg_k, (128, rows)))[:, :1]
    return jnp.where(seg_k == seg_q, gap, FAR)


def attention_forward_kernel(
    rows, heads, dim, info, slopes, x0, x1, x2, x3, w, seg_rows,
    qkv_out, out, out_t, lse, qs, ks, vt, dist, acc, peak, total,
):
    rank = info[0]
    width = heads * dim
    for at, x in enumerate((x0, x1, x2, x3)):
        qkv = dot(x[...], w[...]).astype(BF16)
        here = pl.ds(at * rows, rows)
        qkv_out[here, :] = qkv
        for h in range(heads):
            qs[h, here, :] = (qkv[:, h * dim : (h + 1) * dim] * dim**-0.5).astype(BF16)
            ks[h, here, :] = qkv[:, width + h * dim : width + (h + 1) * dim]
        vt[:, here] = jnp.transpose(qkv[:, 2 * width :])

    def query_block(a, carry):
        mine = pl.ds(pl.multiple_of(a * rows, rows), rows)
        peak[...] = jnp.full_like(peak, -jnp.inf)
        total[...] = jnp.zeros_like(total)
        acc[...] = jnp.zeros_like(acc)

        def key_block(b, carry):
            @pl.when(pair_active(info, rank, a, b, rows))
            def _():
                theirs = pl.ds(pl.multiple_of(b * rows, rows), rows)
                dist[...] = pair_distance(seg_rows, rank, b, a, rows)
                for h in range(heads):
                    slope = slopes[rank * heads + h]
                    s = dot_nt(ks[h, theirs, :], qs[h, mine, :]) - slope * dist[...]
                    old = peak[h : h + 1, :]
                    new = jnp.maximum(old, jnp.max(s, axis=0, keepdims=True))
                    p = jnp.exp(s - new)
                    fade = jnp.exp(old - new)
                    add = jnp.sum(p, axis=0, keepdims=True)
                    total[h : h + 1, :] = total[h : h + 1, :] * fade + add
                    peak[h : h + 1, :] = new
                    span = slice(h * dim, (h + 1) * dim)
                    acc[span, :] = acc[span, :] * fade + dot(vt[span, theirs], p.astype(BF16))

            return carry

        lax.fori_loop(0, RANKS, key_block, 0)
        for h in range(heads):
            span = slice(h * dim, (h + 1) * dim)
            acc[span, :] = acc[span, :] / total[h : h + 1, :]
            lse[h : h + 1, mine] = peak[h : h + 1, :] + jnp.log(total[h : h + 1, :])
        value = acc[...].astype(BF16)
        out_t[:, mine] = value
        out[a] = jnp.transpose(value)
        return carry

    lax.fori_loop(0, RANKS, query_block, 0)


def attention_forward(info, slopes, blocks, w, seg_rows, heads, dim):
    rows = blocks[0].shape[0]
    tok, lw = rows * RANKS, heads * dim
    return pl.pallas_call(
        functools.partial(attention_forward_kernel, rows, heads, dim),
        name="attention_forward",
        out_shape=(
            shape((tok, 3 * lw), BF16),
            shape((RANKS, rows, lw), BF16),
            shape((lw, tok), BF16),
            shape((heads, tok), F32),
        ),
        in_specs=[SM, SM] + [VM] * 6,
        out_specs=(VM,) * 4,
        scratch_shapes=[
            scratch((heads, tok, dim), BF16),
            scratch((heads, tok, dim), BF16),
            scratch((lw, tok), BF16),
            scratch((rows, rows), F32),
            scratch((lw, rows), F32),
            scratch((heads, rows), F32),
            scratch((heads, rows), F32),
        ],
        compiler_params=params(40),
        cost_estimate=pl.CostEstimate(
            flops=4 * 10**9, bytes_accessed=6 * 10**6, transcendentals=3 * 10**6
        ),
    )(info, slopes, *blocks, w, seg_rows)


def attention_backward_kernel(
    rows, heads, dim, info, slopes, g0, g1, g2, g3, w, qkv, lse, seg_rows,
    d_qkv, qs, ks, kt, vs, do, dist, prob, dprob, dk, dv, dqt, delta,
):
    rank = info[0]
    width = heads * dim
    scale = dim**-0.5
    w_rank = w[pl.ds(pl.multiple_of(rank * width, width), width), :]
    for at, g in enumerate((g0, g1, g2, g3)):
        here = pl.ds(at * rows, rows)
        grad = dot_nt(g[0:rows, :], w_rank).astype(BF16)
        value = qkv[here, :]
        kt[:, here] = jnp.transpose(value[:, width : 2 * width])
        for h in range(heads):
            do[h, here, :] = grad[:, h * dim : (h + 1) * dim]
            qs[h, here, :] = (value[:, h * dim : (h + 1) * dim] * scale).astype(BF16)
            ks[h, here, :] = value[:, width + h * dim : width + (h + 1) * dim]
            vs[h, here, :] = value[:, 2 * width + h * dim : 2 * width + (h + 1) * dim]
    dk[...] = jnp.zeros_like(dk)
    dv[...] = jnp.zeros_like(dv)

    def query_block(a, carry):
        mine = pl.ds(pl.multiple_of(a * rows, rows), rows)
        delta[...] = jnp.zeros_like(delta)
        dqt[...] = jnp.zeros_like(dqt)

        def first_pass(b, carry):
            @pl.when(pair_active(info, rank, a, b, rows))
            def _():
                theirs = pl.ds(pl.multiple_of(b * rows, rows), rows)
                dist[...] = pair_distance(seg_rows, rank, b, a, rows)
                for h in range(heads):
                    slope = slopes[rank * heads + h]
                    s = dot_nt(ks[h, theirs, :], qs[h, mine, :]) - slope * dist[...]
                    p = jnp.exp(s - lse[h : h + 1, mine])
                    dp = dot_nt(vs[h, theirs, :], do[h, mine, :])
                    delta[h : h + 1, :] += jnp.sum(p * dp, axis=0, keepdims=True)
                    prob[h, theirs, :] = p
                    dprob[h, theirs, :] = dp

            return carry

        lax.fori_loop(0, RANKS, first_pass, 0)

        def second_pass(b, carry):
            @pl.when(pair_active(info, rank, a, b, rows))
            def _():
                theirs = pl.ds(pl.multiple_of(b * rows, rows), rows)
                for h in range(heads):
                    p = prob[h, theirs, :]
                    ds = (p * (dprob[h, theirs, :] - delta[h : h + 1, :])).astype(BF16)
                    dv[h, theirs, :] += dot(p.astype(BF16), do[h, mine, :])
                    dk[h, theirs, :] += dot(ds, qs[h, mine, :])
                    span = slice(h * dim, (h + 1) * dim)
                    dqt[span, :] += dot(kt[span, theirs], ds)

            return carry

        lax.fori_loop(0, RANKS, second_pass, 0)
        d_qkv[a, :, 0:width] = jnp.transpose(dqt[...] * scale).astype(BF16)
        return carry

    lax.fori_loop(0, RANKS, query_block, 0)
    for at in range(RANKS):
        here = pl.ds(at * rows, rows)
        for h in range(heads):
            first = width + h * dim
            d_qkv[at, :, first : first + dim] = dk[h, here, :].astype(BF16)
            first = 2 * width + h * dim
            d_qkv[at, :, first : first + dim] = dv[h, here, :].astype(BF16)


def attention_backward(info, slopes, blocks, w, qkv, lse, seg_rows, heads, dim):
    tok, lw = qkv.shape[0], heads * dim
    rows = tok // RANKS
    return pl.pallas_call(
        functools.partial(attention_backward_kernel, rows, heads, dim),
        name="attention_backward",
        out_shape=shape((RANKS, rows, 3 * lw), BF16),
        in_specs=[SM, SM] + [VM] * 8,
        out_specs=VM,
        scratch_shapes=[
            scratch((heads, tok, dim), BF16),
            scratch((heads, tok, dim), BF16),
            scratch((lw, tok), BF16),
            scratch((heads, tok, dim), BF16),
            scratch((heads, tok, dim), BF16),
            scratch((rows, rows), F32),
            scratch((heads, tok, rows), F32),
            scratch((heads, tok, rows), F32),
            scratch((heads, tok, dim), F32),
            scratch((heads, tok, dim), F32),
            scratch((lw, rows), F32),
            scratch((heads, rows), F32),
        ],
        compiler_params=params(48),
        cost_estimate=pl.CostEstimate(
            flops=8 * 10**9, bytes_accessed=6 * 10**6, transcendentals=3 * 10**6
        ),
    )(info, slopes, *blocks, w, qkv, lse, seg_rows)


def norm_one_kernel(
    info, own, near, far, cross, start, w, gain, shift, low, unit, inverse
):
    rank = info[0]
    part_width = near.shape[1]
    total = start[...].astype(F32)
    for step, value in enumerate((own[0], near[...], far[0], cross[...])):
        rows = pl.ds(pl.multiple_of((rank ^ step) * part_width, part_width), part_width)
        total = total + dot(value, w[rows, :])
    x, inv = standardize(total)
    unit[...] = x
    inverse[...] = inv
    low[...] = (x * gain[...] + shift[...]).astype(BF16)


def norm_one(info, own, near, far, cross, start, w, gain, shift):
    rows, width = start.shape
    return pl.pallas_call(
        norm_one_kernel,
        name="norm_one",
        out_shape=(shape((rows, width), BF16), shape((rows, width), F32), shape((rows, 1), F32)),
        in_specs=[SM] + [VM] * 8,
        out_specs=(VM,) * 3,
        cost_estimate=pl.CostEstimate(
            flops=2 * rows * width * width, bytes_accessed=4 * 10**6, transcendentals=0
        ),
    )(info, own, near, far, cross, start, w, gain, shift)


def ffn_forward_kernel(
    low, unit, gain1, shift1, gain2, shift2, masked, cot, w_gate, w_up, w_down,
    layer_out, d_h2, d_ff, slope, act, sums, acc,
):
    step = pl.program_id(0)
    gate = dot(low[...], w_gate[...])
    up = dot(low[...], w_up[...])
    value, grad = gelu_pair(gate)
    act[...] = value.astype(BF16)
    slope[...] = (up * grad).astype(BF16)
    part = dot((value * up).astype(BF16), w_down[...])

    @pl.when(step == 0)
    def _():
        acc[...] = unit[...] * gain1[...] + shift1[...] + part

    @pl.when(step > 0)
    def _():
        acc[...] += part

    @pl.when(step == pl.num_programs(0) - 1)
    def _():
        x, inv = standardize(acc[...])
        layer_out[...] = (x * gain2[...] + shift2[...]).astype(BF16)
        places = lax.broadcasted_iota(jnp.int32, (low.shape[0], masked.shape[1]), 0)
        dy = exact_dot((places == masked[...]).astype(F32), cot[...])
        sums[0:1, :] = jnp.sum(dy * x, axis=0, keepdims=True)
        sums[1:2, :] = jnp.sum(dy, axis=0, keepdims=True)
        grad_in = standardize_back(dy * gain2[...], x, inv)
        d_h2[...] = grad_in
        d_ff[...] = grad_in.astype(BF16)


def ffn_forward(low, unit, gain1, shift1, gain2, shift2, masked, cot, w_in, w_out, size):
    rows, width = low.shape
    hid = w_out.shape[0]
    count = hid // size
    full = lambda dims: pl.BlockSpec(dims, lambda j: (0, 0))
    act = pl.BlockSpec((rows, size), lambda j: (0, j))
    return pl.pallas_call(
        ffn_forward_kernel,
        name="ffn_forward",
        grid=(count,),
        out_shape=(
            shape((rows, width), BF16),
            shape((rows, width), F32),
            shape((rows, width), BF16),
            shape((rows, hid), BF16),
            shape((rows, hid), BF16),
            shape((2, width), F32),
        ),
        in_specs=[full((rows, width))] * 2
        + [full((1, width))] * 4
        + [
            full(masked.shape),
            full(cot.shape),
            pl.BlockSpec((width, size), lambda j: (0, j)),
            pl.BlockSpec((width, size), lambda j: (0, count + j)),
            pl.BlockSpec((size, width), lambda j: (j, 0)),
        ],
        out_specs=(full((rows, width)),) * 3 + (act, act, full((2, width))),
        scratch_shapes=[scratch((rows, width), F32)],
        compiler_params=params(48),
        cost_estimate=pl.CostEstimate(
            flops=6 * rows * width * hid, bytes_accessed=18 * 10**6, transcendentals=2 * rows * hid
        ),
    )(low, unit, gain1, shift1, gain2, shift2, masked, cot, w_in, w_in, w_out)


def ffn_backward_kernel(
    d_ff, d_h2, unit, inverse, gain1, sums2, act, slope, w_gate, w_up, w_down, d_h1, sent, acc
):
    step = pl.program_id(0)
    d_hidden = dot_nt(d_ff[...], w_down[...])
    d_gate = (d_hidden * slope[...].astype(F32)).astype(BF16)
    d_up = (d_hidden * act[...].astype(F32)).astype(BF16)
    part = dot_nt(d_gate, w_gate[...]) + dot_nt(d_up, w_up[...])

    @pl.when(step == 0)
    def _():
        acc[...] = d_h2[...] + part

    @pl.when(step > 0)
    def _():
        acc[...] += part

    @pl.when(step == pl.num_programs(0) - 1)
    def _():
        total = acc[...]
        rows = total.shape[0]
        x = unit[...]
        gain_sum = jnp.sum(total * x, axis=0, keepdims=True)
        shift_sum = jnp.sum(total, axis=0, keepdims=True)
        sums = jnp.concatenate([gain_sum, shift_sum, sums2[...]], axis=0)
        high = sums.astype(BF16).astype(F32)
        tail = jnp.concatenate([high, sums - high, jnp.zeros((8, sums.shape[1]), F32)], axis=0)
        grad = standardize_back(total * gain1[...], x, inverse[...])
        d_h1[...] = grad
        sent[0:rows, :] = grad.astype(BF16)
        sent[rows : rows + 16, :] = tail.astype(BF16)


def ffn_backward(d_ff, d_h2, unit, inverse, gain1, sums2, act, slope, w_in, w_out, size):
    rows, width = d_ff.shape
    hid = w_out.shape[0]
    count = hid // size
    full = lambda dims: pl.BlockSpec(dims, lambda j: (0, 0))
    part = pl.BlockSpec((rows, size), lambda j: (0, j))
    return pl.pallas_call(
        ffn_backward_kernel,
        name="ffn_backward",
        grid=(count,),
        out_shape=(shape((rows, width), F32), shape((rows + 16, width), BF16)),
        in_specs=[full((rows, width))] * 3
        + [
            full((rows, 1)),
            full((1, width)),
            full((2, width)),
            part,
            part,
            pl.BlockSpec((width, size), lambda j: (0, j)),
            pl.BlockSpec((width, size), lambda j: (0, count + j)),
            pl.BlockSpec((size, width), lambda j: (j, 0)),
        ],
        out_specs=(full((rows, width)), full((rows + 16, width))),
        scratch_shapes=[scratch((rows, width), F32)],
        compiler_params=params(48),
        cost_estimate=pl.CostEstimate(
            flops=6 * rows * width * hid, bytes_accessed=20 * 10**6, transcendentals=0
        ),
    )(d_ff, d_h2, unit, inverse, gain1, sums2, act, slope, w_in, w_in, w_out)


def ffn_grad_kernel(
    info, n0, n1, n2, n3, f0, f1, f2, f3, w_gate, w_up, w_down, g_gate, g_up, g_down,
    tok, tok_t, d_ff,
):
    rows = n0.shape[0]

    @pl.when(pl.program_id(0) == 0)
    def _():
        for at, (n, f) in enumerate(zip((n0, n1, n2, n3), (f0, f1, f2, f3))):
            here = pl.ds(at * rows, rows)
            tok[here, :] = n[...]
            d_ff[here, :] = f[...]
            tok_t[:, here] = jnp.transpose(n[...])

    gate = dot(tok[...], w_gate[...])
    up = dot(tok[...], w_up[...])
    value, grad = gelu_pair(gate)
    g_down[...] = dot_tn((value * up).astype(BF16), d_ff[...]).astype(BF16)
    d_hidden = dot_nt(d_ff[...], w_down[...])
    g_gate[...] = dot(tok_t[...], (d_hidden * up * grad).astype(BF16)).astype(BF16)
    g_up[...] = dot(tok_t[...], (d_hidden * value).astype(BF16)).astype(BF16)


def ffn_grad(info, toks, grads, w_in, w_out, size):
    rows, width = toks[0].shape
    part = w_out.shape[0] // RANKS
    count = part // size
    tok = rows * RANKS
    full = pl.BlockSpec((rows, width), lambda j, info: (0, 0))
    wide = lambda where: pl.BlockSpec((width, size), lambda j, info: (0, where(j, info)))
    tall = lambda where: pl.BlockSpec((size, width), lambda j, info: (where(j, info), 0))
    return pl.pallas_call(
        ffn_grad_kernel,
        name="ffn_grad",
        out_shape=(shape((width, part), BF16), shape((width, part), BF16), shape((part, width), BF16)),
        grid_spec=pltpu.PrefetchScalarGridSpec(
            num_scalar_prefetch=1,
            grid=(count,),
            in_specs=[full] * 8
            + [
                wide(lambda j, info: info[0] * count + j),
                wide(lambda j, info: (RANKS + info[0]) * count + j),
                tall(lambda j, info: info[0] * count + j),
            ],
            out_specs=(
                wide(lambda j, info: j),
                wide(lambda j, info: j),
                tall(lambda j, info: j),
            ),
            scratch_shapes=[
                scratch((tok, width), BF16),
                scratch((width, tok), BF16),
                scratch((tok, width), BF16),
            ],
        ),
        compiler_params=params(48),
        cost_estimate=pl.CostEstimate(
            flops=12 * tok * width * part, bytes_accessed=14 * 10**6, transcendentals=2 * tok * part
        ),
    )(info, *toks, *grads, w_in, w_in, w_out)


def out_grad_kernel(out_t, g0, g1, g2, g3, grad, sums):
    rows = g0.shape[0] - 16
    total = 0.0
    extra = 0.0
    for at, g in enumerate((g0, g1, g2, g3)):
        total = total + dot(out_t[:, at * rows : (at + 1) * rows], g[0:rows, :])
        pair = g[rows : rows + 16, :].astype(F32)
        extra = extra + pair[0:4] + pair[4:8]
    grad[...] = total.astype(BF16)
    sums[...] = extra


def out_grad(out_t, blocks):
    width = blocks[0].shape[1]
    return pl.pallas_call(
        out_grad_kernel,
        name="out_grad",
        out_shape=(shape((out_t.shape[0], width), BF16), shape((4, width), F32)),
        in_specs=[VM] * 5,
        out_specs=(VM, VM),
        cost_estimate=pl.CostEstimate(
            flops=2 * out_t.shape[0] * out_t.shape[1] * width,
            bytes_accessed=3 * 10**6,
            transcendentals=0,
        ),
    )(out_t, *blocks)


def qkv_grad_kernel(x0, x1, x2, x3, d_qkv, grad):
    total = 0.0
    for at, x in enumerate((x0, x1, x2, x3)):
        total = total + dot_tn(x[...], d_qkv[at])
    grad[...] = total.astype(BF16)


def qkv_grad(blocks, d_qkv):
    rows, width = blocks[0].shape
    return pl.pallas_call(
        qkv_grad_kernel,
        name="qkv_grad",
        out_shape=shape((width, d_qkv.shape[2]), BF16),
        in_specs=[VM] * 5,
        out_specs=VM,
        cost_estimate=pl.CostEstimate(
            flops=8 * rows * width * d_qkv.shape[2], bytes_accessed=4 * 10**6, transcendentals=0
        ),
    )(*blocks, d_qkv)


def token_grad_kernel(
    info, own, near, far, cross, w, d_h1, masked_row, masked_col, tokens, replacement, joined
):
    rank = info[0]
    rows, width = d_h1.shape
    part = near.shape[1] // 3
    for value in range(RANKS):

        @pl.when(rank == value)
        def _():
            for step, block in enumerate((own[0], near[...], far[0], cross[...])):
                for third in range(3):
                    first = third * width + (value ^ step) * part
                    joined[:, first : first + part] = block[:, third * part : (third + 1) * part]

    grad = d_h1[...] + dot_nt(joined[...], w[...])
    count = masked_row.shape[1]
    places = lax.broadcasted_iota(jnp.int32, (rows, count), 0)
    hit = jnp.max((places == masked_row[...]).astype(F32), axis=1, keepdims=True)
    tokens[...] = jnp.where(hit > 0.5, 0.0, grad)
    places = lax.broadcasted_iota(jnp.int32, (count, rows), 1)
    replacement[...] = exact_dot((places == masked_col[...]).astype(F32), grad)


def token_grad(info, own, near, far, cross, w, d_h1, masked):
    rows, width = d_h1.shape
    count = masked.shape[0]
    return pl.pallas_call(
        token_grad_kernel,
        name="token_grad",
        out_shape=(shape((rows, width), F32), shape((count, width), F32)),
        in_specs=[SM] + [VM] * 8,
        out_specs=(VM, VM),
        scratch_shapes=[scratch((rows, 3 * width), BF16)],
        cost_estimate=pl.CostEstimate(
            flops=6 * rows * width * width, bytes_accessed=8 * 10**6, transcendentals=0
        ),
    )(info, own, near, far, cross, w, d_h1, masked.reshape(1, count), masked.reshape(count, 1))


def flip(value, axis, bits):
    count = lax.axis_size(axis)
    return lax.ppermute(value, axis, [(index, index ^ bits) for index in range(count)])


def gather_blocks(value):
    far = flip(value, "sp", 2)
    near = flip(value, "sp", 1)
    cross = flip(far, "sp", 1)
    return [value, near, far, cross]


def exchange_blocks(blocks):
    far = flip(blocks[2:4], "sp", 2)
    near = flip(blocks[1], "sp", 1)
    cross = flip(far[1], "sp", 1)
    return blocks, near, far, cross


def pick(value, index):
    return lax.dynamic_index_in_dim(value, index, 0, keepdims=False)


def natural_order(blocks, rank):
    stacked = jnp.stack(blocks)
    return [pick(stacked, rank ^ index) for index in range(len(blocks))]


def split_sum(value):
    high = value.astype(BF16)
    low = (value - high.astype(F32)).astype(BF16)
    return jnp.concatenate([high, low], axis=0)


def join_sum(pair):
    half = pair.shape[0] // 2
    return pair[:half].astype(F32) + pair[half:].astype(F32)


def reduce_rows(grad):
    count = lax.axis_size("dp")
    if count != 8:
        return lax.psum_scatter(grad.astype(F32), "dp", scatter_dimension=0, tiled=True)
    place = lax.axis_index("dp")
    outer, inner = place // 2, place % 2
    view = grad.reshape(4, 2, grad.shape[0] // 8, grad.shape[1])
    keep = lax.dynamic_index_in_dim(view, inner, 1, keepdims=False)
    send = lax.dynamic_index_in_dim(view, 1 - inner, 1, keepdims=False)
    came = flip(send, "dp", 1)
    total = pick(keep, outer).astype(F32) + pick(came, outer).astype(F32)
    for step in (1, 2, 3):
        part = pick(keep, outer ^ step).astype(F32) + pick(came, outer ^ step).astype(F32)
        total = total + flip(part.astype(BF16), "dp", 2 * step).astype(F32)
    return total


def reduce_quarter_rows(pieces, sums):
    count = lax.axis_size("dp")
    if count != 8:
        moves = []
        for place in range(count):
            for quarter in range(4):
                target = quarter * (count // 4) + place // 4
                moves.append((place * 4 + quarter, target * 4 + place % 4))
        results = []
        for grad in pieces:
            shard = lax.psum_scatter(grad.astype(F32), "dp", scatter_dimension=0, tiled=True)
            results.append(lax.ppermute(shard, ("dp", "sp"), moves))
        return results, lax.psum(sums, "dp")
    place = lax.axis_index("dp")
    outer, inner = place // 2, place % 2
    width = pieces[0].shape[1]
    sizes = [grad.shape[0] // 8 for grad in pieces]
    packed = jnp.concatenate(
        [grad.reshape(2, 4, size, width) for grad, size in zip(pieces, sizes)], axis=2
    ).astype(BF16)
    each = packed.shape[2]
    keep = pick(packed, inner)
    send = pick(packed, 1 - inner).reshape(4 * each, width)
    came = flip(jnp.concatenate([send, split_sum(sums)], axis=0), "dp", 1)
    sums = sums + join_sum(came[4 * each :])
    came = came[: 4 * each].reshape(4, each, width)
    total = 0.0
    for step in range(4):
        moves = []
        for z in range(4):
            for x in range(2):
                for quarter in range(4):
                    moves.append(((z * 2 + x) * 4 + quarter, (quarter * 2 + x) * 4 + (z ^ step)))
        part = pick(keep, outer ^ step).astype(F32) + pick(came, outer ^ step).astype(F32)
        part = jnp.concatenate([part.astype(BF16), split_sum(sums)], axis=0)
        part = lax.ppermute(part, ("dp", "sp"), moves)
        part = jnp.concatenate([part[:each].astype(F32), join_sum(part[each:])], axis=0)
        total = total + part
    results = []
    first = 0
    for size in sizes:
        results.append(total[first : first + size])
        first += size
    return results, total[each:]


def local(
    tokens,
    segment_ids,
    masked_rows,
    replacement,
    cotangent,
    w_qkv,
    w_out_attn,
    w_in_ff,
    w_out_ff,
    gain_one,
    shift_one,
    gain_two,
    shift_two,
):
    rows_dev, width = tokens.shape
    rank = lax.axis_index("sp")
    heads = HEADS // RANKS
    dim = width // HEADS
    part = heads * dim
    group_seg = segment_ids[0].astype(jnp.int32)
    info = jnp.concatenate([rank.astype(jnp.int32).reshape(1), group_seg])
    seg_rows = group_seg.reshape(1, -1)
    slopes = alibi_slopes(HEADS)
    gain_one, shift_one = gain_one.reshape(1, -1), shift_one.reshape(1, -1)
    gain_two, shift_two = gain_two.reshape(1, -1), shift_two.reshape(1, -1)

    select = jnp.arange(rows_dev, dtype=jnp.int32)[:, None] == masked_rows[None, :]
    hit = jnp.any(select, axis=1, keepdims=True)
    placed = dot(select.astype(BF16), replacement)
    start = jnp.where(hit, placed.astype(BF16), tokens)
    start_blocks = gather_blocks(start)

    w_rank = jnp.concatenate(
        [
            lax.dynamic_slice_in_dim(w_qkv, third * width + rank * part, part, 1)
            for third in range(3)
        ],
        axis=1,
    )
    qkv, attn, attn_t, lse = attention_forward(
        info, slopes, start_blocks, w_rank, seg_rows, heads, dim
    )
    own, near, far, cross = exchange_blocks(attn)
    low, unit, inverse = norm_one(
        info, own, near, far, cross, start, w_out_attn, gain_one, shift_one
    )
    low_blocks = gather_blocks(low)
    layer_out, d_h2, d_ff, slope, act, sums2 = ffn_forward(
        low, unit, gain_one, shift_one, gain_two, shift_two,
        masked_rows.reshape(1, -1), cotangent, w_in_ff, w_out_ff, 512,
    )
    d_ff_blocks = gather_blocks(d_ff)
    d_h1, sent = ffn_backward(
        d_ff, d_h2, unit, inverse, gain_one, sums2, act, slope, w_in_ff, w_out_ff, 512
    )
    d_proj_blocks = gather_blocks(sent)
    g_gate, g_up, g_down = ffn_grad(info, low_blocks, d_ff_blocks, w_in_ff, w_out_ff, 256)
    g_out, norm_sums = out_grad(attn_t, d_proj_blocks)
    share_gate = reduce_rows(g_gate)
    share_up = reduce_rows(g_up)
    (share_down, share_out), norm_sums = reduce_quarter_rows([g_down, g_out], norm_sums)

    d_qkv = attention_backward(
        info, slopes, d_proj_blocks, w_out_attn, qkv, lse, seg_rows, heads, dim
    )
    g_qkv = qkv_grad(start_blocks, d_qkv)
    share_qkv = reduce_rows(g_qkv)
    own, near, far, cross = exchange_blocks(d_qkv)
    grad_tokens, grad_replacement = token_grad(
        info, own, near, far, cross, w_qkv, d_h1, masked_rows
    )

    def columns(share, halves):
        blocks = natural_order(gather_blocks(share.astype(BF16)), rank)
        each = share.shape[1] // halves
        parts = [block[:, i * each : (i + 1) * each] for i in range(halves) for block in blocks]
        return jnp.concatenate(parts, axis=1).astype(F32)

    def rows(share):
        blocks = natural_order(gather_blocks(share.astype(BF16)), rank)
        return jnp.concatenate(blocks, axis=0).astype(F32)

    return (
        layer_out,
        grad_tokens,
        grad_replacement,
        columns(share_qkv, 3),
        rows(share_out),
        columns(jnp.concatenate([share_gate, share_up], axis=1), 2),
        rows(share_down),
        norm_sums[0],
        norm_sums[1],
        norm_sums[2],
        norm_sums[3],
    )


def solution(mesh):
    tokens = P(("dp", "sp"), None)
    rows = P("dp", None)
    return jax.shard_map(
        local,
        mesh=mesh,
        in_specs=(tokens, rows, P(("dp", "sp")), tokens, tokens) + (P(),) * 8,
        out_specs=(tokens,) * 3 + (rows,) * 4 + (P(),) * 4,
        check_vma=False,
    )
```

```python
import functools
import math

import jax
import jax.numpy as jnp
from jax import lax
from jax.experimental import pallas as pl
from jax.experimental.pallas import tpu as pltpu
from jax.sharding import PartitionSpec as P

HEADS = 12
RANKS = 4
EPSILON = 1e-05
FAR = 1e30
F32 = jnp.float32
BF16 = jnp.bfloat16
VM = pl.BlockSpec(memory_space=pltpu.VMEM)
SM = pl.BlockSpec(memory_space=pltpu.SMEM)


def shape(dims, kind):
    return jax.ShapeDtypeStruct(dims, kind)


def scratch(dims, kind):
    return pltpu.VMEM(dims, kind)


def params(mebibytes):
    return pltpu.CompilerParams(vmem_limit_bytes=mebibytes << 20)


def alibi_slopes(head_count):
    nearest = 2 ** int(math.floor(math.log2(head_count)))
    base_list = [2.0 ** (-8.0 * (index + 1) / nearest) for index in range(nearest)]
    extra_list = [
        2.0 ** (-8.0 * (2 * index + 1) / (2 * nearest)) for index in range(head_count - nearest)
    ]
    return jnp.array(base_list + extra_list, dtype=F32)


def dot(a, b):
    return jnp.dot(a, b, preferred_element_type=F32)


def dot_nt(a, b):
    return lax.dot_general(a, b, (((1,), (1,)), ((), ())), preferred_element_type=F32)


def dot_tn(a, b):
    return lax.dot_general(a, b, (((0,), (0,)), ((), ())), preferred_element_type=F32)


def exact_dot(a, b):
    return jnp.dot(a, b, precision=lax.Precision.HIGHEST, preferred_element_type=F32)


def standardize(value):
    center = value - jnp.mean(value, axis=-1, keepdims=True)
    spread = jnp.mean(center * center, axis=-1, keepdims=True)
    inverse = lax.rsqrt(spread + EPSILON)
    return center * inverse, inverse


def standardize_back(grad, unit, inverse):
    mean = jnp.mean(grad, axis=-1, keepdims=True)
    return inverse * (grad - mean - unit * jnp.mean(grad * unit, axis=-1, keepdims=True))


def gelu_pair(x):
    cdf = 0.5 * (1.0 + lax.erf(x * math.sqrt(0.5)))
    pdf = jnp.exp(-0.5 * x * x) * (1.0 / math.sqrt(2.0 * math.pi))
    return x * cdf, cdf + x * pdf


def pair_active(info, rank, first, second, rows):
    one, two = rank ^ first, rank ^ second
    low, high = jnp.minimum(one, two), jnp.maximum(one, two)
    return jnp.logical_or(one == two, info[low * rows + rows] == info[high * rows + 1])


def pair_distance(seg_rows, rank, keys_at, query_at, rows):
    key_pos, query_pos = (rank ^ keys_at) * rows, (rank ^ query_at) * rows
    down = lax.broadcasted_iota(jnp.int32, (rows, rows), 0)
    across = lax.broadcasted_iota(jnp.int32, (rows, rows), 1)
    gap = jnp.abs(down - across + (key_pos - query_pos)).astype(F32)
    seg_q = seg_rows[:, pl.ds(pl.multiple_of(query_pos, rows), rows)]
    seg_k = seg_rows[:, pl.ds(pl.multiple_of(key_pos, rows), rows)]
    seg_k = jnp.transpose(jnp.broadcast_to(seg_k, (128, rows)))[:, :1]
    return jnp.where(seg_k == seg_q, gap, FAR)


def attention_forward_kernel(
    rows, heads, dim, info, slopes, x0, x1, x2, x3, w, seg_rows,
    qkv_out, o0, o1, o2, o3, out_t, lse, qs, ks, vt, dist, acc, peak, total,
):
    rank = info[0]
    width = heads * dim
    for at, x in enumerate((x0, x1, x2, x3)):
        qkv = dot(x[...], w[...]).astype(BF16)
        here = pl.ds(at * rows, rows)
        qkv_out[here, :] = qkv
        for h in range(heads):
            qs[h, here, :] = (qkv[:, h * dim : (h + 1) * dim] * dim**-0.5).astype(BF16)
            ks[h, here, :] = qkv[:, width + h * dim : width + (h + 1) * dim]
        vt[:, here] = jnp.transpose(qkv[:, 2 * width :])

    for a, out in enumerate((o0, o1, o2, o3)):
        mine = pl.ds(a * rows, rows)
        peak[...] = jnp.full_like(peak, -jnp.inf)
        total[...] = jnp.zeros_like(total)
        acc[...] = jnp.zeros_like(acc)

        def key_block(b, carry):
            @pl.when(pair_active(info, rank, a, b, rows))
            def _():
                theirs = pl.ds(pl.multiple_of(b * rows, rows), rows)
                dist[...] = pair_distance(seg_rows, rank, b, a, rows)
                for h in range(heads):
                    slope = slopes[rank * heads + h]
                    s = dot_nt(ks[h, theirs, :], qs[h, mine, :]) - slope * dist[...]
                    old = peak[h : h + 1, :]
                    new = jnp.maximum(old, jnp.max(s, axis=0, keepdims=True))
                    p = jnp.exp(s - new)
                    fade = jnp.exp(old - new)
                    add = jnp.sum(p, axis=0, keepdims=True)
                    total[h : h + 1, :] = total[h : h + 1, :] * fade + add
                    peak[h : h + 1, :] = new
                    span = slice(h * dim, (h + 1) * dim)
                    acc[span, :] = acc[span, :] * fade + dot(vt[span, theirs], p.astype(BF16))

            return carry

        lax.fori_loop(0, RANKS, key_block, 0)
        for h in range(heads):
            span = slice(h * dim, (h + 1) * dim)
            acc[span, :] = acc[span, :] / total[h : h + 1, :]
            lse[h : h + 1, mine] = peak[h : h + 1, :] + jnp.log(total[h : h + 1, :])
        value = acc[...].astype(BF16)
        out_t[:, mine] = value
        out[...] = jnp.transpose(value)


def attention_forward(info, slopes, blocks, w, seg_rows, heads, dim):
    rows = blocks[0].shape[0]
    tok, lw = rows * RANKS, heads * dim
    results = pl.pallas_call(
        functools.partial(attention_forward_kernel, rows, heads, dim),
        name="attention_forward",
        out_shape=(shape((tok, 3 * lw), BF16),)
        + (shape((rows, lw), BF16),) * RANKS
        + (shape((lw, tok), BF16), shape((heads, tok), F32)),
        in_specs=[SM, SM] + [VM] * 6,
        out_specs=(VM,) * 7,
        scratch_shapes=[
            scratch((heads, tok, dim), BF16),
            scratch((heads, tok, dim), BF16),
            scratch((lw, tok), BF16),
            scratch((rows, rows), F32),
            scratch((lw, rows), F32),
            scratch((heads, rows), F32),
            scratch((heads, rows), F32),
        ],
        compiler_params=params(40),
        cost_estimate=pl.CostEstimate(
            flops=4 * 10**9, bytes_accessed=6 * 10**6, transcendentals=3 * 10**6
        ),
    )(info, slopes, *blocks, w, seg_rows)
    return results[0], results[1:5], results[5], results[6]


def attention_backward_kernel(
    rows, heads, dim, info, slopes, g0, g1, g2, g3, w, qkv, lse, seg_rows,
    d0, d1, d2, d3, qs, ks, kt, vs, do, dist, prob, dprob, dk, dv, dqt, delta,
):
    rank = info[0]
    width = heads * dim
    scale = dim**-0.5
    w_rank = w[pl.ds(pl.multiple_of(rank * width, width), width), :]
    for at, g in enumerate((g0, g1, g2, g3)):
        here = pl.ds(at * rows, rows)
        grad = dot_nt(g[0:rows, :], w_rank).astype(BF16)
        value = qkv[here, :]
        kt[:, here] = jnp.transpose(value[:, width : 2 * width])
        for h in range(heads):
            do[h, here, :] = grad[:, h * dim : (h + 1) * dim]
            qs[h, here, :] = (value[:, h * dim : (h + 1) * dim] * scale).astype(BF16)
            ks[h, here, :] = value[:, width + h * dim : width + (h + 1) * dim]
            vs[h, here, :] = value[:, 2 * width + h * dim : 2 * width + (h + 1) * dim]
    dk[...] = jnp.zeros_like(dk)
    dv[...] = jnp.zeros_like(dv)

    for a, d_qkv in enumerate((d0, d1, d2, d3)):
        mine = pl.ds(a * rows, rows)
        delta[...] = jnp.zeros_like(delta)
        dqt[...] = jnp.zeros_like(dqt)

        def first_pass(b, carry):
            @pl.when(pair_active(info, rank, a, b, rows))
            def _():
                theirs = pl.ds(pl.multiple_of(b * rows, rows), rows)
                dist[...] = pair_distance(seg_rows, rank, b, a, rows)
                for h in range(heads):
                    slope = slopes[rank * heads + h]
                    s = dot_nt(ks[h, theirs, :], qs[h, mine, :]) - slope * dist[...]
                    p = jnp.exp(s - lse[h : h + 1, mine])
                    dp = dot_nt(vs[h, theirs, :], do[h, mine, :])
                    delta[h : h + 1, :] += jnp.sum(p * dp, axis=0, keepdims=True)
                    prob[h, theirs, :] = p
                    dprob[h, theirs, :] = dp

            return carry

        lax.fori_loop(0, RANKS, first_pass, 0)

        def second_pass(b, carry):
            @pl.when(pair_active(info, rank, a, b, rows))
            def _():
                theirs = pl.ds(pl.multiple_of(b * rows, rows), rows)
                for h in range(heads):
                    p = prob[h, theirs, :]
                    ds = (p * (dprob[h, theirs, :] - delta[h : h + 1, :])).astype(BF16)
                    dv[h, theirs, :] += dot(p.astype(BF16), do[h, mine, :])
                    dk[h, theirs, :] += dot(ds, qs[h, mine, :])
                    span = slice(h * dim, (h + 1) * dim)
                    dqt[span, :] += dot(kt[span, theirs], ds)

            return carry

        lax.fori_loop(0, RANKS, second_pass, 0)
        d_qkv[:, 0:width] = jnp.transpose(dqt[...] * scale).astype(BF16)

    for at, d_qkv in enumerate((d0, d1, d2, d3)):
        here = pl.ds(at * rows, rows)
        for h in range(heads):
            first = width + h * dim
            d_qkv[:, first : first + dim] = dk[h, here, :].astype(BF16)
            first = 2 * width + h * dim
            d_qkv[:, first : first + dim] = dv[h, here, :].astype(BF16)


def attention_backward(info, slopes, blocks, w, qkv, lse, seg_rows, heads, dim):
    tok, lw = qkv.shape[0], heads * dim
    rows = tok // RANKS
    return pl.pallas_call(
        functools.partial(attention_backward_kernel, rows, heads, dim),
        name="attention_backward",
        out_shape=(shape((rows, 3 * lw), BF16),) * RANKS,
        in_specs=[SM, SM] + [VM] * 8,
        out_specs=(VM,) * RANKS,
        scratch_shapes=[
            scratch((heads, tok, dim), BF16),
            scratch((heads, tok, dim), BF16),
            scratch((lw, tok), BF16),
            scratch((heads, tok, dim), BF16),
            scratch((heads, tok, dim), BF16),
            scratch((rows, rows), F32),
            scratch((heads, tok, rows), F32),
            scratch((heads, tok, rows), F32),
            scratch((heads, tok, dim), F32),
            scratch((heads, tok, dim), F32),
            scratch((lw, rows), F32),
            scratch((heads, rows), F32),
        ],
        compiler_params=params(48),
        cost_estimate=pl.CostEstimate(
            flops=8 * 10**9, bytes_accessed=6 * 10**6, transcendentals=3 * 10**6
        ),
    )(info, slopes, *blocks, w, qkv, lse, seg_rows)


def norm_one_kernel(
    info, own, near, far, cross, start, w, gain, shift, low, unit, inverse
):
    rank = info[0]
    part_width = near.shape[1]
    total = start[...].astype(F32)
    for step, part in enumerate((own, near, far, cross)):
        rows = pl.ds(pl.multiple_of((rank ^ step) * part_width, part_width), part_width)
        total = total + dot(part[...], w[rows, :])
    x, inv = standardize(total)
    unit[...] = x
    inverse[...] = inv
    low[...] = (x * gain[...] + shift[...]).astype(BF16)


def norm_one(info, own, near, far, cross, start, w, gain, shift):
    rows, width = start.shape
    return pl.pallas_call(
        norm_one_kernel,
        name="norm_one",
        out_shape=(shape((rows, width), BF16), shape((rows, width), F32), shape((rows, 1), F32)),
        in_specs=[SM] + [VM] * 8,
        out_specs=(VM,) * 3,
        cost_estimate=pl.CostEstimate(
            flops=2 * rows * width * width, bytes_accessed=4 * 10**6, transcendentals=0
        ),
    )(info, own, near, far, cross, start, w, gain, shift)


def ffn_forward_kernel(
    low, unit, gain1, shift1, gain2, shift2, masked, cot, w_gate, w_up, w_down,
    layer_out, d_h2, d_ff, slope, act, sums, acc,
):
    step = pl.program_id(0)
    gate = dot(low[...], w_gate[...])
    up = dot(low[...], w_up[...])
    value, grad = gelu_pair(gate)
    act[...] = value.astype(BF16)
    slope[...] = (up * grad).astype(BF16)
    part = dot((value * up).astype(BF16), w_down[...])

    @pl.when(step == 0)
    def _():
        acc[...] = unit[...] * gain1[...] + shift1[...] + part

    @pl.when(step > 0)
    def _():
        acc[...] += part

    @pl.when(step == pl.num_programs(0) - 1)
    def _():
        x, inv = standardize(acc[...])
        layer_out[...] = (x * gain2[...] + shift2[...]).astype(BF16)
        places = lax.broadcasted_iota(jnp.int32, (low.shape[0], masked.shape[1]), 0)
        dy = exact_dot((places == masked[...]).astype(F32), cot[...])
        sums[0:1, :] = jnp.sum(dy * x, axis=0, keepdims=True)
        sums[1:2, :] = jnp.sum(dy, axis=0, keepdims=True)
        grad_in = standardize_back(dy * gain2[...], x, inv)
        d_h2[...] = grad_in
        d_ff[...] = grad_in.astype(BF16)


def ffn_forward(low, unit, gain1, shift1, gain2, shift2, masked, cot, w_in, w_out, size):
    rows, width = low.shape
    hid = w_out.shape[0]
    count = hid // size
    full = lambda dims: pl.BlockSpec(dims, lambda j: (0, 0))
    act = pl.BlockSpec((rows, size), lambda j: (0, j))
    return pl.pallas_call(
        ffn_forward_kernel,
        name="ffn_forward",
        grid=(count,),
        out_shape=(
            shape((rows, width), BF16),
            shape((rows, width), F32),
            shape((rows, width), BF16),
            shape((rows, hid), BF16),
            shape((rows, hid), BF16),
            shape((2, width), F32),
        ),
        in_specs=[full((rows, width))] * 2
        + [full((1, width))] * 4
        + [
            full(masked.shape),
            full(cot.shape),
            pl.BlockSpec((width, size), lambda j: (0, j)),
            pl.BlockSpec((width, size), lambda j: (0, count + j)),
            pl.BlockSpec((size, width), lambda j: (j, 0)),
        ],
        out_specs=(full((rows, width)),) * 3 + (act, act, full((2, width))),
        scratch_shapes=[scratch((rows, width), F32)],
        compiler_params=params(48),
        cost_estimate=pl.CostEstimate(
            flops=6 * rows * width * hid, bytes_accessed=18 * 10**6, transcendentals=2 * rows * hid
        ),
    )(low, unit, gain1, shift1, gain2, shift2, masked, cot, w_in, w_in, w_out)


def ffn_backward_kernel(
    d_ff, d_h2, unit, inverse, gain1, sums2, act, slope, w_gate, w_up, w_down, d_h1, sent, acc
):
    step = pl.program_id(0)
    d_hidden = dot_nt(d_ff[...], w_down[...])
    d_gate = (d_hidden * slope[...].astype(F32)).astype(BF16)
    d_up = (d_hidden * act[...].astype(F32)).astype(BF16)
    part = dot_nt(d_gate, w_gate[...]) + dot_nt(d_up, w_up[...])

    @pl.when(step == 0)
    def _():
        acc[...] = d_h2[...] + part

    @pl.when(step > 0)
    def _():
        acc[...] += part

    @pl.when(step == pl.num_programs(0) - 1)
    def _():
        total = acc[...]
        rows = total.shape[0]
        x = unit[...]
        gain_sum = jnp.sum(total * x, axis=0, keepdims=True)
        shift_sum = jnp.sum(total, axis=0, keepdims=True)
        sums = jnp.concatenate([gain_sum, shift_sum, sums2[...]], axis=0)
        high = sums.astype(BF16).astype(F32)
        tail = jnp.concatenate([high, sums - high, jnp.zeros((8, sums.shape[1]), F32)], axis=0)
        grad = standardize_back(total * gain1[...], x, inverse[...])
        d_h1[...] = grad
        sent[0:rows, :] = grad.astype(BF16)
        sent[rows : rows + 16, :] = tail.astype(BF16)


def ffn_backward(d_ff, d_h2, unit, inverse, gain1, sums2, act, slope, w_in, w_out, size):
    rows, width = d_ff.shape
    hid = w_out.shape[0]
    count = hid // size
    full = lambda dims: pl.BlockSpec(dims, lambda j: (0, 0))
    part = pl.BlockSpec((rows, size), lambda j: (0, j))
    return pl.pallas_call(
        ffn_backward_kernel,
        name="ffn_backward",
        grid=(count,),
        out_shape=(shape((rows, width), F32), shape((rows + 16, width), BF16)),
        in_specs=[full((rows, width))] * 3
        + [
            full((rows, 1)),
            full((1, width)),
            full((2, width)),
            part,
            part,
            pl.BlockSpec((width, size), lambda j: (0, j)),
            pl.BlockSpec((width, size), lambda j: (0, count + j)),
            pl.BlockSpec((size, width), lambda j: (j, 0)),
        ],
        out_specs=(full((rows, width)), full((rows + 16, width))),
        scratch_shapes=[scratch((rows, width), F32)],
        compiler_params=params(48),
        cost_estimate=pl.CostEstimate(
            flops=6 * rows * width * hid, bytes_accessed=20 * 10**6, transcendentals=0
        ),
    )(d_ff, d_h2, unit, inverse, gain1, sums2, act, slope, w_in, w_in, w_out)


def store_blocks(grad, keep, send, info, columns):
    outer, inner = info[1], info[2]
    each = grad.shape[0] // 8
    for index in range(4):
        even = grad[2 * index * each : (2 * index + 1) * each]
        odd = grad[(2 * index + 1) * each : (2 * index + 2) * each]
        keep[index ^ outer, :, columns] = jnp.where(inner == 0, even, odd).astype(BF16)
        send[index ^ outer, :, columns] = jnp.where(inner == 0, odd, even).astype(BF16)


def ffn_grad_kernel(
    joint, info, n0, n1, n2, n3, f0, f1, f2, f3, w_gate, w_up, w_down, *rest
):
    if joint:
        keep_gate, send_gate, g_down, tok, tok_t, d_ff = rest
        keep_up, send_up = keep_gate, send_gate
    else:
        keep_gate, send_gate, keep_up, send_up, g_down, tok, tok_t, d_ff = rest
    rows = n0.shape[0]
    size = w_gate.shape[1]

    @pl.when(pl.program_id(0) == 0)
    def _():
        for at, (n, f) in enumerate(zip((n0, n1, n2, n3), (f0, f1, f2, f3))):
            here = pl.ds(at * rows, rows)
            tok[here, :] = n[...]
            d_ff[here, :] = f[...]
            tok_t[:, here] = jnp.transpose(n[...])

    gate = dot(tok[...], w_gate[...])
    up = dot(tok[...], w_up[...])
    value, grad = gelu_pair(gate)
    g_down[...] = dot_tn((value * up).astype(BF16), d_ff[...]).astype(BF16)
    d_hidden = dot_nt(d_ff[...], w_down[...])
    g_gate = dot(tok_t[...], (d_hidden * up * grad).astype(BF16))
    g_up = dot(tok_t[...], (d_hidden * value).astype(BF16))
    store_blocks(g_gate, keep_gate, send_gate, info, slice(0, size))
    first = size if joint else 0
    store_blocks(g_up, keep_up, send_up, info, slice(first, first + size))


def ffn_grad(info, toks, grads, w_in, w_out, size, first, steps):
    rows, width = toks[0].shape
    count = w_out.shape[0] // RANKS // size
    tok = rows * RANKS
    joint = steps == 1
    full = pl.BlockSpec((rows, width), lambda j, info: (0, 0))
    wide = lambda base: pl.BlockSpec(
        (width, size), lambda j, info: (0, (base + info[0]) * count + first + j)
    )
    columns = 2 * size if joint else size
    blocks = shape((4, width // 8, columns * steps), BF16)
    block_spec = pl.BlockSpec((4, width // 8, columns), lambda j, info: (0, 0, j))
    outs = 2 if joint else 4
    return pl.pallas_call(
        functools.partial(ffn_grad_kernel, joint),
        name="ffn_grad",
        out_shape=(blocks,) * outs + (shape((size * steps, width), BF16),),
        grid_spec=pltpu.PrefetchScalarGridSpec(
            num_scalar_prefetch=1,
            grid=(steps,),
            in_specs=[full] * 8
            + [
                wide(0),
                wide(RANKS),
                pl.BlockSpec((size, width), lambda j, info: (info[0] * count + first + j, 0)),
            ],
            out_specs=(block_spec,) * outs + (pl.BlockSpec((size, width), lambda j, info: (j, 0)),),
            scratch_shapes=[
                scratch((tok, width), BF16),
                scratch((width, tok), BF16),
                scratch((tok, width), BF16),
            ],
        ),
        compiler_params=params(48),
        cost_estimate=pl.CostEstimate(
            flops=12 * tok * width * size * steps,
            bytes_accessed=8 * 10**6,
            transcendentals=2 * tok * size * steps,
        ),
    )(info, *toks, *grads, w_in, w_in, w_out)


def row_grad_kernel(info, out_t, g0, g1, g2, g3, down_a, down_b, keep, send):
    outer, inner = info[1], info[2]
    rows = g0.shape[0] - 16
    grad = 0.0
    sums = 0.0
    for at, g in enumerate((g0, g1, g2, g3)):
        grad = grad + dot(out_t[:, at * rows : (at + 1) * rows], g[0:rows, :])
        pair = g[rows : rows + 16, :].astype(F32)
        sums = sums + pair[0:4] + pair[4:8]
    high = sums.astype(BF16).astype(F32)
    tail = jnp.concatenate([high, sums - high], axis=0)
    down = jnp.concatenate([down_a[...], down_b[...]], axis=0).astype(F32)
    many, few = down.shape[0] // 8, grad.shape[0] // 8
    for index in range(4):
        parts = []
        for bit in range(2):
            at = bit * 4 + index
            parts.append(
                jnp.concatenate(
                    [down[at * many : (at + 1) * many], grad[at * few : (at + 1) * few], tail], axis=0
                )
            )
        keep[index ^ outer] = jnp.where(inner == 0, parts[0], parts[1]).astype(BF16)
        send[index ^ outer] = jnp.where(inner == 0, parts[1], parts[0]).astype(BF16)


def row_grad(info, out_t, blocks, down_a, down_b):
    width = blocks[0].shape[1]
    each = (down_a.shape[0] + down_b.shape[0] + out_t.shape[0]) // 8 + 8
    return pl.pallas_call(
        row_grad_kernel,
        name="row_grad",
        out_shape=(shape((4, each, width), BF16),) * 2,
        in_specs=[SM] + [VM] * 7,
        out_specs=(VM, VM),
        cost_estimate=pl.CostEstimate(
            flops=2 * out_t.shape[0] * out_t.shape[1] * width,
            bytes_accessed=6 * 10**6,
            transcendentals=0,
        ),
    )(info, out_t, *blocks, down_a, down_b)


def qkv_grad_kernel(info, x0, x1, x2, x3, d0, d1, d2, d3, keep, send):
    total = 0.0
    for x, d_qkv in zip((x0, x1, x2, x3), (d0, d1, d2, d3)):
        total = total + dot_tn(x[...], d_qkv[...])
    store_blocks(total, keep, send, info, slice(None))


def qkv_grad(info, blocks, d_qkv):
    rows, width = blocks[0].shape
    columns = d_qkv[0].shape[1]
    return pl.pallas_call(
        qkv_grad_kernel,
        name="qkv_grad",
        out_shape=(shape((4, width // 8, columns), BF16),) * 2,
        in_specs=[SM] + [VM] * 8,
        out_specs=(VM, VM),
        cost_estimate=pl.CostEstimate(
            flops=8 * rows * width * columns, bytes_accessed=4 * 10**6, transcendentals=0
        ),
    )(info, *blocks, *d_qkv)


def join_wide_kernel(info, b0, b1, b2, b3, out):
    rank = info[0]
    half = out.shape[1] // 2
    part = half // RANKS
    one = part // 3
    for step, block in enumerate((b0, b1, b2, b3)):
        base = pl.multiple_of((rank ^ step) * part, part)
        value = block[...].astype(F32)
        out[:, pl.ds(base, one)] = value[:, 0:one]
        out[:, pl.ds(pl.multiple_of(half + base, one), one)] = value[:, one : 2 * one]
        out[:, pl.ds(pl.multiple_of(base + one, one), 2 * one)] = value[:, 2 * one : 4 * one]
        out[:, pl.ds(pl.multiple_of(half + base + one, one), 2 * one)] = value[:, 4 * one :]


def join_wide(info, blocks):
    rows, columns = blocks[0].shape
    return pl.pallas_call(
        join_wide_kernel,
        name="join_wide",
        out_shape=shape((rows, columns * RANKS), F32),
        in_specs=[SM] + [VM] * 4,
        out_specs=VM,
        cost_estimate=pl.CostEstimate(flops=10**6, bytes_accessed=4 * 10**6, transcendentals=0),
    )(info, *blocks)


def join_rows_kernel(info, b0, b1, b2, b3, down, out):
    rank = info[0]
    many, few = down.shape[0] // RANKS, out.shape[0] // RANKS
    for step, block in enumerate((b0, b1, b2, b3)):
        place = rank ^ step
        value = block[...].astype(F32)
        down[pl.ds(place * many, many), :] = value[0:many]
        out[pl.ds(place * few, few), :] = value[many : many + few]


def join_rows(info, blocks, many):
    rows, columns = blocks[0].shape
    if many % 8 or (rows - many) % 8:
        stacked = jnp.stack(blocks)[info[0] ^ jnp.arange(RANKS)].astype(F32)
        return stacked[:, :many].reshape(-1, columns), stacked[:, many:].reshape(-1, columns)
    return pl.pallas_call(
        join_rows_kernel,
        name="join_rows",
        out_shape=(
            shape((many * RANKS, columns), F32),
            shape(((rows - many) * RANKS, columns), F32),
        ),
        in_specs=[SM] + [VM] * 4,
        out_specs=(VM, VM),
        cost_estimate=pl.CostEstimate(flops=10**6, bytes_accessed=2 * 10**6, transcendentals=0),
    )(info, *blocks)


def join_heads_kernel(info, b0, b1, b2, b3, out):
    rank = info[0]
    width = out.shape[1] // 3
    part = width // RANKS
    for value in range(RANKS):

        @pl.when(rank == value)
        def _():
            for step, block in enumerate((b0, b1, b2, b3)):
                for third in range(3):
                    first = third * width + (value ^ step) * part
                    piece = block[:, third * part : (third + 1) * part]
                    out[:, first : first + part] = piece.astype(F32)


def join_heads(info, blocks):
    rows, columns = blocks[0].shape
    return pl.pallas_call(
        join_heads_kernel,
        name="join_heads",
        out_shape=shape((rows, columns * RANKS), F32),
        in_specs=[SM] + [VM] * 4,
        out_specs=VM,
        cost_estimate=pl.CostEstimate(flops=10**6, bytes_accessed=2 * 10**6, transcendentals=0),
    )(info, *blocks)


def token_grad_kernel(
    info, own, near, far, cross, w, d_h1, masked_row, masked_col, tokens, replacement, joined
):
    rank = info[0]
    rows, width = d_h1.shape
    part = near.shape[1] // 3
    for value in range(RANKS):

        @pl.when(rank == value)
        def _():
            for step, block in enumerate((own, near, far, cross)):
                for third in range(3):
                    first = third * width + (value ^ step) * part
                    joined[:, first : first + part] = block[:, third * part : (third + 1) * part]

    grad = d_h1[...] + dot_nt(joined[...], w[...])
    count = masked_row.shape[1]
    places = lax.broadcasted_iota(jnp.int32, (rows, count), 0)
    hit = jnp.max((places == masked_row[...]).astype(F32), axis=1, keepdims=True)
    tokens[...] = jnp.where(hit > 0.5, 0.0, grad)
    places = lax.broadcasted_iota(jnp.int32, (count, rows), 1)
    replacement[...] = exact_dot((places == masked_col[...]).astype(F32), grad)


def token_grad(info, own, near, far, cross, w, d_h1, masked):
    rows, width = d_h1.shape
    count = masked.shape[0]
    return pl.pallas_call(
        token_grad_kernel,
        name="token_grad",
        out_shape=(shape((rows, width), F32), shape((count, width), F32)),
        in_specs=[SM] + [VM] * 8,
        out_specs=(VM, VM),
        scratch_shapes=[scratch((rows, 3 * width), BF16)],
        cost_estimate=pl.CostEstimate(
            flops=6 * rows * width * width, bytes_accessed=8 * 10**6, transcendentals=0
        ),
    )(info, own, near, far, cross, w, d_h1, masked.reshape(1, count), masked.reshape(count, 1))


def after(value, *others):
    return lax.optimization_barrier((value,) + others)[0]


def flip(value, axis, bits):
    count = lax.axis_size(axis)
    return lax.ppermute(value, axis, [(index, index ^ bits) for index in range(count)])


def gather_blocks(value):
    far = flip(value, "sp", 2)
    near = flip(value, "sp", 1)
    cross = flip(far, "sp", 1)
    return [value, near, far, cross]


def exchange_blocks(blocks):
    via = flip(blocks[3], "sp", 1)
    near = flip(blocks[1], "sp", 1)
    far = flip(blocks[2], "sp", 2)
    cross = flip(via, "sp", 2)
    return blocks[0], near, far, cross


def small_mesh():
    return lax.axis_size("dp") == 8


def add_low(a, b):
    return (a.astype(F32) + b.astype(F32)).astype(BF16)


def start_sum(send):
    return flip(send, "dp", 1) if small_mesh() else send


def spread_sum(keep, came):
    if not small_mesh():
        return None
    return [flip(add_low(keep[step], came[step]), "dp", 2 * step) for step in (1, 2, 3)]


def finish_sum(keep, came, others):
    if not small_mesh():
        grad = jnp.stack([keep, came], axis=1)
        grad = grad.reshape(-1, grad.shape[-1]).astype(F32)
        return lax.psum_scatter(grad, "dp", scatter_dimension=0, tiled=True).astype(BF16)
    total = keep[0].astype(F32) + came[0].astype(F32)
    for other in others:
        total = total + other.astype(F32)
    return total.astype(BF16)


def join_sum(pair):
    half = pair.shape[0] // 2
    return pair[:half].astype(F32) + pair[half:].astype(F32)


def spread_rows(keep, came):
    if not small_mesh():
        return None
    each = keep.shape[1] - 8
    sums = join_sum(keep[0, each:]) + join_sum(came[0, each:])
    high = sums.astype(BF16)
    tail = jnp.concatenate([high, (sums - high.astype(F32)).astype(BF16)], axis=0)
    parts = []
    for step in range(4):
        moves = []
        for z in range(4):
            for x in range(2):
                for quarter in range(4):
                    moves.append(((z * 2 + x) * 4 + quarter, (quarter * 2 + x) * 4 + (z ^ step)))
        part = jnp.concatenate([add_low(keep[step, :each], came[step, :each]), tail], axis=0)
        parts.append(lax.ppermute(part, ("dp", "sp"), moves))
    return parts


def finish_rows(keep, came, parts, many):
    each = keep.shape[1] - 8
    if small_mesh():
        total = 0.0
        for part in parts:
            total = total + part[:each].astype(F32)
        sums = sum(join_sum(part[each:]) for part in parts)
        return total.astype(BF16), sums
    count = lax.axis_size("dp")
    moves = []
    for place in range(count):
        for quarter in range(4):
            target = quarter * (count // 4) + place // 4
            moves.append((place * 4 + quarter, target * 4 + place % 4))
    both = jnp.stack([keep, came]).astype(F32)
    results = []
    for grad in (both[:, :, :many], both[:, :, many:each]):
        grad = grad.reshape(-1, grad.shape[-1])
        shard = lax.psum_scatter(grad, "dp", scatter_dimension=0, tiled=True).astype(BF16)
        results.append(lax.ppermute(shard, ("dp", "sp"), moves))
    return jnp.concatenate(results, axis=0), lax.psum(join_sum(keep[0, each:]), "dp")


def local(
    tokens,
    segment_ids,
    masked_rows,
    replacement,
    cotangent,
    w_qkv,
    w_out_attn,
    w_in_ff,
    w_out_ff,
    gain_one,
    shift_one,
    gain_two,
    shift_two,
):
    rows_dev, width = tokens.shape
    rank = lax.axis_index("sp")
    heads = HEADS // RANKS
    dim = width // HEADS
    part = heads * dim
    group_seg = segment_ids[0].astype(jnp.int32)
    info = jnp.concatenate([rank.astype(jnp.int32).reshape(1), group_seg])
    seg_rows = group_seg.reshape(1, -1)
    slopes = alibi_slopes(HEADS)
    gain_one, shift_one = gain_one.reshape(1, -1), shift_one.reshape(1, -1)
    gain_two, shift_two = gain_two.reshape(1, -1), shift_two.reshape(1, -1)

    select = jnp.arange(rows_dev, dtype=jnp.int32)[:, None] == masked_rows[None, :]
    hit = jnp.any(select, axis=1, keepdims=True)
    placed = dot(select.astype(BF16), replacement)
    start = jnp.where(hit, placed.astype(BF16), tokens)
    start_blocks = gather_blocks(start)
    place = lax.axis_index("dp")
    outer, inner = (place // 2, place % 2) if small_mesh() else (place * 0, place * 0)
    spot = jnp.stack([rank, outer, inner]).astype(jnp.int32)

    w_rank = jnp.concatenate(
        [
            lax.dynamic_slice_in_dim(w_qkv, third * width + rank * part, part, 1)
            for third in range(3)
        ],
        axis=1,
    )
    qkv, attn, attn_t, lse = attention_forward(
        info, slopes, start_blocks, w_rank, seg_rows, heads, dim
    )
    own, near, far, cross = exchange_blocks(attn)
    low, unit, inverse = norm_one(
        info, own, near, far, cross, start, w_out_attn, gain_one, shift_one
    )
    low_blocks = gather_blocks(low)
    layer_out, d_h2, d_ff, slope, act, sums2 = ffn_forward(
        low, unit, gain_one, shift_one, gain_two, shift_two,
        masked_rows.reshape(1, -1), cotangent, w_in_ff, w_out_ff, 512,
    )
    d_ff_blocks = gather_blocks(d_ff)
    d_h1, sent = ffn_backward(
        d_ff, d_h2, unit, inverse, gain_one, sums2, act, slope, w_in_ff, w_out_ff, 512
    )
    far = flip(sent, "sp", 2)
    near = flip(sent, "sp", 1)

    units = w_out_ff.shape[0] // RANKS // 3
    keep_a, send_a, down_a = ffn_grad(
        spot, low_blocks, d_ff_blocks, w_in_ff, w_out_ff, units, 0, 1
    )
    came_a = start_sum(send_a)
    keep_g, send_g, keep_u, send_u, down_b = ffn_grad(
        after(spot, down_a), low_blocks, d_ff_blocks, w_in_ff, w_out_ff, units, 1, 2
    )
    came_g = start_sum(send_g)
    came_u = start_sum(send_u)
    cross = flip(after(far, down_b), "sp", 1)
    d_proj_blocks = [sent, near, far, cross]
    keep_r, send_r = row_grad(spot, attn_t, d_proj_blocks, down_a, down_b)
    came_r = start_sum(send_r)
    others_a = spread_sum(keep_a, after(came_a, keep_r))

    d_qkv = attention_backward(
        after(info, keep_r), slopes, d_proj_blocks, w_out_attn, qkv, lse, seg_rows, heads, dim
    )
    own, near, far, cross = exchange_blocks(d_qkv)
    keep_q, send_q = qkv_grad(spot, start_blocks, d_qkv)
    came_q = start_sum(send_q)
    others_g = spread_sum(keep_g, after(came_g, keep_q))
    others_u = spread_sum(keep_u, after(came_u, keep_q))
    grad_tokens, grad_replacement = token_grad(
        after(info, keep_q), own, near, far, cross, w_qkv, d_h1, masked_rows
    )
    others_r = spread_rows(keep_r, after(came_r, keep_q))
    others_q = spread_sum(keep_q, after(came_q, grad_tokens))
    wide = jnp.concatenate(
        [
            finish_sum(keep_a, came_a, others_a),
            finish_sum(keep_g, came_g, others_g),
            finish_sum(keep_u, came_u, others_u),
        ],
        axis=1,
    )
    wide_blocks = gather_blocks(wide)
    many = w_out_ff.shape[0] // lax.axis_size("dp") // RANKS
    row_share, norm_sums = finish_rows(keep_r, came_r, others_r, w_out_ff.shape[0] // RANKS // 8)
    row_blocks = gather_blocks(row_share)
    head_blocks = gather_blocks(finish_sum(keep_q, came_q, others_q))
    grad_down, grad_out = join_rows(spot, row_blocks, many)

    return (
        layer_out,
        grad_tokens,
        grad_replacement,
        join_heads(spot, head_blocks),
        grad_out,
        join_wide(spot, wide_blocks),
        grad_down,
        norm_sums[0],
        norm_sums[1],
        norm_sums[2],
        norm_sums[3],
    )


def solution(mesh):
    tokens = P(("dp", "sp"), None)
    rows = P("dp", None)
    return jax.shard_map(
        local,
        mesh=mesh,
        in_specs=(tokens, rows, P(("dp", "sp")), tokens, tokens) + (P(),) * 8,
        out_specs=(tokens,) * 3 + (rows,) * 4 + (P(),) * 4,
        check_vma=False,
    )
```

```python
import functools
import math

import jax
import jax.numpy as jnp
from jax import lax
from jax.experimental import pallas as pl
from jax.experimental.pallas import tpu as pltpu
from jax.sharding import PartitionSpec as P

HEADS = 12
RANKS = 4
EPSILON = 1e-05
FAR = 1e30
F32 = jnp.float32
BF16 = jnp.bfloat16
VM = pl.BlockSpec(memory_space=pltpu.VMEM)
SM = pl.BlockSpec(memory_space=pltpu.SMEM)


def shape(dims, kind):
    return jax.ShapeDtypeStruct(dims, kind)


def scratch(dims, kind):
    return pltpu.VMEM(dims, kind)


def params(mebibytes):
    return pltpu.CompilerParams(vmem_limit_bytes=mebibytes << 20)


def alibi_slopes(head_count):
    nearest = 2 ** int(math.floor(math.log2(head_count)))
    base_list = [2.0 ** (-8.0 * (index + 1) / nearest) for index in range(nearest)]
    extra_list = [
        2.0 ** (-8.0 * (2 * index + 1) / (2 * nearest)) for index in range(head_count - nearest)
    ]
    return jnp.array(base_list + extra_list, dtype=F32)


def dot(a, b):
    return jnp.dot(a, b, preferred_element_type=F32)


def dot_nt(a, b):
    return lax.dot_general(a, b, (((1,), (1,)), ((), ())), preferred_element_type=F32)


def dot_tn(a, b):
    return lax.dot_general(a, b, (((0,), (0,)), ((), ())), preferred_element_type=F32)


def exact_dot(a, b):
    return jnp.dot(a, b, precision=lax.Precision.HIGHEST, preferred_element_type=F32)


def standardize(value):
    center = value - jnp.mean(value, axis=-1, keepdims=True)
    spread = jnp.mean(center * center, axis=-1, keepdims=True)
    inverse = lax.rsqrt(spread + EPSILON)
    return center * inverse, inverse


def standardize_back(grad, unit, inverse):
    mean = jnp.mean(grad, axis=-1, keepdims=True)
    return inverse * (grad - mean - unit * jnp.mean(grad * unit, axis=-1, keepdims=True))


def gelu_pair(x):
    cdf = 0.5 * (1.0 + lax.erf(x * math.sqrt(0.5)))
    pdf = jnp.exp(-0.5 * x * x) * (1.0 / math.sqrt(2.0 * math.pi))
    return x * cdf, cdf + x * pdf


def pair_active(seg, rank, first, second, rows):
    one, two = rank ^ first, rank ^ second
    low, high = jnp.minimum(one, two), jnp.maximum(one, two)
    return jnp.logical_or(one == two, seg[0, low * rows + rows - 1] == seg[0, high * rows])


def pair_distance(seg_rows, rank, keys_at, query_at, rows):
    key_pos, query_pos = (rank ^ keys_at) * rows, (rank ^ query_at) * rows
    down = lax.broadcasted_iota(jnp.int32, (rows, rows), 0)
    across = lax.broadcasted_iota(jnp.int32, (rows, rows), 1)
    gap = jnp.abs(down - across + (key_pos - query_pos)).astype(F32)
    seg_q = seg_rows[:, pl.ds(pl.multiple_of(query_pos, rows), rows)]
    seg_k = seg_rows[:, pl.ds(pl.multiple_of(key_pos, rows), rows)]
    seg_k = jnp.transpose(jnp.broadcast_to(seg_k, (128, rows)))[:, :1]
    return jnp.where(seg_k == seg_q, gap, FAR)


def attention_forward_kernel(
    rows, heads, dim, info, seg, slopes, x0, x1, x2, x3, w, seg_rows,
    qkv_out, out, lse, qs, ks, vt, dist, acc, peak, total,
):
    rank = info[0]
    width = heads * dim
    for at, x in enumerate((x0, x1, x2, x3)):
        qkv = dot(x[...], w[...]).astype(BF16)
        here = pl.ds(at * rows, rows)
        qkv_out[here, :] = qkv
        for h in range(heads):
            qs[h, here, :] = (qkv[:, h * dim : (h + 1) * dim] * dim**-0.5).astype(BF16)
            ks[h, here, :] = qkv[:, width + h * dim : width + (h + 1) * dim]
        vt[:, here] = jnp.transpose(qkv[:, 2 * width :])

    for a in range(RANKS):
        mine = pl.ds(a * rows, rows)
        peak[...] = jnp.full_like(peak, -jnp.inf)
        total[...] = jnp.zeros_like(total)
        acc[...] = jnp.zeros_like(acc)

        def key_block(b, carry):
            @pl.when(pair_active(seg, rank, a, b, rows))
            def _():
                theirs = pl.ds(pl.multiple_of(b * rows, rows), rows)
                dist[...] = pair_distance(seg_rows, rank, b, a, rows)
                for h in range(heads):
                    slope = slopes[rank * heads + h]
                    s = dot_nt(ks[h, theirs, :], qs[h, mine, :]) - slope * dist[...]
                    old = peak[h : h + 1, :]
                    new = jnp.maximum(old, jnp.max(s, axis=0, keepdims=True))
                    p = jnp.exp(s - new)
                    fade = jnp.exp(old - new)
                    add = jnp.sum(p, axis=0, keepdims=True)
                    total[h : h + 1, :] = total[h : h + 1, :] * fade + add
                    peak[h : h + 1, :] = new
                    span = slice(h * dim, (h + 1) * dim)
                    acc[span, :] = acc[span, :] * fade + dot(vt[span, theirs], p.astype(BF16))

            return carry

        lax.fori_loop(0, RANKS, key_block, 0)
        for h in range(heads):
            span = slice(h * dim, (h + 1) * dim)
            acc[span, :] = acc[span, :] / total[h : h + 1, :]
            lse[h : h + 1, mine] = peak[h : h + 1, :] + jnp.log(total[h : h + 1, :])
        out[rank ^ a] = acc[...].astype(BF16)


def attention_forward(info, seg, slopes, blocks, w, heads, dim):
    rows = blocks[0].shape[0]
    tok, lw = rows * RANKS, heads * dim
    return pl.pallas_call(
        functools.partial(attention_forward_kernel, rows, heads, dim),
        name="attention_forward",
        out_shape=(
            shape((tok, 3 * lw), BF16),
            shape((RANKS, lw, rows), BF16),
            shape((heads, tok), F32),
        ),
        in_specs=[SM] * 3 + [VM] * 6,
        out_specs=(VM,) * 3,
        scratch_shapes=[
            scratch((heads, tok, dim), BF16),
            scratch((heads, tok, dim), BF16),
            scratch((lw, tok), BF16),
            scratch((rows, rows), F32),
            scratch((lw, rows), F32),
            scratch((heads, rows), F32),
            scratch((heads, rows), F32),
        ],
        compiler_params=params(16),
        cost_estimate=pl.CostEstimate(
            flops=4 * 10**9, bytes_accessed=6 * 10**6, transcendentals=3 * 10**6
        ),
    )(info, seg, slopes, *blocks, w, seg)


def attention_backward_kernel(
    rows, heads, dim, info, seg, slopes, g0, g1, g2, g3, w, qkv, lse, seg_rows,
    d_qkv, qs, ks, kt, vs, do, dist, prob, dprob, dk, dv, dqt, delta,
):
    rank = info[0]
    width = heads * dim
    scale = dim**-0.5
    w_rank = w[pl.ds(pl.multiple_of(rank * width, width), width), :]
    for at, g in enumerate((g0, g1, g2, g3)):
        here = pl.ds(at * rows, rows)
        grad = dot_nt(g[0:rows, :], w_rank).astype(BF16)
        value = qkv[here, :]
        kt[:, here] = jnp.transpose(value[:, width : 2 * width])
        for h in range(heads):
            do[h, here, :] = grad[:, h * dim : (h + 1) * dim]
            qs[h, here, :] = (value[:, h * dim : (h + 1) * dim] * scale).astype(BF16)
            ks[h, here, :] = value[:, width + h * dim : width + (h + 1) * dim]
            vs[h, here, :] = value[:, 2 * width + h * dim : 2 * width + (h + 1) * dim]
    dk[...] = jnp.zeros_like(dk)
    dv[...] = jnp.zeros_like(dv)

    for a in range(RANKS):
        mine = pl.ds(a * rows, rows)
        delta[...] = jnp.zeros_like(delta)
        dqt[...] = jnp.zeros_like(dqt)

        def first_pass(b, carry):
            @pl.when(pair_active(seg, rank, a, b, rows))
            def _():
                theirs = pl.ds(pl.multiple_of(b * rows, rows), rows)
                dist[...] = pair_distance(seg_rows, rank, b, a, rows)
                for h in range(heads):
                    slope = slopes[rank * heads + h]
                    s = dot_nt(ks[h, theirs, :], qs[h, mine, :]) - slope * dist[...]
                    p = jnp.exp(s - lse[h : h + 1, mine])
                    dp = dot_nt(vs[h, theirs, :], do[h, mine, :])
                    delta[h : h + 1, :] += jnp.sum(p * dp, axis=0, keepdims=True)
                    prob[h, theirs, :] = p
                    dprob[h, theirs, :] = dp

            return carry

        lax.fori_loop(0, RANKS, first_pass, 0)

        def second_pass(b, carry):
            @pl.when(pair_active(seg, rank, a, b, rows))
            def _():
                theirs = pl.ds(pl.multiple_of(b * rows, rows), rows)
                for h in range(heads):
                    p = prob[h, theirs, :]
                    ds = (p * (dprob[h, theirs, :] - delta[h : h + 1, :])).astype(BF16)
                    dv[h, theirs, :] += dot(p.astype(BF16), do[h, mine, :])
                    dk[h, theirs, :] += dot(ds, qs[h, mine, :])
                    span = slice(h * dim, (h + 1) * dim)
                    dqt[span, :] += dot(kt[span, theirs], ds)

            return carry

        lax.fori_loop(0, RANKS, second_pass, 0)
        d_qkv[rank ^ a, 0:width, :] = (dqt[...] * scale).astype(BF16)

    for at in range(RANKS):
        here = pl.ds(at * rows, rows)
        for h in range(heads):
            first = width + h * dim
            d_qkv[rank ^ at, first : first + dim, :] = jnp.transpose(dk[h, here, :]).astype(BF16)
            first = 2 * width + h * dim
            d_qkv[rank ^ at, first : first + dim, :] = jnp.transpose(dv[h, here, :]).astype(BF16)


def attention_backward(info, seg, slopes, blocks, w, qkv, lse, heads, dim):
    tok, lw = qkv.shape[0], heads * dim
    rows = tok // RANKS
    return pl.pallas_call(
        functools.partial(attention_backward_kernel, rows, heads, dim),
        name="attention_backward",
        out_shape=shape((RANKS, 3 * lw, rows), BF16),
        in_specs=[SM] * 3 + [VM] * 8,
        out_specs=VM,
        scratch_shapes=[
            scratch((heads, tok, dim), BF16),
            scratch((heads, tok, dim), BF16),
            scratch((lw, tok), BF16),
            scratch((heads, tok, dim), BF16),
            scratch((heads, tok, dim), BF16),
            scratch((rows, rows), F32),
            scratch((heads, tok, rows), F32),
            scratch((heads, tok, rows), F32),
            scratch((heads, tok, dim), F32),
            scratch((heads, tok, dim), F32),
            scratch((lw, rows), F32),
            scratch((heads, rows), F32),
        ],
        compiler_params=params(24),
        cost_estimate=pl.CostEstimate(
            flops=8 * 10**9, bytes_accessed=6 * 10**6, transcendentals=3 * 10**6
        ),
    )(info, seg, slopes, *blocks, w, qkv, lse, seg)


def line(vector):
    return vector[...].reshape(1, -1)


def norm_one_kernel(attn, start, w, gain, shift, low, unit, inverse):
    parts = attn[...].reshape(-1, start.shape[0])
    x, inv = standardize(start[...].astype(F32) + dot_tn(parts, w[...]))
    unit[...] = x
    inverse[...] = inv
    low[...] = (x * line(gain) + line(shift)).astype(BF16)


def norm_one(attn, start, w, gain, shift):
    rows, width = start.shape
    return pl.pallas_call(
        norm_one_kernel,
        name="norm_one",
        out_shape=(shape((rows, width), BF16), shape((rows, width), F32), shape((rows, 1), F32)),
        in_specs=[VM] * 5,
        out_specs=(VM,) * 3,
        compiler_params=params(16),
        cost_estimate=pl.CostEstimate(
            flops=2 * rows * width * width, bytes_accessed=4 * 10**6, transcendentals=0
        ),
    )(attn, start, w, gain, shift)


def ffn_forward_kernel(
    low, unit, gain1, shift1, gain2, shift2, masked, cot, w_gate, w_up, w_down,
    layer_out, d_h2, d_ff, slope, act, sums, acc,
):
    step = pl.program_id(0)
    gate = dot(low[...], w_gate[...])
    up = dot(low[...], w_up[...])
    value, grad = gelu_pair(gate)
    act[...] = value.astype(BF16)
    slope[...] = (up * grad).astype(BF16)
    part = dot((value * up).astype(BF16), w_down[...])

    @pl.when(step == 0)
    def _():
        acc[...] = unit[...] * line(gain1) + line(shift1) + part

    @pl.when(step > 0)
    def _():
        acc[...] += part

    @pl.when(step == pl.num_programs(0) - 1)
    def _():
        x, inv = standardize(acc[...])
        layer_out[...] = (x * line(gain2) + line(shift2)).astype(BF16)
        places = lax.broadcasted_iota(jnp.int32, (low.shape[0], masked.shape[0]), 0)
        dy = exact_dot((places == line(masked)).astype(F32), cot[...])
        sums[0:1, :] = jnp.sum(dy * x, axis=0, keepdims=True)
        sums[1:2, :] = jnp.sum(dy, axis=0, keepdims=True)
        grad_in = standardize_back(dy * line(gain2), x, inv)
        d_h2[...] = grad_in
        d_ff[...] = grad_in.astype(BF16)


def ffn_forward(low, unit, gain1, shift1, gain2, shift2, masked, cot, w_in, w_out, size):
    rows, width = low.shape
    hid = w_out.shape[0]
    count = hid // size
    full = lambda dims: pl.BlockSpec(dims, lambda j: (0,) * len(dims))
    act = pl.BlockSpec((rows, size), lambda j: (0, j))
    return pl.pallas_call(
        ffn_forward_kernel,
        name="ffn_forward",
        grid=(count,),
        out_shape=(
            shape((rows, width), BF16),
            shape((rows, width), F32),
            shape((rows, width), BF16),
            shape((rows, hid), BF16),
            shape((rows, hid), BF16),
            shape((2, width), F32),
        ),
        in_specs=[full((rows, width))] * 2
        + [full((width,))] * 4
        + [
            full(masked.shape),
            full(cot.shape),
            pl.BlockSpec((width, size), lambda j: (0, j)),
            pl.BlockSpec((width, size), lambda j: (0, count + j)),
            pl.BlockSpec((size, width), lambda j: (j, 0)),
        ],
        out_specs=(full((rows, width)),) * 3 + (act, act, full((2, width))),
        scratch_shapes=[scratch((rows, width), F32)],
        compiler_params=params(22),
        cost_estimate=pl.CostEstimate(
            flops=6 * rows * width * hid, bytes_accessed=18 * 10**6, transcendentals=2 * rows * hid
        ),
    )(low, unit, gain1, shift1, gain2, shift2, masked, cot, w_in, w_in, w_out)


def ffn_backward_kernel(
    d_ff, d_h2, unit, inverse, gain1, sums2, act, slope, w_gate, w_up, w_down, d_h1, sent, acc
):
    step = pl.program_id(0)
    d_hidden = dot_nt(d_ff[...], w_down[...])
    d_gate = (d_hidden * slope[...].astype(F32)).astype(BF16)
    d_up = (d_hidden * act[...].astype(F32)).astype(BF16)
    part = dot_nt(d_gate, w_gate[...]) + dot_nt(d_up, w_up[...])

    @pl.when(step == 0)
    def _():
        acc[...] = d_h2[...] + part

    @pl.when(step > 0)
    def _():
        acc[...] += part

    @pl.when(step == pl.num_programs(0) - 1)
    def _():
        total = acc[...]
        rows = total.shape[0]
        x = unit[...]
        gain_sum = jnp.sum(total * x, axis=0, keepdims=True)
        shift_sum = jnp.sum(total, axis=0, keepdims=True)
        sums = jnp.concatenate([gain_sum, shift_sum, sums2[...]], axis=0)
        high = sums.astype(BF16).astype(F32)
        tail = jnp.concatenate([high, sums - high, jnp.zeros((8, sums.shape[1]), F32)], axis=0)
        grad = standardize_back(total * line(gain1), x, inverse[...])
        d_h1[...] = grad
        sent[0:rows, :] = grad.astype(BF16)
        sent[rows : rows + 16, :] = tail.astype(BF16)


def ffn_backward(d_ff, d_h2, unit, inverse, gain1, sums2, act, slope, w_in, w_out, size):
    rows, width = d_ff.shape
    hid = w_out.shape[0]
    count = hid // size
    full = lambda dims: pl.BlockSpec(dims, lambda j: (0,) * len(dims))
    part = pl.BlockSpec((rows, size), lambda j: (0, j))
    return pl.pallas_call(
        ffn_backward_kernel,
        name="ffn_backward",
        grid=(count,),
        out_shape=(shape((rows, width), F32), shape((rows + 16, width), BF16)),
        in_specs=[full((rows, width))] * 3
        + [
            full((rows, 1)),
            full((width,)),
            full((2, width)),
            part,
            part,
            pl.BlockSpec((width, size), lambda j: (0, j)),
            pl.BlockSpec((width, size), lambda j: (0, count + j)),
            pl.BlockSpec((size, width), lambda j: (j, 0)),
        ],
        out_specs=(full((rows, width)), full((rows + 16, width))),
        scratch_shapes=[scratch((rows, width), F32)],
        compiler_params=params(22),
        cost_estimate=pl.CostEstimate(
            flops=6 * rows * width * hid, bytes_accessed=20 * 10**6, transcendentals=0
        ),
    )(d_ff, d_h2, unit, inverse, gain1, sums2, act, slope, w_in, w_in, w_out)


X_FIRST = (1, 2, 4)
Z_FIRST = (2, 1, 4)


def bit_of(value, mask):
    return (value // mask) % 2


def store_blocks(blocks, keep, send, place, order, columns):
    one, two, three = order
    odd = bit_of(place, one) == 1
    for index in range(8):
        if index & one:
            continue
        spot = bit_of(place ^ index, two) * 2 + bit_of(place ^ index, three)
        low, high = blocks(index), blocks(index | one)
        keep[spot, :, columns] = jnp.where(odd, high, low).astype(BF16)
        send[spot, :, columns] = jnp.where(odd, low, high).astype(BF16)


def row_blocks(grad):
    each = grad.shape[0] // 8
    return lambda index: grad[index * each : (index + 1) * each]


def ffn_grad_kernel(
    order, info, n0, n1, n2, n3, f0, f1, f2, f3, w_gate, w_up, w_down, *rest
):
    keep, send, g_down, tok, tok_t, d_ff = rest
    rows = n0.shape[0]
    size = w_gate.shape[1]

    @pl.when(pl.program_id(0) == 0)
    def _():
        for at, (n, f) in enumerate(zip((n0, n1, n2, n3), (f0, f1, f2, f3))):
            here = pl.ds(at * rows, rows)
            tok[here, :] = n[...]
            d_ff[here, :] = f[...]
            tok_t[:, here] = jnp.transpose(n[...])

    gate = dot(tok[...], w_gate[...])
    up = dot(tok[...], w_up[...])
    value, grad = gelu_pair(gate)
    g_down[...] = dot_tn((value * up).astype(BF16), d_ff[...]).astype(BF16)
    d_hidden = dot_nt(d_ff[...], w_down[...])
    g_gate = dot(tok_t[...], (d_hidden * up * grad).astype(BF16))
    g_up = dot(tok_t[...], (d_hidden * value).astype(BF16))
    step = pl.program_id(0)
    for other, grad in enumerate((g_gate, g_up)):
        first = (other * pl.num_programs(0) + step) * size
        columns = pl.ds(pl.multiple_of(first, size), size)
        store_blocks(row_blocks(grad), keep, send, info[1], order, columns)


def ffn_grad(info, toks, grads, w_in, w_out, size, first, steps, order):
    rows, width = toks[0].shape
    count = w_out.shape[0] // RANKS // size
    tok = rows * RANKS
    full = pl.BlockSpec((rows, width), lambda j, info: (0, 0))
    wide = lambda base: pl.BlockSpec(
        (width, size), lambda j, info: (0, (base + info[0]) * count + first + j)
    )
    dims = (4, width // 8, 2 * size * steps)
    block_spec = pl.BlockSpec(dims, lambda j, info: (0, 0, 0))
    return pl.pallas_call(
        functools.partial(ffn_grad_kernel, order),
        name="ffn_grad",
        out_shape=(shape(dims, BF16),) * 2 + (shape((size * steps, width), BF16),),
        grid_spec=pltpu.PrefetchScalarGridSpec(
            num_scalar_prefetch=1,
            grid=(steps,),
            in_specs=[full] * 8
            + [
                wide(0),
                wide(RANKS),
                pl.BlockSpec((size, width), lambda j, info: (info[0] * count + first + j, 0)),
            ],
            out_specs=(block_spec,) * 2 + (pl.BlockSpec((size, width), lambda j, info: (j, 0)),),
            scratch_shapes=[
                scratch((tok, width), BF16),
                scratch((width, tok), BF16),
                scratch((tok, width), BF16),
            ],
        ),
        compiler_params=params(26),
        cost_estimate=pl.CostEstimate(
            flops=12 * tok * width * size * steps,
            bytes_accessed=8 * 10**6,
            transcendentals=2 * tok * size * steps,
        ),
    )(info, *toks, *grads, w_in, w_in, w_out)


def row_grad_kernel(info, attn, g0, g1, g2, g3, down_a, down_b, keep, send):
    rows = g0.shape[0] - 16
    grad = 0.0
    sums = 0.0
    for at, g in enumerate((g0, g1, g2, g3)):
        grad = grad + dot(attn[info[0] ^ at], g[0:rows, :])
        pair = g[rows : rows + 16, :].astype(F32)
        sums = sums + pair[0:4] + pair[4:8]
    high = sums.astype(BF16).astype(F32)
    tail = jnp.concatenate([high, sums - high], axis=0)
    down = jnp.concatenate([down_a[...], down_b[...]], axis=0).astype(F32)
    many, few = down.shape[0] // 8, grad.shape[0] // 8

    def blocks(index):
        at = index % 2 * 4 + index // 2
        parts = [down[at * many : (at + 1) * many], grad[at * few : (at + 1) * few], tail]
        return jnp.concatenate(parts, axis=0)

    store_blocks(blocks, keep, send, info[1], X_FIRST, slice(None))


def row_grad(info, attn, blocks, down_a, down_b):
    width = blocks[0].shape[1]
    each = (down_a.shape[0] + down_b.shape[0] + attn.shape[1]) // 8 + 8
    return pl.pallas_call(
        row_grad_kernel,
        name="row_grad",
        out_shape=(shape((4, each, width), BF16),) * 2,
        in_specs=[SM] + [VM] * 7,
        out_specs=(VM, VM),
        cost_estimate=pl.CostEstimate(
            flops=2 * attn.size * width,
            bytes_accessed=6 * 10**6,
            transcendentals=0,
        ),
    )(info, attn, *blocks, down_a, down_b)


def qkv_grad_kernel(info, x0, x1, x2, x3, d_qkv, keep, send):
    total = 0.0
    for at, x in enumerate((x0, x1, x2, x3)):
        total = total + dot(d_qkv[info[0] ^ at], x[...])
    store_blocks(row_blocks(jnp.transpose(total)), keep, send, info[1], X_FIRST, slice(None))


def qkv_grad(info, blocks, d_qkv):
    rows, width = blocks[0].shape
    columns = d_qkv.shape[1]
    return pl.pallas_call(
        qkv_grad_kernel,
        name="qkv_grad",
        out_shape=(shape((4, width // 8, columns), BF16),) * 2,
        in_specs=[SM] + [VM] * 5,
        out_specs=(VM, VM),
        compiler_params=params(16),
        cost_estimate=pl.CostEstimate(
            flops=8 * rows * width * columns, bytes_accessed=4 * 10**6, transcendentals=0
        ),
    )(info, *blocks, d_qkv)


def join_wide_kernel(info, b0, b1, b2, b3, out):
    rank = info[0]
    half = out.shape[1] // 2
    part = half // RANKS
    one = part // 3
    for step, block in enumerate((b0, b1, b2, b3)):
        base = pl.multiple_of((rank ^ step) * part, part)
        value = block[...].astype(F32)
        out[:, pl.ds(base, one)] = value[:, 0:one]
        out[:, pl.ds(pl.multiple_of(half + base, one), one)] = value[:, one : 2 * one]
        out[:, pl.ds(pl.multiple_of(base + one, one), 2 * one)] = value[:, 2 * one : 4 * one]
        out[:, pl.ds(pl.multiple_of(half + base + one, one), 2 * one)] = value[:, 4 * one :]


def join_wide(info, blocks):
    rows, columns = blocks[0].shape
    return pl.pallas_call(
        join_wide_kernel,
        name="join_wide",
        out_shape=shape((rows, columns * RANKS), F32),
        in_specs=[SM] + [VM] * 4,
        out_specs=VM,
        cost_estimate=pl.CostEstimate(flops=10**6, bytes_accessed=4 * 10**6, transcendentals=0),
    )(info, *blocks)


def join_rows_kernel(info, b0, b1, b2, b3, down, out):
    rank = info[0]
    many, few = down.shape[0] // RANKS, out.shape[0] // RANKS
    for step, block in enumerate((b0, b1, b2, b3)):
        place = rank ^ step
        value = block[...].astype(F32)
        down[pl.ds(place * many, many), :] = value[0:many]
        out[pl.ds(place * few, few), :] = value[many : many + few]


def join_rows(info, blocks, many):
    rows, columns = blocks[0].shape
    if many % 8 or (rows - many) % 8:
        stacked = jnp.stack(blocks)[info[0] ^ jnp.arange(RANKS)].astype(F32)
        return stacked[:, :many].reshape(-1, columns), stacked[:, many:].reshape(-1, columns)
    return pl.pallas_call(
        join_rows_kernel,
        name="join_rows",
        out_shape=(
            shape((many * RANKS, columns), F32),
            shape(((rows - many) * RANKS, columns), F32),
        ),
        in_specs=[SM] + [VM] * 4,
        out_specs=(VM, VM),
        cost_estimate=pl.CostEstimate(flops=10**6, bytes_accessed=2 * 10**6, transcendentals=0),
    )(info, *blocks)


def join_heads_kernel(info, b0, b1, b2, b3, out):
    rank = info[0]
    width = out.shape[1] // 3
    part = width // RANKS
    for value in range(RANKS):

        @pl.when(rank == value)
        def _():
            for step, block in enumerate((b0, b1, b2, b3)):
                for third in range(3):
                    first = third * width + (value ^ step) * part
                    piece = block[:, third * part : (third + 1) * part]
                    out[:, first : first + part] = piece.astype(F32)


def join_heads(info, blocks):
    rows, columns = blocks[0].shape
    return pl.pallas_call(
        join_heads_kernel,
        name="join_heads",
        out_shape=shape((rows, columns * RANKS), F32),
        in_specs=[SM] + [VM] * 4,
        out_specs=VM,
        cost_estimate=pl.CostEstimate(flops=10**6, bytes_accessed=2 * 10**6, transcendentals=0),
    )(info, *blocks)


def token_grad_kernel(parts, w, d_h1, masked, tokens, replacement, joined):
    rows, width = d_h1.shape
    part = width // RANKS
    for rank in range(RANKS):
        for third in range(3):
            first = third * width + rank * part
            joined[first : first + part, :] = parts[rank, third * part : (third + 1) * part, :]
    grad = d_h1[...] + jnp.transpose(dot(w[...], joined[...]))
    count = masked.shape[0]
    places = lax.broadcasted_iota(jnp.int32, (rows, count), 0)
    select = (places == line(masked)).astype(F32)
    hit = jnp.max(select, axis=1, keepdims=True)
    tokens[...] = jnp.where(hit > 0.5, 0.0, grad)
    replacement[...] = lax.dot_general(
        select, grad, (((0,), (0,)), ((), ())),
        precision=lax.Precision.HIGHEST, preferred_element_type=F32,
    )


def token_grad(parts, w, d_h1, masked):
    rows, width = d_h1.shape
    return pl.pallas_call(
        token_grad_kernel,
        name="token_grad",
        out_shape=(shape((rows, width), F32), shape((masked.shape[0], width), F32)),
        in_specs=[VM] * 4,
        out_specs=(VM, VM),
        scratch_shapes=[scratch((3 * width, rows), BF16)],
        compiler_params=params(16),
        cost_estimate=pl.CostEstimate(
            flops=6 * rows * width * width, bytes_accessed=8 * 10**6, transcendentals=0
        ),
    )(parts, w, d_h1, masked)


def after(value, *others):
    return lax.optimization_barrier((value,) + others)[0]


def flip(value, axis, bits):
    count = lax.axis_size(axis)
    return lax.ppermute(value, axis, [(index, index ^ bits) for index in range(count)])


def gather_blocks(value):
    far = flip(value, "sp", 2)
    near = flip(value, "sp", 1)
    cross = flip(far, "sp", 1)
    return [value, near, far, cross]


def exchange(parts):
    return lax.all_to_all(parts, "sp", 0, 0, tiled=True)


def small_mesh():
    return lax.axis_size("dp") == 8


def halve(keep, came):
    half = keep.shape[0] // 2
    kept = keep[:half].astype(F32) + came[:half].astype(F32)
    sent = keep[half:].astype(F32) + came[half:].astype(F32)
    return kept, sent.astype(BF16)


def send_first(send, order):
    return flip(send, "dp", order[0]) if small_mesh() else send


def send_second(keep, came, order):
    if not small_mesh():
        return keep, came
    kept, sent = halve(keep, came)
    return kept, flip(sent, "dp", order[1])


def send_third(keep, came, order):
    if not small_mesh():
        return keep, came
    kept, sent = halve(keep, came)
    return kept, flip(sent, "dp", order[2])


def natural_blocks(keep, send, order):
    both = jnp.concatenate([keep, send], axis=0).astype(F32)
    places = []
    for index in range(8):
        bits = [1 if index & mask else 0 for mask in order]
        places.append(both[bits[0] * 4 + bits[1] * 2 + bits[2]])
    return places


def finish_sum(keep, came, order):
    if small_mesh():
        return (keep[0] + came[0].astype(F32)).astype(BF16)
    grad = jnp.concatenate(natural_blocks(keep, came, order), axis=0)
    return lax.psum_scatter(grad, "dp", scatter_dimension=0, tiled=True).astype(BF16)


def tidy_sums(value):
    first = value.shape[1] - 8
    sums = value[:, first : first + 4] + value[:, first + 4 :]
    high = sums.astype(BF16).astype(F32)
    return jnp.concatenate([value[:, :first], high, sums - high], axis=1)


def halve_kernel(keep, came, kept, sent):
    half = keep.shape[0] // 2
    value = tidy_sums(keep[...].astype(F32) + came[...].astype(F32))
    kept[...] = value[:half]
    sent[...] = value[half:].astype(BF16)


def halve_sums(keep, came):
    dims = (keep.shape[0] // 2,) + keep.shape[1:]
    return pl.pallas_call(
        halve_kernel,
        name="halve_sums",
        out_shape=(shape(dims, F32), shape(dims, BF16)),
        in_specs=[VM] * 2,
        out_specs=(VM, VM),
        cost_estimate=pl.CostEstimate(flops=10**6, bytes_accessed=2 * 10**6, transcendentals=0),
    )(keep, came)


def send_rows_second(keep, came):
    if not small_mesh():
        return keep, came
    kept, sent = halve_sums(keep, came)
    return kept, flip(sent, "dp", X_FIRST[1])


def send_rows_third(keep, came):
    if not small_mesh():
        return keep, came
    kept, sent = halve_sums(keep, came)
    return kept, flip(sent, "dp", X_FIRST[2])


def finish_rows(keep, came, many):
    count = lax.axis_size("dp")
    each = keep.shape[1] - 8
    moves = []
    if small_mesh():
        for z in range(4):
            for x in range(2):
                for rank in range(4):
                    moves.append(((z * 2 + x) * 4 + rank, (rank * 2 + x) * 4 + z))
        total = keep[0] + came[0].astype(F32)
        shard = total[:each].astype(BF16)
        sums = total[each : each + 4] + total[each + 4 :]
        return lax.ppermute(shard, ("dp", "sp"), moves), sums
    for place in range(count):
        for rank in range(4):
            target = rank * (count // 4) + place // 4
            moves.append((place * 4 + rank, target * 4 + place % 4))
    blocks = natural_blocks(keep, came, X_FIRST)
    blocks = [blocks[index * 2 + bit] for bit in range(2) for index in range(4)]
    results = []
    for first, last in ((0, many), (many, each)):
        grad = jnp.concatenate([block[first:last] for block in blocks], axis=0)
        shard = lax.psum_scatter(grad, "dp", scatter_dimension=0, tiled=True).astype(BF16)
        results.append(lax.ppermute(shard, ("dp", "sp"), moves))
    sums = blocks[0][each : each + 4] + blocks[0][each + 4 :]
    return jnp.concatenate(results, axis=0), lax.psum(sums, "dp")


def local(
    tokens,
    segment_ids,
    masked_rows,
    replacement,
    cotangent,
    w_qkv,
    w_out_attn,
    w_in_ff,
    w_out_ff,
    gain_one,
    shift_one,
    gain_two,
    shift_two,
):
    rows_dev, width = tokens.shape
    rank = lax.axis_index("sp")
    heads = HEADS // RANKS
    dim = width // HEADS
    part = heads * dim
    slopes = alibi_slopes(HEADS)

    select = jnp.arange(rows_dev, dtype=jnp.int32)[:, None] == masked_rows[None, :]
    hit = jnp.any(select, axis=1, keepdims=True)
    placed = dot(select.astype(BF16), replacement)
    start = jnp.where(hit, placed.astype(BF16), tokens)
    start_blocks = gather_blocks(start)
    place = lax.axis_index("dp")
    place = place if small_mesh() else place * 0
    spot = jnp.stack([rank, place]).astype(jnp.int32)

    w_rank = jnp.concatenate(
        [
            lax.dynamic_slice_in_dim(w_qkv, third * width + rank * part, part, 1)
            for third in range(3)
        ],
        axis=1,
    )
    qkv, attn, lse = attention_forward(
        spot, segment_ids, slopes, start_blocks, w_rank, heads, dim
    )
    low, unit, inverse = norm_one(exchange(attn), start, w_out_attn, gain_one, shift_one)
    low_far = flip(low, "sp", 2)
    low_near = flip(low, "sp", 1)
    layer_out, d_h2, d_ff, slope, act, sums2 = ffn_forward(
        low, unit, gain_one, shift_one, gain_two, shift_two,
        masked_rows, cotangent, w_in_ff, w_out_ff, 512,
    )
    d_ff_far = flip(d_ff, "sp", 2)
    d_ff_near = flip(d_ff, "sp", 1)
    low_far = after(low_far, d_ff)
    low_cross = flip(low_far, "sp", 1)
    low_blocks = [low, low_near, low_far, low_cross]
    d_h1, sent = ffn_backward(
        after(d_ff, low_far), d_h2, unit, inverse, gain_one, sums2, act, slope, w_in_ff, w_out_ff, 512
    )
    far = flip(sent, "sp", 2)
    near = flip(sent, "sp", 1)
    d_ff_cross = flip(after(d_ff_far, sent), "sp", 1)
    d_ff_blocks = [d_ff, d_ff_near, d_ff_far, d_ff_cross]

    units = w_out_ff.shape[0] // RANKS // 3
    keep_a, send_a, down_a = ffn_grad(
        spot, low_blocks, d_ff_blocks, w_in_ff, w_out_ff, units, 0, 1, X_FIRST
    )
    came_a = send_first(send_a, X_FIRST)
    keep_b, send_b, down_b = ffn_grad(
        after(spot, down_a), low_blocks, d_ff_blocks, w_in_ff, w_out_ff, units, 1, 2, Z_FIRST
    )
    came_b = send_first(send_b, Z_FIRST)
    cross = flip(after(far, down_b), "sp", 1)
    d_proj_blocks = [sent, near, far, cross]
    keep_r, send_r = row_grad(spot, attn, d_proj_blocks, down_a, down_b)
    came_r = send_first(send_r, X_FIRST)
    keep_a, came_a = send_second(keep_a, after(came_a, keep_r), X_FIRST)

    d_qkv = attention_backward(
        after(spot, keep_a), segment_ids, slopes, d_proj_blocks, w_out_attn, qkv, lse, heads, dim
    )
    parts = exchange(d_qkv)
    keep_q, send_q = qkv_grad(spot, start_blocks, d_qkv)
    came_q = send_first(send_q, X_FIRST)
    keep_b, came_b = send_second(keep_b, after(came_b, keep_q), Z_FIRST)
    keep_a, came_a = send_third(keep_a, after(came_a, keep_b), X_FIRST)
    keep_r, came_r = send_rows_second(keep_r, after(came_r, keep_a))
    grad_tokens, grad_replacement = token_grad(
        after(parts, keep_r), w_qkv, d_h1, masked_rows
    )
    keep_q, came_q = send_second(keep_q, after(came_q, grad_tokens), X_FIRST)
    keep_b, came_b = send_third(keep_b, after(came_b, keep_q), Z_FIRST)
    keep_r, came_r = send_rows_third(keep_r, after(came_r, keep_b))
    keep_q, came_q = send_third(keep_q, after(came_q, keep_r), X_FIRST)
    wide_a = finish_sum(keep_a, came_a, X_FIRST)
    wide_b = finish_sum(keep_b, came_b, Z_FIRST)
    wide_blocks = gather_blocks(jnp.concatenate([wide_a, wide_b], axis=1))
    many = w_out_ff.shape[0] // RANKS // 8
    row_share, norm_sums = finish_rows(keep_r, came_r, many)
    head_blocks = gather_blocks(finish_sum(keep_q, came_q, X_FIRST))
    row_blocks_ = gather_blocks(row_share)
    many = w_out_ff.shape[0] // lax.axis_size("dp") // RANKS
    grad_down, grad_out = join_rows(spot, row_blocks_, many)

    return (
        layer_out,
        grad_tokens,
        grad_replacement,
        join_heads(spot, head_blocks),
        grad_out,
        join_wide(spot, wide_blocks),
        grad_down,
        norm_sums[0],
        norm_sums[1],
        norm_sums[2],
        norm_sums[3],
    )


def solution(mesh):
    tokens = P(("dp", "sp"), None)
    rows = P("dp", None)
    return jax.shard_map(
        local,
        mesh=mesh,
        in_specs=(tokens, rows, P(("dp", "sp")), tokens, tokens) + (P(),) * 8,
        out_specs=(tokens,) * 3 + (rows,) * 4 + (P(),) * 4,
        check_vma=False,
    )
```

```python
import functools
import math

import jax
import jax.numpy as jnp
from jax import lax
from jax.experimental import pallas as pl
from jax.experimental.pallas import tpu as pltpu
from jax.sharding import PartitionSpec as P

HEADS = 12
RANKS = 4
EPSILON = 1e-05
FAR = 1e30
F32 = jnp.float32
BF16 = jnp.bfloat16
VM = pl.BlockSpec(memory_space=pltpu.VMEM)
SM = pl.BlockSpec(memory_space=pltpu.SMEM)


def shape(dims, kind):
    return jax.ShapeDtypeStruct(dims, kind)


def scratch(dims, kind):
    return pltpu.VMEM(dims, kind)


def params(mebibytes):
    return pltpu.CompilerParams(vmem_limit_bytes=mebibytes << 20)


def alibi_slopes(head_count):
    nearest = 2 ** int(math.floor(math.log2(head_count)))
    base_list = [2.0 ** (-8.0 * (index + 1) / nearest) for index in range(nearest)]
    extra_list = [
        2.0 ** (-8.0 * (2 * index + 1) / (2 * nearest)) for index in range(head_count - nearest)
    ]
    return jnp.array(base_list + extra_list, dtype=F32)


def dot(a, b):
    return jnp.dot(a, b, preferred_element_type=F32)


def dot_nt(a, b):
    return lax.dot_general(a, b, (((1,), (1,)), ((), ())), preferred_element_type=F32)


def dot_tn(a, b):
    return lax.dot_general(a, b, (((0,), (0,)), ((), ())), preferred_element_type=F32)


def exact_dot(a, b):
    return jnp.dot(a, b, precision=lax.Precision.HIGHEST, preferred_element_type=F32)


def standardize(value):
    center = value - jnp.mean(value, axis=-1, keepdims=True)
    spread = jnp.mean(center * center, axis=-1, keepdims=True)
    inverse = lax.rsqrt(spread + EPSILON)
    return center * inverse, inverse


def standardize_back(grad, unit, inverse):
    mean = jnp.mean(grad, axis=-1, keepdims=True)
    return inverse * (grad - mean - unit * jnp.mean(grad * unit, axis=-1, keepdims=True))


def gelu_pair(x):
    cdf = 0.5 * (1.0 + lax.erf(x * math.sqrt(0.5)))
    pdf = jnp.exp(-0.5 * x * x) * (1.0 / math.sqrt(2.0 * math.pi))
    return x * cdf, cdf + x * pdf


def pair_active(seg, rank, first, second, rows):
    one, two = rank ^ first, rank ^ second
    low, high = jnp.minimum(one, two), jnp.maximum(one, two)
    return jnp.logical_or(one == two, seg[0, low * rows + rows - 1] == seg[0, high * rows])


def pair_distance(seg_rows, rank, keys_at, query_at, rows):
    key_pos, query_pos = (rank ^ keys_at) * rows, (rank ^ query_at) * rows
    down = lax.broadcasted_iota(jnp.int32, (rows, rows), 0)
    across = lax.broadcasted_iota(jnp.int32, (rows, rows), 1)
    gap = jnp.abs(down - across + (key_pos - query_pos)).astype(F32)
    seg_q = seg_rows[:, pl.ds(pl.multiple_of(query_pos, rows), rows)]
    seg_k = seg_rows[:, pl.ds(pl.multiple_of(key_pos, rows), rows)]
    seg_k = jnp.transpose(jnp.broadcast_to(seg_k, (128, rows)))[:, :1]
    return jnp.where(seg_k == seg_q, gap, FAR)


def attention_forward_kernel(
    rows, heads, dim, info, seg, slopes, x0, x1, x2, x3, w, seg_rows,
    qkv_out, o0, o1, o2, o3, lse, qs, ks, vt, dist, acc, peak, total,
):
    rank = info[0]
    width = heads * dim
    for at, x in enumerate((x0, x1, x2, x3)):
        qkv = dot(x[...], w[...]).astype(BF16)
        here = pl.ds(at * rows, rows)
        qkv_out[here, :] = qkv
        for h in range(heads):
            qs[h, here, :] = (qkv[:, h * dim : (h + 1) * dim] * dim**-0.5).astype(BF16)
            ks[h, here, :] = qkv[:, width + h * dim : width + (h + 1) * dim]
        vt[:, here] = jnp.transpose(qkv[:, 2 * width :])

    for a in range(RANKS):
        mine = pl.ds(a * rows, rows)
        peak[...] = jnp.full_like(peak, -jnp.inf)
        total[...] = jnp.zeros_like(total)
        acc[...] = jnp.zeros_like(acc)

        def key_block(b, carry):
            @pl.when(pair_active(seg, rank, a, b, rows))
            def _():
                theirs = pl.ds(pl.multiple_of(b * rows, rows), rows)
                dist[...] = pair_distance(seg_rows, rank, b, a, rows)
                for h in range(heads):
                    slope = slopes[rank * heads + h]
                    s = dot_nt(ks[h, theirs, :], qs[h, mine, :]) - slope * dist[...]
                    old = peak[h : h + 1, :]
                    new = jnp.maximum(old, jnp.max(s, axis=0, keepdims=True))
                    p = jnp.exp(s - new)
                    fade = jnp.exp(old - new)
                    add = jnp.sum(p, axis=0, keepdims=True)
                    total[h : h + 1, :] = total[h : h + 1, :] * fade + add
                    peak[h : h + 1, :] = new
                    span = slice(h * dim, (h + 1) * dim)
                    acc[span, :] = acc[span, :] * fade + dot(vt[span, theirs], p.astype(BF16))

            return carry

        lax.fori_loop(0, RANKS, key_block, 0)
        for h in range(heads):
            span = slice(h * dim, (h + 1) * dim)
            acc[span, :] = acc[span, :] / total[h : h + 1, :]
            lse[h : h + 1, mine] = peak[h : h + 1, :] + jnp.log(total[h : h + 1, :])
        (o0, o1, o2, o3)[a][...] = acc[...].astype(BF16)


def attention_forward(info, seg, slopes, blocks, w, heads, dim):
    rows = blocks[0].shape[0]
    tok, lw = rows * RANKS, heads * dim
    return pl.pallas_call(
        functools.partial(attention_forward_kernel, rows, heads, dim),
        name="attention_forward",
        out_shape=(shape((tok, 3 * lw), BF16),)
        + (shape((lw, rows), BF16),) * RANKS
        + (shape((heads, tok), F32),),
        in_specs=[SM] * 3 + [VM] * 6,
        out_specs=(VM,) * 6,
        scratch_shapes=[
            scratch((heads, tok, dim), BF16),
            scratch((heads, tok, dim), BF16),
            scratch((lw, tok), BF16),
            scratch((rows, rows), F32),
            scratch((lw, rows), F32),
            scratch((heads, rows), F32),
            scratch((heads, rows), F32),
        ],
        compiler_params=params(16),
        cost_estimate=pl.CostEstimate(
            flops=4 * 10**9, bytes_accessed=6 * 10**6, transcendentals=3 * 10**6
        ),
    )(info, seg, slopes, *blocks, w, seg)


def attention_backward_kernel(
    rows, heads, dim, info, seg, slopes, g0, g1, g2, g3, w, qkv, lse, seg_rows,
    d_qkv, qs, ks, kt, vs, do, dist, prob, dprob, dk, dv, dqt, delta,
):
    rank = info[0]
    width = heads * dim
    scale = dim**-0.5
    w_rank = w[pl.ds(pl.multiple_of(rank * width, width), width), :]
    for at, g in enumerate((g0, g1, g2, g3)):
        here = pl.ds(at * rows, rows)
        grad = dot_nt(g[0:rows, :], w_rank).astype(BF16)
        value = qkv[here, :]
        kt[:, here] = jnp.transpose(value[:, width : 2 * width])
        for h in range(heads):
            do[h, here, :] = grad[:, h * dim : (h + 1) * dim]
            qs[h, here, :] = (value[:, h * dim : (h + 1) * dim] * scale).astype(BF16)
            ks[h, here, :] = value[:, width + h * dim : width + (h + 1) * dim]
            vs[h, here, :] = value[:, 2 * width + h * dim : 2 * width + (h + 1) * dim]
    dk[...] = jnp.zeros_like(dk)
    dv[...] = jnp.zeros_like(dv)

    for a in range(RANKS):
        mine = pl.ds(a * rows, rows)
        delta[...] = jnp.zeros_like(delta)
        dqt[...] = jnp.zeros_like(dqt)

        def first_pass(b, carry):
            @pl.when(pair_active(seg, rank, a, b, rows))
            def _():
                theirs = pl.ds(pl.multiple_of(b * rows, rows), rows)
                dist[...] = pair_distance(seg_rows, rank, b, a, rows)
                for h in range(heads):
                    slope = slopes[rank * heads + h]
                    s = dot_nt(ks[h, theirs, :], qs[h, mine, :]) - slope * dist[...]
                    p = jnp.exp(s - lse[h : h + 1, mine])
                    dp = dot_nt(vs[h, theirs, :], do[h, mine, :])
                    delta[h : h + 1, :] += jnp.sum(p * dp, axis=0, keepdims=True)
                    prob[h, theirs, :] = p
                    dprob[h, theirs, :] = dp

            return carry

        lax.fori_loop(0, RANKS, first_pass, 0)

        def second_pass(b, carry):
            @pl.when(pair_active(seg, rank, a, b, rows))
            def _():
                theirs = pl.ds(pl.multiple_of(b * rows, rows), rows)
                for h in range(heads):
                    p = prob[h, theirs, :]
                    ds = (p * (dprob[h, theirs, :] - delta[h : h + 1, :])).astype(BF16)
                    dv[h, theirs, :] += dot(p.astype(BF16), do[h, mine, :])
                    dk[h, theirs, :] += dot(ds, qs[h, mine, :])
                    span = slice(h * dim, (h + 1) * dim)
                    dqt[span, :] += dot(kt[span, theirs], ds)

            return carry

        lax.fori_loop(0, RANKS, second_pass, 0)
        d_qkv[rank ^ a, 0:width, :] = (dqt[...] * scale).astype(BF16)

    for at in range(RANKS):
        here = pl.ds(at * rows, rows)
        for h in range(heads):
            first = width + h * dim
            d_qkv[rank ^ at, first : first + dim, :] = jnp.transpose(dk[h, here, :]).astype(BF16)
            first = 2 * width + h * dim
            d_qkv[rank ^ at, first : first + dim, :] = jnp.transpose(dv[h, here, :]).astype(BF16)


def attention_backward(info, seg, slopes, blocks, w, qkv, lse, heads, dim):
    tok, lw = qkv.shape[0], heads * dim
    rows = tok // RANKS
    return pl.pallas_call(
        functools.partial(attention_backward_kernel, rows, heads, dim),
        name="attention_backward",
        out_shape=shape((RANKS, 3 * lw, rows), BF16),
        in_specs=[SM] * 3 + [VM] * 8,
        out_specs=VM,
        scratch_shapes=[
            scratch((heads, tok, dim), BF16),
            scratch((heads, tok, dim), BF16),
            scratch((lw, tok), BF16),
            scratch((heads, tok, dim), BF16),
            scratch((heads, tok, dim), BF16),
            scratch((rows, rows), F32),
            scratch((heads, tok, rows), F32),
            scratch((heads, tok, rows), F32),
            scratch((heads, tok, dim), F32),
            scratch((heads, tok, dim), F32),
            scratch((lw, rows), F32),
            scratch((heads, rows), F32),
        ],
        compiler_params=params(24),
        cost_estimate=pl.CostEstimate(
            flops=8 * 10**9, bytes_accessed=6 * 10**6, transcendentals=3 * 10**6
        ),
    )(info, seg, slopes, *blocks, w, qkv, lse, seg)


def line(vector):
    return vector[...].reshape(1, -1)


def norm_one_kernel(
    info, own, near, far, cross, start, w, gain, shift, low, unit, inverse, joined
):
    part = own.shape[0]
    for step, value in enumerate((own, near, far, cross)):
        first = pl.multiple_of((info[0] ^ step) * part, part)
        joined[pl.ds(first, part), :] = value[...]
    x, inv = standardize(start[...].astype(F32) + dot_tn(joined[...], w[...]))
    unit[...] = x
    inverse[...] = inv
    low[...] = (x * line(gain) + line(shift)).astype(BF16)


def norm_one(info, parts, start, w, gain, shift):
    rows, width = start.shape
    return pl.pallas_call(
        norm_one_kernel,
        name="norm_one",
        out_shape=(shape((rows, width), BF16), shape((rows, width), F32), shape((rows, 1), F32)),
        in_specs=[SM] + [VM] * 8,
        out_specs=(VM,) * 3,
        scratch_shapes=[scratch((width, rows), BF16)],
        compiler_params=params(16),
        cost_estimate=pl.CostEstimate(
            flops=2 * rows * width * width, bytes_accessed=4 * 10**6, transcendentals=0
        ),
    )(info, *parts, start, w, gain, shift)


def ffn_forward_kernel(
    low, unit, gain1, shift1, gain2, shift2, masked, cot, w_gate, w_up, w_down,
    layer_out, d_h2, d_ff, slope, act, sums, acc,
):
    step = pl.program_id(0)
    gate = dot(low[...], w_gate[...])
    up = dot(low[...], w_up[...])
    value, grad = gelu_pair(gate)
    act[...] = value.astype(BF16)
    slope[...] = (up * grad).astype(BF16)
    part = dot((value * up).astype(BF16), w_down[...])

    @pl.when(step == 0)
    def _():
        acc[...] = unit[...] * line(gain1) + line(shift1) + part

    @pl.when(step > 0)
    def _():
        acc[...] += part

    @pl.when(step == pl.num_programs(0) - 1)
    def _():
        x, inv = standardize(acc[...])
        layer_out[...] = (x * line(gain2) + line(shift2)).astype(BF16)
        places = lax.broadcasted_iota(jnp.int32, (low.shape[0], masked.shape[0]), 0)
        dy = exact_dot((places == line(masked)).astype(F32), cot[...])
        sums[0:1, :] = jnp.sum(dy * x, axis=0, keepdims=True)
        sums[1:2, :] = jnp.sum(dy, axis=0, keepdims=True)
        grad_in = standardize_back(dy * line(gain2), x, inv)
        d_h2[...] = grad_in
        d_ff[...] = grad_in.astype(BF16)


def ffn_forward(low, unit, gain1, shift1, gain2, shift2, masked, cot, w_in, w_out, size):
    rows, width = low.shape
    hid = w_out.shape[0]
    count = hid // size
    full = lambda dims: pl.BlockSpec(dims, lambda j: (0,) * len(dims))
    act = pl.BlockSpec((rows, size), lambda j: (0, j))
    return pl.pallas_call(
        ffn_forward_kernel,
        name="ffn_forward",
        grid=(count,),
        out_shape=(
            shape((rows, width), BF16),
            shape((rows, width), F32),
            shape((rows, width), BF16),
            shape((rows, hid), BF16),
            shape((rows, hid), BF16),
            shape((2, width), F32),
        ),
        in_specs=[full((rows, width))] * 2
        + [full((width,))] * 4
        + [
            full(masked.shape),
            full(cot.shape),
            pl.BlockSpec((width, size), lambda j: (0, j)),
            pl.BlockSpec((width, size), lambda j: (0, count + j)),
            pl.BlockSpec((size, width), lambda j: (j, 0)),
        ],
        out_specs=(full((rows, width)),) * 3 + (act, act, full((2, width))),
        scratch_shapes=[scratch((rows, width), F32)],
        compiler_params=params(22),
        cost_estimate=pl.CostEstimate(
            flops=6 * rows * width * hid, bytes_accessed=18 * 10**6, transcendentals=2 * rows * hid
        ),
    )(low, unit, gain1, shift1, gain2, shift2, masked, cot, w_in, w_in, w_out)


def ffn_backward_kernel(
    d_ff, d_h2, unit, inverse, gain1, sums2, act, slope, w_gate, w_up, w_down, d_h1, sent, acc
):
    step = pl.program_id(0)
    d_hidden = dot_nt(d_ff[...], w_down[...])
    d_gate = (d_hidden * slope[...].astype(F32)).astype(BF16)
    d_up = (d_hidden * act[...].astype(F32)).astype(BF16)
    part = dot_nt(d_gate, w_gate[...]) + dot_nt(d_up, w_up[...])

    @pl.when(step == 0)
    def _():
        acc[...] = d_h2[...] + part

    @pl.when(step > 0)
    def _():
        acc[...] += part

    @pl.when(step == pl.num_programs(0) - 1)
    def _():
        total = acc[...]
        rows = total.shape[0]
        x = unit[...]
        gain_sum = jnp.sum(total * x, axis=0, keepdims=True)
        shift_sum = jnp.sum(total, axis=0, keepdims=True)
        sums = jnp.concatenate([gain_sum, shift_sum, sums2[...]], axis=0)
        high = sums.astype(BF16).astype(F32)
        tail = jnp.concatenate([high, sums - high, jnp.zeros((8, sums.shape[1]), F32)], axis=0)
        grad = standardize_back(total * line(gain1), x, inverse[...])
        d_h1[...] = grad
        sent[0:rows, :] = grad.astype(BF16)
        sent[rows : rows + 16, :] = tail.astype(BF16)


def ffn_backward(d_ff, d_h2, unit, inverse, gain1, sums2, act, slope, w_in, w_out, size):
    rows, width = d_ff.shape
    hid = w_out.shape[0]
    count = hid // size
    full = lambda dims: pl.BlockSpec(dims, lambda j: (0,) * len(dims))
    part = pl.BlockSpec((rows, size), lambda j: (0, j))
    return pl.pallas_call(
        ffn_backward_kernel,
        name="ffn_backward",
        grid=(count,),
        out_shape=(shape((rows, width), F32), shape((rows + 16, width), BF16)),
        in_specs=[full((rows, width))] * 3
        + [
            full((rows, 1)),
            full((width,)),
            full((2, width)),
            part,
            part,
            pl.BlockSpec((width, size), lambda j: (0, j)),
            pl.BlockSpec((width, size), lambda j: (0, count + j)),
            pl.BlockSpec((size, width), lambda j: (j, 0)),
        ],
        out_specs=(full((rows, width)), full((rows + 16, width))),
        scratch_shapes=[scratch((rows, width), F32)],
        compiler_params=params(22),
        cost_estimate=pl.CostEstimate(
            flops=6 * rows * width * hid, bytes_accessed=20 * 10**6, transcendentals=0
        ),
    )(d_ff, d_h2, unit, inverse, gain1, sums2, act, slope, w_in, w_in, w_out)


X_FIRST = (1, 2, 4)
Z_FIRST = (2, 1, 4)


def bit_of(value, mask):
    return (value // mask) % 2


def store_blocks(blocks, keep, send, place, order, columns):
    one, two, three = order
    odd = bit_of(place, one) == 1
    for index in range(8):
        if index & one:
            continue
        spot = bit_of(place ^ index, two) * 2 + bit_of(place ^ index, three)
        low, high = blocks(index), blocks(index | one)
        keep[spot, :, columns] = jnp.where(odd, high, low).astype(BF16)
        send[spot, :, columns] = jnp.where(odd, low, high).astype(BF16)


def row_blocks(grad):
    each = grad.shape[0] // 8
    return lambda index: grad[index * each : (index + 1) * each]


def quarter_blocks(grad):
    each = grad.shape[0] // 8

    def block(index):
        at = index % 2 * 4 + index // 2
        return grad[at * each : (at + 1) * each]

    return block


def ffn_grad_kernel(
    order, info, n0, n1, n2, n3, f0, f1, f2, f3, w_gate, w_up, w_down, *rest
):
    if len(rest) == 6:
        keep, send, g_down, tok, tok_t, d_ff = rest
    else:
        down_a, keep, send, keep_down, send_down, tok, tok_t, d_ff, down = rest
    rows = n0.shape[0]
    size = w_gate.shape[1]

    @pl.when(pl.program_id(0) == 0)
    def _():
        for at, (n, f) in enumerate(zip((n0, n1, n2, n3), (f0, f1, f2, f3))):
            here = pl.ds(at * rows, rows)
            tok[here, :] = n[...]
            d_ff[here, :] = f[...]
            tok_t[:, here] = jnp.transpose(n[...])

    gate = dot(tok[...], w_gate[...])
    up = dot(tok[...], w_up[...])
    value, grad = gelu_pair(gate)
    part = dot_tn((value * up).astype(BF16), d_ff[...])
    d_hidden = dot_nt(d_ff[...], w_down[...])
    g_gate = dot(tok_t[...], (d_hidden * up * grad).astype(BF16))
    g_up = dot(tok_t[...], (d_hidden * value).astype(BF16))
    step = pl.program_id(0)
    for other, grad in enumerate((g_gate, g_up)):
        first = (other * pl.num_programs(0) + step) * size
        columns = pl.ds(pl.multiple_of(first, size), size)
        store_blocks(row_blocks(grad), keep, send, info[1], order, columns)
    if len(rest) == 6:
        g_down[...] = part.astype(BF16)
        return
    done = down_a.shape[0]
    down[pl.ds(pl.multiple_of(done + step * size, size), size), :] = part

    @pl.when(step == pl.num_programs(0) - 1)
    def _():
        down[0:done, :] = down_a[...].astype(F32)
        store_blocks(quarter_blocks(down), keep_down, send_down, info[1], X_FIRST, slice(None))


def ffn_grad(info, toks, grads, w_in, w_out, size, first, steps, order, down=None):
    rows, width = toks[0].shape
    count = w_out.shape[0] // RANKS // size
    tok = rows * RANKS
    whole = lambda dims: pl.BlockSpec(dims, lambda j, info: (0,) * len(dims))
    wide = lambda base: pl.BlockSpec(
        (width, size), lambda j, info: (0, (base + info[0]) * count + first + j)
    )
    wide_dims = (4, width // 8, 2 * size * steps)
    down_dims = (4, count * size // 8, width)
    more, out_dims = [], [wide_dims] * 2
    in_specs = [whole((rows, width))] * 8 + [
        wide(0),
        wide(RANKS),
        pl.BlockSpec((size, width), lambda j, info: (info[0] * count + first + j, 0)),
    ]
    scratch_shapes = [
        scratch((tok, width), BF16),
        scratch((width, tok), BF16),
        scratch((tok, width), BF16),
    ]
    if down is None:
        out_dims += [(size, width)]
    else:
        more = [down]
        in_specs += [whole(down.shape)]
        out_dims += [down_dims] * 2
        scratch_shapes += [scratch((count * size, width), F32)]
    return pl.pallas_call(
        functools.partial(ffn_grad_kernel, order),
        name="ffn_grad",
        out_shape=[shape(dims, BF16) for dims in out_dims],
        grid_spec=pltpu.PrefetchScalarGridSpec(
            num_scalar_prefetch=1,
            grid=(steps,),
            in_specs=in_specs,
            out_specs=[whole(dims) for dims in out_dims],
            scratch_shapes=scratch_shapes,
        ),
        compiler_params=params(30),
        cost_estimate=pl.CostEstimate(
            flops=12 * tok * width * size * steps,
            bytes_accessed=8 * 10**6,
            transcendentals=2 * tok * size * steps,
        ),
    )(info, *toks, *grads, w_in, w_in, w_out, *more)


def row_grad_kernel(info, a0, a1, a2, a3, g0, g1, g2, g3, keep, send):
    rows = g0.shape[0] - 16
    grad = 0.0
    sums = 0.0
    for attn, g in zip((a0, a1, a2, a3), (g0, g1, g2, g3)):
        grad = grad + dot(attn[...], g[0:rows, :])
        pair = g[rows : rows + 16, :].astype(F32)
        sums = sums + pair[0:4] + pair[4:8]
    high = sums.astype(BF16).astype(F32)
    tail = jnp.concatenate([high, sums - high], axis=0)
    part = quarter_blocks(grad)

    def blocks(index):
        return jnp.concatenate([part(index), tail], axis=0)

    store_blocks(blocks, keep, send, info[1], X_FIRST, slice(None))


def row_grad(info, attn, blocks):
    width = blocks[0].shape[1]
    dims = (4, attn[0].shape[0] // 8 + 8, width)
    return pl.pallas_call(
        row_grad_kernel,
        name="row_grad",
        out_shape=(shape(dims, BF16),) * 2,
        in_specs=[SM] + [VM] * 8,
        out_specs=(VM, VM),
        compiler_params=params(16),
        cost_estimate=pl.CostEstimate(
            flops=8 * attn[0].size * width, bytes_accessed=3 * 10**6, transcendentals=0
        ),
    )(info, *attn, *blocks)


def qkv_grad_kernel(info, x0, x1, x2, x3, d_qkv, keep, send):
    total = 0.0
    for at, x in enumerate((x0, x1, x2, x3)):
        total = total + dot(d_qkv[info[0] ^ at], x[...])
    store_blocks(row_blocks(jnp.transpose(total)), keep, send, info[1], X_FIRST, slice(None))


def qkv_grad(info, blocks, d_qkv):
    rows, width = blocks[0].shape
    columns = d_qkv.shape[1]
    return pl.pallas_call(
        qkv_grad_kernel,
        name="qkv_grad",
        out_shape=(shape((4, width // 8, columns), BF16),) * 2,
        in_specs=[SM] + [VM] * 5,
        out_specs=(VM, VM),
        compiler_params=params(16),
        cost_estimate=pl.CostEstimate(
            flops=8 * rows * width * columns, bytes_accessed=4 * 10**6, transcendentals=0
        ),
    )(info, *blocks, d_qkv)


def join_wide_kernel(info, b0, b1, b2, b3, out):
    rank = info[0]
    half = out.shape[1] // 2
    part = half // RANKS
    one = part // 3
    for step, block in enumerate((b0, b1, b2, b3)):
        base = pl.multiple_of((rank ^ step) * part, part)
        value = block[...].astype(F32)
        out[:, pl.ds(base, one)] = value[:, 0:one]
        out[:, pl.ds(pl.multiple_of(half + base, one), one)] = value[:, one : 2 * one]
        out[:, pl.ds(pl.multiple_of(base + one, one), 2 * one)] = value[:, 2 * one : 4 * one]
        out[:, pl.ds(pl.multiple_of(half + base + one, one), 2 * one)] = value[:, 4 * one :]


def join_wide(info, blocks):
    rows, columns = blocks[0].shape
    return pl.pallas_call(
        join_wide_kernel,
        name="join_wide",
        out_shape=shape((rows, columns * RANKS), F32),
        in_specs=[SM] + [VM] * 4,
        out_specs=VM,
        cost_estimate=pl.CostEstimate(flops=10**6, bytes_accessed=4 * 10**6, transcendentals=0),
    )(info, *blocks)


def join_rows_kernel(info, b0, b1, b2, b3, down, out):
    rank = info[0]
    many, few = down.shape[0] // RANKS, out.shape[0] // RANKS
    for step, block in enumerate((b0, b1, b2, b3)):
        place = rank ^ step
        value = block[...].astype(F32)
        down[pl.ds(place * many, many), :] = value[0:many]
        out[pl.ds(place * few, few), :] = value[many : many + few]


def join_rows(info, blocks, many):
    rows, columns = blocks[0].shape
    if many % 8 or (rows - many) % 8:
        stacked = jnp.stack(blocks)[info[0] ^ jnp.arange(RANKS)].astype(F32)
        return stacked[:, :many].reshape(-1, columns), stacked[:, many:].reshape(-1, columns)
    return pl.pallas_call(
        join_rows_kernel,
        name="join_rows",
        out_shape=(
            shape((many * RANKS, columns), F32),
            shape(((rows - many) * RANKS, columns), F32),
        ),
        in_specs=[SM] + [VM] * 4,
        out_specs=(VM, VM),
        cost_estimate=pl.CostEstimate(flops=10**6, bytes_accessed=2 * 10**6, transcendentals=0),
    )(info, *blocks)


def join_heads_kernel(info, b0, b1, b2, b3, out):
    rank = info[0]
    width = out.shape[1] // 3
    part = width // RANKS
    for value in range(RANKS):

        @pl.when(rank == value)
        def _():
            for step, block in enumerate((b0, b1, b2, b3)):
                for third in range(3):
                    first = third * width + (value ^ step) * part
                    piece = block[:, third * part : (third + 1) * part]
                    out[:, first : first + part] = piece.astype(F32)


def join_heads(info, blocks):
    rows, columns = blocks[0].shape
    return pl.pallas_call(
        join_heads_kernel,
        name="join_heads",
        out_shape=shape((rows, columns * RANKS), F32),
        in_specs=[SM] + [VM] * 4,
        out_specs=VM,
        cost_estimate=pl.CostEstimate(flops=10**6, bytes_accessed=2 * 10**6, transcendentals=0),
    )(info, *blocks)


def token_grad_kernel(parts, w, d_h1, masked, tokens, replacement, joined):
    rows, width = d_h1.shape
    part = width // RANKS
    for rank in range(RANKS):
        for third in range(3):
            first = third * width + rank * part
            joined[first : first + part, :] = parts[rank, third * part : (third + 1) * part, :]
    grad = d_h1[...] + jnp.transpose(dot(w[...], joined[...]))
    count = masked.shape[0]
    places = lax.broadcasted_iota(jnp.int32, (rows, count), 0)
    select = (places == line(masked)).astype(F32)
    hit = jnp.max(select, axis=1, keepdims=True)
    tokens[...] = jnp.where(hit > 0.5, 0.0, grad)
    replacement[...] = lax.dot_general(
        select, grad, (((0,), (0,)), ((), ())),
        precision=lax.Precision.HIGHEST, preferred_element_type=F32,
    )


def token_grad(parts, w, d_h1, masked):
    rows, width = d_h1.shape
    return pl.pallas_call(
        token_grad_kernel,
        name="token_grad",
        out_shape=(shape((rows, width), F32), shape((masked.shape[0], width), F32)),
        in_specs=[VM] * 4,
        out_specs=(VM, VM),
        scratch_shapes=[scratch((3 * width, rows), BF16)],
        compiler_params=params(16),
        cost_estimate=pl.CostEstimate(
            flops=6 * rows * width * width, bytes_accessed=8 * 10**6, transcendentals=0
        ),
    )(parts, w, d_h1, masked)


def after(value, *others):
    return lax.optimization_barrier((value,) + others)[0]


def flip(value, axis, bits):
    count = lax.axis_size(axis)
    return lax.ppermute(value, axis, [(index, index ^ bits) for index in range(count)])


def gather_blocks(value):
    far = flip(value, "sp", 2)
    near = flip(value, "sp", 1)
    cross = flip(far, "sp", 1)
    return [value, near, far, cross]


def exchange_blocks(blocks):
    via = flip(blocks[3], "sp", 1)
    near = flip(blocks[1], "sp", 1)
    far = flip(blocks[2], "sp", 2)
    cross = flip(via, "sp", 2)
    return [blocks[0], near, far, cross]


def exchange(parts):
    return lax.all_to_all(parts, "sp", 0, 0, tiled=True)


def small_mesh():
    return lax.axis_size("dp") == 8


def halve(keep, came):
    half = keep.shape[0] // 2
    kept = keep[:half].astype(F32) + came[:half].astype(F32)
    sent = keep[half:].astype(F32) + came[half:].astype(F32)
    return kept, sent.astype(BF16)


def send_first(send, order):
    return flip(send, "dp", order[0]) if small_mesh() else send


def send_second(keep, came, order):
    if not small_mesh():
        return keep, came
    kept, sent = halve(keep, came)
    return kept, flip(sent, "dp", order[1])


def send_third(keep, came, order):
    if not small_mesh():
        return keep, came
    kept, sent = halve(keep, came)
    return kept, flip(sent, "dp", order[2])


def natural_blocks(keep, send, order):
    both = jnp.concatenate([keep, send], axis=0).astype(F32)
    places = []
    for index in range(8):
        bits = [1 if index & mask else 0 for mask in order]
        places.append(both[bits[0] * 4 + bits[1] * 2 + bits[2]])
    return places


def finish_sum(keep, came, order):
    if small_mesh():
        return (keep[0] + came[0].astype(F32)).astype(BF16)
    grad = jnp.concatenate(natural_blocks(keep, came, order), axis=0)
    return lax.psum_scatter(grad, "dp", scatter_dimension=0, tiled=True).astype(BF16)


def tidy_sums(value):
    first = value.shape[1] - 8
    sums = value[:, first : first + 4] + value[:, first + 4 :]
    high = sums.astype(BF16).astype(F32)
    return jnp.concatenate([value[:, :first], high, sums - high], axis=1)


def join_kernel(keep_a, came_a, keep_b, came_b, kept, sent):
    half = kept.shape[0]
    many = keep_a.shape[1]
    value = keep_a[...].astype(F32) + came_a[...].astype(F32)
    kept[:, :many] = value[:half]
    sent[:, :many] = value[half:].astype(BF16)
    value = tidy_sums(keep_b[...].astype(F32) + came_b[...].astype(F32))
    kept[:, many:] = value[:half]
    sent[:, many:] = value[half:].astype(BF16)


def join_halve(keep_a, came_a, keep_b, came_b):
    count, many, width = keep_a.shape
    dims = (count // 2, many + keep_b.shape[1], width)
    return pl.pallas_call(
        join_kernel,
        name="join_halve",
        out_shape=(shape(dims, F32), shape(dims, BF16)),
        in_specs=[VM] * 4,
        out_specs=(VM, VM),
        compiler_params=params(16),
        cost_estimate=pl.CostEstimate(flops=10**6, bytes_accessed=4 * 10**6, transcendentals=0),
    )(keep_a, came_a, keep_b, came_b)


def halve_kernel(keep, came, kept, sent):
    half = keep.shape[0] // 2
    value = tidy_sums(keep[...].astype(F32) + came[...].astype(F32))
    kept[...] = value[:half]
    sent[...] = value[half:].astype(BF16)


def halve_sums(keep, came):
    dims = (keep.shape[0] // 2,) + keep.shape[1:]
    return pl.pallas_call(
        halve_kernel,
        name="halve_sums",
        out_shape=(shape(dims, F32), shape(dims, BF16)),
        in_specs=[VM] * 2,
        out_specs=(VM, VM),
        compiler_params=params(16),
        cost_estimate=pl.CostEstimate(flops=10**6, bytes_accessed=2 * 10**6, transcendentals=0),
    )(keep, came)


def send_rows_second(keep_a, came_a, keep_b, came_b):
    if not small_mesh():
        return (
            jnp.concatenate([keep_a, keep_b], axis=1),
            jnp.concatenate([came_a, came_b], axis=1),
        )
    kept, sent = join_halve(keep_a, came_a, keep_b, came_b)
    return kept, flip(sent, "dp", X_FIRST[1])


def send_rows_third(keep, came):
    if not small_mesh():
        return keep, came
    kept, sent = halve_sums(keep, came)
    return kept, flip(sent, "dp", X_FIRST[2])


def finish_rows(keep, came, many):
    count = lax.axis_size("dp")
    each = keep.shape[1] - 8
    moves = []
    if small_mesh():
        for z in range(4):
            for x in range(2):
                for rank in range(4):
                    moves.append(((z * 2 + x) * 4 + rank, (rank * 2 + x) * 4 + z))
        total = keep[0] + came[0].astype(F32)
        shard = total[:each].astype(BF16)
        sums = total[each : each + 4] + total[each + 4 :]
        return lax.ppermute(shard, ("dp", "sp"), moves), sums
    for place in range(count):
        for rank in range(4):
            target = rank * (count // 4) + place // 4
            moves.append((place * 4 + rank, target * 4 + place % 4))
    blocks = natural_blocks(keep, came, X_FIRST)
    blocks = [blocks[index * 2 + bit] for bit in range(2) for index in range(4)]
    results = []
    for first, last in ((0, many), (many, each)):
        grad = jnp.concatenate([block[first:last] for block in blocks], axis=0)
        shard = lax.psum_scatter(grad, "dp", scatter_dimension=0, tiled=True).astype(BF16)
        results.append(lax.ppermute(shard, ("dp", "sp"), moves))
    sums = blocks[0][each : each + 4] + blocks[0][each + 4 :]
    return jnp.concatenate(results, axis=0), lax.psum(sums, "dp")


def local(
    tokens,
    segment_ids,
    masked_rows,
    replacement,
    cotangent,
    w_qkv,
    w_out_attn,
    w_in_ff,
    w_out_ff,
    gain_one,
    shift_one,
    gain_two,
    shift_two,
):
    rows_dev, width = tokens.shape
    rank = lax.axis_index("sp")
    heads = HEADS // RANKS
    dim = width // HEADS
    part = heads * dim
    slopes = alibi_slopes(HEADS)

    select = jnp.arange(rows_dev, dtype=jnp.int32)[:, None] == masked_rows[None, :]
    hit = jnp.any(select, axis=1, keepdims=True)
    placed = dot(select.astype(BF16), replacement)
    start = jnp.where(hit, placed.astype(BF16), tokens)
    start_far = flip(start, "sp", 2)
    start_near = flip(start, "sp", 1)
    place = lax.axis_index("dp")
    place = place if small_mesh() else place * 0
    spot = jnp.stack([rank, place]).astype(jnp.int32)

    w_rank = jnp.concatenate(
        [
            lax.dynamic_slice_in_dim(w_qkv, third * width + rank * part, part, 1)
            for third in range(3)
        ],
        axis=1,
    )
    start_cross = flip(after(start_far, w_rank, spot), "sp", 1)
    start_blocks = [start, start_near, start_far, start_cross]
    qkv, *attn, lse = attention_forward(
        spot, segment_ids, slopes, start_blocks, w_rank, heads, dim
    )
    low, unit, inverse = norm_one(
        spot, exchange_blocks(attn), start, w_out_attn, gain_one, shift_one
    )
    low_far = flip(low, "sp", 2)
    low_near = flip(low, "sp", 1)
    layer_out, d_h2, d_ff, slope, act, sums2 = ffn_forward(
        low, unit, gain_one, shift_one, gain_two, shift_two,
        masked_rows, cotangent, w_in_ff, w_out_ff, 512,
    )
    d_ff_far = flip(d_ff, "sp", 2)
    d_ff_near = flip(d_ff, "sp", 1)
    low_far = after(low_far, d_ff)
    low_cross = flip(low_far, "sp", 1)
    low_blocks = [low, low_near, low_far, low_cross]
    d_h1, sent = ffn_backward(
        after(d_ff, low_far), d_h2, unit, inverse, gain_one, sums2, act, slope, w_in_ff, w_out_ff, 512
    )
    far = flip(sent, "sp", 2)
    near = flip(sent, "sp", 1)
    d_ff_cross = flip(after(d_ff_far, sent), "sp", 1)
    d_ff_blocks = [d_ff, d_ff_near, d_ff_far, d_ff_cross]

    units = w_out_ff.shape[0] // RANKS // 3
    keep_a, send_a, down_a = ffn_grad(
        spot, low_blocks, d_ff_blocks, w_in_ff, w_out_ff, units, 0, 1, X_FIRST
    )
    came_a = send_first(send_a, X_FIRST)
    keep_b, send_b, keep_d, send_d = ffn_grad(
        after(spot, down_a),
        low_blocks, d_ff_blocks, w_in_ff, w_out_ff, units, 1, 2, Z_FIRST, down_a,
    )
    came_b = send_first(send_b, Z_FIRST)
    came_d = send_first(send_d, X_FIRST)
    cross = flip(after(far, came_a, keep_b), "sp", 1)
    d_proj_blocks = [sent, near, far, cross]
    keep_r, send_r = row_grad(spot, attn, d_proj_blocks)
    came_r = send_first(send_r, X_FIRST)

    d_qkv = attention_backward(
        after(spot, keep_r), segment_ids, slopes, d_proj_blocks, w_out_attn, qkv, lse, heads, dim
    )
    parts = exchange(d_qkv)
    keep_q, send_q = qkv_grad(
        after(spot, came_b, came_d), start_blocks, d_qkv
    )
    came_q = send_first(send_q, X_FIRST)
    keep_r, came_r = send_rows_second(keep_d, after(came_d, keep_q), keep_r, came_r)
    keep_b, came_b = send_second(keep_b, after(came_b, keep_r), Z_FIRST)
    keep_a, came_a = send_second(keep_a, after(came_a, keep_b), X_FIRST)
    grad_tokens, grad_replacement = token_grad(
        after(parts, keep_a), w_qkv, d_h1, masked_rows
    )
    keep_q, came_q = send_second(keep_q, after(came_q, grad_tokens), X_FIRST)
    keep_r, came_r = send_rows_third(keep_r, after(came_r, keep_q))
    keep_b, came_b = send_third(keep_b, after(came_b, keep_r), Z_FIRST)
    keep_a, came_a = send_third(keep_a, after(came_a, keep_b), X_FIRST)
    keep_q, came_q = send_third(keep_q, after(came_q, keep_a), X_FIRST)
    wide_a = finish_sum(keep_a, came_a, X_FIRST)
    wide_b = finish_sum(keep_b, came_b, Z_FIRST)
    wide_blocks = gather_blocks(jnp.concatenate([wide_a, wide_b], axis=1))
    many = w_out_ff.shape[0] // RANKS // 8
    row_share, norm_sums = finish_rows(keep_r, came_r, many)
    head_blocks = gather_blocks(finish_sum(keep_q, came_q, X_FIRST))
    row_blocks_ = gather_blocks(row_share)
    many = w_out_ff.shape[0] // lax.axis_size("dp") // RANKS
    grad_down, grad_out = join_rows(spot, row_blocks_, many)

    return (
        layer_out,
        grad_tokens,
        grad_replacement,
        join_heads(spot, head_blocks),
        grad_out,
        join_wide(spot, wide_blocks),
        grad_down,
        norm_sums[0],
        norm_sums[1],
        norm_sums[2],
        norm_sums[3],
    )


def solution(mesh):
    tokens = P(("dp", "sp"), None)
    rows = P("dp", None)
    return jax.shard_map(
        local,
        mesh=mesh,
        in_specs=(tokens, rows, P(("dp", "sp")), tokens, tokens) + (P(),) * 8,
        out_specs=(tokens,) * 3 + (rows,) * 4 + (P(),) * 4,
        check_vma=False,
    )
```

```python
import functools
import math

import jax
import jax.numpy as jnp
from jax import lax
from jax.experimental import pallas as pl
from jax.experimental.pallas import tpu as pltpu
from jax.sharding import PartitionSpec as P

HEADS = 12
RANKS = 4
EPSILON = 1e-05
FAR = 1e30
F32 = jnp.float32
BF16 = jnp.bfloat16
VM = pl.BlockSpec(memory_space=pltpu.VMEM)
SM = pl.BlockSpec(memory_space=pltpu.SMEM)


def shape(dims, kind):
    return jax.ShapeDtypeStruct(dims, kind)


def scratch(dims, kind):
    return pltpu.VMEM(dims, kind)


def params(mebibytes):
    return pltpu.CompilerParams(vmem_limit_bytes=mebibytes << 20)


def alibi_slopes(head_count):
    nearest = 2 ** int(math.floor(math.log2(head_count)))
    base_list = [2.0 ** (-8.0 * (index + 1) / nearest) for index in range(nearest)]
    extra_list = [
        2.0 ** (-8.0 * (2 * index + 1) / (2 * nearest)) for index in range(head_count - nearest)
    ]
    return jnp.array(base_list + extra_list, dtype=F32)


def dot(a, b):
    return jnp.dot(a, b, preferred_element_type=F32)


def dot_nt(a, b):
    return lax.dot_general(a, b, (((1,), (1,)), ((), ())), preferred_element_type=F32)


def dot_tn(a, b):
    return lax.dot_general(a, b, (((0,), (0,)), ((), ())), preferred_element_type=F32)


def exact_dot(a, b):
    return jnp.dot(a, b, precision=lax.Precision.HIGHEST, preferred_element_type=F32)


def standardize(value):
    center = value - jnp.mean(value, axis=-1, keepdims=True)
    spread = jnp.mean(center * center, axis=-1, keepdims=True)
    inverse = lax.rsqrt(spread + EPSILON)
    return center * inverse, inverse


def standardize_back(grad, unit, inverse):
    mean = jnp.mean(grad, axis=-1, keepdims=True)
    return inverse * (grad - mean - unit * jnp.mean(grad * unit, axis=-1, keepdims=True))


def gelu_pair(x):
    cdf = 0.5 * (1.0 + lax.erf(x * math.sqrt(0.5)))
    pdf = jnp.exp(-0.5 * x * x) * (1.0 / math.sqrt(2.0 * math.pi))
    return x * cdf, cdf + x * pdf


def pair_active(seg, rank, first, second, rows):
    one, two = rank ^ first, rank ^ second
    low, high = jnp.minimum(one, two), jnp.maximum(one, two)
    return jnp.logical_or(one == two, seg[0, low * rows + rows - 1] == seg[0, high * rows])


def key_sequences(seg_rows, seg_keys, rank, rows):
    for at in range(RANKS):
        first = pl.multiple_of((rank ^ at) * rows, rows)
        line = jnp.broadcast_to(seg_rows[:, pl.ds(first, rows)], (128, rows))
        seg_keys[at * rows : (at + 1) * rows, :] = jnp.transpose(line)


def pair_distance(seg_rows, seg_keys, rank, keys_at, query_at, rows):
    key_pos, query_pos = (rank ^ keys_at) * rows, (rank ^ query_at) * rows
    down = lax.broadcasted_iota(jnp.int32, (rows, rows), 0)
    across = lax.broadcasted_iota(jnp.int32, (rows, rows), 1)
    gap = jnp.abs(down - across + (key_pos - query_pos)).astype(F32)
    seg_q = seg_rows[:, pl.ds(pl.multiple_of(query_pos, rows), rows)]
    seg_k = seg_keys[pl.ds(pl.multiple_of(keys_at * rows, rows), rows), 0:1]
    return jnp.where(seg_k == seg_q, gap, FAR)


def attention_forward_kernel(
    rows, heads, dim, info, seg, slopes, x0, x1, x2, x3, w, seg_rows,
    qkv_out, o0, o1, o2, o3, lse, qs, ks, vt, dist, seg_keys, score, peak,
):
    rank = info[0]
    width = heads * dim
    key_sequences(seg_rows, seg_keys, rank, rows)
    for at, x in enumerate((x0, x1, x2, x3)):
        qkv = dot(x[...], w[...]).astype(BF16)
        here = pl.ds(at * rows, rows)
        qkv_out[here, :] = qkv
        for h in range(heads):
            qs[h, here, :] = (qkv[:, h * dim : (h + 1) * dim] * dim**-0.5).astype(BF16)
            ks[h, here, :] = qkv[:, width + h * dim : width + (h + 1) * dim]
        vt[:, here] = jnp.transpose(qkv[:, 2 * width :])

    for a in range(RANKS):
        mine = pl.ds(a * rows, rows)
        peak[...] = jnp.full_like(peak, -jnp.inf)

        def first_pass(b, carry):
            @pl.when(pair_active(seg, rank, a, b, rows))
            def _():
                theirs = pl.ds(pl.multiple_of(b * rows, rows), rows)
                gap = pair_distance(seg_rows, seg_keys, rank, b, a, rows)
                for h in range(heads):
                    slope = slopes[rank * heads + h]
                    s = dot_nt(ks[h, theirs, :], qs[h, mine, :]) - slope * gap
                    score[h, theirs, :] = s
                    peak[h : h + 1, :] = jnp.maximum(
                        peak[h : h + 1, :], jnp.max(s, axis=0, keepdims=True)
                    )

            return carry

        lax.fori_loop(0, RANKS, first_pass, 0)

        def second_pass(b, carry):
            def add(carry):
                theirs = pl.ds(pl.multiple_of(b * rows, rows), rows)
                result = []
                for h in range(heads):
                    acc, total = carry[h]
                    p = jnp.exp(score[h, theirs, :] - peak[h : h + 1, :])
                    total = total + jnp.sum(p, axis=0, keepdims=True)
                    span = slice(h * dim, (h + 1) * dim)
                    result.append((acc + dot(vt[span, theirs], p.astype(BF16)), total))
                return tuple(result)

            return lax.cond(pair_active(seg, rank, a, b, rows), add, lambda carry: carry, carry)

        empty = (jnp.zeros((dim, rows), F32), jnp.zeros((1, rows), F32))
        sums = lax.fori_loop(0, RANKS, second_pass, (empty,) * heads)
        for h in range(heads):
            acc, total = sums[h]
            span = slice(h * dim, (h + 1) * dim)
            (o0, o1, o2, o3)[a][span, :] = (acc / total).astype(BF16)
            lse[h : h + 1, mine] = peak[h : h + 1, :] + jnp.log(total)


def attention_forward(info, seg, slopes, blocks, w, heads, dim):
    rows = blocks[0].shape[0]
    tok, lw = rows * RANKS, heads * dim
    return pl.pallas_call(
        functools.partial(attention_forward_kernel, rows, heads, dim),
        name="attention_forward",
        out_shape=(shape((tok, 3 * lw), BF16),)
        + (shape((lw, rows), BF16),) * RANKS
        + (shape((heads, tok), F32),),
        in_specs=[SM] * 3 + [VM] * 6,
        out_specs=(VM,) * 6,
        scratch_shapes=[
            scratch((heads, tok, dim), BF16),
            scratch((heads, tok, dim), BF16),
            scratch((lw, tok), BF16),
            scratch((rows, rows), F32),
            scratch((tok, 128), jnp.int32),
            scratch((heads, tok, rows), F32),
            scratch((heads, rows), F32),
        ],
        compiler_params=params(20),
        cost_estimate=pl.CostEstimate(
            flops=4 * 10**9, bytes_accessed=6 * 10**6, transcendentals=3 * 10**6
        ),
    )(info, seg, slopes, *blocks, w, seg)


def attention_backward_kernel(
    rows, heads, dim, info, seg, slopes, g0, g1, g2, g3, w, qkv, lse, seg_rows,
    d_qkv, qs, ks, kt, vs, do, seg_keys, prob, dprob, dk, dv, dqt, delta,
):
    rank = info[0]
    width = heads * dim
    scale = dim**-0.5
    key_sequences(seg_rows, seg_keys, rank, rows)
    w_rank = w[pl.ds(pl.multiple_of(rank * width, width), width), :]
    for at, g in enumerate((g0, g1, g2, g3)):
        here = pl.ds(at * rows, rows)
        grad = dot_nt(g[0:rows, :], w_rank).astype(BF16)
        value = qkv[here, :]
        kt[:, here] = jnp.transpose(value[:, width : 2 * width])
        for h in range(heads):
            do[h, here, :] = grad[:, h * dim : (h + 1) * dim]
            qs[h, here, :] = (value[:, h * dim : (h + 1) * dim] * scale).astype(BF16)
            ks[h, here, :] = value[:, width + h * dim : width + (h + 1) * dim]
            vs[h, here, :] = value[:, 2 * width + h * dim : 2 * width + (h + 1) * dim]
    dk[...] = jnp.zeros_like(dk)
    dv[...] = jnp.zeros_like(dv)

    for a in range(RANKS):
        mine = pl.ds(a * rows, rows)
        delta[...] = jnp.zeros_like(delta)
        dqt[...] = jnp.zeros_like(dqt)

        def first_pass(b, carry):
            @pl.when(pair_active(seg, rank, a, b, rows))
            def _():
                theirs = pl.ds(pl.multiple_of(b * rows, rows), rows)
                gap = pair_distance(seg_rows, seg_keys, rank, b, a, rows)
                for h in range(heads):
                    slope = slopes[rank * heads + h]
                    s = dot_nt(ks[h, theirs, :], qs[h, mine, :]) - slope * gap
                    p = jnp.exp(s - lse[h : h + 1, mine])
                    dp = dot_nt(vs[h, theirs, :], do[h, mine, :])
                    delta[h : h + 1, :] += jnp.sum(p * dp, axis=0, keepdims=True)
                    prob[h, theirs, :] = p
                    dprob[h, theirs, :] = dp

            return carry

        lax.fori_loop(0, RANKS, first_pass, 0)

        def second_pass(b, carry):
            @pl.when(pair_active(seg, rank, a, b, rows))
            def _():
                theirs = pl.ds(pl.multiple_of(b * rows, rows), rows)
                for h in range(heads):
                    p = prob[h, theirs, :]
                    ds = (p * (dprob[h, theirs, :] - delta[h : h + 1, :])).astype(BF16)
                    dv[h, theirs, :] += dot(p.astype(BF16), do[h, mine, :])
                    dk[h, theirs, :] += dot(ds, qs[h, mine, :])
                    span = slice(h * dim, (h + 1) * dim)
                    dqt[span, :] += dot(kt[span, theirs], ds)

            return carry

        lax.fori_loop(0, RANKS, second_pass, 0)
        d_qkv[rank ^ a, 0:width, :] = (dqt[...] * scale).astype(BF16)

    for at in range(RANKS):
        here = pl.ds(at * rows, rows)
        for h in range(heads):
            first = width + h * dim
            d_qkv[rank ^ at, first : first + dim, :] = jnp.transpose(dk[h, here, :]).astype(BF16)
            first = 2 * width + h * dim
            d_qkv[rank ^ at, first : first + dim, :] = jnp.transpose(dv[h, here, :]).astype(BF16)


def attention_backward(info, seg, slopes, blocks, w, qkv, lse, heads, dim):
    tok, lw = qkv.shape[0], heads * dim
    rows = tok // RANKS
    return pl.pallas_call(
        functools.partial(attention_backward_kernel, rows, heads, dim),
        name="attention_backward",
        out_shape=shape((RANKS, 3 * lw, rows), BF16),
        in_specs=[SM] * 3 + [VM] * 8,
        out_specs=VM,
        scratch_shapes=[
            scratch((heads, tok, dim), BF16),
            scratch((heads, tok, dim), BF16),
            scratch((lw, tok), BF16),
            scratch((heads, tok, dim), BF16),
            scratch((heads, tok, dim), BF16),
            scratch((tok, 128), jnp.int32),
            scratch((heads, tok, rows), F32),
            scratch((heads, tok, rows), F32),
            scratch((heads, tok, dim), F32),
            scratch((heads, tok, dim), F32),
            scratch((lw, rows), F32),
            scratch((heads, rows), F32),
        ],
        compiler_params=params(24),
        cost_estimate=pl.CostEstimate(
            flops=8 * 10**9, bytes_accessed=6 * 10**6, transcendentals=3 * 10**6
        ),
    )(info, seg, slopes, *blocks, w, qkv, lse, seg)


def line(vector):
    return vector[...].reshape(1, -1)


def norm_one_kernel(
    info, own, near, far, cross, start, w, gain, shift, low, unit, inverse, joined
):
    part = own.shape[0]
    for step, value in enumerate((own, near, far, cross)):
        first = pl.multiple_of((info[0] ^ step) * part, part)
        joined[pl.ds(first, part), :] = value[...]
    x, inv = standardize(start[...].astype(F32) + dot_tn(joined[...], w[...]))
    unit[...] = x
    inverse[...] = inv
    low[...] = (x * line(gain) + line(shift)).astype(BF16)


def norm_one(info, parts, start, w, gain, shift):
    rows, width = start.shape
    return pl.pallas_call(
        norm_one_kernel,
        name="norm_one",
        out_shape=(shape((rows, width), BF16), shape((rows, width), F32), shape((rows, 1), F32)),
        in_specs=[SM] + [VM] * 8,
        out_specs=(VM,) * 3,
        scratch_shapes=[scratch((width, rows), BF16)],
        compiler_params=params(16),
        cost_estimate=pl.CostEstimate(
            flops=2 * rows * width * width, bytes_accessed=4 * 10**6, transcendentals=0
        ),
    )(info, *parts, start, w, gain, shift)


def ffn_forward_kernel(
    low, unit, gain1, shift1, gain2, shift2, masked, cot, w_in, w_down,
    layer_out, d_h2, d_ff, slope, act, sums, acc, gates, ups,
):
    hid = w_down.shape[0]
    size = gates.shape[2]
    count = hid // size

    def project(block, slot):
        first = pl.multiple_of(block * size, size)
        gates[slot] = dot(low[...], w_in[:, pl.ds(first, size)])
        ups[slot] = dot(low[...], w_in[:, pl.ds(pl.multiple_of(hid + first, size), size)])

    def finish(block, slot):
        here = pl.ds(pl.multiple_of(block * size, size), size)
        up = ups[slot]
        value, grad = gelu_pair(gates[slot])
        act[:, here] = value.astype(BF16)
        slope[:, here] = (up * grad).astype(BF16)
        acc[...] += dot((value * up).astype(BF16), w_down[here, :])

    acc[...] = unit[...] * line(gain1) + line(shift1)
    project(0, 0)

    def pair(index, carry):
        block = index * 2
        project(block + 1, 1)
        finish(block, 0)
        project(block + 2, 0)
        finish(block + 1, 1)
        return carry

    lax.fori_loop(0, count // 2 - 1, pair, 0)
    project(count - 1, 1)
    finish(count - 2, 0)
    finish(count - 1, 1)
    x, inv = standardize(acc[...])
    layer_out[...] = (x * line(gain2) + line(shift2)).astype(BF16)
    places = lax.broadcasted_iota(jnp.int32, (low.shape[0], masked.shape[0]), 0)
    dy = exact_dot((places == line(masked)).astype(F32), cot[...])
    sums[0:1, :] = jnp.sum(dy * x, axis=0, keepdims=True)
    sums[1:2, :] = jnp.sum(dy, axis=0, keepdims=True)
    grad_in = standardize_back(dy * line(gain2), x, inv)
    d_h2[...] = grad_in
    d_ff[...] = grad_in.astype(BF16)


def ffn_forward(low, unit, gain1, shift1, gain2, shift2, masked, cot, w_in, w_out, size):
    rows, width = low.shape
    hid = w_out.shape[0]
    return pl.pallas_call(
        ffn_forward_kernel,
        name="ffn_forward",
        out_shape=(
            shape((rows, width), BF16),
            shape((rows, width), F32),
            shape((rows, width), BF16),
            shape((rows, hid), BF16),
            shape((rows, hid), BF16),
            shape((2, width), F32),
        ),
        in_specs=[VM] * 10,
        out_specs=(VM,) * 6,
        scratch_shapes=[
            scratch((rows, width), F32),
            scratch((2, rows, size), F32),
            scratch((2, rows, size), F32),
        ],
        compiler_params=params(30),
        cost_estimate=pl.CostEstimate(
            flops=6 * rows * width * hid, bytes_accessed=18 * 10**6, transcendentals=2 * rows * hid
        ),
    )(low, unit, gain1, shift1, gain2, shift2, masked, cot, w_in, w_out)


def ffn_backward_kernel(
    d_ff, d_h2, unit, inverse, gain1, sums2, act, slope, w_in, w_down, d_h1, sent, acc, hidden
):
    hid = w_down.shape[0]
    size = hidden.shape[2]
    count = hid // size

    def project(block, slot):
        here = pl.ds(pl.multiple_of(block * size, size), size)
        hidden[slot] = dot_nt(d_ff[...], w_down[here, :])

    def finish(block, slot):
        first = pl.multiple_of(block * size, size)
        here, there = pl.ds(first, size), pl.ds(pl.multiple_of(hid + first, size), size)
        d_hidden = hidden[slot]
        d_gate = (d_hidden * slope[:, here].astype(F32)).astype(BF16)
        d_up = (d_hidden * act[:, here].astype(F32)).astype(BF16)
        acc[...] += dot_nt(d_gate, w_in[:, here]) + dot_nt(d_up, w_in[:, there])

    acc[...] = d_h2[...]
    project(0, 0)

    def pair(index, carry):
        block = index * 2
        project(block + 1, 1)
        finish(block, 0)
        project(block + 2, 0)
        finish(block + 1, 1)
        return carry

    lax.fori_loop(0, count // 2 - 1, pair, 0)
    project(count - 1, 1)
    finish(count - 2, 0)
    finish(count - 1, 1)
    total = acc[...]
    rows = total.shape[0]
    x = unit[...]
    gain_sum = jnp.sum(total * x, axis=0, keepdims=True)
    shift_sum = jnp.sum(total, axis=0, keepdims=True)
    sums = jnp.concatenate([gain_sum, shift_sum, sums2[...]], axis=0)
    high = sums.astype(BF16).astype(F32)
    tail = jnp.concatenate([high, sums - high, jnp.zeros((8, sums.shape[1]), F32)], axis=0)
    grad = standardize_back(total * line(gain1), x, inverse[...])
    d_h1[...] = grad
    sent[0:rows, :] = grad.astype(BF16)
    sent[rows : rows + 16, :] = tail.astype(BF16)


def ffn_backward(d_ff, d_h2, unit, inverse, gain1, sums2, act, slope, w_in, w_out, size):
    rows, width = d_ff.shape
    hid = w_out.shape[0]
    return pl.pallas_call(
        ffn_backward_kernel,
        name="ffn_backward",
        out_shape=(shape((rows, width), F32), shape((rows + 16, width), BF16)),
        in_specs=[VM] * 10,
        out_specs=(VM,) * 2,
        scratch_shapes=[scratch((rows, width), F32), scratch((2, rows, size), F32)],
        compiler_params=params(30),
        cost_estimate=pl.CostEstimate(
            flops=6 * rows * width * hid, bytes_accessed=20 * 10**6, transcendentals=0
        ),
    )(d_ff, d_h2, unit, inverse, gain1, sums2, act, slope, w_in, w_out)


X_FIRST = (1, 2, 4)
Z_FIRST = (2, 1, 4)


def bit_of(value, mask):
    return (value // mask) % 2


def store_blocks(blocks, keep, send, place, order, columns):
    one, two, three = order
    odd = bit_of(place, one) == 1
    for index in range(8):
        if index & one:
            continue
        spot = bit_of(place ^ index, two) * 2 + bit_of(place ^ index, three)
        low, high = blocks(index), blocks(index | one)
        keep[spot, :, columns] = jnp.where(odd, high, low).astype(BF16)
        send[spot, :, columns] = jnp.where(odd, low, high).astype(BF16)


def row_blocks(grad):
    each = grad.shape[0] // 8
    return lambda index: grad[index * each : (index + 1) * each]


def quarter_blocks(grad):
    each = grad.shape[0] // 8

    def block(index):
        at = index % 2 * 4 + index // 2
        return grad[at * each : (at + 1) * each]

    return block


def ffn_grad_kernel(
    order, size, first, steps, info, n0, n1, n2, n3, f0, f1, f2, f3, w_in, w_down, *rest
):
    if first == 0:
        keep, send, g_down, tok_t, gates, ups, d_hiddens, hidden_t, d_gate, d_up, d_ff = rest
    else:
        tok_t, down_a, keep, send, keep_down, send_down = rest[:6]
        gates, ups, d_hiddens, hidden_t, d_gate, d_up, d_ff, down = rest[6:]
    toks, grads = (n0, n1, n2, n3), (f0, f1, f2, f3)
    rows = n0.shape[0]
    hid = w_down.shape[0]
    for at in range(RANKS):
        here = slice(at * rows, (at + 1) * rows)
        d_ff[here, :] = grads[at][...]
        if first == 0:
            tok_t[:, here] = jnp.transpose(toks[at][...])

    def unit_block(step, carry):
        base = pl.multiple_of(info[0] * (hid // RANKS) + (first + step) * size, size)
        w_gate = w_in[:, pl.ds(base, size)]
        w_up = w_in[:, pl.ds(pl.multiple_of(hid + base, size), size)]
        w_rows = w_down[pl.ds(base, size), :]

        def project(at):
            slot = at % 2
            gates[slot] = dot(toks[at][...], w_gate)
            ups[slot] = dot(toks[at][...], w_up)
            d_hiddens[slot] = dot_nt(grads[at][...], w_rows)

        def finish(at):
            slot = at % 2
            here = slice(at * rows, (at + 1) * rows)
            value, grad = gelu_pair(gates[slot])
            up, d_hidden = ups[slot], d_hiddens[slot]
            hidden_t[:, here] = jnp.transpose((value * up).astype(BF16))
            d_gate[here, :] = (d_hidden * up * grad).astype(BF16)
            d_up[here, :] = (d_hidden * value).astype(BF16)

        project(0)
        for at in range(RANKS):
            if at + 1 < RANKS:
                project(at + 1)
            finish(at)
        for other, grad in enumerate((d_gate, d_up)):
            columns = pl.ds(pl.multiple_of((other * steps + step) * size, size), size)
            total = dot(tok_t[...], grad[...])
            store_blocks(row_blocks(total), keep, send, info[1], order, columns)
        part = dot(hidden_t[...], d_ff[...])
        if first == 0:
            g_down[...] = part.astype(BF16)
        else:
            down[pl.ds(pl.multiple_of((first + step) * size, size), size), :] = part
        return carry

    if steps == 1:
        unit_block(0, 0)
    else:
        lax.fori_loop(0, steps, unit_block, 0)
    if first:
        down[0 : first * size, :] = down_a[...].astype(F32)
        store_blocks(quarter_blocks(down), keep_down, send_down, info[1], X_FIRST, slice(None))


def ffn_grad(info, toks, grads, w_in, w_out, size, first, steps, order, more=()):
    rows, width = toks[0].shape
    part = w_out.shape[0] // RANKS
    tok = rows * RANKS
    dims = [(4, width // 8, 2 * size * steps)] * 2
    scratch_shapes = [
        scratch((2, rows, size), F32),
        scratch((2, rows, size), F32),
        scratch((2, rows, size), F32),
        scratch((size, tok), BF16),
        scratch((tok, size), BF16),
        scratch((tok, size), BF16),
        scratch((tok, width), BF16),
    ]
    if first == 0:
        dims += [(size, width), (width, tok)]
    else:
        dims += [(4, part // 8, width)] * 2
        scratch_shapes += [scratch((part, width), F32)]
    return pl.pallas_call(
        functools.partial(ffn_grad_kernel, order, size, first, steps),
        name="ffn_grad",
        out_shape=[shape(each, BF16) for each in dims],
        in_specs=[SM] + [VM] * (10 + len(more)),
        out_specs=[VM] * len(dims),
        scratch_shapes=scratch_shapes,
        compiler_params=params(26),
        cost_estimate=pl.CostEstimate(
            flops=12 * tok * width * size * steps,
            bytes_accessed=8 * 10**6,
            transcendentals=2 * tok * size * steps,
        ),
    )(info, *toks, *grads, w_in, w_out, *more)


def row_grad_kernel(info, a0, a1, a2, a3, g0, g1, g2, g3, keep, send):
    rows = g0.shape[0] - 16
    grad = 0.0
    sums = 0.0
    for attn, g in zip((a0, a1, a2, a3), (g0, g1, g2, g3)):
        grad = grad + dot(attn[...], g[0:rows, :])
        pair = g[rows : rows + 16, :].astype(F32)
        sums = sums + pair[0:4] + pair[4:8]
    high = sums.astype(BF16).astype(F32)
    tail = jnp.concatenate([high, sums - high], axis=0)
    part = quarter_blocks(grad)

    def blocks(index):
        return jnp.concatenate([part(index), tail], axis=0)

    store_blocks(blocks, keep, send, info[1], X_FIRST, slice(None))


def row_grad(info, attn, blocks):
    width = blocks[0].shape[1]
    dims = (4, attn[0].shape[0] // 8 + 8, width)
    return pl.pallas_call(
        row_grad_kernel,
        name="row_grad",
        out_shape=(shape(dims, BF16),) * 2,
        in_specs=[SM] + [VM] * 8,
        out_specs=(VM, VM),
        compiler_params=params(16),
        cost_estimate=pl.CostEstimate(
            flops=8 * attn[0].size * width, bytes_accessed=3 * 10**6, transcendentals=0
        ),
    )(info, *attn, *blocks)


def qkv_grad_kernel(info, x0, x1, x2, x3, d_qkv, keep, send):
    total = 0.0
    for at, x in enumerate((x0, x1, x2, x3)):
        total = total + dot(d_qkv[info[0] ^ at], x[...])
    store_blocks(row_blocks(jnp.transpose(total)), keep, send, info[1], X_FIRST, slice(None))


def qkv_grad(info, blocks, d_qkv):
    rows, width = blocks[0].shape
    columns = d_qkv.shape[1]
    return pl.pallas_call(
        qkv_grad_kernel,
        name="qkv_grad",
        out_shape=(shape((4, width // 8, columns), BF16),) * 2,
        in_specs=[SM] + [VM] * 5,
        out_specs=(VM, VM),
        compiler_params=params(16),
        cost_estimate=pl.CostEstimate(
            flops=8 * rows * width * columns, bytes_accessed=4 * 10**6, transcendentals=0
        ),
    )(info, *blocks, d_qkv)


def join_wide_kernel(info, b0, b1, b2, b3, out):
    rank = info[0]
    half = out.shape[1] // 2
    part = half // RANKS
    one = part // 3
    for step, block in enumerate((b0, b1, b2, b3)):
        base = pl.multiple_of((rank ^ step) * part, part)
        value = block[...].astype(F32)
        out[:, pl.ds(base, one)] = value[:, 0:one]
        out[:, pl.ds(pl.multiple_of(half + base, one), one)] = value[:, one : 2 * one]
        out[:, pl.ds(pl.multiple_of(base + one, one), 2 * one)] = value[:, 2 * one : 4 * one]
        out[:, pl.ds(pl.multiple_of(half + base + one, one), 2 * one)] = value[:, 4 * one :]


def join_wide(info, blocks):
    rows, columns = blocks[0].shape
    return pl.pallas_call(
        join_wide_kernel,
        name="join_wide",
        out_shape=shape((rows, columns * RANKS), F32),
        in_specs=[SM] + [VM] * 4,
        out_specs=VM,
        cost_estimate=pl.CostEstimate(flops=10**6, bytes_accessed=4 * 10**6, transcendentals=0),
    )(info, *blocks)


def join_rows_kernel(info, b0, b1, b2, b3, down, out):
    rank = info[0]
    many, few = down.shape[0] // RANKS, out.shape[0] // RANKS
    for step, block in enumerate((b0, b1, b2, b3)):
        place = rank ^ step
        value = block[...].astype(F32)
        down[pl.ds(place * many, many), :] = value[0:many]
        out[pl.ds(place * few, few), :] = value[many : many + few]


def join_rows(info, blocks, many):
    rows, columns = blocks[0].shape
    if many % 8 or (rows - many) % 8:
        stacked = jnp.stack(blocks)[info[0] ^ jnp.arange(RANKS)].astype(F32)
        return stacked[:, :many].reshape(-1, columns), stacked[:, many:].reshape(-1, columns)
    return pl.pallas_call(
        join_rows_kernel,
        name="join_rows",
        out_shape=(
            shape((many * RANKS, columns), F32),
            shape(((rows - many) * RANKS, columns), F32),
        ),
        in_specs=[SM] + [VM] * 4,
        out_specs=(VM, VM),
        cost_estimate=pl.CostEstimate(flops=10**6, bytes_accessed=2 * 10**6, transcendentals=0),
    )(info, *blocks)


def join_heads_kernel(info, b0, b1, b2, b3, out):
    rank = info[0]
    width = out.shape[1] // 3
    part = width // RANKS
    for value in range(RANKS):

        @pl.when(rank == value)
        def _():
            for step, block in enumerate((b0, b1, b2, b3)):
                for third in range(3):
                    first = third * width + (value ^ step) * part
                    piece = block[:, third * part : (third + 1) * part]
                    out[:, first : first + part] = piece.astype(F32)


def join_heads(info, blocks):
    rows, columns = blocks[0].shape
    return pl.pallas_call(
        join_heads_kernel,
        name="join_heads",
        out_shape=shape((rows, columns * RANKS), F32),
        in_specs=[SM] + [VM] * 4,
        out_specs=VM,
        cost_estimate=pl.CostEstimate(flops=10**6, bytes_accessed=2 * 10**6, transcendentals=0),
    )(info, *blocks)


def token_grad_kernel(parts, w, d_h1, masked, tokens, replacement, joined):
    rows, width = d_h1.shape
    part = width // RANKS
    for rank in range(RANKS):
        for third in range(3):
            first = third * width + rank * part
            joined[first : first + part, :] = parts[rank, third * part : (third + 1) * part, :]
    grad = d_h1[...] + jnp.transpose(dot(w[...], joined[...]))
    count = masked.shape[0]
    places = lax.broadcasted_iota(jnp.int32, (rows, count), 0)
    select = (places == line(masked)).astype(F32)
    hit = jnp.max(select, axis=1, keepdims=True)
    tokens[...] = jnp.where(hit > 0.5, 0.0, grad)
    replacement[...] = lax.dot_general(
        select, grad, (((0,), (0,)), ((), ())),
        precision=lax.Precision.HIGHEST, preferred_element_type=F32,
    )


def token_grad(parts, w, d_h1, masked):
    rows, width = d_h1.shape
    return pl.pallas_call(
        token_grad_kernel,
        name="token_grad",
        out_shape=(shape((rows, width), F32), shape((masked.shape[0], width), F32)),
        in_specs=[VM] * 4,
        out_specs=(VM, VM),
        scratch_shapes=[scratch((3 * width, rows), BF16)],
        compiler_params=params(16),
        cost_estimate=pl.CostEstimate(
            flops=6 * rows * width * width, bytes_accessed=8 * 10**6, transcendentals=0
        ),
    )(parts, w, d_h1, masked)


def after(value, *others):
    return lax.optimization_barrier((value,) + others)[0]


def flip(value, axis, bits):
    count = lax.axis_size(axis)
    return lax.ppermute(value, axis, [(index, index ^ bits) for index in range(count)])


def gather_blocks(value):
    far = flip(value, "sp", 2)
    near = flip(value, "sp", 1)
    cross = flip(far, "sp", 1)
    return [value, near, far, cross]


def exchange_blocks(blocks):
    via = flip(blocks[3], "sp", 1)
    near = flip(blocks[1], "sp", 1)
    far = flip(blocks[2], "sp", 2)
    cross = flip(via, "sp", 2)
    return [blocks[0], near, far, cross]


def exchange(parts):
    return lax.all_to_all(parts, "sp", 0, 0, tiled=True)


def small_mesh():
    return lax.axis_size("dp") == 8


def halve(keep, came):
    half = keep.shape[0] // 2
    kept = keep[:half].astype(F32) + came[:half].astype(F32)
    sent = keep[half:].astype(F32) + came[half:].astype(F32)
    return kept, sent.astype(BF16)


def send_first(send, order):
    return flip(send, "dp", order[0]) if small_mesh() else send


def send_second(keep, came, order):
    if not small_mesh():
        return keep, came
    kept, sent = halve(keep, came)
    return kept, flip(sent, "dp", order[1])


def send_third(keep, came, order):
    if not small_mesh():
        return keep, came
    kept, sent = halve(keep, came)
    return kept, flip(sent, "dp", order[2])


def natural_blocks(keep, send, order):
    both = jnp.concatenate([keep, send], axis=0).astype(F32)
    places = []
    for index in range(8):
        bits = [1 if index & mask else 0 for mask in order]
        places.append(both[bits[0] * 4 + bits[1] * 2 + bits[2]])
    return places


def finish_sum(keep, came, order):
    if small_mesh():
        return (keep[0] + came[0].astype(F32)).astype(BF16)
    grad = jnp.concatenate(natural_blocks(keep, came, order), axis=0)
    return lax.psum_scatter(grad, "dp", scatter_dimension=0, tiled=True).astype(BF16)


def tidy_sums(value):
    first = value.shape[1] - 8
    sums = value[:, first : first + 4] + value[:, first + 4 :]
    high = sums.astype(BF16).astype(F32)
    return jnp.concatenate([value[:, :first], high, sums - high], axis=1)


def join_kernel(keep_a, came_a, keep_b, came_b, kept, sent):
    half = kept.shape[0]
    many = keep_a.shape[1]
    value = keep_a[...].astype(F32) + came_a[...].astype(F32)
    kept[:, :many] = value[:half]
    sent[:, :many] = value[half:].astype(BF16)
    value = tidy_sums(keep_b[...].astype(F32) + came_b[...].astype(F32))
    kept[:, many:] = value[:half]
    sent[:, many:] = value[half:].astype(BF16)


def join_halve(keep_a, came_a, keep_b, came_b):
    count, many, width = keep_a.shape
    dims = (count // 2, many + keep_b.shape[1], width)
    return pl.pallas_call(
        join_kernel,
        name="join_halve",
        out_shape=(shape(dims, F32), shape(dims, BF16)),
        in_specs=[VM] * 4,
        out_specs=(VM, VM),
        compiler_params=params(16),
        cost_estimate=pl.CostEstimate(flops=10**6, bytes_accessed=4 * 10**6, transcendentals=0),
    )(keep_a, came_a, keep_b, came_b)


def halve_kernel(keep, came, kept, sent):
    half = keep.shape[0] // 2
    value = tidy_sums(keep[...].astype(F32) + came[...].astype(F32))
    kept[...] = value[:half]
    sent[...] = value[half:].astype(BF16)


def halve_sums(keep, came):
    dims = (keep.shape[0] // 2,) + keep.shape[1:]
    return pl.pallas_call(
        halve_kernel,
        name="halve_sums",
        out_shape=(shape(dims, F32), shape(dims, BF16)),
        in_specs=[VM] * 2,
        out_specs=(VM, VM),
        compiler_params=params(16),
        cost_estimate=pl.CostEstimate(flops=10**6, bytes_accessed=2 * 10**6, transcendentals=0),
    )(keep, came)


def send_rows_second(keep_a, came_a, keep_b, came_b):
    if not small_mesh():
        return (
            jnp.concatenate([keep_a, keep_b], axis=1),
            jnp.concatenate([came_a, came_b], axis=1),
        )
    kept, sent = join_halve(keep_a, came_a, keep_b, came_b)
    return kept, flip(sent, "dp", X_FIRST[1])


def send_rows_third(keep, came):
    if not small_mesh():
        return keep, came
    kept, sent = halve_sums(keep, came)
    return kept, flip(sent, "dp", X_FIRST[2])


def finish_rows(keep, came, many):
    count = lax.axis_size("dp")
    each = keep.shape[1] - 8
    moves = []
    if small_mesh():
        for z in range(4):
            for x in range(2):
                for rank in range(4):
                    moves.append(((z * 2 + x) * 4 + rank, (rank * 2 + x) * 4 + z))
        total = keep[0] + came[0].astype(F32)
        shard = total[:each].astype(BF16)
        sums = total[each : each + 4] + total[each + 4 :]
        return lax.ppermute(shard, ("dp", "sp"), moves), sums
    for place in range(count):
        for rank in range(4):
            target = rank * (count // 4) + place // 4
            moves.append((place * 4 + rank, target * 4 + place % 4))
    blocks = natural_blocks(keep, came, X_FIRST)
    blocks = [blocks[index * 2 + bit] for bit in range(2) for index in range(4)]
    results = []
    for first, last in ((0, many), (many, each)):
        grad = jnp.concatenate([block[first:last] for block in blocks], axis=0)
        shard = lax.psum_scatter(grad, "dp", scatter_dimension=0, tiled=True).astype(BF16)
        results.append(lax.ppermute(shard, ("dp", "sp"), moves))
    sums = blocks[0][each : each + 4] + blocks[0][each + 4 :]
    return jnp.concatenate(results, axis=0), lax.psum(sums, "dp")


def local(
    tokens,
    segment_ids,
    masked_rows,
    replacement,
    cotangent,
    w_qkv,
    w_out_attn,
    w_in_ff,
    w_out_ff,
    gain_one,
    shift_one,
    gain_two,
    shift_two,
):
    rows_dev, width = tokens.shape
    rank = lax.axis_index("sp")
    heads = HEADS // RANKS
    dim = width // HEADS
    part = heads * dim
    slopes = alibi_slopes(HEADS)

    select = jnp.arange(rows_dev, dtype=jnp.int32)[:, None] == masked_rows[None, :]
    hit = jnp.any(select, axis=1, keepdims=True)
    placed = dot(select.astype(BF16), replacement)
    start = jnp.where(hit, placed.astype(BF16), tokens)
    start_far = flip(start, "sp", 2)
    start_near = flip(start, "sp", 1)
    place = lax.axis_index("dp")
    place = place if small_mesh() else place * 0
    spot = jnp.stack([rank, place]).astype(jnp.int32)

    w_rank = jnp.concatenate(
        [
            lax.dynamic_slice_in_dim(w_qkv, third * width + rank * part, part, 1)
            for third in range(3)
        ],
        axis=1,
    )
    start_cross = flip(after(start_far, w_rank, spot), "sp", 1)
    start_blocks = [start, start_near, start_far, start_cross]
    qkv, *attn, lse = attention_forward(
        spot, segment_ids, slopes, start_blocks, w_rank, heads, dim
    )
    low, unit, inverse = norm_one(
        spot, exchange_blocks(attn), start, w_out_attn, gain_one, shift_one
    )
    low_far = flip(low, "sp", 2)
    low_near = flip(low, "sp", 1)
    layer_out, d_h2, d_ff, slope, act, sums2 = ffn_forward(
        low, unit, gain_one, shift_one, gain_two, shift_two,
        masked_rows, cotangent, w_in_ff, w_out_ff, 768,
    )
    d_ff_far = flip(d_ff, "sp", 2)
    d_ff_near = flip(d_ff, "sp", 1)
    low_far = after(low_far, d_ff)
    low_cross = flip(low_far, "sp", 1)
    low_blocks = [low, low_near, low_far, low_cross]
    d_h1, sent = ffn_backward(
        after(d_ff, low_far), d_h2, unit, inverse, gain_one, sums2, act, slope, w_in_ff, w_out_ff, 768
    )
    far = flip(sent, "sp", 2)
    near = flip(sent, "sp", 1)
    d_ff_cross = flip(after(d_ff_far, sent), "sp", 1)
    d_ff_blocks = [d_ff, d_ff_near, d_ff_far, d_ff_cross]

    units = w_out_ff.shape[0] // RANKS // 3
    keep_a, send_a, down_a, low_t = ffn_grad(
        spot, low_blocks, d_ff_blocks, w_in_ff, w_out_ff, units, 0, 1, X_FIRST
    )
    came_a = send_first(send_a, X_FIRST)
    keep_b, send_b, keep_d, send_d = ffn_grad(
        after(spot, down_a),
        low_blocks, d_ff_blocks, w_in_ff, w_out_ff, units, 1, 2, Z_FIRST, (low_t, down_a),
    )
    came_b = send_first(send_b, Z_FIRST)
    came_d = send_first(send_d, X_FIRST)
    cross = flip(after(far, came_a, keep_b), "sp", 1)
    d_proj_blocks = [sent, near, far, cross]
    keep_r, send_r = row_grad(spot, attn, d_proj_blocks)
    came_r = send_first(send_r, X_FIRST)

    d_qkv = attention_backward(
        after(spot, keep_r), segment_ids, slopes, d_proj_blocks, w_out_attn, qkv, lse, heads, dim
    )
    parts = exchange(d_qkv)
    keep_q, send_q = qkv_grad(
        after(spot, came_b, came_d), start_blocks, d_qkv
    )
    came_q = send_first(send_q, X_FIRST)
    keep_r, came_r = send_rows_second(keep_d, after(came_d, keep_q), keep_r, came_r)
    keep_b, came_b = send_second(keep_b, after(came_b, keep_r), Z_FIRST)
    keep_a, came_a = send_second(keep_a, after(came_a, keep_b), X_FIRST)
    grad_tokens, grad_replacement = token_grad(
        after(parts, keep_a), w_qkv, d_h1, masked_rows
    )
    keep_q, came_q = send_second(keep_q, after(came_q, grad_tokens), X_FIRST)
    keep_r, came_r = send_rows_third(keep_r, after(came_r, keep_q))
    keep_b, came_b = send_third(keep_b, after(came_b, keep_r), Z_FIRST)
    keep_a, came_a = send_third(keep_a, after(came_a, keep_b), X_FIRST)
    keep_q, came_q = send_third(keep_q, after(came_q, keep_a), X_FIRST)
    wide_a = finish_sum(keep_a, came_a, X_FIRST)
    wide_b = finish_sum(keep_b, came_b, Z_FIRST)
    wide_blocks = gather_blocks(jnp.concatenate([wide_a, wide_b], axis=1))
    many = w_out_ff.shape[0] // RANKS // 8
    row_share, norm_sums = finish_rows(keep_r, came_r, many)
    head_blocks = gather_blocks(finish_sum(keep_q, came_q, X_FIRST))
    row_blocks_ = gather_blocks(row_share)
    many = w_out_ff.shape[0] // lax.axis_size("dp") // RANKS
    grad_down, grad_out = join_rows(spot, row_blocks_, many)

    return (
        layer_out,
        grad_tokens,
        grad_replacement,
        join_heads(spot, head_blocks),
        grad_out,
        join_wide(spot, wide_blocks),
        grad_down,
        norm_sums[0],
        norm_sums[1],
        norm_sums[2],
        norm_sums[3],
    )


def solution(mesh):
    tokens = P(("dp", "sp"), None)
    rows = P("dp", None)
    return jax.shard_map(
        local,
        mesh=mesh,
        in_specs=(tokens, rows, P(("dp", "sp")), tokens, tokens) + (P(),) * 8,
        out_specs=(tokens,) * 3 + (rows,) * 4 + (P(),) * 4,
        check_vma=False,
    )
```

```python
import functools
import math

import jax
import jax.numpy as jnp
from jax import lax
from jax.experimental import pallas as pl
from jax.experimental.pallas import tpu as pltpu
from jax.sharding import PartitionSpec as P

HEADS = 12
RANKS = 4
EPSILON = 1e-05
FAR = 1e30
F32 = jnp.float32
BF16 = jnp.bfloat16
VM = pl.BlockSpec(memory_space=pltpu.VMEM)
SM = pl.BlockSpec(memory_space=pltpu.SMEM)


def shape(dims, kind):
    return jax.ShapeDtypeStruct(dims, kind)


def scratch(dims, kind):
    return pltpu.VMEM(dims, kind)


def params(mebibytes):
    return pltpu.CompilerParams(vmem_limit_bytes=mebibytes << 20)


def alibi_slopes(head_count):
    nearest = 2 ** int(math.floor(math.log2(head_count)))
    base_list = [2.0 ** (-8.0 * (index + 1) / nearest) for index in range(nearest)]
    extra_list = [
        2.0 ** (-8.0 * (2 * index + 1) / (2 * nearest)) for index in range(head_count - nearest)
    ]
    return jnp.array(base_list + extra_list, dtype=F32)


def dot(a, b):
    return jnp.dot(a, b, preferred_element_type=F32)


def dot_nt(a, b):
    return lax.dot_general(a, b, (((1,), (1,)), ((), ())), preferred_element_type=F32)


def dot_tn(a, b):
    return lax.dot_general(a, b, (((0,), (0,)), ((), ())), preferred_element_type=F32)


def exact_dot(a, b):
    return jnp.dot(a, b, precision=lax.Precision.HIGHEST, preferred_element_type=F32)


def standardize(value):
    center = value - jnp.mean(value, axis=-1, keepdims=True)
    spread = jnp.mean(center * center, axis=-1, keepdims=True)
    inverse = lax.rsqrt(spread + EPSILON)
    return center * inverse, inverse


def standardize_back(grad, unit, inverse):
    mean = jnp.mean(grad, axis=-1, keepdims=True)
    return inverse * (grad - mean - unit * jnp.mean(grad * unit, axis=-1, keepdims=True))


def gelu_pair(x):
    cdf = 0.5 * (1.0 + lax.erf(x * math.sqrt(0.5)))
    pdf = jnp.exp(-0.5 * x * x) * (1.0 / math.sqrt(2.0 * math.pi))
    return x * cdf, cdf + x * pdf


def pair_active(seg, rank, first, second, rows):
    one, two = rank ^ first, rank ^ second
    low, high = jnp.minimum(one, two), jnp.maximum(one, two)
    return jnp.logical_or(one == two, seg[0, low * rows + rows - 1] == seg[0, high * rows])


def key_sequences(seg_rows, seg_keys, rank, rows):
    for at in range(RANKS):
        first = pl.multiple_of((rank ^ at) * rows, rows)
        line = jnp.broadcast_to(seg_rows[:, pl.ds(first, rows)], (128, rows))
        seg_keys[at * rows : (at + 1) * rows, :] = jnp.transpose(line)


def pair_distance(seg_rows, seg_keys, rank, keys_at, query_at, rows):
    key_pos, query_pos = (rank ^ keys_at) * rows, (rank ^ query_at) * rows
    down = lax.broadcasted_iota(jnp.int32, (rows, rows), 0)
    across = lax.broadcasted_iota(jnp.int32, (rows, rows), 1)
    gap = jnp.abs(down - across + (key_pos - query_pos)).astype(F32)
    seg_q = seg_rows[:, pl.ds(pl.multiple_of(query_pos, rows), rows)]
    seg_k = seg_keys[pl.ds(pl.multiple_of(keys_at * rows, rows), rows), 0:1]
    return jnp.where(seg_k == seg_q, gap, FAR)


def attention_forward_kernel(
    rows, heads, dim, info, seg, slopes, x0, x1, x2, x3, w, seg_rows,
    qkv_out, o0, o1, o2, o3, lse, qs, ks, vt, dist, seg_keys, score, peak,
):
    rank = info[0]
    width = heads * dim
    key_sequences(seg_rows, seg_keys, rank, rows)
    for at, x in enumerate((x0, x1, x2, x3)):
        qkv = dot(x[...], w[...]).astype(BF16)
        here = pl.ds(at * rows, rows)
        qkv_out[here, :] = qkv
        for h in range(heads):
            qs[h, here, :] = (qkv[:, h * dim : (h + 1) * dim] * dim**-0.5).astype(BF16)
            ks[h, here, :] = qkv[:, width + h * dim : width + (h + 1) * dim]
        vt[:, here] = jnp.transpose(qkv[:, 2 * width :])

    for a in range(RANKS):
        mine = pl.ds(a * rows, rows)
        peak[...] = jnp.full_like(peak, -jnp.inf)

        def first_pass(b, carry):
            @pl.when(pair_active(seg, rank, a, b, rows))
            def _():
                theirs = pl.ds(pl.multiple_of(b * rows, rows), rows)
                gap = pair_distance(seg_rows, seg_keys, rank, b, a, rows)
                for h in range(heads):
                    slope = slopes[rank * heads + h]
                    s = dot_nt(ks[h, theirs, :], qs[h, mine, :]) - slope * gap
                    score[h, theirs, :] = s
                    peak[h : h + 1, :] = jnp.maximum(
                        peak[h : h + 1, :], jnp.max(s, axis=0, keepdims=True)
                    )

            return carry

        lax.fori_loop(0, RANKS, first_pass, 0)

        def second_pass(b, carry):
            def add(carry):
                theirs = pl.ds(pl.multiple_of(b * rows, rows), rows)
                result = []
                for h in range(heads):
                    acc, total = carry[h]
                    p = jnp.exp(score[h, theirs, :] - peak[h : h + 1, :])
                    total = total + jnp.sum(p, axis=0, keepdims=True)
                    span = slice(h * dim, (h + 1) * dim)
                    result.append((acc + dot(vt[span, theirs], p.astype(BF16)), total))
                return tuple(result)

            return lax.cond(pair_active(seg, rank, a, b, rows), add, lambda carry: carry, carry)

        empty = (jnp.zeros((dim, rows), F32), jnp.zeros((1, rows), F32))
        sums = lax.fori_loop(0, RANKS, second_pass, (empty,) * heads)
        for h in range(heads):
            acc, total = sums[h]
            span = slice(h * dim, (h + 1) * dim)
            (o0, o1, o2, o3)[a][span, :] = (acc / total).astype(BF16)
            lse[h : h + 1, mine] = peak[h : h + 1, :] + jnp.log(total)


def attention_forward(info, seg, slopes, blocks, w, heads, dim):
    rows = blocks[0].shape[0]
    tok, lw = rows * RANKS, heads * dim
    return pl.pallas_call(
        functools.partial(attention_forward_kernel, rows, heads, dim),
        name="attention_forward",
        out_shape=(shape((tok, 3 * lw), BF16),)
        + (shape((lw, rows), BF16),) * RANKS
        + (shape((heads, tok), F32),),
        in_specs=[SM] * 3 + [VM] * 6,
        out_specs=(VM,) * 6,
        scratch_shapes=[
            scratch((heads, tok, dim), BF16),
            scratch((heads, tok, dim), BF16),
            scratch((lw, tok), BF16),
            scratch((rows, rows), F32),
            scratch((tok, 128), jnp.int32),
            scratch((heads, tok, rows), F32),
            scratch((heads, rows), F32),
        ],
        compiler_params=params(14),
        cost_estimate=pl.CostEstimate(
            flops=4 * 10**9, bytes_accessed=6 * 10**6, transcendentals=3 * 10**6
        ),
    )(info, seg, slopes, *blocks, w, seg)


def attention_backward_kernel(
    rows, heads, dim, info, seg, slopes, g0, g1, g2, g3, w, qkv, lse, seg_rows,
    d_qkv, qs, ks, kt, vs, do, seg_keys, prob, dprob, dk, dv, dqt, delta,
):
    rank = info[0]
    width = heads * dim
    scale = dim**-0.5
    key_sequences(seg_rows, seg_keys, rank, rows)
    w_rank = w[pl.ds(pl.multiple_of(rank * width, width), width), :]
    for at, g in enumerate((g0, g1, g2, g3)):
        here = pl.ds(at * rows, rows)
        grad = dot_nt(g[0:rows, :], w_rank).astype(BF16)
        value = qkv[here, :]
        kt[:, here] = jnp.transpose(value[:, width : 2 * width])
        for h in range(heads):
            do[h, here, :] = grad[:, h * dim : (h + 1) * dim]
            qs[h, here, :] = (value[:, h * dim : (h + 1) * dim] * scale).astype(BF16)
            ks[h, here, :] = value[:, width + h * dim : width + (h + 1) * dim]
            vs[h, here, :] = value[:, 2 * width + h * dim : 2 * width + (h + 1) * dim]
    dk[...] = jnp.zeros_like(dk)
    dv[...] = jnp.zeros_like(dv)

    for a in range(RANKS):
        mine = pl.ds(a * rows, rows)
        delta[...] = jnp.zeros_like(delta)
        dqt[...] = jnp.zeros_like(dqt)

        def first_pass(b, carry):
            @pl.when(pair_active(seg, rank, a, b, rows))
            def _():
                theirs = pl.ds(pl.multiple_of(b * rows, rows), rows)
                gap = pair_distance(seg_rows, seg_keys, rank, b, a, rows)
                for h in range(heads):
                    slope = slopes[rank * heads + h]
                    s = dot_nt(ks[h, theirs, :], qs[h, mine, :]) - slope * gap
                    p = jnp.exp(s - lse[h : h + 1, mine])
                    dp = dot_nt(vs[h, theirs, :], do[h, mine, :])
                    delta[h : h + 1, :] += jnp.sum(p * dp, axis=0, keepdims=True)
                    prob[h, theirs, :] = p
                    dprob[h, theirs, :] = dp

            return carry

        lax.fori_loop(0, RANKS, first_pass, 0)

        def second_pass(b, carry):
            @pl.when(pair_active(seg, rank, a, b, rows))
            def _():
                theirs = pl.ds(pl.multiple_of(b * rows, rows), rows)
                for h in range(heads):
                    p = prob[h, theirs, :]
                    ds = (p * (dprob[h, theirs, :] - delta[h : h + 1, :])).astype(BF16)
                    dv[h, theirs, :] += dot(p.astype(BF16), do[h, mine, :])
                    dk[h, theirs, :] += dot(ds, qs[h, mine, :])
                    span = slice(h * dim, (h + 1) * dim)
                    dqt[span, :] += dot(kt[span, theirs], ds)

            return carry

        lax.fori_loop(0, RANKS, second_pass, 0)
        d_qkv[rank ^ a, 0:width, :] = (dqt[...] * scale).astype(BF16)

    for at in range(RANKS):
        here = pl.ds(at * rows, rows)
        for h in range(heads):
            first = width + h * dim
            d_qkv[rank ^ at, first : first + dim, :] = jnp.transpose(dk[h, here, :]).astype(BF16)
            first = 2 * width + h * dim
            d_qkv[rank ^ at, first : first + dim, :] = jnp.transpose(dv[h, here, :]).astype(BF16)


def attention_backward(info, seg, slopes, blocks, w, qkv, lse, heads, dim):
    tok, lw = qkv.shape[0], heads * dim
    rows = tok // RANKS
    return pl.pallas_call(
        functools.partial(attention_backward_kernel, rows, heads, dim),
        name="attention_backward",
        out_shape=shape((RANKS, 3 * lw, rows), BF16),
        in_specs=[SM] * 3 + [VM] * 8,
        out_specs=VM,
        scratch_shapes=[
            scratch((heads, tok, dim), BF16),
            scratch((heads, tok, dim), BF16),
            scratch((lw, tok), BF16),
            scratch((heads, tok, dim), BF16),
            scratch((heads, tok, dim), BF16),
            scratch((tok, 128), jnp.int32),
            scratch((heads, tok, rows), F32),
            scratch((heads, tok, rows), F32),
            scratch((heads, tok, dim), F32),
            scratch((heads, tok, dim), F32),
            scratch((lw, rows), F32),
            scratch((heads, rows), F32),
        ],
        compiler_params=params(20),
        cost_estimate=pl.CostEstimate(
            flops=8 * 10**9, bytes_accessed=6 * 10**6, transcendentals=3 * 10**6
        ),
    )(info, seg, slopes, *blocks, w, qkv, lse, seg)


def line(vector):
    return vector[...].reshape(1, -1)


def norm_one_kernel(
    info, own, near, far, cross, start, w, gain, shift, low, unit, inverse, joined
):
    part = own.shape[0]
    for step, value in enumerate((own, near, far, cross)):
        first = pl.multiple_of((info[0] ^ step) * part, part)
        joined[pl.ds(first, part), :] = value[...]
    x, inv = standardize(start[...].astype(F32) + dot_tn(joined[...], w[...]))
    unit[...] = x
    inverse[...] = inv
    low[...] = (x * line(gain) + line(shift)).astype(BF16)


def norm_one(info, parts, start, w, gain, shift):
    rows, width = start.shape
    return pl.pallas_call(
        norm_one_kernel,
        name="norm_one",
        out_shape=(shape((rows, width), BF16), shape((rows, width), F32), shape((rows, 1), F32)),
        in_specs=[SM] + [VM] * 8,
        out_specs=(VM,) * 3,
        scratch_shapes=[scratch((width, rows), BF16)],
        compiler_params=params(16),
        cost_estimate=pl.CostEstimate(
            flops=2 * rows * width * width, bytes_accessed=4 * 10**6, transcendentals=0
        ),
    )(info, *parts, start, w, gain, shift)


def packing(rows, columns, part, rank):
    units = lax.broadcasted_iota(jnp.int32, (rows, columns), 0)
    packed = lax.broadcasted_iota(jnp.int32, (1, columns), 1)
    places = packed + rank * part
    for index in range(1, columns // part):
        places = places + jnp.where(packed >= index * part, (RANKS - 1) * part, 0)
    return (units == places).astype(BF16)


def pack_kernel(part, info, w_in, w_down, packed_in, packed_down):
    rank = info[0]
    width, hid = w_in.shape[0], w_down.shape[0]
    run = hid // 2
    select = packing(run, run // RANKS, part, rank)
    for index in range(4):
        piece = dot(w_in[:, index * run : (index + 1) * run], select)
        packed_in[:, index * run // RANKS : (index + 1) * run // RANKS] = piece.astype(BF16)
    if part % 16:
        for index in range(2):
            piece = dot_tn(select, w_down[index * run : (index + 1) * run, :])
            packed_down[index * run // RANKS : (index + 1) * run // RANKS, :] = piece.astype(BF16)
    else:
        for index in range(hid // RANKS // part):
            rows = pl.ds(pl.multiple_of((index * RANKS + rank) * part, part), part)
            packed_down[index * part : (index + 1) * part, :] = w_down[rows, :]


def pack_weights(info, w_in, w_out, part):
    width, hid = w_in.shape[0], w_out.shape[0]
    return pl.pallas_call(
        functools.partial(pack_kernel, part),
        name="pack_weights",
        out_shape=(shape((width, 2 * hid // RANKS), BF16), shape((hid // RANKS, width), BF16)),
        in_specs=[SM, VM, VM],
        out_specs=(VM, VM),
        compiler_params=params(14),
        cost_estimate=pl.CostEstimate(
            flops=4 * 10**9, bytes_accessed=17 * 10**6, transcendentals=0
        ),
    )(info, w_in, w_out)


def ffn_forward_kernel(
    low, unit, gain1, shift1, gain2, shift2, masked, cot, w_in, w_down,
    layer_out, d_h2, d_ff, slope, act, sums, acc, gates, ups,
):
    hid = w_down.shape[0]
    size = gates.shape[2]
    count = hid // size

    def project(block, slot):
        first = pl.multiple_of(block * size, size)
        gates[slot] = dot(low[...], w_in[:, pl.ds(first, size)])
        ups[slot] = dot(low[...], w_in[:, pl.ds(pl.multiple_of(hid + first, size), size)])

    def finish(block, slot):
        here = pl.ds(pl.multiple_of(block * size, size), size)
        up = ups[slot]
        value, grad = gelu_pair(gates[slot])
        act[:, here] = value.astype(BF16)
        slope[:, here] = (up * grad).astype(BF16)
        acc[...] += dot((value * up).astype(BF16), w_down[here, :])

    acc[...] = unit[...] * line(gain1) + line(shift1)
    project(0, 0)

    def pair(index, carry):
        block = index * 2
        project(block + 1, 1)
        finish(block, 0)
        project(block + 2, 0)
        finish(block + 1, 1)
        return carry

    lax.fori_loop(0, count // 2 - 1, pair, 0)
    project(count - 1, 1)
    finish(count - 2, 0)
    finish(count - 1, 1)
    x, inv = standardize(acc[...])
    layer_out[...] = (x * line(gain2) + line(shift2)).astype(BF16)
    places = lax.broadcasted_iota(jnp.int32, (low.shape[0], masked.shape[0]), 0)
    dy = exact_dot((places == line(masked)).astype(F32), cot[...])
    sums[0:1, :] = jnp.sum(dy * x, axis=0, keepdims=True)
    sums[1:2, :] = jnp.sum(dy, axis=0, keepdims=True)
    grad_in = standardize_back(dy * line(gain2), x, inv)
    d_h2[...] = grad_in
    d_ff[...] = grad_in.astype(BF16)


def ffn_forward(low, unit, gain1, shift1, gain2, shift2, masked, cot, w_in, w_out, size):
    rows, width = low.shape
    hid = w_out.shape[0]
    return pl.pallas_call(
        ffn_forward_kernel,
        name="ffn_forward",
        out_shape=(
            shape((rows, width), BF16),
            shape((rows, width), F32),
            shape((rows, width), BF16),
            shape((rows, hid), BF16),
            shape((rows, hid), BF16),
            shape((2, width), F32),
        ),
        in_specs=[VM] * 10,
        out_specs=(VM,) * 6,
        scratch_shapes=[
            scratch((rows, width), F32),
            scratch((2, rows, size), F32),
            scratch((2, rows, size), F32),
        ],
        compiler_params=params(14),
        cost_estimate=pl.CostEstimate(
            flops=6 * rows * width * hid, bytes_accessed=18 * 10**6, transcendentals=2 * rows * hid
        ),
    )(low, unit, gain1, shift1, gain2, shift2, masked, cot, w_in, w_out)


def ffn_backward_kernel(
    d_ff, d_h2, unit, inverse, gain1, sums2, act, slope, w_in, w_down, d_h1, sent, acc, hidden
):
    hid = w_down.shape[0]
    size = hidden.shape[2]
    count = hid // size

    def project(block, slot):
        here = pl.ds(pl.multiple_of(block * size, size), size)
        hidden[slot] = dot_nt(d_ff[...], w_down[here, :])

    def finish(block, slot):
        first = pl.multiple_of(block * size, size)
        here, there = pl.ds(first, size), pl.ds(pl.multiple_of(hid + first, size), size)
        d_hidden = hidden[slot]
        d_gate = (d_hidden * slope[:, here].astype(F32)).astype(BF16)
        d_up = (d_hidden * act[:, here].astype(F32)).astype(BF16)
        acc[...] += dot_nt(d_gate, w_in[:, here]) + dot_nt(d_up, w_in[:, there])

    acc[...] = d_h2[...]
    project(0, 0)

    def pair(index, carry):
        block = index * 2
        project(block + 1, 1)
        finish(block, 0)
        project(block + 2, 0)
        finish(block + 1, 1)
        return carry

    lax.fori_loop(0, count // 2 - 1, pair, 0)
    project(count - 1, 1)
    finish(count - 2, 0)
    finish(count - 1, 1)
    total = acc[...]
    rows = total.shape[0]
    x = unit[...]
    gain_sum = jnp.sum(total * x, axis=0, keepdims=True)
    shift_sum = jnp.sum(total, axis=0, keepdims=True)
    sums = jnp.concatenate([gain_sum, shift_sum, sums2[...]], axis=0)
    high = sums.astype(BF16).astype(F32)
    tail = jnp.concatenate([high, sums - high, jnp.zeros((8, sums.shape[1]), F32)], axis=0)
    grad = standardize_back(total * line(gain1), x, inverse[...])
    d_h1[...] = grad
    sent[0:rows, :] = grad.astype(BF16)
    sent[rows : rows + 16, :] = tail.astype(BF16)


def ffn_backward(d_ff, d_h2, unit, inverse, gain1, sums2, act, slope, w_in, w_out, size):
    rows, width = d_ff.shape
    hid = w_out.shape[0]
    return pl.pallas_call(
        ffn_backward_kernel,
        name="ffn_backward",
        out_shape=(shape((rows, width), F32), shape((rows + 16, width), BF16)),
        in_specs=[VM] * 10,
        out_specs=(VM,) * 2,
        scratch_shapes=[scratch((rows, width), F32), scratch((2, rows, size), F32)],
        compiler_params=params(14),
        cost_estimate=pl.CostEstimate(
            flops=6 * rows * width * hid, bytes_accessed=20 * 10**6, transcendentals=0
        ),
    )(d_ff, d_h2, unit, inverse, gain1, sums2, act, slope, w_in, w_out)


X_FIRST = (1, 2, 4)
Z_FIRST = (2, 1, 4)


def bit_of(value, mask):
    return (value // mask) % 2


def store_blocks(blocks, keep, send, place, order, columns):
    one, two, three = order
    odd = bit_of(place, one) == 1
    for index in range(8):
        if index & one:
            continue
        spot = bit_of(place ^ index, two) * 2 + bit_of(place ^ index, three)
        low, high = blocks(index), blocks(index | one)
        keep[spot, :, columns] = jnp.where(odd, high, low).astype(BF16)
        send[spot, :, columns] = jnp.where(odd, low, high).astype(BF16)


def row_blocks(grad):
    each = grad.shape[0] // 8
    return lambda index: grad[index * each : (index + 1) * each]


def quarter_blocks(grad):
    each = grad.shape[0] // 8

    def block(index):
        at = index % 2 * 4 + index // 2
        return grad[at * each : (at + 1) * each]

    return block


def ffn_grad_kernel(
    size, info, n0, n1, n2, n3, f0, f1, f2, f3, w_in, w_down,
    keep, send, keep_down, send_down,
    tok_t, gates, ups, d_hiddens, hidden_t, d_gate, d_up, d_ff, down,
):
    toks, grads = (n0, n1, n2, n3), (f0, f1, f2, f3)
    rows = n0.shape[0]
    units = w_down.shape[0]
    for at in range(RANKS):
        here = slice(at * rows, (at + 1) * rows)
        d_ff[here, :] = grads[at][...]
        tok_t[:, here] = jnp.transpose(toks[at][...])

    def unit_block(step, carry):
        here = pl.ds(pl.multiple_of(step * size, size), size)
        there = pl.ds(pl.multiple_of(units + step * size, size), size)
        w_gate, w_up, w_rows = w_in[:, here], w_in[:, there], w_down[here, :]

        def project(at):
            slot = at % 2
            gates[slot] = dot(toks[at][...], w_gate)
            ups[slot] = dot(toks[at][...], w_up)
            d_hiddens[slot] = dot_nt(grads[at][...], w_rows)

        def finish(at):
            slot = at % 2
            here = slice(at * rows, (at + 1) * rows)
            value, grad = gelu_pair(gates[slot])
            up, d_hidden = ups[slot], d_hiddens[slot]
            hidden_t[:, here] = jnp.transpose((value * up).astype(BF16))
            d_gate[here, :] = (d_hidden * up * grad).astype(BF16)
            d_up[here, :] = (d_hidden * value).astype(BF16)

        project(0)
        for at in range(RANKS):
            if at + 1 < RANKS:
                project(at + 1)
            finish(at)
        for columns, grad in ((here, d_gate), (there, d_up)):
            total = dot(tok_t[...], grad[...])
            store_blocks(row_blocks(total), keep, send, info[1], Z_FIRST, columns)
        down[here, :] = dot(hidden_t[...], d_ff[...])
        return carry

    lax.fori_loop(0, units // size, unit_block, 0)
    store_blocks(row_blocks(down), keep_down, send_down, info[1], X_FIRST, slice(None))


def ffn_grad(info, toks, grads, w_in, w_down, size):
    rows, width = toks[0].shape
    units = w_down.shape[0]
    tok = rows * RANKS
    dims = [(4, width // 8, 2 * units)] * 2 + [(4, units // 8, width)] * 2
    return pl.pallas_call(
        functools.partial(ffn_grad_kernel, size),
        name="ffn_grad",
        out_shape=[shape(each, BF16) for each in dims],
        in_specs=[SM] + [VM] * 10,
        out_specs=[VM] * 4,
        scratch_shapes=[
            scratch((width, tok), BF16),
            scratch((2, rows, size), F32),
            scratch((2, rows, size), F32),
            scratch((2, rows, size), F32),
            scratch((size, tok), BF16),
            scratch((tok, size), BF16),
            scratch((tok, size), BF16),
            scratch((tok, width), BF16),
            scratch((units, width), F32),
        ],
        compiler_params=params(18),
        cost_estimate=pl.CostEstimate(
            flops=12 * tok * width * units,
            bytes_accessed=8 * 10**6,
            transcendentals=2 * tok * units,
        ),
    )(info, *toks, *grads, w_in, w_down)


def row_grad_kernel(info, a0, a1, a2, a3, g0, g1, g2, g3, keep, send):
    rows = g0.shape[0] - 16
    grad = 0.0
    sums = 0.0
    for attn, g in zip((a0, a1, a2, a3), (g0, g1, g2, g3)):
        grad = grad + dot(attn[...], g[0:rows, :])
        pair = g[rows : rows + 16, :].astype(F32)
        sums = sums + pair[0:4] + pair[4:8]
    high = sums.astype(BF16).astype(F32)
    tail = jnp.concatenate([high, sums - high], axis=0)
    part = quarter_blocks(grad)

    def blocks(index):
        return jnp.concatenate([part(index), tail], axis=0)

    store_blocks(blocks, keep, send, info[1], X_FIRST, slice(None))


def row_grad(info, attn, blocks):
    width = blocks[0].shape[1]
    dims = (4, attn[0].shape[0] // 8 + 8, width)
    return pl.pallas_call(
        row_grad_kernel,
        name="row_grad",
        out_shape=(shape(dims, BF16),) * 2,
        in_specs=[SM] + [VM] * 8,
        out_specs=(VM, VM),
        compiler_params=params(16),
        cost_estimate=pl.CostEstimate(
            flops=8 * attn[0].size * width, bytes_accessed=3 * 10**6, transcendentals=0
        ),
    )(info, *attn, *blocks)


def qkv_grad_kernel(info, x0, x1, x2, x3, d_qkv, keep, send):
    total = 0.0
    for at, x in enumerate((x0, x1, x2, x3)):
        total = total + dot(d_qkv[info[0] ^ at], x[...])
    store_blocks(row_blocks(jnp.transpose(total)), keep, send, info[1], X_FIRST, slice(None))


def qkv_grad(info, blocks, d_qkv):
    rows, width = blocks[0].shape
    columns = d_qkv.shape[1]
    return pl.pallas_call(
        qkv_grad_kernel,
        name="qkv_grad",
        out_shape=(shape((4, width // 8, columns), BF16),) * 2,
        in_specs=[SM] + [VM] * 5,
        out_specs=(VM, VM),
        compiler_params=params(16),
        cost_estimate=pl.CostEstimate(
            flops=8 * rows * width * columns, bytes_accessed=4 * 10**6, transcendentals=0
        ),
    )(info, *blocks, d_qkv)


def join_ffn_kernel(part, info, b0, b1, b2, b3, wide, down):
    rank = info[0]
    rows = b0.shape[0]
    run = wide.shape[1] // 4
    few = run // RANKS
    total = 0.0
    for step, block in enumerate((b0, b1, b2, b3)):
        select = packing(run, few, part, rank ^ step)
        pieces = [block[:, index * few : (index + 1) * few] for index in range(4)]
        total = total + dot_nt(jnp.concatenate(pieces, axis=0), select)
        place = pl.multiple_of((rank ^ step) * rows, rows)
        down[pl.ds(place, rows), :] = block[:, 4 * few :].astype(F32)
    for index in range(4):
        wide[:, index * run : (index + 1) * run] = total[index * rows : (index + 1) * rows]


def join_ffn(info, blocks, part):
    rows, columns = blocks[0].shape
    width = columns // 3
    if rows % 8:
        stacked = jnp.stack(blocks)[info[0] ^ jnp.arange(RANKS)].astype(F32)
        wide = stacked[:, :, : 2 * width].reshape(RANKS, rows, -1, part).transpose(1, 2, 0, 3)
        return wide.reshape(rows, -1), stacked[:, :, 2 * width :].reshape(-1, width)
    return pl.pallas_call(
        functools.partial(join_ffn_kernel, part),
        name="join_ffn",
        out_shape=(shape((rows, 8 * width), F32), shape((rows * RANKS, width), F32)),
        in_specs=[SM] + [VM] * 4,
        out_specs=(VM, VM),
        compiler_params=params(14),
        cost_estimate=pl.CostEstimate(flops=2 * 10**9, bytes_accessed=6 * 10**6, transcendentals=0),
    )(info, *blocks)


def join_heads_kernel(info, b0, b1, b2, b3, out, rest):
    rank = info[0]
    width = out.shape[1] // 3
    part = width // RANKS
    few = rest.shape[0] // RANKS
    for value in range(RANKS):

        @pl.when(rank == value)
        def _():
            for step, block in enumerate((b0, b1, b2, b3)):
                there = value ^ step
                for third in range(3):
                    first = third * width + there * part
                    piece = block[:, third * part : (third + 1) * part]
                    out[:, first : first + part] = piece.astype(F32)
                for index in range(RANKS):
                    piece = block[index * few : (index + 1) * few, 3 * part :].astype(F32)
                    here = slice(there * few, (there + 1) * few)
                    rest[here, index * part : (index + 1) * part] = piece


def join_heads(info, blocks):
    rows, columns = blocks[0].shape
    part = columns // 4
    return pl.pallas_call(
        join_heads_kernel,
        name="join_heads",
        out_shape=(shape((rows, 3 * part * RANKS), F32), shape((rows, part * RANKS), F32)),
        in_specs=[SM] + [VM] * 4,
        out_specs=(VM, VM),
        compiler_params=params(8),
        cost_estimate=pl.CostEstimate(flops=10**6, bytes_accessed=2 * 10**6, transcendentals=0),
    )(info, *blocks)


def token_grad_kernel(parts, w, d_h1, masked, tokens, replacement, joined):
    rows, width = d_h1.shape
    part = width // RANKS
    for rank in range(RANKS):
        for third in range(3):
            first = third * width + rank * part
            joined[first : first + part, :] = parts[rank, third * part : (third + 1) * part, :]
    grad = d_h1[...] + jnp.transpose(dot(w[...], joined[...]))
    count = masked.shape[0]
    places = lax.broadcasted_iota(jnp.int32, (rows, count), 0)
    select = (places == line(masked)).astype(F32)
    hit = jnp.max(select, axis=1, keepdims=True)
    tokens[...] = jnp.where(hit > 0.5, 0.0, grad)
    replacement[...] = lax.dot_general(
        select, grad, (((0,), (0,)), ((), ())),
        precision=lax.Precision.HIGHEST, preferred_element_type=F32,
    )


def token_grad(parts, w, d_h1, masked):
    rows, width = d_h1.shape
    return pl.pallas_call(
        token_grad_kernel,
        name="token_grad",
        out_shape=(shape((rows, width), F32), shape((masked.shape[0], width), F32)),
        in_specs=[VM] * 4,
        out_specs=(VM, VM),
        scratch_shapes=[scratch((3 * width, rows), BF16)],
        compiler_params=params(16),
        cost_estimate=pl.CostEstimate(
            flops=6 * rows * width * width, bytes_accessed=8 * 10**6, transcendentals=0
        ),
    )(parts, w, d_h1, masked)


def after(value, *others):
    return lax.optimization_barrier((value,) + others)[0]


def flip(value, axis, bits):
    count = lax.axis_size(axis)
    return lax.ppermute(value, axis, [(index, index ^ bits) for index in range(count)])


def gather_blocks(value):
    far = flip(value, "sp", 2)
    near = flip(value, "sp", 1)
    cross = flip(far, "sp", 1)
    return [value, near, far, cross]


def exchange_blocks(blocks):
    via = flip(blocks[3], "sp", 1)
    near = flip(blocks[1], "sp", 1)
    far = flip(blocks[2], "sp", 2)
    cross = flip(via, "sp", 2)
    return [blocks[0], near, far, cross]


def exchange(parts):
    return lax.all_to_all(parts, "sp", 0, 0, tiled=True)


def small_mesh():
    return lax.axis_size("dp") == 8


def halve(keep, came):
    half = keep.shape[0] // 2
    kept = keep[:half].astype(F32) + came[:half].astype(F32)
    sent = keep[half:].astype(F32) + came[half:].astype(F32)
    return kept, sent.astype(BF16)


def send_first(send, order):
    return flip(send, "dp", order[0]) if small_mesh() else send


def send_second(keep, came, order):
    if not small_mesh():
        return keep, came
    kept, sent = halve(keep, came)
    return kept, flip(sent, "dp", order[1])


def send_third(keep, came, order):
    if not small_mesh():
        return keep, came
    kept, sent = halve(keep, came)
    return kept, flip(sent, "dp", order[2])


def natural_blocks(keep, send, order):
    both = jnp.concatenate([keep, send], axis=0).astype(F32)
    places = []
    for index in range(8):
        bits = [1 if index & mask else 0 for mask in order]
        places.append(both[bits[0] * 4 + bits[1] * 2 + bits[2]])
    return places


def finish_sum(keep, came, order):
    if small_mesh():
        return (keep[0] + came[0].astype(F32)).astype(BF16)
    grad = jnp.concatenate(natural_blocks(keep, came, order), axis=0)
    return lax.psum_scatter(grad, "dp", scatter_dimension=0, tiled=True).astype(BF16)


def tidy_sums(value):
    first = value.shape[1] - 8
    sums = value[:, first : first + 4] + value[:, first + 4 :]
    high = sums.astype(BF16).astype(F32)
    return jnp.concatenate([value[:, :first], high, sums - high], axis=1)


def join_kernel(keep_a, came_a, keep_b, came_b, kept, sent):
    half = kept.shape[0]
    many = keep_a.shape[1]
    value = keep_a[...].astype(F32) + came_a[...].astype(F32)
    kept[:, :many] = value[:half]
    sent[:, :many] = value[half:].astype(BF16)
    value = tidy_sums(keep_b[...].astype(F32) + came_b[...].astype(F32))
    kept[:, many:] = value[:half]
    sent[:, many:] = value[half:].astype(BF16)


def join_halve(keep_a, came_a, keep_b, came_b):
    count, many, width = keep_a.shape
    dims = (count // 2, many + keep_b.shape[1], width)
    return pl.pallas_call(
        join_kernel,
        name="join_halve",
        out_shape=(shape(dims, F32), shape(dims, BF16)),
        in_specs=[VM] * 4,
        out_specs=(VM, VM),
        compiler_params=params(16),
        cost_estimate=pl.CostEstimate(flops=10**6, bytes_accessed=4 * 10**6, transcendentals=0),
    )(keep_a, came_a, keep_b, came_b)


def halve_kernel(keep, came, kept, sent):
    half = keep.shape[0] // 2
    value = tidy_sums(keep[...].astype(F32) + came[...].astype(F32))
    kept[...] = value[:half]
    sent[...] = value[half:].astype(BF16)


def halve_sums(keep, came):
    dims = (keep.shape[0] // 2,) + keep.shape[1:]
    return pl.pallas_call(
        halve_kernel,
        name="halve_sums",
        out_shape=(shape(dims, F32), shape(dims, BF16)),
        in_specs=[VM] * 2,
        out_specs=(VM, VM),
        compiler_params=params(16),
        cost_estimate=pl.CostEstimate(flops=10**6, bytes_accessed=2 * 10**6, transcendentals=0),
    )(keep, came)


def send_rows_second(keep_a, came_a, keep_b, came_b):
    if not small_mesh():
        return (
            jnp.concatenate([keep_a, keep_b], axis=1),
            jnp.concatenate([came_a, came_b], axis=1),
        )
    kept, sent = join_halve(keep_a, came_a, keep_b, came_b)
    return kept, flip(sent, "dp", X_FIRST[1])


def send_rows_third(keep, came):
    if not small_mesh():
        return keep, came
    kept, sent = halve_sums(keep, came)
    return kept, flip(sent, "dp", X_FIRST[2])


def finish_rows(keep, came, many):
    count = lax.axis_size("dp")
    each = keep.shape[1] - 8
    moves = []
    for place in range(count):
        for rank in range(RANKS):
            if small_mesh():
                place_to, rank_to = rank * 2 + place % 2, place // 2
            else:
                place_to, rank_to = rank * (count // 4) + place // 4, place % 4
            moves.append((place * RANKS + rank, place_to * RANKS + rank_to))
    if small_mesh():
        total = keep[0] + came[0].astype(F32)
        down, out = total[:many].astype(BF16), total[many:each].astype(BF16)
        sums = total[each : each + 4] + total[each + 4 :]
    else:
        blocks = natural_blocks(keep, came, X_FIRST)
        grad = jnp.concatenate([block[:many] for block in blocks], axis=0)
        down = lax.psum_scatter(grad, "dp", scatter_dimension=0, tiled=True).astype(BF16)
        blocks = [blocks[index * 2 + bit] for bit in range(2) for index in range(4)]
        grad = jnp.concatenate([block[many:each] for block in blocks], axis=0)
        out = lax.psum_scatter(grad, "dp", scatter_dimension=0, tiled=True).astype(BF16)
        sums = blocks[0][each : each + 4] + blocks[0][each + 4 :]
        sums = lax.psum(sums, "dp")
    return down, lax.ppermute(out, ("dp", "sp"), moves), sums


def beside(wide, rows):
    part = rows.shape[1] // RANKS
    runs = [rows[:, index * part : (index + 1) * part] for index in range(RANKS)]
    return jnp.concatenate([wide, jnp.concatenate(runs, axis=0)], axis=1)


def local(
    tokens,
    segment_ids,
    masked_rows,
    replacement,
    cotangent,
    w_qkv,
    w_out_attn,
    w_in_ff,
    w_out_ff,
    gain_one,
    shift_one,
    gain_two,
    shift_two,
):
    rows_dev, width = tokens.shape
    rank = lax.axis_index("sp")
    heads = HEADS // RANKS
    dim = width // HEADS
    part = heads * dim
    slopes = alibi_slopes(HEADS)

    select = jnp.arange(rows_dev, dtype=jnp.int32)[:, None] == masked_rows[None, :]
    hit = jnp.any(select, axis=1, keepdims=True)
    placed = dot(select.astype(BF16), replacement)
    start = jnp.where(hit, placed.astype(BF16), tokens)
    start_far = flip(start, "sp", 2)
    start_near = flip(start, "sp", 1)
    place = lax.axis_index("dp")
    place = place if small_mesh() else place * 0
    spot = jnp.stack([rank, place]).astype(jnp.int32)

    w_rank = jnp.concatenate(
        [
            lax.dynamic_slice_in_dim(w_qkv, third * width + rank * part, part, 1)
            for third in range(3)
        ],
        axis=1,
    )
    part_units = w_out_ff.shape[0] // lax.axis_size("dp") // RANKS
    packed_in, packed_down = pack_weights(spot, w_in_ff, w_out_ff, part_units)
    start_cross = flip(after(start_far, w_rank, packed_in), "sp", 1)
    start_blocks = [start, start_near, start_far, start_cross]
    qkv, *attn, lse = attention_forward(
        spot, segment_ids, slopes, start_blocks, w_rank, heads, dim
    )
    low, unit, inverse = norm_one(
        spot, exchange_blocks(attn), start, w_out_attn, gain_one, shift_one
    )
    low_far = flip(low, "sp", 2)
    low_near = flip(low, "sp", 1)
    layer_out, d_h2, d_ff, slope, act, sums2 = ffn_forward(
        low, unit, gain_one, shift_one, gain_two, shift_two,
        masked_rows, cotangent, w_in_ff, w_out_ff, 768,
    )
    d_ff_far = flip(d_ff, "sp", 2)
    d_ff_near = flip(d_ff, "sp", 1)
    low_far = after(low_far, d_ff)
    low_cross = flip(low_far, "sp", 1)
    low_blocks = [low, low_near, low_far, low_cross]
    d_h1, sent = ffn_backward(
        after(d_ff, low_far), d_h2, unit, inverse, gain_one, sums2, act, slope, w_in_ff, w_out_ff, 768
    )
    far = flip(sent, "sp", 2)
    near = flip(sent, "sp", 1)
    d_ff_cross = flip(after(d_ff_far, sent), "sp", 1)
    d_ff_blocks = [d_ff, d_ff_near, d_ff_far, d_ff_cross]

    keep_b, send_b, keep_d, send_d = ffn_grad(
        spot, low_blocks, d_ff_blocks, packed_in, packed_down, 256
    )
    came_b = send_first(send_b, Z_FIRST)
    came_d = send_first(send_d, X_FIRST)
    cross = flip(after(far, keep_b), "sp", 1)
    d_proj_blocks = [sent, near, far, cross]
    keep_r, send_r = row_grad(spot, attn, d_proj_blocks)
    came_r = send_first(send_r, X_FIRST)

    d_qkv = attention_backward(
        after(spot, keep_r), segment_ids, slopes, d_proj_blocks, w_out_attn, qkv, lse, heads, dim
    )
    parts = exchange(d_qkv)
    keep_q, send_q = qkv_grad(
        after(spot, came_b, came_d), start_blocks, d_qkv
    )
    came_q = send_first(send_q, X_FIRST)
    keep_r, came_r = send_rows_second(keep_d, after(came_d, keep_q), keep_r, came_r)
    keep_b, came_b = send_second(keep_b, after(came_b, keep_r), Z_FIRST)
    grad_tokens, grad_replacement = token_grad(
        after(parts, keep_b), w_qkv, d_h1, masked_rows
    )
    keep_q, came_q = send_second(keep_q, after(came_q, grad_tokens), X_FIRST)
    keep_r, came_r = send_rows_third(keep_r, after(came_r, keep_q))
    keep_b, came_b = send_third(keep_b, after(came_b, keep_r, came_q), Z_FIRST)
    keep_q, came_q = send_third(keep_q, after(came_q, keep_b), X_FIRST)
    many = w_out_ff.shape[0] // RANKS // 8
    down_share, out_share, norm_sums = finish_rows(keep_r, after(came_r, keep_q), many)
    wide = finish_sum(keep_b, came_b, Z_FIRST)
    ffn_blocks = gather_blocks(jnp.concatenate([wide, down_share], axis=1))
    heads_share = finish_sum(keep_q, came_q, X_FIRST)
    head_blocks = gather_blocks(beside(heads_share, out_share))
    grad_in, grad_down = join_ffn(spot, ffn_blocks, part_units)
    grad_qkv, grad_out = join_heads(spot, head_blocks)

    return (
        layer_out,
        grad_tokens,
        grad_replacement,
        grad_qkv,
        grad_out,
        grad_in,
        grad_down,
        norm_sums[0],
        norm_sums[1],
        norm_sums[2],
        norm_sums[3],
    )


def solution(mesh):
    tokens = P(("dp", "sp"), None)
    rows = P("dp", None)
    return jax.shard_map(
        local,
        mesh=mesh,
        in_specs=(tokens, rows, P(("dp", "sp")), tokens, tokens) + (P(),) * 8,
        out_specs=(tokens,) * 3 + (rows,) * 4 + (P(),) * 4,
        check_vma=False,
    )
```

```python
import functools
import math

import jax
import jax.numpy as jnp
from jax import lax
from jax.experimental import pallas as pl
from jax.experimental.pallas import tpu as pltpu
from jax.sharding import PartitionSpec as P

HEADS = 12
RANKS = 4
EPSILON = 1e-05
FAR = 1e30
F32 = jnp.float32
BF16 = jnp.bfloat16
VM = pl.BlockSpec(memory_space=pltpu.VMEM)
SM = pl.BlockSpec(memory_space=pltpu.SMEM)


def shape(dims, kind):
    return jax.ShapeDtypeStruct(dims, kind)


def scratch(dims, kind):
    return pltpu.VMEM(dims, kind)


def params(mebibytes):
    return pltpu.CompilerParams(vmem_limit_bytes=mebibytes << 20)


def alibi_slopes(head_count):
    nearest = 2 ** int(math.floor(math.log2(head_count)))
    base_list = [2.0 ** (-8.0 * (index + 1) / nearest) for index in range(nearest)]
    extra_list = [
        2.0 ** (-8.0 * (2 * index + 1) / (2 * nearest)) for index in range(head_count - nearest)
    ]
    return jnp.array(base_list + extra_list, dtype=F32)


def dot(a, b):
    return jnp.dot(a, b, preferred_element_type=F32)


def dot_nt(a, b):
    return lax.dot_general(a, b, (((1,), (1,)), ((), ())), preferred_element_type=F32)


def dot_tn(a, b):
    return lax.dot_general(a, b, (((0,), (0,)), ((), ())), preferred_element_type=F32)


def exact_dot(a, b):
    return jnp.dot(a, b, precision=lax.Precision.HIGHEST, preferred_element_type=F32)


def standardize(value):
    center = value - jnp.mean(value, axis=-1, keepdims=True)
    spread = jnp.mean(center * center, axis=-1, keepdims=True)
    inverse = lax.rsqrt(spread + EPSILON)
    return center * inverse, inverse


def standardize_back(grad, unit, inverse):
    mean = jnp.mean(grad, axis=-1, keepdims=True)
    return inverse * (grad - mean - unit * jnp.mean(grad * unit, axis=-1, keepdims=True))


def gelu_pair(x):
    cdf = 0.5 * (1.0 + lax.erf(x * math.sqrt(0.5)))
    pdf = jnp.exp(-0.5 * x * x) * (1.0 / math.sqrt(2.0 * math.pi))
    return x * cdf, cdf + x * pdf


def pair_active(seg, rank, first, second, rows):
    one, two = rank ^ first, rank ^ second
    low, high = jnp.minimum(one, two), jnp.maximum(one, two)
    return jnp.logical_or(one == two, seg[0, low * rows + rows - 1] == seg[0, high * rows])


def key_sequences(seg_rows, seg_keys, rank, rows):
    for at in range(RANKS):
        first = pl.multiple_of((rank ^ at) * rows, rows)
        line = jnp.broadcast_to(seg_rows[:, pl.ds(first, rows)], (128, rows))
        seg_keys[at * rows : (at + 1) * rows, :] = jnp.transpose(line)


def pair_distance(seg_rows, seg_keys, rank, keys_at, query_at, rows):
    key_pos, query_pos = (rank ^ keys_at) * rows, (rank ^ query_at) * rows
    down = lax.broadcasted_iota(jnp.int32, (rows, rows), 0)
    across = lax.broadcasted_iota(jnp.int32, (rows, rows), 1)
    gap = jnp.abs(down - across + (key_pos - query_pos)).astype(F32)
    seg_q = seg_rows[:, pl.ds(pl.multiple_of(query_pos, rows), rows)]
    seg_k = seg_keys[pl.ds(pl.multiple_of(keys_at * rows, rows), rows), 0:1]
    return jnp.where(seg_k == seg_q, gap, FAR)


def attention_forward_kernel(
    rows, heads, dim, info, seg, slopes, x0, x1, x2, x3, w, seg_rows,
    qkv_out, o0, o1, o2, o3, lse, qs, ks, vt, dist, seg_keys, score, peak,
):
    rank = info[0]
    width = heads * dim
    key_sequences(seg_rows, seg_keys, rank, rows)
    for at, x in enumerate((x0, x1, x2, x3)):
        qkv = dot(x[...], w[...]).astype(BF16)
        here = pl.ds(at * rows, rows)
        qkv_out[here, :] = qkv
        for h in range(heads):
            qs[h, here, :] = (qkv[:, h * dim : (h + 1) * dim] * dim**-0.5).astype(BF16)
            ks[h, here, :] = qkv[:, width + h * dim : width + (h + 1) * dim]
        vt[:, here] = jnp.transpose(qkv[:, 2 * width :])

    for a in range(RANKS):
        mine = pl.ds(a * rows, rows)
        peak[...] = jnp.full_like(peak, -jnp.inf)

        def first_pass(b, carry):
            @pl.when(pair_active(seg, rank, a, b, rows))
            def _():
                theirs = pl.ds(pl.multiple_of(b * rows, rows), rows)
                gap = pair_distance(seg_rows, seg_keys, rank, b, a, rows)
                for h in range(heads):
                    slope = slopes[rank * heads + h]
                    s = dot_nt(ks[h, theirs, :], qs[h, mine, :]) - slope * gap
                    score[h, theirs, :] = s
                    peak[h : h + 1, :] = jnp.maximum(
                        peak[h : h + 1, :], jnp.max(s, axis=0, keepdims=True)
                    )

            return carry

        lax.fori_loop(0, RANKS, first_pass, 0)

        def second_pass(b, carry):
            def add(carry):
                theirs = pl.ds(pl.multiple_of(b * rows, rows), rows)
                result = []
                for h in range(heads):
                    acc, total = carry[h]
                    p = jnp.exp(score[h, theirs, :] - peak[h : h + 1, :])
                    total = total + jnp.sum(p, axis=0, keepdims=True)
                    span = slice(h * dim, (h + 1) * dim)
                    result.append((acc + dot(vt[span, theirs], p.astype(BF16)), total))
                return tuple(result)

            return lax.cond(pair_active(seg, rank, a, b, rows), add, lambda carry: carry, carry)

        empty = (jnp.zeros((dim, rows), F32), jnp.zeros((1, rows), F32))
        sums = lax.fori_loop(0, RANKS, second_pass, (empty,) * heads)
        for h in range(heads):
            acc, total = sums[h]
            span = slice(h * dim, (h + 1) * dim)
            (o0, o1, o2, o3)[a][span, :] = (acc / total).astype(BF16)
            lse[h : h + 1, mine] = peak[h : h + 1, :] + jnp.log(total)


def attention_forward(info, seg, slopes, blocks, w, heads, dim):
    rows = blocks[0].shape[0]
    tok, lw = rows * RANKS, heads * dim
    return pl.pallas_call(
        functools.partial(attention_forward_kernel, rows, heads, dim),
        name="attention_forward",
        out_shape=(shape((tok, 3 * lw), BF16),)
        + (shape((lw, rows), BF16),) * RANKS
        + (shape((heads, tok), F32),),
        in_specs=[SM] * 3 + [VM] * 6,
        out_specs=(VM,) * 6,
        scratch_shapes=[
            scratch((heads, tok, dim), BF16),
            scratch((heads, tok, dim), BF16),
            scratch((lw, tok), BF16),
            scratch((rows, rows), F32),
            scratch((tok, 128), jnp.int32),
            scratch((heads, tok, rows), F32),
            scratch((heads, rows), F32),
        ],
        compiler_params=params(14),
        cost_estimate=pl.CostEstimate(
            flops=4 * 10**9, bytes_accessed=6 * 10**6, transcendentals=3 * 10**6
        ),
    )(info, seg, slopes, *blocks, w, seg)


def attention_backward_kernel(
    rows, heads, dim, info, seg, slopes, g0, g1, g2, g3, w, qkv, lse, seg_rows,
    d_qkv, qs, ks, kt, vs, do, seg_keys, prob, dprob, dk, dv, dqt, delta,
):
    rank = info[0]
    width = heads * dim
    scale = dim**-0.5
    key_sequences(seg_rows, seg_keys, rank, rows)
    w_rank = w[pl.ds(pl.multiple_of(rank * width, width), width), :]
    for at, g in enumerate((g0, g1, g2, g3)):
        here = pl.ds(at * rows, rows)
        grad = dot_nt(g[0:rows, :], w_rank).astype(BF16)
        value = qkv[here, :]
        kt[:, here] = jnp.transpose(value[:, width : 2 * width])
        for h in range(heads):
            do[h, here, :] = grad[:, h * dim : (h + 1) * dim]
            qs[h, here, :] = (value[:, h * dim : (h + 1) * dim] * scale).astype(BF16)
            ks[h, here, :] = value[:, width + h * dim : width + (h + 1) * dim]
            vs[h, here, :] = value[:, 2 * width + h * dim : 2 * width + (h + 1) * dim]
    dk[...] = jnp.zeros_like(dk)
    dv[...] = jnp.zeros_like(dv)

    for a in range(RANKS):
        mine = pl.ds(a * rows, rows)
        delta[...] = jnp.zeros_like(delta)
        dqt[...] = jnp.zeros_like(dqt)

        def first_pass(b, carry):
            @pl.when(pair_active(seg, rank, a, b, rows))
            def _():
                theirs = pl.ds(pl.multiple_of(b * rows, rows), rows)
                gap = pair_distance(seg_rows, seg_keys, rank, b, a, rows)
                for h in range(heads):
                    slope = slopes[rank * heads + h]
                    s = dot_nt(ks[h, theirs, :], qs[h, mine, :]) - slope * gap
                    p = jnp.exp(s - lse[h : h + 1, mine])
                    dp = dot_nt(vs[h, theirs, :], do[h, mine, :])
                    delta[h : h + 1, :] += jnp.sum(p * dp, axis=0, keepdims=True)
                    prob[h, theirs, :] = p
                    dprob[h, theirs, :] = dp

            return carry

        lax.fori_loop(0, RANKS, first_pass, 0)

        def second_pass(b, carry):
            @pl.when(pair_active(seg, rank, a, b, rows))
            def _():
                theirs = pl.ds(pl.multiple_of(b * rows, rows), rows)
                for h in range(heads):
                    p = prob[h, theirs, :]
                    ds = (p * (dprob[h, theirs, :] - delta[h : h + 1, :])).astype(BF16)
                    dv[h, theirs, :] += dot(p.astype(BF16), do[h, mine, :])
                    dk[h, theirs, :] += dot(ds, qs[h, mine, :])
                    span = slice(h * dim, (h + 1) * dim)
                    dqt[span, :] += dot(kt[span, theirs], ds)

            return carry

        lax.fori_loop(0, RANKS, second_pass, 0)
        d_qkv[rank ^ a, 0:width, :] = (dqt[...] * scale).astype(BF16)

    for at in range(RANKS):
        here = pl.ds(at * rows, rows)
        for h in range(heads):
            first = width + h * dim
            d_qkv[rank ^ at, first : first + dim, :] = jnp.transpose(dk[h, here, :]).astype(BF16)
            first = 2 * width + h * dim
            d_qkv[rank ^ at, first : first + dim, :] = jnp.transpose(dv[h, here, :]).astype(BF16)


def attention_backward(info, seg, slopes, blocks, w, qkv, lse, heads, dim):
    tok, lw = qkv.shape[0], heads * dim
    rows = tok // RANKS
    return pl.pallas_call(
        functools.partial(attention_backward_kernel, rows, heads, dim),
        name="attention_backward",
        out_shape=shape((RANKS, 3 * lw, rows), BF16),
        in_specs=[SM] * 3 + [VM] * 8,
        out_specs=VM,
        scratch_shapes=[
            scratch((heads, tok, dim), BF16),
            scratch((heads, tok, dim), BF16),
            scratch((lw, tok), BF16),
            scratch((heads, tok, dim), BF16),
            scratch((heads, tok, dim), BF16),
            scratch((tok, 128), jnp.int32),
            scratch((heads, tok, rows), F32),
            scratch((heads, tok, rows), F32),
            scratch((heads, tok, dim), F32),
            scratch((heads, tok, dim), F32),
            scratch((lw, rows), F32),
            scratch((heads, rows), F32),
        ],
        compiler_params=params(20),
        cost_estimate=pl.CostEstimate(
            flops=8 * 10**9, bytes_accessed=6 * 10**6, transcendentals=3 * 10**6
        ),
    )(info, seg, slopes, *blocks, w, qkv, lse, seg)


def line(vector):
    return vector[...].reshape(1, -1)


def norm_one_kernel(
    info, own, near, far, cross, start, w, gain, shift, low, unit, inverse, joined
):
    part = own.shape[0]
    for step, value in enumerate((own, near, far, cross)):
        first = pl.multiple_of((info[0] ^ step) * part, part)
        joined[pl.ds(first, part), :] = value[...]
    x, inv = standardize(start[...].astype(F32) + dot_tn(joined[...], w[...]))
    unit[...] = x
    inverse[...] = inv
    low[...] = (x * line(gain) + line(shift)).astype(BF16)


def norm_one(info, parts, start, w, gain, shift):
    rows, width = start.shape
    return pl.pallas_call(
        norm_one_kernel,
        name="norm_one",
        out_shape=(shape((rows, width), BF16), shape((rows, width), F32), shape((rows, 1), F32)),
        in_specs=[SM] + [VM] * 8,
        out_specs=(VM,) * 3,
        scratch_shapes=[scratch((width, rows), BF16)],
        compiler_params=params(16),
        cost_estimate=pl.CostEstimate(
            flops=2 * rows * width * width, bytes_accessed=4 * 10**6, transcendentals=0
        ),
    )(info, *parts, start, w, gain, shift)


def ffn_forward_kernel(
    low, unit, gain1, shift1, gain2, shift2, masked, cot, w_in, w_down,
    layer_out, d_h2, d_ff, slope, act, sums, acc, gates, ups,
):
    hid = w_down.shape[0]
    size = gates.shape[2]
    count = hid // size

    def project(block, slot):
        first = pl.multiple_of(block * size, size)
        gates[slot] = dot(low[...], w_in[:, pl.ds(first, size)])
        ups[slot] = dot(low[...], w_in[:, pl.ds(pl.multiple_of(hid + first, size), size)])

    def finish(block, slot):
        here = pl.ds(pl.multiple_of(block * size, size), size)
        up = ups[slot]
        value, grad = gelu_pair(gates[slot])
        act[:, here] = value.astype(BF16)
        slope[:, here] = (up * grad).astype(BF16)
        acc[...] += dot((value * up).astype(BF16), w_down[here, :])

    acc[...] = unit[...] * line(gain1) + line(shift1)
    project(0, 0)

    def pair(index, carry):
        block = index * 2
        project(block + 1, 1)
        finish(block, 0)
        project(block + 2, 0)
        finish(block + 1, 1)
        return carry

    lax.fori_loop(0, count // 2 - 1, pair, 0)
    project(count - 1, 1)
    finish(count - 2, 0)
    finish(count - 1, 1)
    x, inv = standardize(acc[...])
    layer_out[...] = (x * line(gain2) + line(shift2)).astype(BF16)
    places = lax.broadcasted_iota(jnp.int32, (low.shape[0], masked.shape[0]), 0)
    dy = exact_dot((places == line(masked)).astype(F32), cot[...])
    sums[0:1, :] = jnp.sum(dy * x, axis=0, keepdims=True)
    sums[1:2, :] = jnp.sum(dy, axis=0, keepdims=True)
    grad_in = standardize_back(dy * line(gain2), x, inv)
    d_h2[...] = grad_in
    d_ff[...] = grad_in.astype(BF16)


def ffn_forward(low, unit, gain1, shift1, gain2, shift2, masked, cot, w_in, w_out, size):
    rows, width = low.shape
    hid = w_out.shape[0]
    return pl.pallas_call(
        ffn_forward_kernel,
        name="ffn_forward",
        out_shape=(
            shape((rows, width), BF16),
            shape((rows, width), F32),
            shape((rows, width), BF16),
            shape((rows, hid), BF16),
            shape((rows, hid), BF16),
            shape((2, width), F32),
        ),
        in_specs=[VM] * 10,
        out_specs=(VM,) * 6,
        scratch_shapes=[
            scratch((rows, width), F32),
            scratch((2, rows, size), F32),
            scratch((2, rows, size), F32),
        ],
        compiler_params=params(14),
        cost_estimate=pl.CostEstimate(
            flops=6 * rows * width * hid, bytes_accessed=18 * 10**6, transcendentals=2 * rows * hid
        ),
    )(low, unit, gain1, shift1, gain2, shift2, masked, cot, w_in, w_out)


def ffn_backward_kernel(
    d_ff, d_h2, unit, inverse, gain1, sums2, act, slope, w_in, w_down, d_h1, sent, acc, hidden
):
    hid = w_down.shape[0]
    size = hidden.shape[2]
    count = hid // size

    def project(block, slot):
        here = pl.ds(pl.multiple_of(block * size, size), size)
        hidden[slot] = dot_nt(d_ff[...], w_down[here, :])

    def finish(block, slot):
        first = pl.multiple_of(block * size, size)
        here, there = pl.ds(first, size), pl.ds(pl.multiple_of(hid + first, size), size)
        d_hidden = hidden[slot]
        d_gate = (d_hidden * slope[:, here].astype(F32)).astype(BF16)
        d_up = (d_hidden * act[:, here].astype(F32)).astype(BF16)
        acc[...] += dot_nt(d_gate, w_in[:, here]) + dot_nt(d_up, w_in[:, there])

    acc[...] = d_h2[...]
    project(0, 0)

    def pair(index, carry):
        block = index * 2
        project(block + 1, 1)
        finish(block, 0)
        project(block + 2, 0)
        finish(block + 1, 1)
        return carry

    lax.fori_loop(0, count // 2 - 1, pair, 0)
    project(count - 1, 1)
    finish(count - 2, 0)
    finish(count - 1, 1)
    total = acc[...]
    rows = total.shape[0]
    x = unit[...]
    gain_sum = jnp.sum(total * x, axis=0, keepdims=True)
    shift_sum = jnp.sum(total, axis=0, keepdims=True)
    sums = jnp.concatenate([gain_sum, shift_sum, sums2[...]], axis=0)
    high = sums.astype(BF16).astype(F32)
    tail = jnp.concatenate([high, sums - high, jnp.zeros((8, sums.shape[1]), F32)], axis=0)
    grad = standardize_back(total * line(gain1), x, inverse[...])
    d_h1[...] = grad
    sent[0:rows, :] = grad.astype(BF16)
    sent[rows : rows + 16, :] = tail.astype(BF16)


def ffn_backward(d_ff, d_h2, unit, inverse, gain1, sums2, act, slope, w_in, w_out, size):
    rows, width = d_ff.shape
    hid = w_out.shape[0]
    return pl.pallas_call(
        ffn_backward_kernel,
        name="ffn_backward",
        out_shape=(shape((rows, width), F32), shape((rows + 16, width), BF16)),
        in_specs=[VM] * 10,
        out_specs=(VM,) * 2,
        scratch_shapes=[scratch((rows, width), F32), scratch((2, rows, size), F32)],
        compiler_params=params(14),
        cost_estimate=pl.CostEstimate(
            flops=6 * rows * width * hid, bytes_accessed=20 * 10**6, transcendentals=0
        ),
    )(d_ff, d_h2, unit, inverse, gain1, sums2, act, slope, w_in, w_out)


X_FIRST = (1, 2, 4)
Z_FIRST = (2, 1, 4)


def bit_of(value, mask):
    return (value // mask) % 2


def store_blocks(blocks, keep, send, place, order, columns):
    one, two, three = order
    odd = bit_of(place, one) == 1
    for index in range(8):
        if index & one:
            continue
        spot = bit_of(place ^ index, two) * 2 + bit_of(place ^ index, three)
        low, high = blocks(index), blocks(index | one)
        keep[spot, :, columns] = jnp.where(odd, high, low).astype(BF16)
        send[spot, :, columns] = jnp.where(odd, low, high).astype(BF16)


def row_blocks(grad):
    each = grad.shape[0] // 8
    return lambda index: grad[index * each : (index + 1) * each]


def quarter_blocks(grad):
    each = grad.shape[0] // 8

    def block(index):
        at = index % 2 * 4 + index // 2
        return grad[at * each : (at + 1) * each]

    return block


def ffn_grad_kernel(
    order, size, first, steps, info, n0, n1, n2, n3, f0, f1, f2, f3, w_in, w_down, *rest
):
    if first == 0:
        keep, send, g_down, tok_t, gates, ups, d_hiddens, hidden_t, d_gate, d_up, d_ff = rest
    else:
        tok_t, down_a, keep, send, keep_down, send_down = rest[:6]
        gates, ups, d_hiddens, hidden_t, d_gate, d_up, d_ff, down = rest[6:]
    toks, grads = (n0, n1, n2, n3), (f0, f1, f2, f3)
    rows = n0.shape[0]
    hid = w_down.shape[0]
    for at in range(RANKS):
        here = slice(at * rows, (at + 1) * rows)
        d_ff[here, :] = grads[at][...]
        if first == 0:
            tok_t[:, here] = jnp.transpose(toks[at][...])

    def unit_block(step, carry):
        base = pl.multiple_of(info[0] * (hid // RANKS) + (first + step) * size, size)
        w_gate = w_in[:, pl.ds(base, size)]
        w_up = w_in[:, pl.ds(pl.multiple_of(hid + base, size), size)]
        w_rows = w_down[pl.ds(base, size), :]

        def project(at):
            slot = at % 2
            gates[slot] = dot(toks[at][...], w_gate)
            ups[slot] = dot(toks[at][...], w_up)
            d_hiddens[slot] = dot_nt(grads[at][...], w_rows)

        def finish(at):
            slot = at % 2
            here = slice(at * rows, (at + 1) * rows)
            value, grad = gelu_pair(gates[slot])
            up, d_hidden = ups[slot], d_hiddens[slot]
            hidden_t[:, here] = jnp.transpose((value * up).astype(BF16))
            d_gate[here, :] = (d_hidden * up * grad).astype(BF16)
            d_up[here, :] = (d_hidden * value).astype(BF16)

        project(0)
        for at in range(RANKS):
            if at + 1 < RANKS:
                project(at + 1)
            finish(at)
        for other, grad in enumerate((d_gate, d_up)):
            columns = pl.ds(pl.multiple_of((other * steps + step) * size, size), size)
            total = dot(tok_t[...], grad[...])
            store_blocks(row_blocks(total), keep, send, info[1], order, columns)
        part = dot(hidden_t[...], d_ff[...])
        if first == 0:
            g_down[...] = part.astype(BF16)
        else:
            down[pl.ds(pl.multiple_of((first + step) * size, size), size), :] = part
        return carry

    if steps == 1:
        unit_block(0, 0)
    else:
        lax.fori_loop(0, steps, unit_block, 0)
    if first:
        down[0 : first * size, :] = down_a[...].astype(F32)
        store_blocks(quarter_blocks(down), keep_down, send_down, info[1], X_FIRST, slice(None))


def ffn_grad(info, toks, grads, w_in, w_out, size, first, steps, order, more=()):
    rows, width = toks[0].shape
    part = w_out.shape[0] // RANKS
    tok = rows * RANKS
    dims = [(4, width // 8, 2 * size * steps)] * 2
    scratch_shapes = [
        scratch((2, rows, size), F32),
        scratch((2, rows, size), F32),
        scratch((2, rows, size), F32),
        scratch((size, tok), BF16),
        scratch((tok, size), BF16),
        scratch((tok, size), BF16),
        scratch((tok, width), BF16),
    ]
    if first == 0:
        dims += [(size, width), (width, tok)]
    else:
        dims += [(4, part // 8, width)] * 2
        scratch_shapes += [scratch((part, width), F32)]
    return pl.pallas_call(
        functools.partial(ffn_grad_kernel, order, size, first, steps),
        name="ffn_grad",
        out_shape=[shape(each, BF16) for each in dims],
        in_specs=[SM] + [VM] * (10 + len(more)),
        out_specs=[VM] * len(dims),
        scratch_shapes=scratch_shapes,
        compiler_params=params(18),
        cost_estimate=pl.CostEstimate(
            flops=12 * tok * width * size * steps,
            bytes_accessed=8 * 10**6,
            transcendentals=2 * tok * size * steps,
        ),
    )(info, *toks, *grads, w_in, w_out, *more)


def row_grad_kernel(
    info, a0, a1, a2, a3, g0, g1, g2, g3, keep_down, send_down, keep, send
):
    many = keep_down.shape[1]
    keep[:, :many] = keep_down[...]
    send[:, :many] = send_down[...]
    rows = g0.shape[0] - 16
    grad = 0.0
    sums = 0.0
    for attn, g in zip((a0, a1, a2, a3), (g0, g1, g2, g3)):
        grad = grad + dot(attn[...], g[0:rows, :])
        pair = g[rows : rows + 16, :].astype(F32)
        sums = sums + pair[0:4] + pair[4:8]
    high = sums.astype(BF16).astype(F32)
    tail = jnp.concatenate([high, sums - high], axis=0)
    part = quarter_blocks(grad)

    def blocks(index):
        return jnp.concatenate([part(index), tail], axis=0)

    store_blocks(
        blocks, keep.at[:, many:], send.at[:, many:], info[1], X_FIRST, slice(None)
    )


def row_grad(info, attn, blocks, keep_down, send_down):
    width = blocks[0].shape[1]
    dims = (4, keep_down.shape[1] + attn[0].shape[0] // 8 + 8, width)
    return pl.pallas_call(
        row_grad_kernel,
        name="row_grad",
        out_shape=(shape(dims, BF16),) * 2,
        in_specs=[SM] + [VM] * 10,
        out_specs=(VM, VM),
        compiler_params=params(16),
        cost_estimate=pl.CostEstimate(
            flops=8 * attn[0].size * width, bytes_accessed=3 * 10**6, transcendentals=0
        ),
    )(info, *attn, *blocks, keep_down, send_down)


def qkv_grad_kernel(info, x0, x1, x2, x3, d_qkv, keep, send):
    total = 0.0
    for at, x in enumerate((x0, x1, x2, x3)):
        total = total + dot(d_qkv[info[0] ^ at], x[...])
    store_blocks(row_blocks(jnp.transpose(total)), keep, send, info[1], X_FIRST, slice(None))


def qkv_grad(info, blocks, d_qkv):
    rows, width = blocks[0].shape
    columns = d_qkv.shape[1]
    return pl.pallas_call(
        qkv_grad_kernel,
        name="qkv_grad",
        out_shape=(shape((4, width // 8, columns), BF16),) * 2,
        in_specs=[SM] + [VM] * 5,
        out_specs=(VM, VM),
        compiler_params=params(16),
        cost_estimate=pl.CostEstimate(
            flops=8 * rows * width * columns, bytes_accessed=4 * 10**6, transcendentals=0
        ),
    )(info, *blocks, d_qkv)


def join_wide_kernel(info, b0, b1, b2, b3, out):
    rank = info[0]
    half = out.shape[1] // 2
    part = half // RANKS
    one = part // 3
    for step, block in enumerate((b0, b1, b2, b3)):
        base = pl.multiple_of((rank ^ step) * part, part)
        value = block[...].astype(F32)
        out[:, pl.ds(base, one)] = value[:, 0:one]
        out[:, pl.ds(pl.multiple_of(half + base, one), one)] = value[:, one : 2 * one]
        out[:, pl.ds(pl.multiple_of(base + one, one), 2 * one)] = value[:, 2 * one : 4 * one]
        out[:, pl.ds(pl.multiple_of(half + base + one, one), 2 * one)] = value[:, 4 * one :]


def join_wide(info, blocks):
    rows, columns = blocks[0].shape
    return pl.pallas_call(
        join_wide_kernel,
        name="join_wide",
        out_shape=shape((rows, columns * RANKS), F32),
        in_specs=[SM] + [VM] * 4,
        out_specs=VM,
        compiler_params=params(10),
        cost_estimate=pl.CostEstimate(flops=10**6, bytes_accessed=4 * 10**6, transcendentals=0),
    )(info, *blocks)


def join_rows_kernel(info, b0, b1, b2, b3, down, out):
    rank = info[0]
    many, few = down.shape[0] // RANKS, out.shape[0] // RANKS
    for step, block in enumerate((b0, b1, b2, b3)):
        place = rank ^ step
        value = block[...].astype(F32)
        down[pl.ds(place * many, many), :] = value[0:many]
        out[pl.ds(place * few, few), :] = value[many : many + few]


def join_rows(info, blocks, many):
    rows, columns = blocks[0].shape
    if many % 8 or (rows - many) % 8:
        stacked = jnp.stack(blocks)[info[0] ^ jnp.arange(RANKS)].astype(F32)
        return stacked[:, :many].reshape(-1, columns), stacked[:, many:].reshape(-1, columns)
    return pl.pallas_call(
        join_rows_kernel,
        name="join_rows",
        out_shape=(
            shape((many * RANKS, columns), F32),
            shape(((rows - many) * RANKS, columns), F32),
        ),
        in_specs=[SM] + [VM] * 4,
        out_specs=(VM, VM),
        compiler_params=params(10),
        cost_estimate=pl.CostEstimate(flops=10**6, bytes_accessed=2 * 10**6, transcendentals=0),
    )(info, *blocks)


def join_heads_kernel(info, b0, b1, b2, b3, out):
    rank = info[0]
    width = out.shape[1] // 3
    part = width // RANKS
    for value in range(RANKS):

        @pl.when(rank == value)
        def _():
            for step, block in enumerate((b0, b1, b2, b3)):
                for third in range(3):
                    first = third * width + (value ^ step) * part
                    piece = block[:, third * part : (third + 1) * part]
                    out[:, first : first + part] = piece.astype(F32)


def join_heads(info, blocks):
    rows, columns = blocks[0].shape
    return pl.pallas_call(
        join_heads_kernel,
        name="join_heads",
        out_shape=shape((rows, columns * RANKS), F32),
        in_specs=[SM] + [VM] * 4,
        out_specs=VM,
        compiler_params=params(10),
        cost_estimate=pl.CostEstimate(flops=10**6, bytes_accessed=2 * 10**6, transcendentals=0),
    )(info, *blocks)


def token_grad_kernel(parts, w, d_h1, masked, tokens, replacement, joined):
    rows, width = d_h1.shape
    part = width // RANKS
    for rank in range(RANKS):
        for third in range(3):
            first = third * width + rank * part
            joined[first : first + part, :] = parts[rank, third * part : (third + 1) * part, :]
    grad = d_h1[...] + jnp.transpose(dot(w[...], joined[...]))
    count = masked.shape[0]
    places = lax.broadcasted_iota(jnp.int32, (rows, count), 0)
    select = (places == line(masked)).astype(F32)
    hit = jnp.max(select, axis=1, keepdims=True)
    tokens[...] = jnp.where(hit > 0.5, 0.0, grad)
    replacement[...] = lax.dot_general(
        select, grad, (((0,), (0,)), ((), ())),
        precision=lax.Precision.HIGHEST, preferred_element_type=F32,
    )


def token_grad(parts, w, d_h1, masked):
    rows, width = d_h1.shape
    return pl.pallas_call(
        token_grad_kernel,
        name="token_grad",
        out_shape=(shape((rows, width), F32), shape((masked.shape[0], width), F32)),
        in_specs=[VM] * 4,
        out_specs=(VM, VM),
        scratch_shapes=[scratch((3 * width, rows), BF16)],
        compiler_params=params(16),
        cost_estimate=pl.CostEstimate(
            flops=6 * rows * width * width, bytes_accessed=8 * 10**6, transcendentals=0
        ),
    )(parts, w, d_h1, masked)


def after(value, *others):
    return lax.optimization_barrier((value,) + others)[0]


def flip(value, axis, bits):
    count = lax.axis_size(axis)
    return lax.ppermute(value, axis, [(index, index ^ bits) for index in range(count)])


def gather_blocks(value):
    far = flip(value, "sp", 2)
    near = flip(value, "sp", 1)
    cross = flip(far, "sp", 1)
    return [value, near, far, cross]


def exchange_blocks(blocks):
    via = flip(blocks[3], "sp", 1)
    near = flip(blocks[1], "sp", 1)
    far = flip(blocks[2], "sp", 2)
    cross = flip(via, "sp", 2)
    return [blocks[0], near, far, cross]


def exchange(parts):
    return lax.all_to_all(parts, "sp", 0, 0, tiled=True)


def small_mesh():
    return lax.axis_size("dp") == 8


NO_COST = pl.CostEstimate(flops=0, bytes_accessed=0, transcendentals=0)


def tidy_sums(value):
    first = value.shape[1] - 8
    sums = value[:, first : first + 4] + value[:, first + 4 :]
    high = sums.astype(BF16).astype(F32)
    return jnp.concatenate([value[:, :first], high, sums - high], axis=1)


def halve_kernel(with_sums, keep, came, kept, sent):
    half = keep.shape[0] // 2
    value = keep[...].astype(F32) + came[...].astype(F32)
    if with_sums:
        value = tidy_sums(value)
    kept[...] = value[:half]
    sent[...] = value[half:].astype(BF16)


def halve(keep, came, with_sums=False):
    dims = (keep.shape[0] // 2,) + keep.shape[1:]
    return pl.pallas_call(
        functools.partial(halve_kernel, with_sums),
        name="halve",
        out_shape=(shape(dims, F32), shape(dims, BF16)),
        in_specs=[VM] * 2,
        out_specs=(VM, VM),
        compiler_params=params(12),
        cost_estimate=NO_COST,
    )(keep, came)


def fold_kernel(keep_a, came_a, keep_r, came_r, kept, sent):
    half = kept.shape[0]
    high, wide = keep_a.shape[1] // 3, keep_a.shape[2] // 2
    for piece in range(6):
        rows = slice(piece // 2 * high, piece // 2 * high + high)
        columns = slice(piece % 2 * wide, piece % 2 * wide + wide)
        value = keep_a[:, rows, columns].astype(F32) + came_a[:, rows, columns].astype(F32)
        rows = slice(piece // 3 * high, piece // 3 * high + high)
        columns = slice(piece % 3 * wide, piece % 3 * wide + wide)
        kept[:, rows, columns] = value[:half]
        sent[:, rows, columns] = value[half:].astype(BF16)
    value = tidy_sums(keep_r[...].astype(F32) + came_r[...].astype(F32))
    kept[:, 2 * high :] = value[:half]
    sent[:, 2 * high :] = value[half:].astype(BF16)


def fold_halve(keep_a, came_a, keep_r, came_r):
    count, high, _ = keep_a.shape
    _, each, width = keep_r.shape
    dims = (count // 2, high // 3 * 2 + each, width)
    return pl.pallas_call(
        fold_kernel,
        name="fold_halve",
        out_shape=(shape(dims, F32), shape(dims, BF16)),
        in_specs=[VM] * 4,
        out_specs=(VM, VM),
        compiler_params=params(12),
        cost_estimate=NO_COST,
    )(keep_a, came_a, keep_r, came_r)


def finish_kernel(keep_b, came_b, keep_r, came_r, wide_out, rows_out, sums_out):
    first = wide_out.shape[1] - keep_b.shape[2]
    wide_out[:, first:] = (keep_b[0] + came_b[0].astype(F32)).astype(BF16)
    total = keep_r[0] + came_r[0].astype(F32)
    high, wide = wide_out.shape[0] // 3, first // 2
    for piece in range(6):
        value = total[
            piece // 3 * high : piece // 3 * high + high,
            piece % 3 * wide : piece % 3 * wide + wide,
        ].astype(BF16)
        rows = slice(piece // 2 * high, piece // 2 * high + high)
        wide_out[rows, piece % 2 * wide : piece % 2 * wide + wide] = value
    last = total.shape[0] - 8
    rows_out[...] = total[2 * high : last].astype(BF16)
    sums_out[...] = total[last : last + 4] + total[last + 4 :]


def send_first(send, order):
    return flip(send, "dp", order[0]) if small_mesh() else send


def send_second(keep, came, order):
    if not small_mesh():
        return keep, came
    kept, sent = halve(keep, came)
    return kept, flip(sent, "dp", order[1])


def send_third(keep, came, order):
    if not small_mesh():
        return keep, came
    kept, sent = halve(keep, came)
    return kept, flip(sent, "dp", order[2])


def natural_blocks(keep, send, order):
    both = jnp.concatenate([keep, send], axis=0).astype(F32)
    places = []
    for index in range(8):
        bits = [1 if index & mask else 0 for mask in order]
        places.append(both[bits[0] * 4 + bits[1] * 2 + bits[2]])
    return places


def scatter_sum(keep, came, order):
    grad = jnp.concatenate(natural_blocks(keep, came, order), axis=0)
    return lax.psum_scatter(grad, "dp", scatter_dimension=0, tiled=True).astype(BF16)


def finish_sum(keep, came, order):
    if small_mesh():
        return (keep[0] + came[0].astype(F32)).astype(BF16)
    return scatter_sum(keep, came, order)


def fold_second(keep_a, came_a, keep_r, came_r):
    if not small_mesh():
        return (keep_a, keep_r), (came_a, came_r)
    kept, sent = fold_halve(keep_a, came_a, keep_r, came_r)
    return kept, flip(sent, "dp", X_FIRST[1])


def fold_third(keep, came):
    if not small_mesh():
        return keep, came
    kept, sent = halve(keep, came, True)
    return kept, flip(sent, "dp", X_FIRST[2])


def finish_ffn(keep_b, came_b, keep, came, columns, many):
    if small_mesh():
        _, high, wide = keep_b.shape
        _, each, width = keep.shape
        return pl.pallas_call(
            finish_kernel,
            name="finish_ffn",
            out_shape=(
                shape((high, columns), BF16),
                shape((each - 8 - high // 3 * 2, width), BF16),
                shape((4, width), F32),
            ),
            in_specs=[VM] * 4,
            out_specs=(VM,) * 3,
            compiler_params=params(10),
            cost_estimate=NO_COST,
        )(keep_b, came_b, keep, came)
    wide = [scatter_sum(keep[0], came[0], X_FIRST), scatter_sum(keep_b, came_b, Z_FIRST)]
    each = keep[1].shape[1] - 8
    blocks = natural_blocks(keep[1], came[1], X_FIRST)
    blocks = [blocks[index * 2 + bit] for bit in range(2) for index in range(4)]
    results = []
    for first, last in ((0, many), (many, each)):
        grad = jnp.concatenate([block[first:last] for block in blocks], axis=0)
        shard = lax.psum_scatter(grad, "dp", scatter_dimension=0, tiled=True)
        results.append(shard.astype(BF16))
    sums = blocks[0][each : each + 4] + blocks[0][each + 4 :]
    return jnp.concatenate(wide, axis=1), jnp.concatenate(results, axis=0), lax.psum(sums, "dp")


def move_rows(rows):
    count = lax.axis_size("dp")
    moves = []
    for place in range(count):
        for rank in range(RANKS):
            if small_mesh():
                place_to, rank_to = rank * 2 + place % 2, place // 2
            else:
                place_to, rank_to = rank * (count // 4) + place // 4, place % 4
            moves.append((place * RANKS + rank, place_to * RANKS + rank_to))
    return lax.ppermute(rows, ("dp", "sp"), moves)


def local(
    tokens,
    segment_ids,
    masked_rows,
    replacement,
    cotangent,
    w_qkv,
    w_out_attn,
    w_in_ff,
    w_out_ff,
    gain_one,
    shift_one,
    gain_two,
    shift_two,
):
    rows_dev, width = tokens.shape
    rank = lax.axis_index("sp")
    heads = HEADS // RANKS
    dim = width // HEADS
    part = heads * dim
    slopes = alibi_slopes(HEADS)

    select = jnp.arange(rows_dev, dtype=jnp.int32)[:, None] == masked_rows[None, :]
    hit = jnp.any(select, axis=1, keepdims=True)
    placed = dot(select.astype(BF16), replacement)
    start = jnp.where(hit, placed.astype(BF16), tokens)
    start_far = flip(start, "sp", 2)
    start_near = flip(start, "sp", 1)
    place = lax.axis_index("dp")
    place = place if small_mesh() else place * 0
    spot = jnp.stack([rank, place]).astype(jnp.int32)

    w_rank = jnp.concatenate(
        [
            lax.dynamic_slice_in_dim(w_qkv, third * width + rank * part, part, 1)
            for third in range(3)
        ],
        axis=1,
    )
    start_cross = flip(after(start_far, w_rank, spot), "sp", 1)
    start_blocks = [start, start_near, start_far, start_cross]
    qkv, *attn, lse = attention_forward(
        spot, segment_ids, slopes, start_blocks, w_rank, heads, dim
    )
    low, unit, inverse = norm_one(
        spot, exchange_blocks(attn), start, w_out_attn, gain_one, shift_one
    )
    low_far = flip(low, "sp", 2)
    low_near = flip(low, "sp", 1)
    layer_out, d_h2, d_ff, slope, act, sums2 = ffn_forward(
        low, unit, gain_one, shift_one, gain_two, shift_two,
        masked_rows, cotangent, w_in_ff, w_out_ff, 768,
    )
    d_ff_far = flip(d_ff, "sp", 2)
    d_ff_near = flip(d_ff, "sp", 1)
    low_far = after(low_far, d_ff)
    low_cross = flip(low_far, "sp", 1)
    low_blocks = [low, low_near, low_far, low_cross]
    d_h1, sent = ffn_backward(
        after(d_ff, low_far), d_h2, unit, inverse, gain_one, sums2, act, slope, w_in_ff, w_out_ff, 768
    )
    far = flip(sent, "sp", 2)
    near = flip(sent, "sp", 1)
    d_ff_cross = flip(after(d_ff_far, sent), "sp", 1)
    d_ff_blocks = [d_ff, d_ff_near, d_ff_far, d_ff_cross]

    units = w_out_ff.shape[0] // RANKS // 3
    keep_a, send_a, down_a, low_t = ffn_grad(
        spot, low_blocks, d_ff_blocks, w_in_ff, w_out_ff, units, 0, 1, X_FIRST
    )
    came_a = send_first(send_a, X_FIRST)
    keep_b, send_b, keep_d, send_d = ffn_grad(
        after(spot, down_a),
        low_blocks, d_ff_blocks, w_in_ff, w_out_ff, units, 1, 2, Z_FIRST, (low_t, down_a),
    )
    came_b = send_first(send_b, Z_FIRST)
    cross = flip(after(far, came_a, keep_b), "sp", 1)
    d_proj_blocks = [sent, near, far, cross]
    keep_r, send_r = row_grad(spot, attn, d_proj_blocks, keep_d, send_d)
    came_r = send_first(send_r, X_FIRST)

    d_qkv = attention_backward(
        after(spot, keep_r), segment_ids, slopes, d_proj_blocks, w_out_attn, qkv, lse, heads, dim
    )
    parts = exchange(d_qkv)
    keep_r, came_r = fold_second(keep_a, came_a, keep_r, after(came_r, d_qkv))
    keep_b, came_b = send_second(keep_b, after(came_b, keep_r), Z_FIRST)
    keep_q, send_q = qkv_grad(after(spot, keep_b), start_blocks, d_qkv)
    came_q = send_first(send_q, X_FIRST)
    grad_tokens, grad_replacement = token_grad(
        after(parts, keep_q), w_qkv, d_h1, masked_rows
    )
    keep_b, came_b = send_third(keep_b, after(came_b, grad_tokens), Z_FIRST)
    keep_r, came_r = fold_third(keep_r, after(came_r, keep_b))
    keep_q, came_q = send_second(keep_q, after(came_q, keep_r), X_FIRST)
    keep_q, came_q = send_third(keep_q, came_q, X_FIRST)
    many = w_out_ff.shape[0] // RANKS // 8
    wide, row_share, norm_sums = finish_ffn(
        keep_b, after(came_b, came_q), keep_r, came_r, w_in_ff.shape[1] // RANKS, many
    )
    heads_share = finish_sum(keep_q, after(came_q, wide), X_FIRST)
    row_share = move_rows(row_share)
    far = flip(wide, "sp", 2)
    near = flip(wide, "sp", 1)
    head_blocks = gather_blocks(heads_share)
    wide_blocks = [wide, near, far, flip(after(far, heads_share), "sp", 1)]
    row_blocks_ = gather_blocks(row_share)
    many = w_out_ff.shape[0] // lax.axis_size("dp") // RANKS
    grad_down, grad_out = join_rows(spot, row_blocks_, many)

    return (
        layer_out,
        grad_tokens,
        grad_replacement,
        join_heads(spot, head_blocks),
        grad_out,
        join_wide(spot, wide_blocks),
        grad_down,
        norm_sums[0],
        norm_sums[1],
        norm_sums[2],
        norm_sums[3],
    )


def solution(mesh):
    tokens = P(("dp", "sp"), None)
    rows = P("dp", None)
    return jax.shard_map(
        local,
        mesh=mesh,
        in_specs=(tokens, rows, P(("dp", "sp")), tokens, tokens) + (P(),) * 8,
        out_specs=(tokens,) * 3 + (rows,) * 4 + (P(),) * 4,
        check_vma=False,
    )
```

```python
import functools
import math

import jax
import jax.numpy as jnp
from jax import lax
from jax.experimental import pallas as pl
from jax.experimental.pallas import tpu as pltpu
from jax.sharding import PartitionSpec as P

HEADS = 12
RANKS = 4
EPSILON = 1e-05
FAR = 1e30
F32 = jnp.float32
BF16 = jnp.bfloat16
VM = pl.BlockSpec(memory_space=pltpu.VMEM)
SM = pl.BlockSpec(memory_space=pltpu.SMEM)


def shape(dims, kind):
    return jax.ShapeDtypeStruct(dims, kind)


def scratch(dims, kind):
    return pltpu.VMEM(dims, kind)


def params(mebibytes):
    return pltpu.CompilerParams(vmem_limit_bytes=mebibytes << 20)


def alibi_slopes(head_count):
    nearest = 2 ** int(math.floor(math.log2(head_count)))
    base_list = [2.0 ** (-8.0 * (index + 1) / nearest) for index in range(nearest)]
    extra_list = [
        2.0 ** (-8.0 * (2 * index + 1) / (2 * nearest)) for index in range(head_count - nearest)
    ]
    return jnp.array(base_list + extra_list, dtype=F32)


def dot(a, b):
    return jnp.dot(a, b, preferred_element_type=F32)


def dot_nt(a, b):
    return lax.dot_general(a, b, (((1,), (1,)), ((), ())), preferred_element_type=F32)


def dot_tn(a, b):
    return lax.dot_general(a, b, (((0,), (0,)), ((), ())), preferred_element_type=F32)


def exact_dot(a, b):
    return jnp.dot(a, b, precision=lax.Precision.HIGHEST, preferred_element_type=F32)


def standardize(value):
    center = value - jnp.mean(value, axis=-1, keepdims=True)
    spread = jnp.mean(center * center, axis=-1, keepdims=True)
    inverse = lax.rsqrt(spread + EPSILON)
    return center * inverse, inverse


def standardize_back(grad, unit, inverse):
    mean = jnp.mean(grad, axis=-1, keepdims=True)
    return inverse * (grad - mean - unit * jnp.mean(grad * unit, axis=-1, keepdims=True))


def gelu_pair(x):
    cdf = 0.5 * (1.0 + lax.erf(x * math.sqrt(0.5)))
    pdf = jnp.exp(-0.5 * x * x) * (1.0 / math.sqrt(2.0 * math.pi))
    return x * cdf, cdf + x * pdf


def pair_active(seg, rank, first, second, rows):
    one, two = rank ^ first, rank ^ second
    low, high = jnp.minimum(one, two), jnp.maximum(one, two)
    return jnp.logical_or(one == two, seg[0, low * rows + rows - 1] == seg[0, high * rows])


def key_sequences(seg_rows, seg_keys, rank, rows):
    for at in range(RANKS):
        first = pl.multiple_of((rank ^ at) * rows, rows)
        line = jnp.broadcast_to(seg_rows[:, pl.ds(first, rows)], (128, rows))
        seg_keys[at * rows : (at + 1) * rows, :] = jnp.transpose(line)


def pair_distance(seg_rows, seg_keys, rank, keys_at, query_at, rows):
    key_pos, query_pos = (rank ^ keys_at) * rows, (rank ^ query_at) * rows
    down = lax.broadcasted_iota(jnp.int32, (rows, rows), 0)
    across = lax.broadcasted_iota(jnp.int32, (rows, rows), 1)
    gap = jnp.abs(down - across + (key_pos - query_pos)).astype(F32)
    seg_q = seg_rows[:, pl.ds(pl.multiple_of(query_pos, rows), rows)]
    seg_k = seg_keys[pl.ds(pl.multiple_of(keys_at * rows, rows), rows), 0:1]
    return jnp.where(seg_k == seg_q, gap, FAR)


def attention_forward_kernel(
    rows, heads, dim, info, seg, slopes, x0, x1, x2, x3, w, seg_rows,
    qkv_out, out_t, lse, qs, ks, vt, dist, seg_keys, score, peak,
):
    rank = info[0]
    width = heads * dim
    key_sequences(seg_rows, seg_keys, rank, rows)
    for at, x in enumerate((x0, x1, x2, x3)):
        qkv = dot(x[...], w[...]).astype(BF16)
        here = pl.ds(at * rows, rows)
        qkv_out[here, :] = qkv
        for h in range(heads):
            qs[h, here, :] = (qkv[:, h * dim : (h + 1) * dim] * dim**-0.5).astype(BF16)
            ks[h, here, :] = qkv[:, width + h * dim : width + (h + 1) * dim]
        vt[:, here] = jnp.transpose(qkv[:, 2 * width :])

    for a in range(RANKS):
        mine = pl.ds(a * rows, rows)
        peak[...] = jnp.full_like(peak, -jnp.inf)

        def first_pass(b, carry):
            @pl.when(pair_active(seg, rank, a, b, rows))
            def _():
                theirs = pl.ds(pl.multiple_of(b * rows, rows), rows)
                gap = pair_distance(seg_rows, seg_keys, rank, b, a, rows)
                for h in range(heads):
                    slope = slopes[rank * heads + h]
                    s = dot_nt(ks[h, theirs, :], qs[h, mine, :]) - slope * gap
                    score[h, theirs, :] = s
                    peak[h : h + 1, :] = jnp.maximum(
                        peak[h : h + 1, :], jnp.max(s, axis=0, keepdims=True)
                    )

            return carry

        lax.fori_loop(0, RANKS, first_pass, 0)

        def second_pass(b, carry):
            def add(carry):
                theirs = pl.ds(pl.multiple_of(b * rows, rows), rows)
                result = []
                for h in range(heads):
                    acc, total = carry[h]
                    p = jnp.exp(score[h, theirs, :] - peak[h : h + 1, :])
                    total = total + jnp.sum(p, axis=0, keepdims=True)
                    span = slice(h * dim, (h + 1) * dim)
                    result.append((acc + dot(vt[span, theirs], p.astype(BF16)), total))
                return tuple(result)

            return lax.cond(pair_active(seg, rank, a, b, rows), add, lambda carry: carry, carry)

        empty = (jnp.zeros((dim, rows), F32), jnp.zeros((1, rows), F32))
        sums = lax.fori_loop(0, RANKS, second_pass, (empty,) * heads)
        for h in range(heads):
            acc, total = sums[h]
            span = slice(h * dim, (h + 1) * dim)
            out_t[span, mine] = (acc / total).astype(BF16)
            lse[h : h + 1, mine] = peak[h : h + 1, :] + jnp.log(total)


def attention_forward(info, seg, slopes, blocks, w, heads, dim):
    rows = blocks[0].shape[0]
    tok, lw = rows * RANKS, heads * dim
    return pl.pallas_call(
        functools.partial(attention_forward_kernel, rows, heads, dim),
        name="attention_forward",
        out_shape=(
            shape((tok, 3 * lw), BF16),
            shape((lw, tok), BF16),
            shape((heads, tok), F32),
        ),
        in_specs=[SM] * 3 + [VM] * 6,
        out_specs=(VM,) * 3,
        scratch_shapes=[
            scratch((heads, tok, dim), BF16),
            scratch((heads, tok, dim), BF16),
            scratch((lw, tok), BF16),
            scratch((rows, rows), F32),
            scratch((tok, 128), jnp.int32),
            scratch((heads, tok, rows), F32),
            scratch((heads, rows), F32),
        ],
        compiler_params=params(14),
        cost_estimate=pl.CostEstimate(
            flops=4 * 10**9, bytes_accessed=6 * 10**6, transcendentals=3 * 10**6
        ),
    )(info, seg, slopes, *blocks, w, seg)


def attention_backward_kernel(
    rows, heads, dim, info, seg, slopes, g0, g1, g2, g3, w, qkv, lse, seg_rows,
    d0, d1, d2, d3, qs, ks, kt, vs, do, seg_keys, prob, dprob, dk, dv, dqt, delta,
):
    rank = info[0]
    width = heads * dim
    scale = dim**-0.5
    key_sequences(seg_rows, seg_keys, rank, rows)
    w_rank = w[pl.ds(pl.multiple_of(rank * width, width), width), :]
    for at, g in enumerate((g0, g1, g2, g3)):
        here = pl.ds(at * rows, rows)
        grad = dot_nt(g[0:rows, :], w_rank).astype(BF16)
        value = qkv[here, :]
        kt[:, here] = jnp.transpose(value[:, width : 2 * width])
        for h in range(heads):
            do[h, here, :] = grad[:, h * dim : (h + 1) * dim]
            qs[h, here, :] = (value[:, h * dim : (h + 1) * dim] * scale).astype(BF16)
            ks[h, here, :] = value[:, width + h * dim : width + (h + 1) * dim]
            vs[h, here, :] = value[:, 2 * width + h * dim : 2 * width + (h + 1) * dim]
    dk[...] = jnp.zeros_like(dk)
    dv[...] = jnp.zeros_like(dv)

    for a in range(RANKS):
        mine = pl.ds(a * rows, rows)
        delta[...] = jnp.zeros_like(delta)
        dqt[...] = jnp.zeros_like(dqt)

        def first_pass(b, carry):
            @pl.when(pair_active(seg, rank, a, b, rows))
            def _():
                theirs = pl.ds(pl.multiple_of(b * rows, rows), rows)
                gap = pair_distance(seg_rows, seg_keys, rank, b, a, rows)
                for h in range(heads):
                    slope = slopes[rank * heads + h]
                    s = dot_nt(ks[h, theirs, :], qs[h, mine, :]) - slope * gap
                    p = jnp.exp(s - lse[h : h + 1, mine])
                    dp = dot_nt(vs[h, theirs, :], do[h, mine, :])
                    delta[h : h + 1, :] += jnp.sum(p * dp, axis=0, keepdims=True)
                    prob[h, theirs, :] = p
                    dprob[h, theirs, :] = dp

            return carry

        lax.fori_loop(0, RANKS, first_pass, 0)

        def second_pass(b, carry):
            @pl.when(pair_active(seg, rank, a, b, rows))
            def _():
                theirs = pl.ds(pl.multiple_of(b * rows, rows), rows)
                for h in range(heads):
                    p = prob[h, theirs, :]
                    ds = (p * (dprob[h, theirs, :] - delta[h : h + 1, :])).astype(BF16)
                    dv[h, theirs, :] += dot(p.astype(BF16), do[h, mine, :])
                    dk[h, theirs, :] += dot(ds, qs[h, mine, :])
                    span = slice(h * dim, (h + 1) * dim)
                    dqt[span, :] += dot(kt[span, theirs], ds)

            return carry

        lax.fori_loop(0, RANKS, second_pass, 0)
        (d0, d1, d2, d3)[a][0:width, :] = (dqt[...] * scale).astype(BF16)

    for at, d_qkv in enumerate((d0, d1, d2, d3)):
        here = pl.ds(at * rows, rows)
        for h in range(heads):
            first = width + h * dim
            d_qkv[first : first + dim, :] = jnp.transpose(dk[h, here, :]).astype(BF16)
            first = 2 * width + h * dim
            d_qkv[first : first + dim, :] = jnp.transpose(dv[h, here, :]).astype(BF16)


def attention_backward(info, seg, slopes, blocks, w, qkv, lse, heads, dim):
    tok, lw = qkv.shape[0], heads * dim
    rows = tok // RANKS
    return pl.pallas_call(
        functools.partial(attention_backward_kernel, rows, heads, dim),
        name="attention_backward",
        out_shape=(shape((3 * lw, rows), BF16),) * RANKS,
        in_specs=[SM] * 3 + [VM] * 8,
        out_specs=(VM,) * RANKS,
        scratch_shapes=[
            scratch((heads, tok, dim), BF16),
            scratch((heads, tok, dim), BF16),
            scratch((lw, tok), BF16),
            scratch((heads, tok, dim), BF16),
            scratch((heads, tok, dim), BF16),
            scratch((tok, 128), jnp.int32),
            scratch((heads, tok, rows), F32),
            scratch((heads, tok, rows), F32),
            scratch((heads, tok, dim), F32),
            scratch((heads, tok, dim), F32),
            scratch((lw, rows), F32),
            scratch((heads, rows), F32),
        ],
        compiler_params=params(20),
        cost_estimate=pl.CostEstimate(
            flops=8 * 10**9, bytes_accessed=6 * 10**6, transcendentals=3 * 10**6
        ),
    )(info, seg, slopes, *blocks, w, qkv, lse, seg)


def line(vector):
    return vector[...].reshape(1, -1)


def join_tokens(rank, arrays, tokens_of, joined):
    part = arrays[0].shape[0]
    rows = arrays[0].shape[1] // RANKS
    for step, array in enumerate(arrays):
        first = pl.multiple_of((rank ^ step) * part, part)
        block = step ^ tokens_of
        joined[pl.ds(first, part), :] = array[:, block * rows : (block + 1) * rows]


def norm_one_kernel(
    info, own, near, far, cross, start, w, gain, shift, low, joined, unit, inverse
):
    join_tokens(info[0], (own, near, far, cross), 0, joined)
    x, inv = standardize(start[...].astype(F32) + dot_tn(joined[...], w[...]))
    unit[...] = x
    inverse[...] = inv
    low[...] = (x * line(gain) + line(shift)).astype(BF16)


def norm_one(info, parts, start, w, gain, shift):
    rows, width = start.shape
    return pl.pallas_call(
        norm_one_kernel,
        name="norm_one",
        out_shape=(
            shape((rows, width), BF16),
            shape((width, rows), BF16),
            shape((rows, width), F32),
            shape((rows, 1), F32),
        ),
        in_specs=[SM] + [VM] * 8,
        out_specs=(VM,) * 4,
        compiler_params=params(12),
        cost_estimate=pl.CostEstimate(
            flops=2 * rows * width * width, bytes_accessed=4 * 10**6, transcendentals=0
        ),
    )(info, *parts, start, w, gain, shift)


def norm_others_kernel(
    info, own, near, far, cross, s1, s2, s3, w, gain, shift, l1, l2, l3, j1, j2, j3
):
    for tokens_of, (start, low, joined) in enumerate(((s1, l1, j1), (s2, l2, j2), (s3, l3, j3))):
        join_tokens(info[0], (own, near, far, cross), tokens_of + 1, joined)
        x, _ = standardize(start[...].astype(F32) + dot_tn(joined[...], w[...]))
        low[...] = (x * line(gain) + line(shift)).astype(BF16)


def norm_others(info, parts, starts, w, gain, shift):
    rows, width = starts[0].shape
    results = pl.pallas_call(
        norm_others_kernel,
        name="norm_others",
        out_shape=(shape((rows, width), BF16),) * 3 + (shape((width, rows), BF16),) * 3,
        in_specs=[SM] + [VM] * 10,
        out_specs=(VM,) * 6,
        compiler_params=params(12),
        cost_estimate=pl.CostEstimate(
            flops=6 * rows * width * width, bytes_accessed=4 * 10**6, transcendentals=0
        ),
    )(info, *parts, *starts, w, gain, shift)
    return results[:3], results[3:]


def packing(rows, columns, part, rank):
    units = lax.broadcasted_iota(jnp.int32, (rows, columns), 0)
    packed = lax.broadcasted_iota(jnp.int32, (1, columns), 1)
    places = packed + rank * part
    for index in range(1, columns // part):
        places = places + jnp.where(packed >= index * part, (RANKS - 1) * part, 0)
    return (units == places).astype(BF16)


def pack_kernel(part, info, w_in, w_down, packed_in, packed_down):
    rank = info[0]
    width, hid = w_in.shape[0], w_down.shape[0]
    run = hid // 2
    select = packing(run, run // RANKS, part, rank)
    for index in range(4):
        piece = dot(w_in[:, index * run : (index + 1) * run], select)
        packed_in[:, index * run // RANKS : (index + 1) * run // RANKS] = piece.astype(BF16)
    if part % 16:
        for index in range(2):
            piece = dot_tn(select, w_down[index * run : (index + 1) * run, :])
            packed_down[index * run // RANKS : (index + 1) * run // RANKS, :] = piece.astype(BF16)
    else:
        for index in range(hid // RANKS // part):
            rows = pl.ds(pl.multiple_of((index * RANKS + rank) * part, part), part)
            packed_down[index * part : (index + 1) * part, :] = w_down[rows, :]


def pack_weights(info, w_in, w_out, part):
    width, hid = w_in.shape[0], w_out.shape[0]
    return pl.pallas_call(
        functools.partial(pack_kernel, part),
        name="pack_weights",
        out_shape=(shape((width, 2 * hid // RANKS), BF16), shape((hid // RANKS, width), BF16)),
        in_specs=[SM, VM, VM],
        out_specs=(VM, VM),
        compiler_params=params(14),
        cost_estimate=pl.CostEstimate(
            flops=4 * 10**9, bytes_accessed=17 * 10**6, transcendentals=0
        ),
    )(info, w_in, w_out)


def ffn_forward_kernel(
    low, unit, gain1, shift1, gain2, shift2, masked, cot, w_in, w_down,
    layer_out, d_h2, d_ff, slope, act, sums, acc, gates, ups,
):
    hid = w_down.shape[0]
    size = gates.shape[2]
    count = hid // size

    def project(block, slot):
        first = pl.multiple_of(block * size, size)
        gates[slot] = dot(low[...], w_in[:, pl.ds(first, size)])
        ups[slot] = dot(low[...], w_in[:, pl.ds(pl.multiple_of(hid + first, size), size)])

    def finish(block, slot):
        here = pl.ds(pl.multiple_of(block * size, size), size)
        up = ups[slot]
        value, grad = gelu_pair(gates[slot])
        act[:, here] = value.astype(BF16)
        slope[:, here] = (up * grad).astype(BF16)
        acc[...] += dot((value * up).astype(BF16), w_down[here, :])

    acc[...] = unit[...] * line(gain1) + line(shift1)
    project(0, 0)

    def pair(index, carry):
        block = index * 2
        project(block + 1, 1)
        finish(block, 0)
        project(block + 2, 0)
        finish(block + 1, 1)
        return carry

    lax.fori_loop(0, count // 2 - 1, pair, 0)
    project(count - 1, 1)
    finish(count - 2, 0)
    finish(count - 1, 1)
    x, inv = standardize(acc[...])
    layer_out[...] = (x * line(gain2) + line(shift2)).astype(BF16)
    places = lax.broadcasted_iota(jnp.int32, (low.shape[0], masked.shape[0]), 0)
    dy = exact_dot((places == line(masked)).astype(F32), cot[...])
    sums[0:1, :] = jnp.sum(dy * x, axis=0, keepdims=True)
    sums[1:2, :] = jnp.sum(dy, axis=0, keepdims=True)
    grad_in = standardize_back(dy * line(gain2), x, inv)
    d_h2[...] = grad_in
    d_ff[...] = grad_in.astype(BF16)


def ffn_forward(low, unit, gain1, shift1, gain2, shift2, masked, cot, w_in, w_out, size):
    rows, width = low.shape
    hid = w_out.shape[0]
    return pl.pallas_call(
        ffn_forward_kernel,
        name="ffn_forward",
        out_shape=(
            shape((rows, width), BF16),
            shape((rows, width), F32),
            shape((rows, width), BF16),
            shape((rows, hid), BF16),
            shape((rows, hid), BF16),
            shape((2, width), F32),
        ),
        in_specs=[VM] * 10,
        out_specs=(VM,) * 6,
        scratch_shapes=[
            scratch((rows, width), F32),
            scratch((2, rows, size), F32),
            scratch((2, rows, size), F32),
        ],
        compiler_params=params(14),
        cost_estimate=pl.CostEstimate(
            flops=6 * rows * width * hid, bytes_accessed=18 * 10**6, transcendentals=2 * rows * hid
        ),
    )(low, unit, gain1, shift1, gain2, shift2, masked, cot, w_in, w_out)


def ffn_backward_kernel(
    d_ff, d_h2, unit, inverse, gain1, sums2, act, slope, w_in, w_down, d_h1, sent, acc, hidden
):
    hid = w_down.shape[0]
    size = hidden.shape[2]
    count = hid // size

    def project(block, slot):
        here = pl.ds(pl.multiple_of(block * size, size), size)
        hidden[slot] = dot_nt(d_ff[...], w_down[here, :])

    def finish(block, slot):
        first = pl.multiple_of(block * size, size)
        here, there = pl.ds(first, size), pl.ds(pl.multiple_of(hid + first, size), size)
        d_hidden = hidden[slot]
        d_gate = (d_hidden * slope[:, here].astype(F32)).astype(BF16)
        d_up = (d_hidden * act[:, here].astype(F32)).astype(BF16)
        acc[...] += dot_nt(d_gate, w_in[:, here]) + dot_nt(d_up, w_in[:, there])

    acc[...] = d_h2[...]
    project(0, 0)

    def pair(index, carry):
        block = index * 2
        project(block + 1, 1)
        finish(block, 0)
        project(block + 2, 0)
        finish(block + 1, 1)
        return carry

    lax.fori_loop(0, count // 2 - 1, pair, 0)
    project(count - 1, 1)
    finish(count - 2, 0)
    finish(count - 1, 1)
    total = acc[...]
    rows = total.shape[0]
    x = unit[...]
    gain_sum = jnp.sum(total * x, axis=0, keepdims=True)
    shift_sum = jnp.sum(total, axis=0, keepdims=True)
    sums = jnp.concatenate([gain_sum, shift_sum, sums2[...]], axis=0)
    high = sums.astype(BF16).astype(F32)
    tail = jnp.concatenate([high, sums - high, jnp.zeros((8, sums.shape[1]), F32)], axis=0)
    grad = standardize_back(total * line(gain1), x, inverse[...])
    d_h1[...] = grad
    sent[0:rows, :] = grad.astype(BF16)
    sent[rows : rows + 16, :] = tail.astype(BF16)


def ffn_backward(d_ff, d_h2, unit, inverse, gain1, sums2, act, slope, w_in, w_out, size):
    rows, width = d_ff.shape
    hid = w_out.shape[0]
    return pl.pallas_call(
        ffn_backward_kernel,
        name="ffn_backward",
        out_shape=(shape((rows, width), F32), shape((rows + 16, width), BF16)),
        in_specs=[VM] * 10,
        out_specs=(VM,) * 2,
        scratch_shapes=[scratch((rows, width), F32), scratch((2, rows, size), F32)],
        compiler_params=params(14),
        cost_estimate=pl.CostEstimate(
            flops=6 * rows * width * hid, bytes_accessed=20 * 10**6, transcendentals=0
        ),
    )(d_ff, d_h2, unit, inverse, gain1, sums2, act, slope, w_in, w_out)


X_FIRST = (1, 2, 4)
Z_FIRST = (2, 1, 4)


def bit_of(value, mask):
    return (value // mask) % 2


def store_blocks(blocks, keep, send, place, order, columns):
    one, two, three = order
    odd = bit_of(place, one) == 1
    for index in range(8):
        if index & one:
            continue
        spot = bit_of(place ^ index, two) * 2 + bit_of(place ^ index, three)
        low, high = blocks(index), blocks(index | one)
        keep[spot, :, columns] = jnp.where(odd, high, low).astype(BF16)
        send[spot, :, columns] = jnp.where(odd, low, high).astype(BF16)


def row_blocks(grad):
    each = grad.shape[0] // 8
    return lambda index: grad[index * each : (index + 1) * each]


def ffn_grad_kernel(
    size, info, n0, n1, n2, n3, f0, f1, f2, f3, w_in, w_down,
    keep, send, keep_down, send_down,
    tok_t, gates, ups, d_hiddens, hidden_t, d_gate, d_up, d_ff, down,
):
    toks, grads = (n0, n1, n2, n3), (f0, f1, f2, f3)
    rows = n0.shape[0]
    units = w_down.shape[0]
    for at in range(RANKS):
        here = slice(at * rows, (at + 1) * rows)
        d_ff[here, :] = grads[at][...]
        tok_t[:, here] = jnp.transpose(toks[at][...])

    def unit_block(step, carry):
        here = pl.ds(pl.multiple_of(step * size, size), size)
        there = pl.ds(pl.multiple_of(units + step * size, size), size)
        w_gate, w_up, w_rows = w_in[:, here], w_in[:, there], w_down[here, :]

        def project(at):
            slot = at % 2
            gates[slot] = dot(toks[at][...], w_gate)
            ups[slot] = dot(toks[at][...], w_up)
            d_hiddens[slot] = dot_nt(grads[at][...], w_rows)

        def finish(at):
            slot = at % 2
            here = slice(at * rows, (at + 1) * rows)
            value, grad = gelu_pair(gates[slot])
            up, d_hidden = ups[slot], d_hiddens[slot]
            hidden_t[:, here] = jnp.transpose((value * up).astype(BF16))
            d_gate[here, :] = (d_hidden * up * grad).astype(BF16)
            d_up[here, :] = (d_hidden * value).astype(BF16)

        project(0)
        for at in range(RANKS):
            if at + 1 < RANKS:
                project(at + 1)
            finish(at)
        for columns, grad in ((here, d_gate), (there, d_up)):
            total = dot(tok_t[...], grad[...])
            store_blocks(row_blocks(total), keep, send, info[1], Z_FIRST, columns)
        down[here, :] = dot(hidden_t[...], d_ff[...])
        return carry

    lax.fori_loop(0, units // size, unit_block, 0)
    store_blocks(row_blocks(down), keep_down, send_down, info[1], X_FIRST, slice(None))


def ffn_grad(info, toks, grads, w_in, w_down, size):
    rows, width = toks[0].shape
    units = w_down.shape[0]
    tok = rows * RANKS
    dims = [(4, width // 8, 2 * units)] * 2 + [(4, units // 8, width)] * 2
    return pl.pallas_call(
        functools.partial(ffn_grad_kernel, size),
        name="ffn_grad",
        out_shape=[shape(each, BF16) for each in dims],
        in_specs=[SM] + [VM] * 10,
        out_specs=[VM] * 4,
        scratch_shapes=[
            scratch((width, tok), BF16),
            scratch((2, rows, size), F32),
            scratch((2, rows, size), F32),
            scratch((2, rows, size), F32),
            scratch((size, tok), BF16),
            scratch((tok, size), BF16),
            scratch((tok, size), BF16),
            scratch((tok, width), BF16),
            scratch((units, width), F32),
        ],
        compiler_params=params(18),
        cost_estimate=pl.CostEstimate(
            flops=12 * tok * width * units,
            bytes_accessed=8 * 10**6,
            transcendentals=2 * tok * units,
        ),
    )(info, *toks, *grads, w_in, w_down)


def qkv_grad_kernel(
    info, x0, x1, x2, x3, d0, d1, d2, d3, j0, j1, j2, j3, g0, g1, g2, g3, keep, send, columns, grad
):
    rows, width = x0.shape
    part = width // RANKS
    total = 0.0
    for x, d_qkv in zip((x0, x1, x2, x3), (d0, d1, d2, d3)):
        total = total + dot(d_qkv[...], x[...])
    grad[:, : 3 * part] = jnp.transpose(total)
    for value in range(RANKS):

        @pl.when(info[0] == value)
        def _():
            for at, g in enumerate((g0, g1, g2, g3)):
                columns[at] = g[0:rows, value * part : (value + 1) * part]

    total = 0.0
    sums = 0.0
    for at, (joined, g) in enumerate(zip((j0, j1, j2, j3), (g0, g1, g2, g3))):
        total = total + dot(joined[...], columns[at])
        pair = g[rows : rows + 16, :].astype(F32)
        sums = sums + pair[0:4] + pair[4:8]
    grad[:, 3 * part :] = total
    high = sums.astype(BF16).astype(F32)
    tail = jnp.concatenate([high, sums - high], axis=0)
    each = width // 8

    def blocks(index):
        return jnp.concatenate([grad[index * each : (index + 1) * each], tail], axis=0)

    store_blocks(blocks, keep, send, info[1], X_FIRST, slice(None))


def qkv_grad(info, blocks, d_qkv, joined, d_proj):
    rows, width = blocks[0].shape
    return pl.pallas_call(
        qkv_grad_kernel,
        name="qkv_grad",
        out_shape=(shape((4, width // 8 + 8, width), BF16),) * 2,
        in_specs=[SM] + [VM] * 16,
        out_specs=(VM, VM),
        scratch_shapes=[
            scratch((RANKS, rows, width // RANKS), BF16),
            scratch((width, width), F32),
        ],
        compiler_params=params(14),
        cost_estimate=pl.CostEstimate(
            flops=8 * rows * width * width, bytes_accessed=4 * 10**6, transcendentals=0
        ),
    )(info, *blocks, *d_qkv, *joined, *d_proj)


def join_ffn_kernel(part, info, b0, b1, b2, b3, wide, down, packed):
    rank = info[0]
    rows = b0.shape[0]
    few = b0.shape[1] // 3
    for step, block in enumerate((b0, b1, b2, b3)):
        there = pl.multiple_of((rank ^ step) * few, few)
        packed[0, :, pl.ds(there, few)] = block[:, :few]
        packed[1, :, pl.ds(there, few)] = block[:, few : 2 * few]
        place = pl.multiple_of((rank ^ step) * rows, rows)
        down[pl.ds(place, rows), :] = block[:, 2 * few :].astype(F32)
    for half in range(2):
        for run in range(few // part):
            pieces = []
            for value in range(RANKS):
                first = value * few + run * part
                pieces.append(packed[half, :, first : first + part])
            first = half * RANKS * few + run * RANKS * part
            piece = jnp.concatenate(pieces, axis=1).astype(F32)
            wide[:, first : first + RANKS * part] = piece


def join_ffn(info, blocks, part):
    rows, columns = blocks[0].shape
    width = columns // 3
    if rows % 8 or RANKS * part % 128:
        stacked = jnp.stack(blocks)[info[0] ^ jnp.arange(RANKS)].astype(F32)
        wide = stacked[:, :, : 2 * width].reshape(RANKS, rows, -1, part).transpose(1, 2, 0, 3)
        return wide.reshape(rows, -1), stacked[:, :, 2 * width :].reshape(-1, width)
    return pl.pallas_call(
        functools.partial(join_ffn_kernel, part),
        name="join_ffn",
        out_shape=(shape((rows, 8 * width), F32), shape((rows * RANKS, width), F32)),
        in_specs=[SM] + [VM] * 4,
        out_specs=(VM, VM),
        scratch_shapes=[scratch((2, rows, RANKS * width), BF16)],
        compiler_params=params(14),
        cost_estimate=pl.CostEstimate(flops=10**6, bytes_accessed=6 * 10**6, transcendentals=0),
    )(info, *blocks)


def join_heads_kernel(info, b0, b1, b2, b3, out, rest):
    rank = info[0]
    width = rest.shape[1]
    part = width // RANKS
    for value in range(RANKS):

        @pl.when(rank == value)
        def _():
            for step, block in enumerate((b0, b1, b2, b3)):
                there = (value ^ step) * part
                for third in range(3):
                    piece = block[:, third * part : (third + 1) * part].astype(F32)
                    out[:, third * width + there : third * width + there + part] = piece
                rest[:, there : there + part] = block[:, 3 * part :].astype(F32)


def join_heads(info, blocks):
    rows, width = blocks[0].shape
    return pl.pallas_call(
        join_heads_kernel,
        name="join_heads",
        out_shape=(shape((rows, 3 * width), F32), shape((rows, width), F32)),
        in_specs=[SM] + [VM] * 4,
        out_specs=(VM, VM),
        compiler_params=params(8),
        cost_estimate=pl.CostEstimate(flops=10**6, bytes_accessed=2 * 10**6, transcendentals=0),
    )(info, *blocks)


def token_grad_kernel(
    info, own, near, far, cross, w, d_h1, masked, tokens, replacement, joined
):
    rows, width = d_h1.shape
    part = width // RANKS
    for step, block in enumerate((own, near, far, cross)):
        for third in range(3):
            first = pl.multiple_of(third * width + (info[0] ^ step) * part, part)
            joined[pl.ds(first, part), :] = block[third * part : (third + 1) * part, :]
    grad = d_h1[...] + jnp.transpose(dot(w[...], joined[...]))
    count = masked.shape[0]
    places = lax.broadcasted_iota(jnp.int32, (rows, count), 0)
    select = (places == line(masked)).astype(F32)
    hit = jnp.max(select, axis=1, keepdims=True)
    tokens[...] = jnp.where(hit > 0.5, 0.0, grad)
    replacement[...] = lax.dot_general(
        select, grad, (((0,), (0,)), ((), ())),
        precision=lax.Precision.HIGHEST, preferred_element_type=F32,
    )


def token_grad(info, parts, w, d_h1, masked):
    rows, width = d_h1.shape
    return pl.pallas_call(
        token_grad_kernel,
        name="token_grad",
        out_shape=(shape((rows, width), F32), shape((masked.shape[0], width), F32)),
        in_specs=[SM] + [VM] * 7,
        out_specs=(VM, VM),
        scratch_shapes=[scratch((3 * width, rows), BF16)],
        compiler_params=params(16),
        cost_estimate=pl.CostEstimate(
            flops=6 * rows * width * width, bytes_accessed=8 * 10**6, transcendentals=0
        ),
    )(info, *parts, w, d_h1, masked)


def after(value, *others):
    return lax.optimization_barrier((value,) + others)[0]


def flip(value, axis, bits):
    count = lax.axis_size(axis)
    return lax.ppermute(value, axis, [(index, index ^ bits) for index in range(count)])


def gather_blocks(value):
    far = flip(value, "sp", 2)
    near = flip(value, "sp", 1)
    cross = flip(far, "sp", 1)
    return [value, near, far, cross]


def exchange_blocks(blocks):
    via = flip(blocks[3], "sp", 1)
    near = flip(blocks[1], "sp", 1)
    far = flip(blocks[2], "sp", 2)
    cross = flip(via, "sp", 2)
    return [blocks[0], near, far, cross]


def small_mesh():
    return lax.axis_size("dp") == 8


NO_COST = pl.CostEstimate(flops=0, bytes_accessed=0, transcendentals=0)


def tidy_sums(value):
    first = value.shape[1] - 8
    sums = value[:, first : first + 4] + value[:, first + 4 :]
    high = sums.astype(BF16).astype(F32)
    return jnp.concatenate([value[:, :first], high, sums - high], axis=1)


def halve_kernel(with_sums, keep, came, kept, sent):
    half = keep.shape[0] // 2
    value = keep[...].astype(F32) + came[...].astype(F32)
    if with_sums:
        value = tidy_sums(value)
    kept[...] = value[:half]
    sent[...] = value[half:].astype(BF16)


def halve(keep, came, with_sums=False):
    dims = (keep.shape[0] // 2,) + keep.shape[1:]
    return pl.pallas_call(
        functools.partial(halve_kernel, with_sums),
        name="halve",
        out_shape=(shape(dims, F32), shape(dims, BF16)),
        in_specs=[VM] * 2,
        out_specs=(VM, VM),
        compiler_params=params(12),
        cost_estimate=NO_COST,
    )(keep, came)


def send_first(send, order):
    return flip(send, "dp", order[0]) if small_mesh() else send


def send_second(keep, came, order, with_sums=False):
    if not small_mesh():
        return keep, came
    kept, sent = halve(keep, came, with_sums)
    return kept, flip(sent, "dp", order[1])


def send_third(keep, came, order, with_sums=False):
    if not small_mesh():
        return keep, came
    kept, sent = halve(keep, came, with_sums)
    return kept, flip(sent, "dp", order[2])


def natural_blocks(keep, send, order):
    both = jnp.concatenate([keep, send], axis=0).astype(F32)
    places = []
    for index in range(8):
        bits = [1 if index & mask else 0 for mask in order]
        places.append(both[bits[0] * 4 + bits[1] * 2 + bits[2]])
    return places


def scatter_sum(blocks):
    grad = jnp.concatenate(blocks, axis=0)
    return lax.psum_scatter(grad, "dp", scatter_dimension=0, tiled=True).astype(BF16)


def finish_ffn_kernel(keep_b, came_b, keep_d, came_d, out):
    columns = keep_b.shape[2]
    out[:, :columns] = (keep_b[0] + came_b[0].astype(F32)).astype(BF16)
    out[:, columns:] = (keep_d[0] + came_d[0].astype(F32)).astype(BF16)


def finish_ffn(keep_b, came_b, keep_d, came_d):
    if not small_mesh():
        wide = scatter_sum(natural_blocks(keep_b, came_b, Z_FIRST))
        down = scatter_sum(natural_blocks(keep_d, came_d, X_FIRST))
        return jnp.concatenate([wide, down], axis=1)
    _, rows, columns = keep_b.shape
    return pl.pallas_call(
        finish_ffn_kernel,
        name="finish_ffn",
        out_shape=shape((rows, columns + keep_d.shape[2]), BF16),
        in_specs=[VM] * 4,
        out_specs=VM,
        compiler_params=params(8),
        cost_estimate=NO_COST,
    )(keep_b, came_b, keep_d, came_d)


def finish_heads_kernel(keep, came, out, sums):
    total = keep[0] + came[0].astype(F32)
    rows = out.shape[0]
    out[...] = total[:rows].astype(BF16)
    sums[...] = total[rows : rows + 4] + total[rows + 4 :]


def finish_heads(keep, came):
    _, rows, columns = keep.shape
    rows = rows - 8
    if not small_mesh():
        blocks = natural_blocks(keep, came, X_FIRST)
        sums = blocks[0][rows : rows + 4] + blocks[0][rows + 4 :]
        return scatter_sum([block[:rows] for block in blocks]), lax.psum(sums, "dp")
    return pl.pallas_call(
        finish_heads_kernel,
        name="finish_heads",
        out_shape=(shape((rows, columns), BF16), shape((4, columns), F32)),
        in_specs=[VM] * 2,
        out_specs=(VM, VM),
        compiler_params=params(8),
        cost_estimate=NO_COST,
    )(keep, came)


def local(
    tokens,
    segment_ids,
    masked_rows,
    replacement,
    cotangent,
    w_qkv,
    w_out_attn,
    w_in_ff,
    w_out_ff,
    gain_one,
    shift_one,
    gain_two,
    shift_two,
):
    rows_dev, width = tokens.shape
    rank = lax.axis_index("sp")
    heads = HEADS // RANKS
    dim = width // HEADS
    part = heads * dim
    slopes = alibi_slopes(HEADS)

    select = jnp.arange(rows_dev, dtype=jnp.int32)[:, None] == masked_rows[None, :]
    hit = jnp.any(select, axis=1, keepdims=True)
    placed = dot(select.astype(BF16), replacement)
    start = jnp.where(hit, placed.astype(BF16), tokens)
    start_far = flip(start, "sp", 2)
    start_near = flip(start, "sp", 1)
    place = lax.axis_index("dp")
    place = place if small_mesh() else place * 0
    spot = jnp.stack([rank, place]).astype(jnp.int32)

    w_rank = jnp.concatenate(
        [
            lax.dynamic_slice_in_dim(w_qkv, third * width + rank * part, part, 1)
            for third in range(3)
        ],
        axis=1,
    )
    start_cross = flip(after(start_far, w_rank, spot), "sp", 1)
    start_blocks = [start, start_near, start_far, start_cross]
    qkv, attn, lse = attention_forward(
        spot, segment_ids, slopes, start_blocks, w_rank, heads, dim
    )
    attn_far = flip(attn, "sp", 2)
    attn_near = flip(attn, "sp", 1)
    part_units = w_out_ff.shape[0] // lax.axis_size("dp") // RANKS
    packed_in, packed_down = pack_weights(after(spot, lse), w_in_ff, w_out_ff, part_units)
    attn_cross = flip(after(attn_far, packed_in), "sp", 1)
    attn_parts = [attn, attn_near, attn_far, attn_cross]
    low, joined, unit, inverse = norm_one(
        spot, attn_parts, start, w_out_attn, gain_one, shift_one
    )
    layer_out, d_h2, d_ff, slope, act, sums2 = ffn_forward(
        low, unit, gain_one, shift_one, gain_two, shift_two,
        masked_rows, cotangent, w_in_ff, w_out_ff, 768,
    )
    d_ff_far = flip(d_ff, "sp", 2)
    d_ff_near = flip(d_ff, "sp", 1)
    d_h1, sent = ffn_backward(
        d_ff, d_h2, unit, inverse, gain_one, sums2, act, slope, w_in_ff, w_out_ff, 768
    )
    lows, others_joined = norm_others(
        after(spot, sent), attn_parts, start_blocks[1:], w_out_attn, gain_one, shift_one
    )
    d_ff_far = after(d_ff_far, lows[0])
    d_ff_cross = flip(d_ff_far, "sp", 1)
    d_ff_blocks = [d_ff, d_ff_near, d_ff_far, d_ff_cross]
    far = flip(sent, "sp", 2)
    near = flip(sent, "sp", 1)

    keep_b, send_b, keep_d, send_d = ffn_grad(
        spot, [low, *lows], d_ff_blocks, packed_in, packed_down, 256
    )
    came_b = send_first(send_b, Z_FIRST)
    came_d = send_first(send_d, X_FIRST)
    cross = flip(after(far, keep_b), "sp", 1)
    d_proj_blocks = [sent, near, far, cross]

    d_qkv = attention_backward(
        spot, segment_ids, slopes, d_proj_blocks, w_out_attn, qkv, lse, heads, dim
    )
    parts = exchange_blocks(d_qkv)
    keep_d, came_d = send_second(keep_d, after(came_d, d_qkv[0]), X_FIRST)
    keep_q, send_q = qkv_grad(
        after(spot, keep_d), start_blocks, d_qkv, [joined, *others_joined], d_proj_blocks
    )
    came_q = send_first(send_q, X_FIRST)
    keep_b, came_b = send_second(keep_b, after(came_b, keep_q), Z_FIRST)
    keep_d, came_d = send_third(keep_d, after(came_d, keep_b), X_FIRST)
    keep_q, came_q = send_second(keep_q, after(came_q, keep_d), X_FIRST, True)
    keep_b, came_b = send_third(keep_b, after(came_b, keep_q), Z_FIRST)
    keep_q, came_q = send_third(keep_q, after(came_q, keep_b, parts), X_FIRST, True)
    wide = finish_ffn(keep_b, after(came_b, keep_q), keep_d, came_d)
    far = flip(wide, "sp", 2)
    near = flip(wide, "sp", 1)
    heads_share, norm_sums = finish_heads(keep_q, after(came_q, wide))
    head_blocks = gather_blocks(heads_share)
    ffn_blocks = [wide, near, far, flip(after(far, heads_share), "sp", 1)]
    grad_tokens, grad_replacement = token_grad(
        after(spot, heads_share), parts, w_qkv, d_h1, masked_rows
    )
    grad_in, grad_down = join_ffn(spot, ffn_blocks, part_units)
    grad_qkv, grad_out = join_heads(spot, head_blocks)

    return (
        layer_out,
        grad_tokens,
        grad_replacement,
        grad_qkv,
        grad_out,
        grad_in,
        grad_down,
        norm_sums[0],
        norm_sums[1],
        norm_sums[2],
        norm_sums[3],
    )


def solution(mesh):
    tokens = P(("dp", "sp"), None)
    rows = P("dp", None)
    return jax.shard_map(
        local,
        mesh=mesh,
        in_specs=(tokens, rows, P(("dp", "sp")), tokens, tokens) + (P(),) * 8,
        out_specs=(tokens,) * 3 + (rows,) * 4 + (P(),) * 4,
        check_vma=False,
    )
```

```python
import functools
import math

import jax
import jax.numpy as jnp
from jax import lax
from jax.experimental import pallas as pl
from jax.experimental.pallas import tpu as pltpu
from jax.sharding import PartitionSpec as P

HEADS = 12
RANKS = 4
EPSILON = 1e-05
FAR = 1e30
F32 = jnp.float32
BF16 = jnp.bfloat16
VM = pl.BlockSpec(memory_space=pltpu.VMEM)
SM = pl.BlockSpec(memory_space=pltpu.SMEM)


def shape(dims, kind):
    return jax.ShapeDtypeStruct(dims, kind)


def scratch(dims, kind):
    return pltpu.VMEM(dims, kind)


def params(mebibytes):
    return pltpu.CompilerParams(vmem_limit_bytes=mebibytes << 20)


def alibi_slopes(head_count):
    nearest = 2 ** int(math.floor(math.log2(head_count)))
    base_list = [2.0 ** (-8.0 * (index + 1) / nearest) for index in range(nearest)]
    extra_list = [
        2.0 ** (-8.0 * (2 * index + 1) / (2 * nearest)) for index in range(head_count - nearest)
    ]
    return jnp.array(base_list + extra_list, dtype=F32)


def dot(a, b):
    return jnp.dot(a, b, preferred_element_type=F32)


def dot_nt(a, b):
    return lax.dot_general(a, b, (((1,), (1,)), ((), ())), preferred_element_type=F32)


def dot_tn(a, b):
    return lax.dot_general(a, b, (((0,), (0,)), ((), ())), preferred_element_type=F32)


def exact_dot(a, b):
    return jnp.dot(a, b, precision=lax.Precision.HIGHEST, preferred_element_type=F32)


def standardize(value):
    center = value - jnp.mean(value, axis=-1, keepdims=True)
    spread = jnp.mean(center * center, axis=-1, keepdims=True)
    inverse = lax.rsqrt(spread + EPSILON)
    return center * inverse, inverse


def standardize_back(grad, unit, inverse):
    mean = jnp.mean(grad, axis=-1, keepdims=True)
    return inverse * (grad - mean - unit * jnp.mean(grad * unit, axis=-1, keepdims=True))


def gelu_pair(x):
    cdf = 0.5 * (1.0 + lax.erf(x * math.sqrt(0.5)))
    pdf = jnp.exp(-0.5 * x * x) * (1.0 / math.sqrt(2.0 * math.pi))
    return x * cdf, cdf + x * pdf


def pair_active(seg, rank, first, second, rows):
    one, two = rank ^ first, rank ^ second
    low, high = jnp.minimum(one, two), jnp.maximum(one, two)
    return jnp.logical_or(one == two, seg[0, low * rows + rows - 1] == seg[0, high * rows])


def key_sequences(seg_rows, seg_keys, rank, rows):
    for at in range(RANKS):
        first = pl.multiple_of((rank ^ at) * rows, rows)
        line = jnp.broadcast_to(seg_rows[:, pl.ds(first, rows)], (128, rows))
        seg_keys[at * rows : (at + 1) * rows, :] = jnp.transpose(line)


def pair_distance(seg_rows, seg_keys, rank, keys_at, query_at, rows):
    key_pos, query_pos = (rank ^ keys_at) * rows, (rank ^ query_at) * rows
    down = lax.broadcasted_iota(jnp.int32, (rows, rows), 0)
    across = lax.broadcasted_iota(jnp.int32, (rows, rows), 1)
    gap = jnp.abs(down - across + (key_pos - query_pos)).astype(F32)
    seg_q = seg_rows[:, pl.ds(pl.multiple_of(query_pos, rows), rows)]
    seg_k = seg_keys[pl.ds(pl.multiple_of(keys_at * rows, rows), rows), 0:1]
    return jnp.where(seg_k == seg_q, gap, FAR)


def attention_forward_kernel(
    rows, heads, dim, info, seg, slopes, x0, x1, x2, x3, w, seg_rows,
    qkv_out, out_t, lse, qs, ks, vt, dist, seg_keys, score, peak,
):
    rank = info[0]
    width = heads * dim
    key_sequences(seg_rows, seg_keys, rank, rows)
    for at, x in enumerate((x0, x1, x2, x3)):
        qkv = dot(x[...], w[...]).astype(BF16)
        here = pl.ds(at * rows, rows)
        qkv_out[here, :] = qkv
        for h in range(heads):
            qs[h, here, :] = (qkv[:, h * dim : (h + 1) * dim] * dim**-0.5).astype(BF16)
            ks[h, here, :] = qkv[:, width + h * dim : width + (h + 1) * dim]
        vt[:, here] = jnp.transpose(qkv[:, 2 * width :])

    for a in range(RANKS):
        mine = pl.ds(a * rows, rows)
        peak[...] = jnp.full_like(peak, -jnp.inf)

        def first_pass(b, carry):
            @pl.when(pair_active(seg, rank, a, b, rows))
            def _():
                theirs = pl.ds(pl.multiple_of(b * rows, rows), rows)
                gap = pair_distance(seg_rows, seg_keys, rank, b, a, rows)
                for h in range(heads):
                    slope = slopes[rank * heads + h]
                    s = dot_nt(ks[h, theirs, :], qs[h, mine, :]) - slope * gap
                    score[h, theirs, :] = s
                    peak[h : h + 1, :] = jnp.maximum(
                        peak[h : h + 1, :], jnp.max(s, axis=0, keepdims=True)
                    )

            return carry

        lax.fori_loop(0, RANKS, first_pass, 0)

        def second_pass(b, carry):
            def add(carry):
                theirs = pl.ds(pl.multiple_of(b * rows, rows), rows)
                result = []
                for h in range(heads):
                    acc, total = carry[h]
                    p = jnp.exp(score[h, theirs, :] - peak[h : h + 1, :])
                    total = total + jnp.sum(p, axis=0, keepdims=True)
                    span = slice(h * dim, (h + 1) * dim)
                    result.append((acc + dot(vt[span, theirs], p.astype(BF16)), total))
                return tuple(result)

            return lax.cond(pair_active(seg, rank, a, b, rows), add, lambda carry: carry, carry)

        empty = (jnp.zeros((dim, rows), F32), jnp.zeros((1, rows), F32))
        sums = lax.fori_loop(0, RANKS, second_pass, (empty,) * heads)
        for h in range(heads):
            acc, total = sums[h]
            span = slice(h * dim, (h + 1) * dim)
            out_t[span, mine] = (acc / total).astype(BF16)
            lse[h : h + 1, mine] = peak[h : h + 1, :] + jnp.log(total)


def attention_forward(info, seg, slopes, blocks, w, heads, dim):
    rows = blocks[0].shape[0]
    tok, lw = rows * RANKS, heads * dim
    return pl.pallas_call(
        functools.partial(attention_forward_kernel, rows, heads, dim),
        name="attention_forward",
        out_shape=(
            shape((tok, 3 * lw), BF16),
            shape((lw, tok), BF16),
            shape((heads, tok), F32),
        ),
        in_specs=[SM] * 3 + [VM] * 6,
        out_specs=(VM,) * 3,
        scratch_shapes=[
            scratch((heads, tok, dim), BF16),
            scratch((heads, tok, dim), BF16),
            scratch((lw, tok), BF16),
            scratch((rows, rows), F32),
            scratch((tok, 128), jnp.int32),
            scratch((heads, tok, rows), F32),
            scratch((heads, rows), F32),
        ],
        compiler_params=params(14),
        cost_estimate=pl.CostEstimate(
            flops=4 * 10**9, bytes_accessed=6 * 10**6, transcendentals=3 * 10**6
        ),
    )(info, seg, slopes, *blocks, w, seg)


def attention_backward_kernel(
    rows, heads, dim, info, seg, slopes, g0, g1, g2, g3, w, qkv, lse, seg_rows,
    d0, d1, d2, d3, qs, ks, kt, vs, do, seg_keys, prob, dprob, dk, dv, dqt, delta,
):
    rank = info[0]
    width = heads * dim
    scale = dim**-0.5
    key_sequences(seg_rows, seg_keys, rank, rows)
    w_rank = w[pl.ds(pl.multiple_of(rank * width, width), width), :]
    for at, g in enumerate((g0, g1, g2, g3)):
        here = pl.ds(at * rows, rows)
        grad = dot_nt(g[0:rows, :], w_rank).astype(BF16)
        value = qkv[here, :]
        kt[:, here] = jnp.transpose(value[:, width : 2 * width])
        for h in range(heads):
            do[h, here, :] = grad[:, h * dim : (h + 1) * dim]
            qs[h, here, :] = (value[:, h * dim : (h + 1) * dim] * scale).astype(BF16)
            ks[h, here, :] = value[:, width + h * dim : width + (h + 1) * dim]
            vs[h, here, :] = value[:, 2 * width + h * dim : 2 * width + (h + 1) * dim]
    dk[...] = jnp.zeros_like(dk)
    dv[...] = jnp.zeros_like(dv)

    for a in range(RANKS):
        mine = pl.ds(a * rows, rows)
        delta[...] = jnp.zeros_like(delta)
        dqt[...] = jnp.zeros_like(dqt)

        def first_pass(b, carry):
            @pl.when(pair_active(seg, rank, a, b, rows))
            def _():
                theirs = pl.ds(pl.multiple_of(b * rows, rows), rows)
                gap = pair_distance(seg_rows, seg_keys, rank, b, a, rows)
                for h in range(heads):
                    slope = slopes[rank * heads + h]
                    s = dot_nt(ks[h, theirs, :], qs[h, mine, :]) - slope * gap
                    p = jnp.exp(s - lse[h : h + 1, mine])
                    dp = dot_nt(vs[h, theirs, :], do[h, mine, :])
                    delta[h : h + 1, :] += jnp.sum(p * dp, axis=0, keepdims=True)
                    prob[h, theirs, :] = p
                    dprob[h, theirs, :] = dp

            return carry

        lax.fori_loop(0, RANKS, first_pass, 0)

        def second_pass(b, carry):
            @pl.when(pair_active(seg, rank, a, b, rows))
            def _():
                theirs = pl.ds(pl.multiple_of(b * rows, rows), rows)
                for h in range(heads):
                    p = prob[h, theirs, :]
                    ds = (p * (dprob[h, theirs, :] - delta[h : h + 1, :])).astype(BF16)
                    dv[h, theirs, :] += dot(p.astype(BF16), do[h, mine, :])
                    dk[h, theirs, :] += dot(ds, qs[h, mine, :])
                    span = slice(h * dim, (h + 1) * dim)
                    dqt[span, :] += dot(kt[span, theirs], ds)

            return carry

        lax.fori_loop(0, RANKS, second_pass, 0)
        (d0, d1, d2, d3)[a][0:width, :] = (dqt[...] * scale).astype(BF16)

    for at, d_qkv in enumerate((d0, d1, d2, d3)):
        here = pl.ds(at * rows, rows)
        for h in range(heads):
            first = width + h * dim
            d_qkv[first : first + dim, :] = jnp.transpose(dk[h, here, :]).astype(BF16)
            first = 2 * width + h * dim
            d_qkv[first : first + dim, :] = jnp.transpose(dv[h, here, :]).astype(BF16)


def attention_backward(info, seg, slopes, blocks, w, qkv, lse, heads, dim):
    tok, lw = qkv.shape[0], heads * dim
    rows = tok // RANKS
    return pl.pallas_call(
        functools.partial(attention_backward_kernel, rows, heads, dim),
        name="attention_backward",
        out_shape=(shape((3 * lw, rows), BF16),) * RANKS,
        in_specs=[SM] * 3 + [VM] * 8,
        out_specs=(VM,) * RANKS,
        scratch_shapes=[
            scratch((heads, tok, dim), BF16),
            scratch((heads, tok, dim), BF16),
            scratch((lw, tok), BF16),
            scratch((heads, tok, dim), BF16),
            scratch((heads, tok, dim), BF16),
            scratch((tok, 128), jnp.int32),
            scratch((heads, tok, rows), F32),
            scratch((heads, tok, rows), F32),
            scratch((heads, tok, dim), F32),
            scratch((heads, tok, dim), F32),
            scratch((lw, rows), F32),
            scratch((heads, rows), F32),
        ],
        compiler_params=params(20),
        cost_estimate=pl.CostEstimate(
            flops=8 * 10**9, bytes_accessed=6 * 10**6, transcendentals=3 * 10**6
        ),
    )(info, seg, slopes, *blocks, w, qkv, lse, seg)


def line(vector):
    return vector[...].reshape(1, -1)


def join_tokens(rank, arrays, tokens_of, joined):
    part = arrays[0].shape[0]
    rows = arrays[0].shape[1] // RANKS
    for step, array in enumerate(arrays):
        first = pl.multiple_of((rank ^ step) * part, part)
        block = step ^ tokens_of
        joined[pl.ds(first, part), :] = array[:, block * rows : (block + 1) * rows]


def norm_one_kernel(
    info, own, near, far, cross, start, w, gain, shift, low, joined, unit, inverse
):
    join_tokens(info[0], (own, near, far, cross), 0, joined)
    x, inv = standardize(start[...].astype(F32) + dot_tn(joined[...], w[...]))
    unit[...] = x
    inverse[...] = inv
    low[...] = (x * line(gain) + line(shift)).astype(BF16)


def norm_one(info, parts, start, w, gain, shift):
    rows, width = start.shape
    return pl.pallas_call(
        norm_one_kernel,
        name="norm_one",
        out_shape=(
            shape((rows, width), BF16),
            shape((width, rows), BF16),
            shape((rows, width), F32),
            shape((rows, 1), F32),
        ),
        in_specs=[SM] + [VM] * 8,
        out_specs=(VM,) * 4,
        compiler_params=params(12),
        cost_estimate=pl.CostEstimate(
            flops=2 * rows * width * width, bytes_accessed=4 * 10**6, transcendentals=0
        ),
    )(info, *parts, start, w, gain, shift)


def norm_others_kernel(
    info, own, near, far, cross, s1, s2, s3, w, gain, shift, l1, l2, l3, j1, j2, j3
):
    for tokens_of, (start, low, joined) in enumerate(((s1, l1, j1), (s2, l2, j2), (s3, l3, j3))):
        join_tokens(info[0], (own, near, far, cross), tokens_of + 1, joined)
        x, _ = standardize(start[...].astype(F32) + dot_tn(joined[...], w[...]))
        low[...] = (x * line(gain) + line(shift)).astype(BF16)


def norm_others(info, parts, starts, w, gain, shift):
    rows, width = starts[0].shape
    results = pl.pallas_call(
        norm_others_kernel,
        name="norm_others",
        out_shape=(shape((rows, width), BF16),) * 3 + (shape((width, rows), BF16),) * 3,
        in_specs=[SM] + [VM] * 10,
        out_specs=(VM,) * 6,
        compiler_params=params(12),
        cost_estimate=pl.CostEstimate(
            flops=6 * rows * width * width, bytes_accessed=4 * 10**6, transcendentals=0
        ),
    )(info, *parts, *starts, w, gain, shift)
    return results[:3], results[3:]


def packing(rows, columns, part, rank):
    units = lax.broadcasted_iota(jnp.int32, (rows, columns), 0)
    packed = lax.broadcasted_iota(jnp.int32, (1, columns), 1)
    places = packed + rank * part
    for index in range(1, columns // part):
        places = places + jnp.where(packed >= index * part, (RANKS - 1) * part, 0)
    return (units == places).astype(BF16)


def pack_kernel(part, info, w_in, w_down, packed_in, packed_down):
    rank = info[0]
    width, hid = w_in.shape[0], w_down.shape[0]
    run = hid // 2
    select = packing(run, run // RANKS, part, rank)
    for index in range(4):
        piece = dot(w_in[:, index * run : (index + 1) * run], select)
        packed_in[:, index * run // RANKS : (index + 1) * run // RANKS] = piece.astype(BF16)
    if part % 16:
        for index in range(2):
            piece = dot_tn(select, w_down[index * run : (index + 1) * run, :])
            packed_down[index * run // RANKS : (index + 1) * run // RANKS, :] = piece.astype(BF16)
    else:
        for index in range(hid // RANKS // part):
            rows = pl.ds(pl.multiple_of((index * RANKS + rank) * part, part), part)
            packed_down[index * part : (index + 1) * part, :] = w_down[rows, :]


def pack_weights(info, w_in, w_out, part):
    width, hid = w_in.shape[0], w_out.shape[0]
    return pl.pallas_call(
        functools.partial(pack_kernel, part),
        name="pack_weights",
        out_shape=(shape((width, 2 * hid // RANKS), BF16), shape((hid // RANKS, width), BF16)),
        in_specs=[SM, VM, VM],
        out_specs=(VM, VM),
        compiler_params=params(14),
        cost_estimate=pl.CostEstimate(
            flops=4 * 10**9, bytes_accessed=17 * 10**6, transcendentals=0
        ),
    )(info, w_in, w_out)


def ffn_forward_kernel(
    low, unit, gain1, shift1, gain2, shift2, masked, cot, w_in, w_down,
    layer_out, d_h2, d_ff, slope, act, sums, acc, gates, ups,
):
    hid = w_down.shape[0]
    size = gates.shape[2]
    count = hid // size

    def project(block, slot):
        first = pl.multiple_of(block * size, size)
        gates[slot] = dot(low[...], w_in[:, pl.ds(first, size)])
        ups[slot] = dot(low[...], w_in[:, pl.ds(pl.multiple_of(hid + first, size), size)])

    def finish(block, slot):
        here = pl.ds(pl.multiple_of(block * size, size), size)
        up = ups[slot]
        value, grad = gelu_pair(gates[slot])
        act[:, here] = value.astype(BF16)
        slope[:, here] = (up * grad).astype(BF16)
        acc[...] += dot((value * up).astype(BF16), w_down[here, :])

    acc[...] = unit[...] * line(gain1) + line(shift1)
    project(0, 0)

    def pair(index, carry):
        block = index * 2
        project(block + 1, 1)
        finish(block, 0)
        project(block + 2, 0)
        finish(block + 1, 1)
        return carry

    lax.fori_loop(0, count // 2 - 1, pair, 0)
    project(count - 1, 1)
    finish(count - 2, 0)
    finish(count - 1, 1)
    x, inv = standardize(acc[...])
    layer_out[...] = (x * line(gain2) + line(shift2)).astype(BF16)
    places = lax.broadcasted_iota(jnp.int32, (low.shape[0], masked.shape[0]), 0)
    dy = exact_dot((places == line(masked)).astype(F32), cot[...])
    sums[0:1, :] = jnp.sum(dy * x, axis=0, keepdims=True)
    sums[1:2, :] = jnp.sum(dy, axis=0, keepdims=True)
    grad_in = standardize_back(dy * line(gain2), x, inv)
    d_h2[...] = grad_in
    d_ff[...] = grad_in.astype(BF16)


def ffn_forward(low, unit, gain1, shift1, gain2, shift2, masked, cot, w_in, w_out, size):
    rows, width = low.shape
    hid = w_out.shape[0]
    return pl.pallas_call(
        ffn_forward_kernel,
        name="ffn_forward",
        out_shape=(
            shape((rows, width), BF16),
            shape((rows, width), F32),
            shape((rows, width), BF16),
            shape((rows, hid), BF16),
            shape((rows, hid), BF16),
            shape((2, width), F32),
        ),
        in_specs=[VM] * 10,
        out_specs=(VM,) * 6,
        scratch_shapes=[
            scratch((rows, width), F32),
            scratch((2, rows, size), F32),
            scratch((2, rows, size), F32),
        ],
        compiler_params=params(14),
        cost_estimate=pl.CostEstimate(
            flops=6 * rows * width * hid, bytes_accessed=18 * 10**6, transcendentals=2 * rows * hid
        ),
    )(low, unit, gain1, shift1, gain2, shift2, masked, cot, w_in, w_out)


def ffn_backward_kernel(
    d_ff, d_h2, unit, inverse, gain1, sums2, act, slope, w_in, w_down, d_h1, sent, acc, hidden
):
    hid = w_down.shape[0]
    size = hidden.shape[2]
    count = hid // size

    def project(block, slot):
        here = pl.ds(pl.multiple_of(block * size, size), size)
        hidden[slot] = dot_nt(d_ff[...], w_down[here, :])

    def finish(block, slot):
        first = pl.multiple_of(block * size, size)
        here, there = pl.ds(first, size), pl.ds(pl.multiple_of(hid + first, size), size)
        d_hidden = hidden[slot]
        d_gate = (d_hidden * slope[:, here].astype(F32)).astype(BF16)
        d_up = (d_hidden * act[:, here].astype(F32)).astype(BF16)
        acc[...] += dot_nt(d_gate, w_in[:, here]) + dot_nt(d_up, w_in[:, there])

    acc[...] = d_h2[...]
    project(0, 0)

    def pair(index, carry):
        block = index * 2
        project(block + 1, 1)
        finish(block, 0)
        project(block + 2, 0)
        finish(block + 1, 1)
        return carry

    lax.fori_loop(0, count // 2 - 1, pair, 0)
    project(count - 1, 1)
    finish(count - 2, 0)
    finish(count - 1, 1)
    total = acc[...]
    rows = total.shape[0]
    x = unit[...]
    gain_sum = jnp.sum(total * x, axis=0, keepdims=True)
    shift_sum = jnp.sum(total, axis=0, keepdims=True)
    sums = jnp.concatenate([gain_sum, shift_sum, sums2[...]], axis=0)
    high = sums.astype(BF16).astype(F32)
    tail = jnp.concatenate([high, sums - high, jnp.zeros((8, sums.shape[1]), F32)], axis=0)
    grad = standardize_back(total * line(gain1), x, inverse[...])
    d_h1[...] = grad
    sent[0:rows, :] = grad.astype(BF16)
    sent[rows : rows + 16, :] = tail.astype(BF16)


def ffn_backward(d_ff, d_h2, unit, inverse, gain1, sums2, act, slope, w_in, w_out, size):
    rows, width = d_ff.shape
    hid = w_out.shape[0]
    return pl.pallas_call(
        ffn_backward_kernel,
        name="ffn_backward",
        out_shape=(shape((rows, width), F32), shape((rows + 16, width), BF16)),
        in_specs=[VM] * 10,
        out_specs=(VM,) * 2,
        scratch_shapes=[scratch((rows, width), F32), scratch((2, rows, size), F32)],
        compiler_params=params(14),
        cost_estimate=pl.CostEstimate(
            flops=6 * rows * width * hid, bytes_accessed=20 * 10**6, transcendentals=0
        ),
    )(d_ff, d_h2, unit, inverse, gain1, sums2, act, slope, w_in, w_out)


X_FIRST = (1, 2, 4)
Z_FIRST = (2, 1, 4)


def bit_of(value, mask):
    return (value // mask) % 2


def store_blocks(blocks, keep, send, place, order, columns):
    one, two, three = order
    odd = bit_of(place, one) == 1
    for index in range(8):
        if index & one:
            continue
        spot = bit_of(place ^ index, two) * 2 + bit_of(place ^ index, three)
        low, high = blocks(index), blocks(index | one)
        keep[spot, :, columns] = jnp.where(odd, high, low).astype(BF16)
        send[spot, :, columns] = jnp.where(odd, low, high).astype(BF16)


def row_blocks(grad):
    each = grad.shape[0] // 8
    return lambda index: grad[index * each : (index + 1) * each]


def ffn_grad_kernel(
    size, info, n0, n1, n2, n3, f0, f1, f2, f3, w_in, w_down,
    keep, send, keep_down, send_down,
    tok_t, gates, ups, d_hiddens, hidden_t, d_gate, d_up, d_ff, down,
):
    toks, grads = (n0, n1, n2, n3), (f0, f1, f2, f3)
    rows = n0.shape[0]
    units = w_down.shape[0]
    for at in range(RANKS):
        here = slice(at * rows, (at + 1) * rows)
        d_ff[here, :] = grads[at][...]
        tok_t[:, here] = jnp.transpose(toks[at][...])

    def unit_block(step, carry):
        here = pl.ds(pl.multiple_of(step * size, size), size)
        there = pl.ds(pl.multiple_of(units + step * size, size), size)
        w_gate, w_up, w_rows = w_in[:, here], w_in[:, there], w_down[here, :]

        def project(at):
            slot = at % 2
            gates[slot] = dot(toks[at][...], w_gate)
            ups[slot] = dot(toks[at][...], w_up)
            d_hiddens[slot] = dot_nt(grads[at][...], w_rows)

        def finish(at):
            slot = at % 2
            here = slice(at * rows, (at + 1) * rows)
            value, grad = gelu_pair(gates[slot])
            up, d_hidden = ups[slot], d_hiddens[slot]
            hidden_t[:, here] = jnp.transpose((value * up).astype(BF16))
            d_gate[here, :] = (d_hidden * up * grad).astype(BF16)
            d_up[here, :] = (d_hidden * value).astype(BF16)

        project(0)
        for at in range(RANKS):
            if at + 1 < RANKS:
                project(at + 1)
            finish(at)
        for columns, grad in ((here, d_gate), (there, d_up)):
            total = dot(tok_t[...], grad[...])
            store_blocks(row_blocks(total), keep, send, info[1], Z_FIRST, columns)
        down[here, :] = dot(hidden_t[...], d_ff[...])
        return carry

    lax.fori_loop(0, units // size, unit_block, 0)
    store_blocks(row_blocks(down), keep_down, send_down, info[1], X_FIRST, slice(None))


def ffn_grad(info, toks, grads, w_in, w_down, size):
    rows, width = toks[0].shape
    units = w_down.shape[0]
    tok = rows * RANKS
    dims = [(4, width // 8, 2 * units)] * 2 + [(4, units // 8, width)] * 2
    return pl.pallas_call(
        functools.partial(ffn_grad_kernel, size),
        name="ffn_grad",
        out_shape=[shape(each, BF16) for each in dims],
        in_specs=[SM] + [VM] * 10,
        out_specs=[VM] * 4,
        scratch_shapes=[
            scratch((width, tok), BF16),
            scratch((2, rows, size), F32),
            scratch((2, rows, size), F32),
            scratch((2, rows, size), F32),
            scratch((size, tok), BF16),
            scratch((tok, size), BF16),
            scratch((tok, size), BF16),
            scratch((tok, width), BF16),
            scratch((units, width), F32),
        ],
        compiler_params=params(18),
        cost_estimate=pl.CostEstimate(
            flops=12 * tok * width * units,
            bytes_accessed=8 * 10**6,
            transcendentals=2 * tok * units,
        ),
    )(info, *toks, *grads, w_in, w_down)


def qkv_grad_kernel(
    info, x0, x1, x2, x3, d0, d1, d2, d3, j0, j1, j2, j3, g0, g1, g2, g3, keep, send, columns, grad
):
    rows, width = x0.shape
    part = width // RANKS
    total = 0.0
    for x, d_qkv in zip((x0, x1, x2, x3), (d0, d1, d2, d3)):
        total = total + dot(d_qkv[...], x[...])
    grad[:, : 3 * part] = jnp.transpose(total)
    for value in range(RANKS):

        @pl.when(info[0] == value)
        def _():
            for at, g in enumerate((g0, g1, g2, g3)):
                columns[at] = g[0:rows, value * part : (value + 1) * part]

    total = 0.0
    sums = 0.0
    for at, (joined, g) in enumerate(zip((j0, j1, j2, j3), (g0, g1, g2, g3))):
        total = total + dot(joined[...], columns[at])
        pair = g[rows : rows + 16, :].astype(F32)
        sums = sums + pair[0:4] + pair[4:8]
    grad[:, 3 * part :] = total
    high = sums.astype(BF16).astype(F32)
    tail = jnp.concatenate([high, sums - high], axis=0)
    each = width // 8

    def blocks(index):
        return jnp.concatenate([grad[index * each : (index + 1) * each], tail], axis=0)

    store_blocks(blocks, keep, send, info[1], X_FIRST, slice(None))


def qkv_grad(info, blocks, d_qkv, joined, d_proj):
    rows, width = blocks[0].shape
    return pl.pallas_call(
        qkv_grad_kernel,
        name="qkv_grad",
        out_shape=(shape((4, width // 8 + 8, width), BF16),) * 2,
        in_specs=[SM] + [VM] * 16,
        out_specs=(VM, VM),
        scratch_shapes=[
            scratch((RANKS, rows, width // RANKS), BF16),
            scratch((width, width), F32),
        ],
        compiler_params=params(14),
        cost_estimate=pl.CostEstimate(
            flops=8 * rows * width * width, bytes_accessed=4 * 10**6, transcendentals=0
        ),
    )(info, *blocks, *d_qkv, *joined, *d_proj)


def join_ffn_kernel(part, info, b0, b1, b2, b3, wide, packed):
    rank = info[0]
    few = b0.shape[1] // 2
    for step, block in enumerate((b0, b1, b2, b3)):
        there = pl.multiple_of((rank ^ step) * few, few)
        packed[0, :, pl.ds(there, few)] = block[:, :few]
        packed[1, :, pl.ds(there, few)] = block[:, few:]
    for half in range(2):
        for run in range(few // part):
            pieces = []
            for value in range(RANKS):
                first = value * few + run * part
                pieces.append(packed[half, :, first : first + part])
            first = half * RANKS * few + run * RANKS * part
            piece = jnp.concatenate(pieces, axis=1).astype(F32)
            wide[:, first : first + RANKS * part] = piece


def join_ffn(info, blocks, part):
    rows, columns = blocks[0].shape
    if RANKS * part % 128:
        stacked = jnp.stack(blocks)[info[0] ^ jnp.arange(RANKS)].astype(F32)
        wide = stacked.reshape(RANKS, rows, -1, part).transpose(1, 2, 0, 3)
        return wide.reshape(rows, -1)
    return pl.pallas_call(
        functools.partial(join_ffn_kernel, part),
        name="join_ffn",
        out_shape=shape((rows, RANKS * columns), F32),
        in_specs=[SM] + [VM] * 4,
        out_specs=VM,
        scratch_shapes=[scratch((2, rows, RANKS * columns // 2), BF16)],
        compiler_params=params(14),
        cost_estimate=NO_COST,
    )(info, *blocks)


def join_rows_kernel(info, b0, b1, b2, b3, out):
    rows = b0.shape[0]
    for step, block in enumerate((b0, b1, b2, b3)):
        place = pl.multiple_of((info[0] ^ step) * rows, rows)
        out[pl.ds(place, rows), :] = block[...].astype(F32)


def join_rows(info, blocks):
    rows, columns = blocks[0].shape
    if rows % 8:
        stacked = jnp.stack(blocks)[info[0] ^ jnp.arange(RANKS)].astype(F32)
        return stacked.reshape(-1, columns)
    return pl.pallas_call(
        join_rows_kernel,
        name="join_rows",
        out_shape=shape((rows * RANKS, columns), F32),
        in_specs=[SM] + [VM] * 4,
        out_specs=VM,
        compiler_params=params(8),
        cost_estimate=NO_COST,
    )(info, *blocks)


def join_heads_kernel(info, b0, b1, b2, b3, out, rest):
    rank = info[0]
    width = rest.shape[1]
    part = width // RANKS
    for value in range(RANKS):

        @pl.when(rank == value)
        def _():
            for step, block in enumerate((b0, b1, b2, b3)):
                there = (value ^ step) * part
                for third in range(3):
                    piece = block[:, third * part : (third + 1) * part].astype(F32)
                    out[:, third * width + there : third * width + there + part] = piece
                rest[:, there : there + part] = block[:, 3 * part :].astype(F32)


def join_heads(info, blocks):
    rows, width = blocks[0].shape
    return pl.pallas_call(
        join_heads_kernel,
        name="join_heads",
        out_shape=(shape((rows, 3 * width), F32), shape((rows, width), F32)),
        in_specs=[SM] + [VM] * 4,
        out_specs=(VM, VM),
        compiler_params=params(8),
        cost_estimate=pl.CostEstimate(flops=10**6, bytes_accessed=2 * 10**6, transcendentals=0),
    )(info, *blocks)


def token_grad_kernel(
    info, own, near, far, cross, w, d_h1, masked, tokens, replacement, joined
):
    rows, width = d_h1.shape
    part = width // RANKS
    for step, block in enumerate((own, near, far, cross)):
        for third in range(3):
            first = pl.multiple_of(third * width + (info[0] ^ step) * part, part)
            joined[pl.ds(first, part), :] = block[third * part : (third + 1) * part, :]
    grad = d_h1[...] + jnp.transpose(dot(w[...], joined[...]))
    count = masked.shape[0]
    places = lax.broadcasted_iota(jnp.int32, (rows, count), 0)
    select = (places == line(masked)).astype(F32)
    hit = jnp.max(select, axis=1, keepdims=True)
    tokens[...] = jnp.where(hit > 0.5, 0.0, grad)
    replacement[...] = lax.dot_general(
        select, grad, (((0,), (0,)), ((), ())),
        precision=lax.Precision.HIGHEST, preferred_element_type=F32,
    )


def token_grad(info, parts, w, d_h1, masked):
    rows, width = d_h1.shape
    return pl.pallas_call(
        token_grad_kernel,
        name="token_grad",
        out_shape=(shape((rows, width), F32), shape((masked.shape[0], width), F32)),
        in_specs=[SM] + [VM] * 7,
        out_specs=(VM, VM),
        scratch_shapes=[scratch((3 * width, rows), BF16)],
        compiler_params=params(16),
        cost_estimate=pl.CostEstimate(
            flops=6 * rows * width * width, bytes_accessed=8 * 10**6, transcendentals=0
        ),
    )(info, *parts, w, d_h1, masked)


def after(value, *others):
    return lax.optimization_barrier((value,) + others)[0]


def flip(value, axis, bits):
    count = lax.axis_size(axis)
    return lax.ppermute(value, axis, [(index, index ^ bits) for index in range(count)])


def gather_blocks(value):
    far = flip(value, "sp", 2)
    near = flip(value, "sp", 1)
    cross = flip(far, "sp", 1)
    return [value, near, far, cross]


def exchange_blocks(blocks):
    via = flip(blocks[3], "sp", 1)
    near = flip(blocks[1], "sp", 1)
    far = flip(blocks[2], "sp", 2)
    cross = flip(via, "sp", 2)
    return [blocks[0], near, far, cross]


def small_mesh():
    return lax.axis_size("dp") == 8


NO_COST = pl.CostEstimate(flops=0, bytes_accessed=0, transcendentals=0)


def tidy_sums(value):
    first = value.shape[1] - 8
    sums = value[:, first : first + 4] + value[:, first + 4 :]
    high = sums.astype(BF16).astype(F32)
    return jnp.concatenate([value[:, :first], high, sums - high], axis=1)


def halve_kernel(with_sums, keep, came, kept, sent):
    half = keep.shape[0] // 2
    value = keep[...].astype(F32) + came[...].astype(F32)
    if with_sums:
        value = tidy_sums(value)
    kept[...] = value[:half]
    sent[...] = value[half:].astype(BF16)


def halve(keep, came, with_sums=False):
    dims = (keep.shape[0] // 2,) + keep.shape[1:]
    return pl.pallas_call(
        functools.partial(halve_kernel, with_sums),
        name="halve",
        out_shape=(shape(dims, F32), shape(dims, BF16)),
        in_specs=[VM] * 2,
        out_specs=(VM, VM),
        compiler_params=params(12),
        cost_estimate=NO_COST,
    )(keep, came)


def send_first(send, order):
    return flip(send, "dp", order[0]) if small_mesh() else send


def send_second(keep, came, order, with_sums=False):
    if not small_mesh():
        return keep, came
    kept, sent = halve(keep, came, with_sums)
    return kept, flip(sent, "dp", order[1])


def send_third(keep, came, order, with_sums=False):
    if not small_mesh():
        return keep, came
    kept, sent = halve(keep, came, with_sums)
    return kept, flip(sent, "dp", order[2])


def natural_blocks(keep, send, order):
    both = jnp.concatenate([keep, send], axis=0).astype(F32)
    places = []
    for index in range(8):
        bits = [1 if index & mask else 0 for mask in order]
        places.append(both[bits[0] * 4 + bits[1] * 2 + bits[2]])
    return places


def scatter_sum(blocks):
    grad = jnp.concatenate(blocks, axis=0)
    return lax.psum_scatter(grad, "dp", scatter_dimension=0, tiled=True).astype(BF16)


def finish_kernel(keep, came, out):
    out[...] = (keep[0] + came[0].astype(F32)).astype(BF16)


def finish_sum(keep, came, order):
    if not small_mesh():
        return scatter_sum(natural_blocks(keep, came, order))
    return pl.pallas_call(
        finish_kernel,
        name="finish_sum",
        out_shape=shape(keep.shape[1:], BF16),
        in_specs=[VM] * 2,
        out_specs=VM,
        compiler_params=params(8),
        cost_estimate=NO_COST,
    )(keep, came)


def finish_heads_kernel(keep, came, out, sums):
    total = keep[0] + came[0].astype(F32)
    rows = out.shape[0]
    out[...] = total[:rows].astype(BF16)
    sums[...] = total[rows : rows + 4] + total[rows + 4 :]


def finish_heads(keep, came):
    _, rows, columns = keep.shape
    rows = rows - 8
    if not small_mesh():
        blocks = natural_blocks(keep, came, X_FIRST)
        sums = blocks[0][rows : rows + 4] + blocks[0][rows + 4 :]
        return scatter_sum([block[:rows] for block in blocks]), lax.psum(sums, "dp")
    return pl.pallas_call(
        finish_heads_kernel,
        name="finish_heads",
        out_shape=(shape((rows, columns), BF16), shape((4, columns), F32)),
        in_specs=[VM] * 2,
        out_specs=(VM, VM),
        compiler_params=params(8),
        cost_estimate=NO_COST,
    )(keep, came)


def local(
    tokens,
    segment_ids,
    masked_rows,
    replacement,
    cotangent,
    w_qkv,
    w_out_attn,
    w_in_ff,
    w_out_ff,
    gain_one,
    shift_one,
    gain_two,
    shift_two,
):
    rows_dev, width = tokens.shape
    rank = lax.axis_index("sp")
    heads = HEADS // RANKS
    dim = width // HEADS
    part = heads * dim
    slopes = alibi_slopes(HEADS)

    select = jnp.arange(rows_dev, dtype=jnp.int32)[:, None] == masked_rows[None, :]
    hit = jnp.any(select, axis=1, keepdims=True)
    placed = dot(select.astype(BF16), replacement)
    start = jnp.where(hit, placed.astype(BF16), tokens)
    start_far = flip(start, "sp", 2)
    start_near = flip(start, "sp", 1)
    place = lax.axis_index("dp")
    place = place if small_mesh() else place * 0
    spot = jnp.stack([rank, place]).astype(jnp.int32)

    w_rank = jnp.concatenate(
        [
            lax.dynamic_slice_in_dim(w_qkv, third * width + rank * part, part, 1)
            for third in range(3)
        ],
        axis=1,
    )
    start_cross = flip(after(start_far, w_rank, spot), "sp", 1)
    start_blocks = [start, start_near, start_far, start_cross]
    qkv, attn, lse = attention_forward(
        spot, segment_ids, slopes, start_blocks, w_rank, heads, dim
    )
    attn_far = flip(attn, "sp", 2)
    attn_near = flip(attn, "sp", 1)
    part_units = w_out_ff.shape[0] // lax.axis_size("dp") // RANKS
    packed_in, packed_down = pack_weights(after(spot, lse), w_in_ff, w_out_ff, part_units)
    attn_cross = flip(after(attn_far, packed_in), "sp", 1)
    attn_parts = [attn, attn_near, attn_far, attn_cross]
    low, joined, unit, inverse = norm_one(
        spot, attn_parts, start, w_out_attn, gain_one, shift_one
    )
    layer_out, d_h2, d_ff, slope, act, sums2 = ffn_forward(
        low, unit, gain_one, shift_one, gain_two, shift_two,
        masked_rows, cotangent, w_in_ff, w_out_ff, 768,
    )
    d_ff_far = flip(d_ff, "sp", 2)
    d_ff_near = flip(d_ff, "sp", 1)
    d_h1, sent = ffn_backward(
        d_ff, d_h2, unit, inverse, gain_one, sums2, act, slope, w_in_ff, w_out_ff, 768
    )
    lows, others_joined = norm_others(
        after(spot, sent), attn_parts, start_blocks[1:], w_out_attn, gain_one, shift_one
    )
    d_ff_far = after(d_ff_far, lows[0])
    d_ff_cross = flip(d_ff_far, "sp", 1)
    d_ff_blocks = [d_ff, d_ff_near, d_ff_far, d_ff_cross]
    far = flip(sent, "sp", 2)
    near = flip(sent, "sp", 1)

    keep_b, send_b, keep_d, send_d = ffn_grad(
        spot, [low, *lows], d_ff_blocks, packed_in, packed_down, 256
    )
    came_b = send_first(send_b, Z_FIRST)
    came_d = send_first(send_d, X_FIRST)
    cross = flip(after(far, keep_b), "sp", 1)
    d_proj_blocks = [sent, near, far, cross]

    d_qkv = attention_backward(
        spot, segment_ids, slopes, d_proj_blocks, w_out_attn, qkv, lse, heads, dim
    )
    parts = exchange_blocks(d_qkv)
    keep_d, came_d = send_second(keep_d, after(came_d, d_qkv[0]), X_FIRST)
    keep_q, send_q = qkv_grad(
        after(spot, keep_d), start_blocks, d_qkv, [joined, *others_joined], d_proj_blocks
    )
    came_q = send_first(send_q, X_FIRST)
    keep_b, came_b = send_second(keep_b, after(came_b, keep_q), Z_FIRST)
    keep_d, came_d = send_third(keep_d, after(came_d, keep_b), X_FIRST)
    keep_q, came_q = send_second(keep_q, after(came_q, keep_d), X_FIRST, True)
    keep_b, came_b = send_third(keep_b, after(came_b, keep_q, came_d), Z_FIRST)
    keep_q, came_q = send_third(keep_q, after(came_q, keep_b, parts), X_FIRST, True)
    down = finish_sum(keep_d, after(came_d, keep_q), X_FIRST)
    down_far = flip(down, "sp", 2)
    down_near = flip(down, "sp", 1)
    wide = finish_sum(keep_b, after(came_b, came_q, down_far), Z_FIRST)
    down_blocks = [down, down_near, down_far, flip(after(down_far, wide), "sp", 1)]
    far = flip(wide, "sp", 2)
    near = flip(wide, "sp", 1)
    heads_share, norm_sums = finish_heads(keep_q, after(came_q, wide))
    head_blocks = gather_blocks(heads_share)
    ffn_blocks = [wide, near, far, flip(after(far, heads_share), "sp", 1)]
    grad_tokens, grad_replacement = token_grad(
        after(spot, heads_share), parts, w_qkv, d_h1, masked_rows
    )
    grad_down = join_rows(after(spot, heads_share), down_blocks)
    grad_in = join_ffn(spot, ffn_blocks, part_units)
    grad_qkv, grad_out = join_heads(spot, head_blocks)

    return (
        layer_out,
        grad_tokens,
        grad_replacement,
        grad_qkv,
        grad_out,
        grad_in,
        grad_down,
        norm_sums[0],
        norm_sums[1],
        norm_sums[2],
        norm_sums[3],
    )


def solution(mesh):
    tokens = P(("dp", "sp"), None)
    rows = P("dp", None)
    return jax.shard_map(
        local,
        mesh=mesh,
        in_specs=(tokens, rows, P(("dp", "sp")), tokens, tokens) + (P(),) * 8,
        out_specs=(tokens,) * 3 + (rows,) * 4 + (P(),) * 4,
        check_vma=False,
    )
```

```python
import functools
import math

import jax
import jax.numpy as jnp
from jax import lax
from jax.experimental import pallas as pl
from jax.experimental.pallas import tpu as pltpu
from jax.sharding import PartitionSpec as P

HEADS = 12
RANKS = 4
EPSILON = 1e-05
FAR = 1e30
F32 = jnp.float32
BF16 = jnp.bfloat16
VM = pl.BlockSpec(memory_space=pltpu.VMEM)
SM = pl.BlockSpec(memory_space=pltpu.SMEM)


def shape(dims, kind):
    return jax.ShapeDtypeStruct(dims, kind)


def scratch(dims, kind):
    return pltpu.VMEM(dims, kind)


def params(mebibytes):
    return pltpu.CompilerParams(vmem_limit_bytes=mebibytes << 20)


def alibi_slopes(head_count):
    nearest = 2 ** int(math.floor(math.log2(head_count)))
    base_list = [2.0 ** (-8.0 * (index + 1) / nearest) for index in range(nearest)]
    extra_list = [
        2.0 ** (-8.0 * (2 * index + 1) / (2 * nearest)) for index in range(head_count - nearest)
    ]
    return jnp.array(base_list + extra_list, dtype=F32)


def dot(a, b):
    return jnp.dot(a, b, preferred_element_type=F32)


def dot_nt(a, b):
    return lax.dot_general(a, b, (((1,), (1,)), ((), ())), preferred_element_type=F32)


def dot_tn(a, b):
    return lax.dot_general(a, b, (((0,), (0,)), ((), ())), preferred_element_type=F32)


def exact_dot(a, b):
    return jnp.dot(a, b, precision=lax.Precision.HIGHEST, preferred_element_type=F32)


def standardize(value):
    center = value - jnp.mean(value, axis=-1, keepdims=True)
    spread = jnp.mean(center * center, axis=-1, keepdims=True)
    inverse = lax.rsqrt(spread + EPSILON)
    return center * inverse, inverse


def standardize_back(grad, unit, inverse):
    mean = jnp.mean(grad, axis=-1, keepdims=True)
    return inverse * (grad - mean - unit * jnp.mean(grad * unit, axis=-1, keepdims=True))


def gelu_pair(x):
    cdf = 0.5 * (1.0 + lax.erf(x * math.sqrt(0.5)))
    pdf = jnp.exp(-0.5 * x * x) * (1.0 / math.sqrt(2.0 * math.pi))
    return x * cdf, cdf + x * pdf


def pair_active(seg, rank, first, second, rows):
    one, two = rank ^ first, rank ^ second
    low, high = jnp.minimum(one, two), jnp.maximum(one, two)
    return jnp.logical_or(one == two, seg[0, low * rows + rows - 1] == seg[0, high * rows])


def key_sequences(seg_rows, seg_keys, rank, rows):
    for at in range(RANKS):
        first = pl.multiple_of((rank ^ at) * rows, rows)
        line = jnp.broadcast_to(seg_rows[:, pl.ds(first, rows)], (128, rows))
        seg_keys[at * rows : (at + 1) * rows, :] = jnp.transpose(line)


def pair_distance(seg_rows, seg_keys, rank, keys_at, query_at, rows):
    key_pos, query_pos = (rank ^ keys_at) * rows, (rank ^ query_at) * rows
    down = lax.broadcasted_iota(jnp.int32, (rows, rows), 0)
    across = lax.broadcasted_iota(jnp.int32, (rows, rows), 1)
    gap = jnp.abs(down - across + (key_pos - query_pos)).astype(F32)
    seg_q = seg_rows[:, pl.ds(pl.multiple_of(query_pos, rows), rows)]
    seg_k = seg_keys[pl.ds(pl.multiple_of(keys_at * rows, rows), rows), 0:1]
    return jnp.where(seg_k == seg_q, gap, FAR)


def attention_forward_kernel(
    rows, heads, dim, info, seg, slopes, x0, x1, x2, x3, w, seg_rows,
    qkv_out, out_t, lse, qs, ks, vt, dist, seg_keys, score, peak,
):
    rank = info[0]
    width = heads * dim
    key_sequences(seg_rows, seg_keys, rank, rows)
    for at, x in enumerate((x0, x1, x2, x3)):
        qkv = dot(x[...], w[...]).astype(BF16)
        here = pl.ds(at * rows, rows)
        qkv_out[here, :] = qkv
        for h in range(heads):
            qs[h, here, :] = (qkv[:, h * dim : (h + 1) * dim] * dim**-0.5).astype(BF16)
            ks[h, here, :] = qkv[:, width + h * dim : width + (h + 1) * dim]
        vt[:, here] = jnp.transpose(qkv[:, 2 * width :])

    for a in range(RANKS):
        mine = pl.ds(a * rows, rows)
        peak[...] = jnp.full_like(peak, -jnp.inf)

        def first_pass(b, carry):
            @pl.when(pair_active(seg, rank, a, b, rows))
            def _():
                theirs = pl.ds(pl.multiple_of(b * rows, rows), rows)
                gap = pair_distance(seg_rows, seg_keys, rank, b, a, rows)
                for h in range(heads):
                    slope = slopes[rank * heads + h]
                    s = dot_nt(ks[h, theirs, :], qs[h, mine, :]) - slope * gap
                    score[h, theirs, :] = s
                    peak[h : h + 1, :] = jnp.maximum(
                        peak[h : h + 1, :], jnp.max(s, axis=0, keepdims=True)
                    )

            return carry

        lax.fori_loop(0, RANKS, first_pass, 0)

        def second_pass(b, carry):
            def add(carry):
                theirs = pl.ds(pl.multiple_of(b * rows, rows), rows)
                result = []
                for h in range(heads):
                    acc, total = carry[h]
                    p = jnp.exp(score[h, theirs, :] - peak[h : h + 1, :])
                    total = total + jnp.sum(p, axis=0, keepdims=True)
                    span = slice(h * dim, (h + 1) * dim)
                    result.append((acc + dot(vt[span, theirs], p.astype(BF16)), total))
                return tuple(result)

            return lax.cond(pair_active(seg, rank, a, b, rows), add, lambda carry: carry, carry)

        empty = (jnp.zeros((dim, rows), F32), jnp.zeros((1, rows), F32))
        sums = lax.fori_loop(0, RANKS, second_pass, (empty,) * heads)
        for h in range(heads):
            acc, total = sums[h]
            span = slice(h * dim, (h + 1) * dim)
            out_t[span, mine] = (acc / total).astype(BF16)
            lse[h : h + 1, mine] = peak[h : h + 1, :] + jnp.log(total)


def attention_forward(info, seg, slopes, blocks, w, heads, dim):
    rows = blocks[0].shape[0]
    tok, lw = rows * RANKS, heads * dim
    return pl.pallas_call(
        functools.partial(attention_forward_kernel, rows, heads, dim),
        name="attention_forward",
        out_shape=(
            shape((tok, 3 * lw), BF16),
            shape((lw, tok), BF16),
            shape((heads, tok), F32),
        ),
        in_specs=[SM] * 3 + [VM] * 6,
        out_specs=(VM,) * 3,
        scratch_shapes=[
            scratch((heads, tok, dim), BF16),
            scratch((heads, tok, dim), BF16),
            scratch((lw, tok), BF16),
            scratch((rows, rows), F32),
            scratch((tok, 128), jnp.int32),
            scratch((heads, tok, rows), F32),
            scratch((heads, rows), F32),
        ],
        compiler_params=params(14),
        cost_estimate=pl.CostEstimate(
            flops=4 * 10**9, bytes_accessed=6 * 10**6, transcendentals=3 * 10**6
        ),
    )(info, seg, slopes, *blocks, w, seg)


def attention_backward_kernel(
    rows, heads, dim, info, seg, slopes, g0, g1, g2, g3, w, qkv, lse, seg_rows,
    d0, d1, d2, d3, qs, ks, kt, vs, do, seg_keys, prob, dprob, dk, dv, dqt, delta,
):
    rank = info[0]
    width = heads * dim
    scale = dim**-0.5
    key_sequences(seg_rows, seg_keys, rank, rows)
    w_rank = w[pl.ds(pl.multiple_of(rank * width, width), width), :]
    for at, g in enumerate((g0, g1, g2, g3)):
        here = pl.ds(at * rows, rows)
        grad = dot_nt(g[0:rows, :], w_rank).astype(BF16)
        value = qkv[here, :]
        kt[:, here] = jnp.transpose(value[:, width : 2 * width])
        for h in range(heads):
            do[h, here, :] = grad[:, h * dim : (h + 1) * dim]
            qs[h, here, :] = (value[:, h * dim : (h + 1) * dim] * scale).astype(BF16)
            ks[h, here, :] = value[:, width + h * dim : width + (h + 1) * dim]
            vs[h, here, :] = value[:, 2 * width + h * dim : 2 * width + (h + 1) * dim]
    dk[...] = jnp.zeros_like(dk)
    dv[...] = jnp.zeros_like(dv)

    for a in range(RANKS):
        mine = pl.ds(a * rows, rows)
        delta[...] = jnp.zeros_like(delta)
        dqt[...] = jnp.zeros_like(dqt)

        def first_pass(b, carry):
            @pl.when(pair_active(seg, rank, a, b, rows))
            def _():
                theirs = pl.ds(pl.multiple_of(b * rows, rows), rows)
                gap = pair_distance(seg_rows, seg_keys, rank, b, a, rows)
                for h in range(heads):
                    slope = slopes[rank * heads + h]
                    s = dot_nt(ks[h, theirs, :], qs[h, mine, :]) - slope * gap
                    p = jnp.exp(s - lse[h : h + 1, mine])
                    dp = dot_nt(vs[h, theirs, :], do[h, mine, :])
                    delta[h : h + 1, :] += jnp.sum(p * dp, axis=0, keepdims=True)
                    prob[h, theirs, :] = p
                    dprob[h, theirs, :] = dp

            return carry

        lax.fori_loop(0, RANKS, first_pass, 0)

        def second_pass(b, carry):
            @pl.when(pair_active(seg, rank, a, b, rows))
            def _():
                theirs = pl.ds(pl.multiple_of(b * rows, rows), rows)
                for h in range(heads):
                    p = prob[h, theirs, :]
                    ds = (p * (dprob[h, theirs, :] - delta[h : h + 1, :])).astype(BF16)
                    dv[h, theirs, :] += dot(p.astype(BF16), do[h, mine, :])
                    dk[h, theirs, :] += dot(ds, qs[h, mine, :])
                    span = slice(h * dim, (h + 1) * dim)
                    dqt[span, :] += dot(kt[span, theirs], ds)

            return carry

        lax.fori_loop(0, RANKS, second_pass, 0)
        (d0, d1, d2, d3)[a][0:width, :] = (dqt[...] * scale).astype(BF16)

    for at, d_qkv in enumerate((d0, d1, d2, d3)):
        here = pl.ds(at * rows, rows)
        for h in range(heads):
            first = width + h * dim
            d_qkv[first : first + dim, :] = jnp.transpose(dk[h, here, :]).astype(BF16)
            first = 2 * width + h * dim
            d_qkv[first : first + dim, :] = jnp.transpose(dv[h, here, :]).astype(BF16)


def attention_backward(info, seg, slopes, blocks, w, qkv, lse, heads, dim):
    tok, lw = qkv.shape[0], heads * dim
    rows = tok // RANKS
    return pl.pallas_call(
        functools.partial(attention_backward_kernel, rows, heads, dim),
        name="attention_backward",
        out_shape=(shape((3 * lw, rows), BF16),) * RANKS,
        in_specs=[SM] * 3 + [VM] * 8,
        out_specs=(VM,) * RANKS,
        scratch_shapes=[
            scratch((heads, tok, dim), BF16),
            scratch((heads, tok, dim), BF16),
            scratch((lw, tok), BF16),
            scratch((heads, tok, dim), BF16),
            scratch((heads, tok, dim), BF16),
            scratch((tok, 128), jnp.int32),
            scratch((heads, tok, rows), F32),
            scratch((heads, tok, rows), F32),
            scratch((heads, tok, dim), F32),
            scratch((heads, tok, dim), F32),
            scratch((lw, rows), F32),
            scratch((heads, rows), F32),
        ],
        compiler_params=params(20),
        cost_estimate=pl.CostEstimate(
            flops=8 * 10**9, bytes_accessed=6 * 10**6, transcendentals=3 * 10**6
        ),
    )(info, seg, slopes, *blocks, w, qkv, lse, seg)


def line(vector):
    return vector[...].reshape(1, -1)


def join_tokens(rank, arrays, tokens_of, joined):
    part = arrays[0].shape[0]
    rows = arrays[0].shape[1] // RANKS
    for step, array in enumerate(arrays):
        first = pl.multiple_of((rank ^ step) * part, part)
        block = step ^ tokens_of
        joined[pl.ds(first, part), :] = array[:, block * rows : (block + 1) * rows]


def norm_one_kernel(
    info, own, near, far, cross, start, w, gain, shift, low, joined, unit, inverse
):
    join_tokens(info[0], (own, near, far, cross), 0, joined)
    x, inv = standardize(start[...].astype(F32) + dot_tn(joined[...], w[...]))
    unit[...] = x
    inverse[...] = inv
    low[...] = (x * line(gain) + line(shift)).astype(BF16)


def norm_one(info, parts, start, w, gain, shift):
    rows, width = start.shape
    return pl.pallas_call(
        norm_one_kernel,
        name="norm_one",
        out_shape=(
            shape((rows, width), BF16),
            shape((width, rows), BF16),
            shape((rows, width), F32),
            shape((rows, 1), F32),
        ),
        in_specs=[SM] + [VM] * 8,
        out_specs=(VM,) * 4,
        compiler_params=params(12),
        cost_estimate=pl.CostEstimate(
            flops=2 * rows * width * width, bytes_accessed=4 * 10**6, transcendentals=0
        ),
    )(info, *parts, start, w, gain, shift)


def norm_others_kernel(
    info, own, near, far, cross, s1, s2, s3, w, gain, shift, l1, l2, l3, j1, j2, j3
):
    for tokens_of, (start, low, joined) in enumerate(((s1, l1, j1), (s2, l2, j2), (s3, l3, j3))):
        join_tokens(info[0], (own, near, far, cross), tokens_of + 1, joined)
        x, _ = standardize(start[...].astype(F32) + dot_tn(joined[...], w[...]))
        low[...] = (x * line(gain) + line(shift)).astype(BF16)


def norm_others(info, parts, starts, w, gain, shift):
    rows, width = starts[0].shape
    results = pl.pallas_call(
        norm_others_kernel,
        name="norm_others",
        out_shape=(shape((rows, width), BF16),) * 3 + (shape((width, rows), BF16),) * 3,
        in_specs=[SM] + [VM] * 10,
        out_specs=(VM,) * 6,
        compiler_params=params(12),
        cost_estimate=pl.CostEstimate(
            flops=6 * rows * width * width, bytes_accessed=4 * 10**6, transcendentals=0
        ),
    )(info, *parts, *starts, w, gain, shift)
    return results[:3], results[3:]


def packing(rows, columns, part, rank):
    units = lax.broadcasted_iota(jnp.int32, (rows, columns), 0)
    packed = lax.broadcasted_iota(jnp.int32, (1, columns), 1)
    places = packed + rank * part
    for index in range(1, columns // part):
        places = places + jnp.where(packed >= index * part, (RANKS - 1) * part, 0)
    return (units == places).astype(BF16)


def pack_kernel(part, info, w_in, w_down, packed_in, packed_down):
    rank = info[0]
    width, hid = w_in.shape[0], w_down.shape[0]
    run = hid // 2
    select = packing(run, run // RANKS, part, rank)
    for index in range(4):
        piece = dot(w_in[:, index * run : (index + 1) * run], select)
        packed_in[:, index * run // RANKS : (index + 1) * run // RANKS] = piece.astype(BF16)
    if part % 16:
        for index in range(2):
            piece = dot_tn(select, w_down[index * run : (index + 1) * run, :])
            packed_down[index * run // RANKS : (index + 1) * run // RANKS, :] = piece.astype(BF16)
    else:
        for index in range(hid // RANKS // part):
            rows = pl.ds(pl.multiple_of((index * RANKS + rank) * part, part), part)
            packed_down[index * part : (index + 1) * part, :] = w_down[rows, :]


def pack_weights(info, w_in, w_out, part):
    width, hid = w_in.shape[0], w_out.shape[0]
    return pl.pallas_call(
        functools.partial(pack_kernel, part),
        name="pack_weights",
        out_shape=(shape((width, 2 * hid // RANKS), BF16), shape((hid // RANKS, width), BF16)),
        in_specs=[SM, VM, VM],
        out_specs=(VM, VM),
        compiler_params=params(14),
        cost_estimate=pl.CostEstimate(
            flops=4 * 10**9, bytes_accessed=17 * 10**6, transcendentals=0
        ),
    )(info, w_in, w_out)


def ffn_forward_kernel(
    low, unit, gain1, shift1, gain2, shift2, masked, cot, w_in, w_down,
    layer_out, d_h2, d_ff, slope, act, sums, acc, gates, ups,
):
    hid = w_down.shape[0]
    size = gates.shape[2]
    count = hid // size

    def project(block, slot):
        first = pl.multiple_of(block * size, size)
        gates[slot] = dot(low[...], w_in[:, pl.ds(first, size)])
        ups[slot] = dot(low[...], w_in[:, pl.ds(pl.multiple_of(hid + first, size), size)])

    def finish(block, slot):
        here = pl.ds(pl.multiple_of(block * size, size), size)
        up = ups[slot]
        value, grad = gelu_pair(gates[slot])
        act[:, here] = value.astype(BF16)
        slope[:, here] = (up * grad).astype(BF16)
        acc[...] += dot((value * up).astype(BF16), w_down[here, :])

    acc[...] = unit[...] * line(gain1) + line(shift1)
    project(0, 0)

    def pair(index, carry):
        block = index * 2
        project(block + 1, 1)
        finish(block, 0)
        project(block + 2, 0)
        finish(block + 1, 1)
        return carry

    lax.fori_loop(0, count // 2 - 1, pair, 0)
    project(count - 1, 1)
    finish(count - 2, 0)
    finish(count - 1, 1)
    x, inv = standardize(acc[...])
    layer_out[...] = (x * line(gain2) + line(shift2)).astype(BF16)
    places = lax.broadcasted_iota(jnp.int32, (low.shape[0], masked.shape[0]), 0)
    dy = exact_dot((places == line(masked)).astype(F32), cot[...])
    sums[0:1, :] = jnp.sum(dy * x, axis=0, keepdims=True)
    sums[1:2, :] = jnp.sum(dy, axis=0, keepdims=True)
    grad_in = standardize_back(dy * line(gain2), x, inv)
    d_h2[...] = grad_in
    d_ff[...] = grad_in.astype(BF16)


def ffn_forward(low, unit, gain1, shift1, gain2, shift2, masked, cot, w_in, w_out, size):
    rows, width = low.shape
    hid = w_out.shape[0]
    return pl.pallas_call(
        ffn_forward_kernel,
        name="ffn_forward",
        out_shape=(
            shape((rows, width), BF16),
            shape((rows, width), F32),
            shape((rows, width), BF16),
            shape((rows, hid), BF16),
            shape((rows, hid), BF16),
            shape((2, width), F32),
        ),
        in_specs=[VM] * 10,
        out_specs=(VM,) * 6,
        scratch_shapes=[
            scratch((rows, width), F32),
            scratch((2, rows, size), F32),
            scratch((2, rows, size), F32),
        ],
        compiler_params=params(14),
        cost_estimate=pl.CostEstimate(
            flops=6 * rows * width * hid, bytes_accessed=18 * 10**6, transcendentals=2 * rows * hid
        ),
    )(low, unit, gain1, shift1, gain2, shift2, masked, cot, w_in, w_out)


def ffn_backward_kernel(
    d_ff, d_h2, unit, inverse, gain1, sums2, act, slope, w_in, w_down, d_h1, sent, acc, hidden
):
    hid = w_down.shape[0]
    size = hidden.shape[2]
    count = hid // size

    def project(block, slot):
        here = pl.ds(pl.multiple_of(block * size, size), size)
        hidden[slot] = dot_nt(d_ff[...], w_down[here, :])

    def finish(block, slot):
        first = pl.multiple_of(block * size, size)
        here, there = pl.ds(first, size), pl.ds(pl.multiple_of(hid + first, size), size)
        d_hidden = hidden[slot]
        d_gate = (d_hidden * slope[:, here].astype(F32)).astype(BF16)
        d_up = (d_hidden * act[:, here].astype(F32)).astype(BF16)
        acc[...] += dot_nt(d_gate, w_in[:, here]) + dot_nt(d_up, w_in[:, there])

    acc[...] = d_h2[...]
    project(0, 0)

    def pair(index, carry):
        block = index * 2
        project(block + 1, 1)
        finish(block, 0)
        project(block + 2, 0)
        finish(block + 1, 1)
        return carry

    lax.fori_loop(0, count // 2 - 1, pair, 0)
    project(count - 1, 1)
    finish(count - 2, 0)
    finish(count - 1, 1)
    total = acc[...]
    rows = total.shape[0]
    x = unit[...]
    gain_sum = jnp.sum(total * x, axis=0, keepdims=True)
    shift_sum = jnp.sum(total, axis=0, keepdims=True)
    sums = jnp.concatenate([gain_sum, shift_sum, sums2[...]], axis=0)
    high = sums.astype(BF16).astype(F32)
    tail = jnp.concatenate([high, sums - high, jnp.zeros((8, sums.shape[1]), F32)], axis=0)
    grad = standardize_back(total * line(gain1), x, inverse[...])
    d_h1[...] = grad
    sent[0:rows, :] = grad.astype(BF16)
    sent[rows : rows + 16, :] = tail.astype(BF16)


def ffn_backward(d_ff, d_h2, unit, inverse, gain1, sums2, act, slope, w_in, w_out, size):
    rows, width = d_ff.shape
    hid = w_out.shape[0]
    return pl.pallas_call(
        ffn_backward_kernel,
        name="ffn_backward",
        out_shape=(shape((rows, width), F32), shape((rows + 16, width), BF16)),
        in_specs=[VM] * 10,
        out_specs=(VM,) * 2,
        scratch_shapes=[scratch((rows, width), F32), scratch((2, rows, size), F32)],
        compiler_params=params(14),
        cost_estimate=pl.CostEstimate(
            flops=6 * rows * width * hid, bytes_accessed=20 * 10**6, transcendentals=0
        ),
    )(d_ff, d_h2, unit, inverse, gain1, sums2, act, slope, w_in, w_out)


X_FIRST = (1, 2, 4)
Z_FIRST = (2, 1, 4)


def bit_of(value, mask):
    return (value // mask) % 2


def store_blocks(blocks, keep, send, place, order, columns):
    one, two, three = order
    odd = bit_of(place, one) == 1
    for index in range(8):
        if index & one:
            continue
        spot = bit_of(place ^ index, two) * 2 + bit_of(place ^ index, three)
        low, high = blocks(index), blocks(index | one)
        keep[spot, :, columns] = jnp.where(odd, high, low).astype(BF16)
        send[spot, :, columns] = jnp.where(odd, low, high).astype(BF16)


def row_blocks(grad):
    each = grad.shape[0] // 8
    return lambda index: grad[index * each : (index + 1) * each]


def ffn_grad_kernel(
    size, info, n0, n1, n2, n3, f0, f1, f2, f3, w_in, w_down,
    keep_gate, send_gate, keep_up, send_up, keep_down, send_down,
    tok_t, gates, ups, d_hiddens, hidden_t, d_gate, d_up, d_ff, down,
):
    toks, grads = (n0, n1, n2, n3), (f0, f1, f2, f3)
    rows = n0.shape[0]
    units = w_down.shape[0]
    for at in range(RANKS):
        here = slice(at * rows, (at + 1) * rows)
        d_ff[here, :] = grads[at][...]
        tok_t[:, here] = jnp.transpose(toks[at][...])

    def unit_block(step, carry):
        here = pl.ds(pl.multiple_of(step * size, size), size)
        there = pl.ds(pl.multiple_of(units + step * size, size), size)
        w_gate, w_up, w_rows = w_in[:, here], w_in[:, there], w_down[here, :]

        def project(at):
            slot = at % 2
            gates[slot] = dot(toks[at][...], w_gate)
            ups[slot] = dot(toks[at][...], w_up)
            d_hiddens[slot] = dot_nt(grads[at][...], w_rows)

        def finish(at):
            slot = at % 2
            here = slice(at * rows, (at + 1) * rows)
            value, grad = gelu_pair(gates[slot])
            up, d_hidden = ups[slot], d_hiddens[slot]
            hidden_t[:, here] = jnp.transpose((value * up).astype(BF16))
            d_gate[here, :] = (d_hidden * up * grad).astype(BF16)
            d_up[here, :] = (d_hidden * value).astype(BF16)

        project(0)
        for at in range(RANKS):
            if at + 1 < RANKS:
                project(at + 1)
            finish(at)
        total = dot(tok_t[...], d_gate[...])
        store_blocks(row_blocks(total), keep_gate, send_gate, info[1], Z_FIRST, here)
        total = dot(tok_t[...], d_up[...])
        store_blocks(row_blocks(total), keep_up, send_up, info[1], Z_FIRST, here)
        down[here, :] = dot(hidden_t[...], d_ff[...])
        return carry

    lax.fori_loop(0, units // size, unit_block, 0)
    store_blocks(row_blocks(down), keep_down, send_down, info[1], X_FIRST, slice(None))


def ffn_grad(info, toks, grads, w_in, w_down, size):
    rows, width = toks[0].shape
    units = w_down.shape[0]
    tok = rows * RANKS
    dims = [(4, width // 8, units)] * 4 + [(4, units // 8, width)] * 2
    return pl.pallas_call(
        functools.partial(ffn_grad_kernel, size),
        name="ffn_grad",
        out_shape=[shape(each, BF16) for each in dims],
        in_specs=[SM] + [VM] * 10,
        out_specs=[VM] * 6,
        scratch_shapes=[
            scratch((width, tok), BF16),
            scratch((2, rows, size), F32),
            scratch((2, rows, size), F32),
            scratch((2, rows, size), F32),
            scratch((size, tok), BF16),
            scratch((tok, size), BF16),
            scratch((tok, size), BF16),
            scratch((tok, width), BF16),
            scratch((units, width), F32),
        ],
        compiler_params=params(18),
        cost_estimate=pl.CostEstimate(
            flops=12 * tok * width * units,
            bytes_accessed=8 * 10**6,
            transcendentals=2 * tok * units,
        ),
    )(info, *toks, *grads, w_in, w_down)


def qkv_grad_kernel(
    info, x0, x1, x2, x3, d0, d1, d2, d3, j0, j1, j2, j3, g0, g1, g2, g3, keep, send, columns, grad
):
    rows, width = x0.shape
    part = width // RANKS
    total = 0.0
    for x, d_qkv in zip((x0, x1, x2, x3), (d0, d1, d2, d3)):
        total = total + dot(d_qkv[...], x[...])
    grad[:, : 3 * part] = jnp.transpose(total)
    for value in range(RANKS):

        @pl.when(info[0] == value)
        def _():
            for at, g in enumerate((g0, g1, g2, g3)):
                columns[at] = g[0:rows, value * part : (value + 1) * part]

    total = 0.0
    sums = 0.0
    for at, (joined, g) in enumerate(zip((j0, j1, j2, j3), (g0, g1, g2, g3))):
        total = total + dot(joined[...], columns[at])
        pair = g[rows : rows + 16, :].astype(F32)
        sums = sums + pair[0:4] + pair[4:8]
    grad[:, 3 * part :] = total
    high = sums.astype(BF16).astype(F32)
    tail = jnp.concatenate([high, sums - high], axis=0)
    each = width // 8

    def blocks(index):
        return jnp.concatenate([grad[index * each : (index + 1) * each], tail], axis=0)

    store_blocks(blocks, keep, send, info[1], X_FIRST, slice(None))


def qkv_grad(info, blocks, d_qkv, joined, d_proj):
    rows, width = blocks[0].shape
    return pl.pallas_call(
        qkv_grad_kernel,
        name="qkv_grad",
        out_shape=(shape((4, width // 8 + 8, width), BF16),) * 2,
        in_specs=[SM] + [VM] * 16,
        out_specs=(VM, VM),
        scratch_shapes=[
            scratch((RANKS, rows, width // RANKS), BF16),
            scratch((width, width), F32),
        ],
        compiler_params=params(14),
        cost_estimate=pl.CostEstimate(
            flops=8 * rows * width * width, bytes_accessed=4 * 10**6, transcendentals=0
        ),
    )(info, *blocks, *d_qkv, *joined, *d_proj)


def unpack(part, packed, wide, first):
    few = packed.shape[1] // RANKS
    for run in range(few // part):
        pieces = []
        for value in range(RANKS):
            at = value * few + run * part
            pieces.append(packed[:, at : at + part])
        at = first + run * RANKS * part
        wide[:, at : at + RANKS * part] = jnp.concatenate(pieces, axis=1).astype(F32)


def join_early_kernel(info, b0, b1, b2, b3, down, packed):
    rows, columns = b0.shape
    few = columns // 2
    for step, block in enumerate((b0, b1, b2, b3)):
        there = info[0] ^ step
        packed[:, pl.ds(pl.multiple_of(there * few, few), few)] = block[:, few:]
        down[pl.ds(pl.multiple_of(there * rows, rows), rows), :] = block[:, :few].astype(F32)


def join_late_kernel(part, info, b0, b1, b2, b3, gates, wide, out, rest, ups):
    width = rest.shape[1]
    heads = width // RANKS
    few = gates.shape[1] // RANKS
    blocks = (b0, b1, b2, b3)
    for step, block in enumerate(blocks):
        there = pl.multiple_of((info[0] ^ step) * few, few)
        ups[:, pl.ds(there, few)] = block[:, :few]
    unpack(part, gates, wide, 0)
    unpack(part, ups, wide, RANKS * few)
    for value in range(RANKS):

        @pl.when(info[0] == value)
        def _():
            for step, block in enumerate(blocks):
                there = (value ^ step) * heads
                for third in range(3):
                    first = few + third * heads
                    at = third * width + there
                    out[:, at : at + heads] = block[:, first : first + heads].astype(F32)
                first = few + 3 * heads
                rest[:, there : there + heads] = block[:, first:].astype(F32)


def join_early(info, blocks):
    rows, columns = blocks[0].shape
    if rows % 8:
        stacked = jnp.stack(blocks)[info[0] ^ jnp.arange(RANKS)]
        few = columns // 2
        gates = jnp.concatenate(list(stacked[:, :, few:]), axis=1)
        return stacked[:, :, :few].reshape(-1, few).astype(F32), gates
    return pl.pallas_call(
        join_early_kernel,
        name="join_early",
        out_shape=(
            shape((rows * RANKS, columns // 2), F32),
            shape((rows, RANKS * columns // 2), BF16),
        ),
        in_specs=[SM] + [VM] * 4,
        out_specs=(VM, VM),
        compiler_params=params(8),
        cost_estimate=NO_COST,
    )(info, *blocks)


def join_late(info, blocks, gates, part):
    rows, columns = blocks[0].shape
    width = columns // 2
    if RANKS * part % 128:
        stacked = jnp.stack(blocks)[info[0] ^ jnp.arange(RANKS)].astype(F32)
        both = [gates.astype(F32), jnp.concatenate(list(stacked[:, :, :width]), axis=1)]
        wide = [each.reshape(rows, RANKS, -1, part).transpose(0, 2, 1, 3) for each in both]
        wide = jnp.concatenate([each.reshape(rows, -1) for each in wide], axis=1)
        heads = stacked[:, :, width:].reshape(RANKS, rows, RANKS, -1).transpose(1, 2, 0, 3)
        heads = heads.reshape(rows, RANKS, -1)
        return wide, heads[:, :3].reshape(rows, -1), heads[:, 3]
    return pl.pallas_call(
        functools.partial(join_late_kernel, part),
        name="join_late",
        out_shape=(
            shape((rows, 2 * RANKS * width), F32),
            shape((rows, 3 * width), F32),
            shape((rows, width), F32),
        ),
        in_specs=[SM] + [VM] * 5,
        out_specs=(VM,) * 3,
        scratch_shapes=[scratch((rows, RANKS * width), BF16)],
        compiler_params=params(14),
        cost_estimate=NO_COST,
    )(info, *blocks, gates)


def token_grad_kernel(
    info, own, near, far, cross, w, d_h1, masked, tokens, replacement, joined
):
    rows, width = d_h1.shape
    part = width // RANKS
    for step, block in enumerate((own, near, far, cross)):
        for third in range(3):
            first = pl.multiple_of(third * width + (info[0] ^ step) * part, part)
            joined[pl.ds(first, part), :] = block[third * part : (third + 1) * part, :]
    grad = d_h1[...] + jnp.transpose(dot(w[...], joined[...]))
    count = masked.shape[0]
    places = lax.broadcasted_iota(jnp.int32, (rows, count), 0)
    select = (places == line(masked)).astype(F32)
    hit = jnp.max(select, axis=1, keepdims=True)
    tokens[...] = jnp.where(hit > 0.5, 0.0, grad)
    replacement[...] = lax.dot_general(
        select, grad, (((0,), (0,)), ((), ())),
        precision=lax.Precision.HIGHEST, preferred_element_type=F32,
    )


def token_grad(info, parts, w, d_h1, masked):
    rows, width = d_h1.shape
    return pl.pallas_call(
        token_grad_kernel,
        name="token_grad",
        out_shape=(shape((rows, width), F32), shape((masked.shape[0], width), F32)),
        in_specs=[SM] + [VM] * 7,
        out_specs=(VM, VM),
        scratch_shapes=[scratch((3 * width, rows), BF16)],
        compiler_params=params(16),
        cost_estimate=pl.CostEstimate(
            flops=6 * rows * width * width, bytes_accessed=8 * 10**6, transcendentals=0
        ),
    )(info, *parts, w, d_h1, masked)


def after(value, *others):
    return lax.optimization_barrier((value,) + others)[0]


def flip(value, axis, bits):
    count = lax.axis_size(axis)
    return lax.ppermute(value, axis, [(index, index ^ bits) for index in range(count)])


def gather_blocks(value):
    far = flip(value, "sp", 2)
    near = flip(value, "sp", 1)
    cross = flip(far, "sp", 1)
    return [value, near, far, cross]


def exchange_blocks(blocks):
    via = flip(blocks[3], "sp", 1)
    near = flip(blocks[1], "sp", 1)
    far = flip(blocks[2], "sp", 2)
    cross = flip(via, "sp", 2)
    return [blocks[0], near, far, cross]


def small_mesh():
    return lax.axis_size("dp") == 8


NO_COST = pl.CostEstimate(flops=0, bytes_accessed=0, transcendentals=0)


def tidy_sums(value):
    first = value.shape[1] - 8
    sums = value[:, first : first + 4] + value[:, first + 4 :]
    high = sums.astype(BF16).astype(F32)
    return jnp.concatenate([value[:, :first], high, sums - high], axis=1)


def halve_kernel(with_sums, keep, came, kept, sent):
    half = keep.shape[0] // 2
    value = keep[...].astype(F32) + came[...].astype(F32)
    if with_sums:
        value = tidy_sums(value)
    kept[...] = value[:half]
    sent[...] = value[half:].astype(BF16)


def halve(keep, came, with_sums=False):
    dims = (keep.shape[0] // 2,) + keep.shape[1:]
    return pl.pallas_call(
        functools.partial(halve_kernel, with_sums),
        name="halve",
        out_shape=(shape(dims, F32), shape(dims, BF16)),
        in_specs=[VM] * 2,
        out_specs=(VM, VM),
        compiler_params=params(12),
        cost_estimate=NO_COST,
    )(keep, came)


def send_first(send, order):
    return flip(send, "dp", order[0]) if small_mesh() else send


def send_second(keep, came, order, with_sums=False):
    if not small_mesh():
        return keep, came
    kept, sent = halve(keep, came, with_sums)
    return kept, flip(sent, "dp", order[1])


def send_third(keep, came, order, with_sums=False):
    if not small_mesh():
        return keep, came
    kept, sent = halve(keep, came, with_sums)
    return kept, flip(sent, "dp", order[2])


def natural_blocks(keep, send, order):
    both = jnp.concatenate([keep, send], axis=0).astype(F32)
    places = []
    for index in range(8):
        bits = [1 if index & mask else 0 for mask in order]
        places.append(both[bits[0] * 4 + bits[1] * 2 + bits[2]])
    return places


def scatter_sum(blocks):
    grad = jnp.concatenate(blocks, axis=0)
    return lax.psum_scatter(grad, "dp", scatter_dimension=0, tiled=True).astype(BF16)


def finish_pair_kernel(keep_a, came_a, keep_b, came_b, out):
    columns = keep_a.shape[2]
    out[:, :columns] = (keep_a[0] + came_a[0].astype(F32)).astype(BF16)
    out[:, columns:] = (keep_b[0] + came_b[0].astype(F32)).astype(BF16)


def finish_pair(keep_a, came_a, order_a, keep_b, came_b, order_b):
    if not small_mesh():
        first = scatter_sum(natural_blocks(keep_a, came_a, order_a))
        second = scatter_sum(natural_blocks(keep_b, came_b, order_b))
        return jnp.concatenate([first, second], axis=1)
    _, rows, columns = keep_a.shape
    return pl.pallas_call(
        finish_pair_kernel,
        name="finish_pair",
        out_shape=shape((rows, columns + keep_b.shape[2]), BF16),
        in_specs=[VM] * 4,
        out_specs=VM,
        compiler_params=params(8),
        cost_estimate=NO_COST,
    )(keep_a, came_a, keep_b, came_b)


def finish_heads_kernel(keep_u, came_u, keep, came, out, sums):
    columns = keep_u.shape[2]
    rows = out.shape[0]
    out[:, :columns] = (keep_u[0] + came_u[0].astype(F32)).astype(BF16)
    total = keep[0] + came[0].astype(F32)
    out[:, columns:] = total[:rows].astype(BF16)
    sums[...] = total[rows : rows + 4] + total[rows + 4 :]


def finish_heads(keep_u, came_u, keep, came):
    _, rows, columns = keep.shape
    rows = rows - 8
    if not small_mesh():
        blocks = natural_blocks(keep, came, X_FIRST)
        sums = blocks[0][rows : rows + 4] + blocks[0][rows + 4 :]
        first = scatter_sum(natural_blocks(keep_u, came_u, Z_FIRST))
        second = scatter_sum([block[:rows] for block in blocks])
        return jnp.concatenate([first, second], axis=1), lax.psum(sums, "dp")
    return pl.pallas_call(
        finish_heads_kernel,
        name="finish_heads",
        out_shape=(shape((rows, keep_u.shape[2] + columns), BF16), shape((4, columns), F32)),
        in_specs=[VM] * 4,
        out_specs=(VM, VM),
        compiler_params=params(8),
        cost_estimate=NO_COST,
    )(keep_u, came_u, keep, came)


def local(
    tokens,
    segment_ids,
    masked_rows,
    replacement,
    cotangent,
    w_qkv,
    w_out_attn,
    w_in_ff,
    w_out_ff,
    gain_one,
    shift_one,
    gain_two,
    shift_two,
):
    rows_dev, width = tokens.shape
    rank = lax.axis_index("sp")
    heads = HEADS // RANKS
    dim = width // HEADS
    part = heads * dim
    slopes = alibi_slopes(HEADS)

    select = jnp.arange(rows_dev, dtype=jnp.int32)[:, None] == masked_rows[None, :]
    hit = jnp.any(select, axis=1, keepdims=True)
    placed = dot(select.astype(BF16), replacement)
    start = jnp.where(hit, placed.astype(BF16), tokens)
    start_far = flip(start, "sp", 2)
    start_near = flip(start, "sp", 1)
    place = lax.axis_index("dp")
    place = place if small_mesh() else place * 0
    spot = jnp.stack([rank, place]).astype(jnp.int32)

    w_rank = jnp.concatenate(
        [
            lax.dynamic_slice_in_dim(w_qkv, third * width + rank * part, part, 1)
            for third in range(3)
        ],
        axis=1,
    )
    start_cross = flip(after(start_far, w_rank, spot), "sp", 1)
    start_blocks = [start, start_near, start_far, start_cross]
    qkv, attn, lse = attention_forward(
        spot, segment_ids, slopes, start_blocks, w_rank, heads, dim
    )
    attn_far = flip(attn, "sp", 2)
    attn_near = flip(attn, "sp", 1)
    part_units = w_out_ff.shape[0] // lax.axis_size("dp") // RANKS
    packed_in, packed_down = pack_weights(after(spot, lse), w_in_ff, w_out_ff, part_units)
    attn_cross = flip(after(attn_far, packed_in), "sp", 1)
    attn_parts = [attn, attn_near, attn_far, attn_cross]
    low, joined, unit, inverse = norm_one(
        spot, attn_parts, start, w_out_attn, gain_one, shift_one
    )
    layer_out, d_h2, d_ff, slope, act, sums2 = ffn_forward(
        low, unit, gain_one, shift_one, gain_two, shift_two,
        masked_rows, cotangent, w_in_ff, w_out_ff, 768,
    )
    d_ff_far = flip(d_ff, "sp", 2)
    d_ff_near = flip(d_ff, "sp", 1)
    d_h1, sent = ffn_backward(
        d_ff, d_h2, unit, inverse, gain_one, sums2, act, slope, w_in_ff, w_out_ff, 768
    )
    lows, others_joined = norm_others(
        after(spot, sent), attn_parts, start_blocks[1:], w_out_attn, gain_one, shift_one
    )
    d_ff_far = after(d_ff_far, lows[0])
    d_ff_cross = flip(d_ff_far, "sp", 1)
    d_ff_blocks = [d_ff, d_ff_near, d_ff_far, d_ff_cross]
    far = flip(sent, "sp", 2)
    near = flip(sent, "sp", 1)

    keep_g, send_g, keep_u, send_u, keep_d, send_d = ffn_grad(
        spot, [low, *lows], d_ff_blocks, packed_in, packed_down, 256
    )
    came_g = send_first(send_g, Z_FIRST)
    came_d = send_first(send_d, X_FIRST)
    cross = flip(after(far, keep_g), "sp", 1)
    d_proj_blocks = [sent, near, far, cross]

    d_qkv = attention_backward(
        spot, segment_ids, slopes, d_proj_blocks, w_out_attn, qkv, lse, heads, dim
    )
    parts = exchange_blocks(d_qkv)
    came_u = send_first(after(send_u, d_qkv[0]), Z_FIRST)
    keep_g, came_g = send_second(keep_g, after(came_g, d_qkv[0]), Z_FIRST)
    keep_d, came_d = send_second(keep_d, after(came_d, keep_g), X_FIRST)
    keep_q, send_q = qkv_grad(
        after(spot, keep_d), start_blocks, d_qkv, [joined, *others_joined], d_proj_blocks
    )
    came_q = send_first(send_q, X_FIRST)
    keep_g, came_g = send_third(keep_g, after(came_g, keep_q), Z_FIRST)
    keep_d, came_d = send_third(keep_d, after(came_d, keep_g), X_FIRST)
    keep_u, came_u = send_second(keep_u, after(came_u, keep_d), Z_FIRST)
    keep_q, came_q = send_second(keep_q, after(came_q, keep_u), X_FIRST, True)
    early = finish_pair(keep_d, after(came_d, keep_q), X_FIRST, keep_g, came_g, Z_FIRST)
    far = flip(early, "sp", 2)
    near = flip(early, "sp", 1)
    keep_u, came_u = send_third(keep_u, after(came_u, early), Z_FIRST)
    keep_q, came_q = send_third(keep_q, after(came_q, keep_u, came_u, parts), X_FIRST, True)
    late, norm_sums = finish_heads(keep_u, came_u, keep_q, came_q)
    early_blocks = [early, near, far, flip(after(far, late), "sp", 1)]
    late_blocks = gather_blocks(late)
    grad_tokens, grad_replacement = token_grad(
        after(spot, late), parts, w_qkv, d_h1, masked_rows
    )
    grad_down, gates = join_early(after(spot, late), early_blocks)
    grad_in, grad_qkv, grad_out = join_late(spot, late_blocks, gates, part_units)

    return (
        layer_out,
        grad_tokens,
        grad_replacement,
        grad_qkv,
        grad_out,
        grad_in,
        grad_down,
        norm_sums[0],
        norm_sums[1],
        norm_sums[2],
        norm_sums[3],
    )


def solution(mesh):
    tokens = P(("dp", "sp"), None)
    rows = P("dp", None)
    return jax.shard_map(
        local,
        mesh=mesh,
        in_specs=(tokens, rows, P(("dp", "sp")), tokens, tokens) + (P(),) * 8,
        out_specs=(tokens,) * 3 + (rows,) * 4 + (P(),) * 4,
        check_vma=False,
    )
```

```python
import functools
import math

import jax
import jax.numpy as jnp
from jax import lax
from jax.experimental import pallas as pl
from jax.experimental.pallas import tpu as pltpu
from jax.sharding import PartitionSpec as P

HEADS = 12
RANKS = 4
EPSILON = 1e-05
FAR = 1e30
F32 = jnp.float32
BF16 = jnp.bfloat16
VM = pl.BlockSpec(memory_space=pltpu.VMEM)
SM = pl.BlockSpec(memory_space=pltpu.SMEM)


def shape(dims, kind):
    return jax.ShapeDtypeStruct(dims, kind)


def scratch(dims, kind):
    return pltpu.VMEM(dims, kind)


def params(mebibytes):
    return pltpu.CompilerParams(vmem_limit_bytes=mebibytes << 20)


def alibi_slopes(head_count):
    nearest = 2 ** int(math.floor(math.log2(head_count)))
    base_list = [2.0 ** (-8.0 * (index + 1) / nearest) for index in range(nearest)]
    extra_list = [
        2.0 ** (-8.0 * (2 * index + 1) / (2 * nearest)) for index in range(head_count - nearest)
    ]
    return jnp.array(base_list + extra_list, dtype=F32)


def dot(a, b):
    return jnp.dot(a, b, preferred_element_type=F32)


def dot_nt(a, b):
    return lax.dot_general(a, b, (((1,), (1,)), ((), ())), preferred_element_type=F32)


def dot_tn(a, b):
    return lax.dot_general(a, b, (((0,), (0,)), ((), ())), preferred_element_type=F32)


def exact_dot(a, b):
    return jnp.dot(a, b, precision=lax.Precision.HIGHEST, preferred_element_type=F32)


def standardize(value):
    center = value - jnp.mean(value, axis=-1, keepdims=True)
    spread = jnp.mean(center * center, axis=-1, keepdims=True)
    inverse = lax.rsqrt(spread + EPSILON)
    return center * inverse, inverse


def standardize_back(grad, unit, inverse):
    mean = jnp.mean(grad, axis=-1, keepdims=True)
    return inverse * (grad - mean - unit * jnp.mean(grad * unit, axis=-1, keepdims=True))


def gelu_pair(x):
    cdf = 0.5 * (1.0 + lax.erf(x * math.sqrt(0.5)))
    pdf = jnp.exp(-0.5 * x * x) * (1.0 / math.sqrt(2.0 * math.pi))
    return x * cdf, cdf + x * pdf


def pair_active(seg, rank, first, second, rows):
    one, two = rank ^ first, rank ^ second
    low, high = jnp.minimum(one, two), jnp.maximum(one, two)
    return jnp.logical_or(one == two, seg[0, low * rows + rows - 1] == seg[0, high * rows])


def key_sequences(seg_rows, seg_keys, rank, rows):
    for at in range(RANKS):
        first = pl.multiple_of((rank ^ at) * rows, rows)
        line = jnp.broadcast_to(seg_rows[:, pl.ds(first, rows)], (128, rows))
        seg_keys[at * rows : (at + 1) * rows, :] = jnp.transpose(line)


def pair_distance(seg_rows, seg_keys, rank, keys_at, query_at, rows):
    key_pos, query_pos = (rank ^ keys_at) * rows, (rank ^ query_at) * rows
    down = lax.broadcasted_iota(jnp.int32, (rows, rows), 0)
    across = lax.broadcasted_iota(jnp.int32, (rows, rows), 1)
    gap = jnp.abs(down - across + (key_pos - query_pos)).astype(F32)
    seg_q = seg_rows[:, pl.ds(pl.multiple_of(query_pos, rows), rows)]
    seg_k = seg_keys[pl.ds(pl.multiple_of(keys_at * rows, rows), rows), 0:1]
    return jnp.where(seg_k == seg_q, gap, FAR)


def attention_forward_kernel(
    rows, heads, dim, info, seg, slopes, x0, x1, x2, x3, w, seg_rows,
    qkv_out, out_t, lse, qs, ks, vt, dist, seg_keys, score, peak,
):
    rank = info[0]
    width = heads * dim
    key_sequences(seg_rows, seg_keys, rank, rows)
    for at, x in enumerate((x0, x1, x2, x3)):
        qkv = dot(x[...], w[...]).astype(BF16)
        here = pl.ds(at * rows, rows)
        qkv_out[here, :] = qkv
        for h in range(heads):
            qs[h, here, :] = (qkv[:, h * dim : (h + 1) * dim] * dim**-0.5).astype(BF16)
            ks[h, here, :] = qkv[:, width + h * dim : width + (h + 1) * dim]
        vt[:, here] = jnp.transpose(qkv[:, 2 * width :])

    for a in range(RANKS):
        mine = pl.ds(a * rows, rows)
        peak[...] = jnp.full_like(peak, -jnp.inf)

        def first_pass(b, carry):
            @pl.when(pair_active(seg, rank, a, b, rows))
            def _():
                theirs = pl.ds(pl.multiple_of(b * rows, rows), rows)
                gap = pair_distance(seg_rows, seg_keys, rank, b, a, rows)
                for h in range(heads):
                    slope = slopes[rank * heads + h]
                    s = dot_nt(ks[h, theirs, :], qs[h, mine, :]) - slope * gap
                    score[h, theirs, :] = s
                    peak[h : h + 1, :] = jnp.maximum(
                        peak[h : h + 1, :], jnp.max(s, axis=0, keepdims=True)
                    )

            return carry

        lax.fori_loop(0, RANKS, first_pass, 0)

        def second_pass(b, carry):
            def add(carry):
                theirs = pl.ds(pl.multiple_of(b * rows, rows), rows)
                result = []
                for h in range(heads):
                    acc, total = carry[h]
                    p = jnp.exp(score[h, theirs, :] - peak[h : h + 1, :])
                    total = total + jnp.sum(p, axis=0, keepdims=True)
                    span = slice(h * dim, (h + 1) * dim)
                    result.append((acc + dot(vt[span, theirs], p.astype(BF16)), total))
                return tuple(result)

            return lax.cond(pair_active(seg, rank, a, b, rows), add, lambda carry: carry, carry)

        empty = (jnp.zeros((dim, rows), F32), jnp.zeros((1, rows), F32))
        sums = lax.fori_loop(0, RANKS, second_pass, (empty,) * heads)
        for h in range(heads):
            acc, total = sums[h]
            span = slice(h * dim, (h + 1) * dim)
            out_t[span, mine] = (acc / total).astype(BF16)
            lse[h : h + 1, mine] = peak[h : h + 1, :] + jnp.log(total)


def attention_forward(info, seg, slopes, blocks, w, heads, dim):
    rows = blocks[0].shape[0]
    tok, lw = rows * RANKS, heads * dim
    return pl.pallas_call(
        functools.partial(attention_forward_kernel, rows, heads, dim),
        name="attention_forward",
        out_shape=(
            shape((tok, 3 * lw), BF16),
            shape((lw, tok), BF16),
            shape((heads, tok), F32),
        ),
        in_specs=[SM] * 3 + [VM] * 6,
        out_specs=(VM,) * 3,
        scratch_shapes=[
            scratch((heads, tok, dim), BF16),
            scratch((heads, tok, dim), BF16),
            scratch((lw, tok), BF16),
            scratch((rows, rows), F32),
            scratch((tok, 128), jnp.int32),
            scratch((heads, tok, rows), F32),
            scratch((heads, rows), F32),
        ],
        compiler_params=params(14),
        cost_estimate=pl.CostEstimate(
            flops=4 * 10**9, bytes_accessed=6 * 10**6, transcendentals=3 * 10**6
        ),
    )(info, seg, slopes, *blocks, w, seg)


def attention_backward_kernel(
    rows, heads, dim, info, seg, slopes, g0, g1, g2, g3, w, qkv, lse, seg_rows,
    d0, d1, d2, d3, qs, ks, kt, vs, do, seg_keys, prob, dprob, dk, dv, dqt, delta,
):
    rank = info[0]
    width = heads * dim
    scale = dim**-0.5
    key_sequences(seg_rows, seg_keys, rank, rows)
    w_rank = w[pl.ds(pl.multiple_of(rank * width, width), width), :]
    for at, g in enumerate((g0, g1, g2, g3)):
        here = pl.ds(at * rows, rows)
        grad = dot_nt(g[0:rows, :], w_rank).astype(BF16)
        value = qkv[here, :]
        kt[:, here] = jnp.transpose(value[:, width : 2 * width])
        for h in range(heads):
            do[h, here, :] = grad[:, h * dim : (h + 1) * dim]
            qs[h, here, :] = (value[:, h * dim : (h + 1) * dim] * scale).astype(BF16)
            ks[h, here, :] = value[:, width + h * dim : width + (h + 1) * dim]
            vs[h, here, :] = value[:, 2 * width + h * dim : 2 * width + (h + 1) * dim]
    dk[...] = jnp.zeros_like(dk)
    dv[...] = jnp.zeros_like(dv)

    for a in range(RANKS):
        mine = pl.ds(a * rows, rows)
        delta[...] = jnp.zeros_like(delta)
        dqt[...] = jnp.zeros_like(dqt)

        def first_pass(b, carry):
            @pl.when(pair_active(seg, rank, a, b, rows))
            def _():
                theirs = pl.ds(pl.multiple_of(b * rows, rows), rows)
                gap = pair_distance(seg_rows, seg_keys, rank, b, a, rows)
                for h in range(heads):
                    slope = slopes[rank * heads + h]
                    s = dot_nt(ks[h, theirs, :], qs[h, mine, :]) - slope * gap
                    p = jnp.exp(s - lse[h : h + 1, mine])
                    dp = dot_nt(vs[h, theirs, :], do[h, mine, :])
                    delta[h : h + 1, :] += jnp.sum(p * dp, axis=0, keepdims=True)
                    prob[h, theirs, :] = p
                    dprob[h, theirs, :] = dp

            return carry

        lax.fori_loop(0, RANKS, first_pass, 0)

        def second_pass(b, carry):
            @pl.when(pair_active(seg, rank, a, b, rows))
            def _():
                theirs = pl.ds(pl.multiple_of(b * rows, rows), rows)
                for h in range(heads):
                    p = prob[h, theirs, :]
                    ds = (p * (dprob[h, theirs, :] - delta[h : h + 1, :])).astype(BF16)
                    dv[h, theirs, :] += dot(p.astype(BF16), do[h, mine, :])
                    dk[h, theirs, :] += dot(ds, qs[h, mine, :])
                    span = slice(h * dim, (h + 1) * dim)
                    dqt[span, :] += dot(kt[span, theirs], ds)

            return carry

        lax.fori_loop(0, RANKS, second_pass, 0)
        (d0, d1, d2, d3)[a][0:width, :] = (dqt[...] * scale).astype(BF16)

    for at, d_qkv in enumerate((d0, d1, d2, d3)):
        here = pl.ds(at * rows, rows)
        for h in range(heads):
            first = width + h * dim
            d_qkv[first : first + dim, :] = jnp.transpose(dk[h, here, :]).astype(BF16)
            first = 2 * width + h * dim
            d_qkv[first : first + dim, :] = jnp.transpose(dv[h, here, :]).astype(BF16)


def attention_backward(info, seg, slopes, blocks, w, qkv, lse, heads, dim):
    tok, lw = qkv.shape[0], heads * dim
    rows = tok // RANKS
    return pl.pallas_call(
        functools.partial(attention_backward_kernel, rows, heads, dim),
        name="attention_backward",
        out_shape=(shape((3 * lw, rows), BF16),) * RANKS,
        in_specs=[SM] * 3 + [VM] * 8,
        out_specs=(VM,) * RANKS,
        scratch_shapes=[
            scratch((heads, tok, dim), BF16),
            scratch((heads, tok, dim), BF16),
            scratch((lw, tok), BF16),
            scratch((heads, tok, dim), BF16),
            scratch((heads, tok, dim), BF16),
            scratch((tok, 128), jnp.int32),
            scratch((heads, tok, rows), F32),
            scratch((heads, tok, rows), F32),
            scratch((heads, tok, dim), F32),
            scratch((heads, tok, dim), F32),
            scratch((lw, rows), F32),
            scratch((heads, rows), F32),
        ],
        compiler_params=params(20),
        cost_estimate=pl.CostEstimate(
            flops=8 * 10**9, bytes_accessed=6 * 10**6, transcendentals=3 * 10**6
        ),
    )(info, seg, slopes, *blocks, w, qkv, lse, seg)


def line(vector):
    return vector[...].reshape(1, -1)


def join_tokens(rank, arrays, tokens_of, joined):
    part = arrays[0].shape[0]
    rows = arrays[0].shape[1] // RANKS
    for step, array in enumerate(arrays):
        first = pl.multiple_of((rank ^ step) * part, part)
        block = step ^ tokens_of
        joined[pl.ds(first, part), :] = array[:, block * rows : (block + 1) * rows]


def norm_one_kernel(
    info, own, near, far, cross, start, w, gain, shift, low, joined, unit, inverse
):
    join_tokens(info[0], (own, near, far, cross), 0, joined)
    x, inv = standardize(start[...].astype(F32) + dot_tn(joined[...], w[...]))
    unit[...] = x
    inverse[...] = inv
    low[...] = (x * line(gain) + line(shift)).astype(BF16)


def norm_one(info, parts, start, w, gain, shift):
    rows, width = start.shape
    return pl.pallas_call(
        norm_one_kernel,
        name="norm_one",
        out_shape=(
            shape((rows, width), BF16),
            shape((width, rows), BF16),
            shape((rows, width), F32),
            shape((rows, 1), F32),
        ),
        in_specs=[SM] + [VM] * 8,
        out_specs=(VM,) * 4,
        compiler_params=params(12),
        cost_estimate=pl.CostEstimate(
            flops=2 * rows * width * width, bytes_accessed=4 * 10**6, transcendentals=0
        ),
    )(info, *parts, start, w, gain, shift)


def norm_others_kernel(
    info, own, near, far, cross, s1, s2, s3, w, gain, shift, l1, l2, l3, j1, j2, j3
):
    for tokens_of, (start, low, joined) in enumerate(((s1, l1, j1), (s2, l2, j2), (s3, l3, j3))):
        join_tokens(info[0], (own, near, far, cross), tokens_of + 1, joined)
        x, _ = standardize(start[...].astype(F32) + dot_tn(joined[...], w[...]))
        low[...] = (x * line(gain) + line(shift)).astype(BF16)


def norm_others(info, parts, starts, w, gain, shift):
    rows, width = starts[0].shape
    results = pl.pallas_call(
        norm_others_kernel,
        name="norm_others",
        out_shape=(shape((rows, width), BF16),) * 3 + (shape((width, rows), BF16),) * 3,
        in_specs=[SM] + [VM] * 10,
        out_specs=(VM,) * 6,
        compiler_params=params(12),
        cost_estimate=pl.CostEstimate(
            flops=6 * rows * width * width, bytes_accessed=4 * 10**6, transcendentals=0
        ),
    )(info, *parts, *starts, w, gain, shift)
    return results[:3], results[3:]


def packing(rows, columns, part, rank):
    units = lax.broadcasted_iota(jnp.int32, (rows, columns), 0)
    packed = lax.broadcasted_iota(jnp.int32, (1, columns), 1)
    places = packed + rank * part
    for index in range(1, columns // part):
        places = places + jnp.where(packed >= index * part, (RANKS - 1) * part, 0)
    return (units == places).astype(BF16)


def pack_kernel(part, info, w_in, w_down, packed_in, packed_down):
    rank = info[0]
    width, hid = w_in.shape[0], w_down.shape[0]
    run = hid // 2
    select = packing(run, run // RANKS, part, rank)
    for index in range(4):
        piece = dot(w_in[:, index * run : (index + 1) * run], select)
        packed_in[:, index * run // RANKS : (index + 1) * run // RANKS] = piece.astype(BF16)
    if part % 16:
        for index in range(2):
            piece = dot_tn(select, w_down[index * run : (index + 1) * run, :])
            packed_down[index * run // RANKS : (index + 1) * run // RANKS, :] = piece.astype(BF16)
    else:
        for index in range(hid // RANKS // part):
            rows = pl.ds(pl.multiple_of((index * RANKS + rank) * part, part), part)
            packed_down[index * part : (index + 1) * part, :] = w_down[rows, :]


def pack_weights(info, w_in, w_out, part):
    width, hid = w_in.shape[0], w_out.shape[0]
    return pl.pallas_call(
        functools.partial(pack_kernel, part),
        name="pack_weights",
        out_shape=(shape((width, 2 * hid // RANKS), BF16), shape((hid // RANKS, width), BF16)),
        in_specs=[SM, VM, VM],
        out_specs=(VM, VM),
        compiler_params=params(14),
        cost_estimate=pl.CostEstimate(
            flops=4 * 10**9, bytes_accessed=17 * 10**6, transcendentals=0
        ),
    )(info, w_in, w_out)


def ffn_forward_kernel(
    low, unit, gain1, shift1, gain2, shift2, masked, cot, w_in, w_down,
    layer_out, d_h2, d_ff, slope, act, sums, acc, gates, ups,
):
    hid = w_down.shape[0]
    size = gates.shape[2]
    count = hid // size

    def project(block, slot):
        first = pl.multiple_of(block * size, size)
        gates[slot] = dot(low[...], w_in[:, pl.ds(first, size)])
        ups[slot] = dot(low[...], w_in[:, pl.ds(pl.multiple_of(hid + first, size), size)])

    def finish(block, slot):
        here = pl.ds(pl.multiple_of(block * size, size), size)
        up = ups[slot]
        value, grad = gelu_pair(gates[slot])
        act[:, here] = value.astype(BF16)
        slope[:, here] = (up * grad).astype(BF16)
        acc[...] += dot((value * up).astype(BF16), w_down[here, :])

    acc[...] = unit[...] * line(gain1) + line(shift1)
    project(0, 0)

    def pair(index, carry):
        block = index * 2
        project(block + 1, 1)
        finish(block, 0)
        project(block + 2, 0)
        finish(block + 1, 1)
        return carry

    lax.fori_loop(0, count // 2 - 1, pair, 0)
    project(count - 1, 1)
    finish(count - 2, 0)
    finish(count - 1, 1)
    x, inv = standardize(acc[...])
    layer_out[...] = (x * line(gain2) + line(shift2)).astype(BF16)
    places = lax.broadcasted_iota(jnp.int32, (low.shape[0], masked.shape[0]), 0)
    dy = exact_dot((places == line(masked)).astype(F32), cot[...])
    sums[0:1, :] = jnp.sum(dy * x, axis=0, keepdims=True)
    sums[1:2, :] = jnp.sum(dy, axis=0, keepdims=True)
    grad_in = standardize_back(dy * line(gain2), x, inv)
    d_h2[...] = grad_in
    d_ff[...] = grad_in.astype(BF16)


def ffn_forward(low, unit, gain1, shift1, gain2, shift2, masked, cot, w_in, w_out, size):
    rows, width = low.shape
    hid = w_out.shape[0]
    return pl.pallas_call(
        ffn_forward_kernel,
        name="ffn_forward",
        out_shape=(
            shape((rows, width), BF16),
            shape((rows, width), F32),
            shape((rows, width), BF16),
            shape((rows, hid), BF16),
            shape((rows, hid), BF16),
            shape((2, width), F32),
        ),
        in_specs=[VM] * 10,
        out_specs=(VM,) * 6,
        scratch_shapes=[
            scratch((rows, width), F32),
            scratch((2, rows, size), F32),
            scratch((2, rows, size), F32),
        ],
        compiler_params=params(14),
        cost_estimate=pl.CostEstimate(
            flops=6 * rows * width * hid, bytes_accessed=18 * 10**6, transcendentals=2 * rows * hid
        ),
    )(low, unit, gain1, shift1, gain2, shift2, masked, cot, w_in, w_out)


def ffn_backward_kernel(
    d_ff, d_h2, unit, inverse, gain1, sums2, act, slope, w_in, w_down, d_h1, sent, acc, hidden
):
    hid = w_down.shape[0]
    size = hidden.shape[2]
    count = hid // size

    def project(block, slot):
        here = pl.ds(pl.multiple_of(block * size, size), size)
        hidden[slot] = dot_nt(d_ff[...], w_down[here, :])

    def finish(block, slot):
        first = pl.multiple_of(block * size, size)
        here, there = pl.ds(first, size), pl.ds(pl.multiple_of(hid + first, size), size)
        d_hidden = hidden[slot]
        d_gate = (d_hidden * slope[:, here].astype(F32)).astype(BF16)
        d_up = (d_hidden * act[:, here].astype(F32)).astype(BF16)
        acc[...] += dot_nt(d_gate, w_in[:, here]) + dot_nt(d_up, w_in[:, there])

    acc[...] = d_h2[...]
    project(0, 0)

    def pair(index, carry):
        block = index * 2
        project(block + 1, 1)
        finish(block, 0)
        project(block + 2, 0)
        finish(block + 1, 1)
        return carry

    lax.fori_loop(0, count // 2 - 1, pair, 0)
    project(count - 1, 1)
    finish(count - 2, 0)
    finish(count - 1, 1)
    total = acc[...]
    rows = total.shape[0]
    x = unit[...]
    gain_sum = jnp.sum(total * x, axis=0, keepdims=True)
    shift_sum = jnp.sum(total, axis=0, keepdims=True)
    sums = jnp.concatenate([gain_sum, shift_sum, sums2[...]], axis=0)
    high = sums.astype(BF16).astype(F32)
    tail = jnp.concatenate([high, sums - high, jnp.zeros((8, sums.shape[1]), F32)], axis=0)
    grad = standardize_back(total * line(gain1), x, inverse[...])
    d_h1[...] = grad
    sent[0:rows, :] = grad.astype(BF16)
    sent[rows : rows + 16, :] = tail.astype(BF16)


def ffn_backward(d_ff, d_h2, unit, inverse, gain1, sums2, act, slope, w_in, w_out, size):
    rows, width = d_ff.shape
    hid = w_out.shape[0]
    return pl.pallas_call(
        ffn_backward_kernel,
        name="ffn_backward",
        out_shape=(shape((rows, width), F32), shape((rows + 16, width), BF16)),
        in_specs=[VM] * 10,
        out_specs=(VM,) * 2,
        scratch_shapes=[scratch((rows, width), F32), scratch((2, rows, size), F32)],
        compiler_params=params(14),
        cost_estimate=pl.CostEstimate(
            flops=6 * rows * width * hid, bytes_accessed=20 * 10**6, transcendentals=0
        ),
    )(d_ff, d_h2, unit, inverse, gain1, sums2, act, slope, w_in, w_out)


X_FIRST = (1, 2, 4)
Z_FIRST = (2, 1, 4)


def bit_of(value, mask):
    return (value // mask) % 2


def store_blocks(blocks, keep, send, place, order, columns):
    one, two, three = order
    odd = bit_of(place, one) == 1
    for index in range(8):
        if index & one:
            continue
        spot = bit_of(place ^ index, two) * 2 + bit_of(place ^ index, three)
        low, high = blocks(index), blocks(index | one)
        keep[spot, :, columns] = jnp.where(odd, high, low).astype(BF16)
        send[spot, :, columns] = jnp.where(odd, low, high).astype(BF16)


def row_blocks(grad):
    each = grad.shape[0] // 8
    return lambda index: grad[index * each : (index + 1) * each]


def ffn_grad_kernel(
    size, info, n0, n1, n2, n3, f0, f1, f2, f3, w_in, w_down,
    keep_gate, send_gate, keep_up, send_up, keep_down, send_down,
    tok_t, gates, ups, d_hiddens, hidden_t, d_gate, d_up, d_ff, down,
):
    toks, grads = (n0, n1, n2, n3), (f0, f1, f2, f3)
    rows = n0.shape[0]
    units = w_down.shape[0]
    for at in range(RANKS):
        here = slice(at * rows, (at + 1) * rows)
        d_ff[here, :] = grads[at][...]
        tok_t[:, here] = jnp.transpose(toks[at][...])

    def unit_block(step, carry):
        here = pl.ds(pl.multiple_of(step * size, size), size)
        there = pl.ds(pl.multiple_of(units + step * size, size), size)
        w_gate, w_up, w_rows = w_in[:, here], w_in[:, there], w_down[here, :]

        def project(at):
            slot = at % 2
            gates[slot] = dot(toks[at][...], w_gate)
            ups[slot] = dot(toks[at][...], w_up)
            d_hiddens[slot] = dot_nt(grads[at][...], w_rows)

        def finish(at):
            slot = at % 2
            here = slice(at * rows, (at + 1) * rows)
            value, grad = gelu_pair(gates[slot])
            up, d_hidden = ups[slot], d_hiddens[slot]
            hidden_t[:, here] = jnp.transpose((value * up).astype(BF16))
            d_gate[here, :] = (d_hidden * up * grad).astype(BF16)
            d_up[here, :] = (d_hidden * value).astype(BF16)

        project(0)
        for at in range(RANKS):
            if at + 1 < RANKS:
                project(at + 1)
            finish(at)
        total = dot(tok_t[...], d_gate[...])
        store_blocks(row_blocks(total), keep_gate, send_gate, info[1], Z_FIRST, here)
        total = dot(tok_t[...], d_up[...])
        store_blocks(row_blocks(total), keep_up, send_up, info[1], Z_FIRST, here)
        down[here, :] = dot(hidden_t[...], d_ff[...])
        return carry

    lax.fori_loop(0, units // size, unit_block, 0)
    store_blocks(row_blocks(down), keep_down, send_down, info[1], X_FIRST, slice(None))


def ffn_grad(info, toks, grads, w_in, w_down, size):
    rows, width = toks[0].shape
    units = w_down.shape[0]
    tok = rows * RANKS
    dims = [(4, width // 8, units)] * 4 + [(4, units // 8, width)] * 2
    return pl.pallas_call(
        functools.partial(ffn_grad_kernel, size),
        name="ffn_grad",
        out_shape=[shape(each, BF16) for each in dims],
        in_specs=[SM] + [VM] * 10,
        out_specs=[VM] * 6,
        scratch_shapes=[
            scratch((width, tok), BF16),
            scratch((2, rows, size), F32),
            scratch((2, rows, size), F32),
            scratch((2, rows, size), F32),
            scratch((size, tok), BF16),
            scratch((tok, size), BF16),
            scratch((tok, size), BF16),
            scratch((tok, width), BF16),
            scratch((units, width), F32),
        ],
        compiler_params=params(18),
        cost_estimate=pl.CostEstimate(
            flops=12 * tok * width * units,
            bytes_accessed=8 * 10**6,
            transcendentals=2 * tok * units,
        ),
    )(info, *toks, *grads, w_in, w_down)


def qkv_grad_kernel(
    info, x0, x1, x2, x3, d0, d1, d2, d3, j0, j1, j2, j3, g0, g1, g2, g3, keep, send, columns, grad
):
    rows, width = x0.shape
    part = width // RANKS
    total = 0.0
    for x, d_qkv in zip((x0, x1, x2, x3), (d0, d1, d2, d3)):
        total = total + dot(d_qkv[...], x[...])
    grad[:, : 3 * part] = jnp.transpose(total)
    for value in range(RANKS):

        @pl.when(info[0] == value)
        def _():
            for at, g in enumerate((g0, g1, g2, g3)):
                columns[at] = g[0:rows, value * part : (value + 1) * part]

    total = 0.0
    sums = 0.0
    for at, (joined, g) in enumerate(zip((j0, j1, j2, j3), (g0, g1, g2, g3))):
        total = total + dot(joined[...], columns[at])
        pair = g[rows : rows + 16, :].astype(F32)
        sums = sums + pair[0:4] + pair[4:8]
    grad[:, 3 * part :] = total
    high = sums.astype(BF16).astype(F32)
    tail = jnp.concatenate([high, sums - high], axis=0)
    each = width // 8

    def blocks(index):
        return jnp.concatenate([grad[index * each : (index + 1) * each], tail], axis=0)

    store_blocks(blocks, keep, send, info[1], X_FIRST, slice(None))


def qkv_grad(info, blocks, d_qkv, joined, d_proj):
    rows, width = blocks[0].shape
    return pl.pallas_call(
        qkv_grad_kernel,
        name="qkv_grad",
        out_shape=(shape((4, width // 8 + 8, width), BF16),) * 2,
        in_specs=[SM] + [VM] * 16,
        out_specs=(VM, VM),
        scratch_shapes=[
            scratch((RANKS, rows, width // RANKS), BF16),
            scratch((width, width), F32),
        ],
        compiler_params=params(14),
        cost_estimate=pl.CostEstimate(
            flops=8 * rows * width * width, bytes_accessed=4 * 10**6, transcendentals=0
        ),
    )(info, *blocks, *d_qkv, *joined, *d_proj)


def unpack(part, packed, wide, first):
    few = packed.shape[1] // RANKS
    for run in range(few // part):
        pieces = []
        for value in range(RANKS):
            at = value * few + run * part
            pieces.append(packed[:, at : at + part])
        at = first + run * RANKS * part
        wide[:, at : at + RANKS * part] = jnp.concatenate(pieces, axis=1).astype(F32)


def join_early_kernel(info, b0, b1, b2, b3, down, packed):
    rows, columns = b0.shape
    few = columns // 2
    for step, block in enumerate((b0, b1, b2, b3)):
        there = info[0] ^ step
        packed[:, pl.ds(pl.multiple_of(there * few, few), few)] = block[:, few:]
        down[pl.ds(pl.multiple_of(there * rows, rows), rows), :] = block[:, :few].astype(F32)


def join_late_kernel(part, info, b0, b1, b2, b3, gates, wide, out, rest, ups):
    width = rest.shape[1]
    heads = width // RANKS
    few = gates.shape[1] // RANKS
    blocks = (b0, b1, b2, b3)
    for step, block in enumerate(blocks):
        there = pl.multiple_of((info[0] ^ step) * few, few)
        ups[:, pl.ds(there, few)] = block[:, :few]
    unpack(part, gates, wide, 0)
    unpack(part, ups, wide, RANKS * few)
    for value in range(RANKS):

        @pl.when(info[0] == value)
        def _():
            for step, block in enumerate(blocks):
                there = (value ^ step) * heads
                for third in range(3):
                    first = few + third * heads
                    at = third * width + there
                    out[:, at : at + heads] = block[:, first : first + heads].astype(F32)
                first = few + 3 * heads
                rest[:, there : there + heads] = block[:, first:].astype(F32)


def join_early(info, blocks):
    rows, columns = blocks[0].shape
    if rows % 8:
        stacked = jnp.stack(blocks)[info[0] ^ jnp.arange(RANKS)]
        few = columns // 2
        gates = jnp.concatenate(list(stacked[:, :, few:]), axis=1)
        return stacked[:, :, :few].reshape(-1, few).astype(F32), gates
    return pl.pallas_call(
        join_early_kernel,
        name="join_early",
        out_shape=(
            shape((rows * RANKS, columns // 2), F32),
            shape((rows, RANKS * columns // 2), BF16),
        ),
        in_specs=[SM] + [VM] * 4,
        out_specs=(VM, VM),
        compiler_params=params(8),
        cost_estimate=NO_COST,
    )(info, *blocks)


def join_late(info, blocks, gates, part):
    rows, columns = blocks[0].shape
    width = columns // 2
    if RANKS * part % 128:
        stacked = jnp.stack(blocks)[info[0] ^ jnp.arange(RANKS)].astype(F32)
        both = [gates.astype(F32), jnp.concatenate(list(stacked[:, :, :width]), axis=1)]
        wide = [each.reshape(rows, RANKS, -1, part).transpose(0, 2, 1, 3) for each in both]
        wide = jnp.concatenate([each.reshape(rows, -1) for each in wide], axis=1)
        heads = stacked[:, :, width:].reshape(RANKS, rows, RANKS, -1).transpose(1, 2, 0, 3)
        heads = heads.reshape(rows, RANKS, -1)
        return wide, heads[:, :3].reshape(rows, -1), heads[:, 3]
    return pl.pallas_call(
        functools.partial(join_late_kernel, part),
        name="join_late",
        out_shape=(
            shape((rows, 2 * RANKS * width), F32),
            shape((rows, 3 * width), F32),
            shape((rows, width), F32),
        ),
        in_specs=[SM] + [VM] * 5,
        out_specs=(VM,) * 3,
        scratch_shapes=[scratch((rows, RANKS * width), BF16)],
        compiler_params=params(14),
        cost_estimate=NO_COST,
    )(info, *blocks, gates)


def token_grad_kernel(
    info, own, near, far, cross, w, d_h1, masked, tokens, replacement, joined
):
    rows, width = d_h1.shape
    part = width // RANKS
    for step, block in enumerate((own, near, far, cross)):
        for third in range(3):
            first = pl.multiple_of(third * width + (info[0] ^ step) * part, part)
            joined[pl.ds(first, part), :] = block[third * part : (third + 1) * part, :]
    grad = d_h1[...] + jnp.transpose(dot(w[...], joined[...]))
    count = masked.shape[0]
    places = lax.broadcasted_iota(jnp.int32, (rows, count), 0)
    select = (places == line(masked)).astype(F32)
    hit = jnp.max(select, axis=1, keepdims=True)
    tokens[...] = jnp.where(hit > 0.5, 0.0, grad)
    replacement[...] = lax.dot_general(
        select, grad, (((0,), (0,)), ((), ())),
        precision=lax.Precision.HIGHEST, preferred_element_type=F32,
    )


def token_grad(info, parts, w, d_h1, masked):
    rows, width = d_h1.shape
    return pl.pallas_call(
        token_grad_kernel,
        name="token_grad",
        out_shape=(shape((rows, width), F32), shape((masked.shape[0], width), F32)),
        in_specs=[SM] + [VM] * 7,
        out_specs=(VM, VM),
        scratch_shapes=[scratch((3 * width, rows), BF16)],
        compiler_params=params(16),
        cost_estimate=pl.CostEstimate(
            flops=6 * rows * width * width, bytes_accessed=8 * 10**6, transcendentals=0
        ),
    )(info, *parts, w, d_h1, masked)


def after(value, *others):
    return lax.optimization_barrier((value,) + others)[0]


def flip(value, axis, bits):
    count = lax.axis_size(axis)
    return lax.ppermute(value, axis, [(index, index ^ bits) for index in range(count)])


def gather_blocks(value):
    far = flip(value, "sp", 2)
    near = flip(value, "sp", 1)
    cross = flip(far, "sp", 1)
    return [value, near, far, cross]


def exchange_blocks(blocks):
    via = flip(blocks[3], "sp", 1)
    near = flip(blocks[1], "sp", 1)
    far = flip(blocks[2], "sp", 2)
    cross = flip(via, "sp", 2)
    return [blocks[0], near, far, cross]


def small_mesh():
    return lax.axis_size("dp") == 8


NO_COST = pl.CostEstimate(flops=0, bytes_accessed=0, transcendentals=0)


def tidy_sums(value):
    first = value.shape[1] - 8
    sums = value[:, first : first + 4] + value[:, first + 4 :]
    high = sums.astype(BF16).astype(F32)
    return jnp.concatenate([value[:, :first], high, sums - high], axis=1)


def halve_kernel(with_sums, keep, came, kept, sent):
    half = keep.shape[0] // 2
    value = keep[...].astype(F32) + came[...].astype(F32)
    if with_sums:
        value = tidy_sums(value)
    kept[...] = value[:half]
    sent[...] = value[half:].astype(BF16)


def halve(keep, came, with_sums=False):
    dims = (keep.shape[0] // 2,) + keep.shape[1:]
    return pl.pallas_call(
        functools.partial(halve_kernel, with_sums),
        name="halve",
        out_shape=(shape(dims, F32), shape(dims, BF16)),
        in_specs=[VM] * 2,
        out_specs=(VM, VM),
        compiler_params=params(12),
        cost_estimate=NO_COST,
    )(keep, came)


def send_first(send, order):
    return flip(send, "dp", order[0]) if small_mesh() else send


def next_half(keep, came, with_sums=False):
    return halve(keep, came, with_sums) if small_mesh() else (keep, came)


def send_on(send, bits):
    return flip(send, "dp", bits) if small_mesh() else send


def send_second(keep, came, order, with_sums=False):
    keep, send = next_half(keep, came, with_sums)
    return keep, send_on(send, order[1])


def send_third(keep, came, order, with_sums=False):
    keep, send = next_half(keep, came, with_sums)
    return keep, send_on(send, order[2])


def natural_blocks(keep, send, order):
    both = jnp.concatenate([keep, send], axis=0).astype(F32)
    places = []
    for index in range(8):
        bits = [1 if index & mask else 0 for mask in order]
        places.append(both[bits[0] * 4 + bits[1] * 2 + bits[2]])
    return places


def scatter_sum(blocks):
    grad = jnp.concatenate(blocks, axis=0)
    return lax.psum_scatter(grad, "dp", scatter_dimension=0, tiled=True).astype(BF16)


def finish_pair_kernel(keep_a, came_a, keep_b, came_b, out):
    columns = keep_a.shape[2]
    out[:, :columns] = (keep_a[0] + came_a[0].astype(F32)).astype(BF16)
    out[:, columns:] = (keep_b[0] + came_b[0].astype(F32)).astype(BF16)


def finish_pair(keep_a, came_a, order_a, keep_b, came_b, order_b):
    if not small_mesh():
        first = scatter_sum(natural_blocks(keep_a, came_a, order_a))
        second = scatter_sum(natural_blocks(keep_b, came_b, order_b))
        return jnp.concatenate([first, second], axis=1)
    _, rows, columns = keep_a.shape
    return pl.pallas_call(
        finish_pair_kernel,
        name="finish_pair",
        out_shape=shape((rows, columns + keep_b.shape[2]), BF16),
        in_specs=[VM] * 4,
        out_specs=VM,
        compiler_params=params(8),
        cost_estimate=NO_COST,
    )(keep_a, came_a, keep_b, came_b)


def finish_heads_kernel(keep_u, came_u, keep, came, out, sums):
    columns = keep_u.shape[2]
    rows = out.shape[0]
    out[:, :columns] = (keep_u[0] + came_u[0].astype(F32)).astype(BF16)
    total = keep[0] + came[0].astype(F32)
    out[:, columns:] = total[:rows].astype(BF16)
    sums[...] = total[rows : rows + 4] + total[rows + 4 :]


def finish_heads(keep_u, came_u, keep, came):
    _, rows, columns = keep.shape
    rows = rows - 8
    if not small_mesh():
        blocks = natural_blocks(keep, came, X_FIRST)
        sums = blocks[0][rows : rows + 4] + blocks[0][rows + 4 :]
        first = scatter_sum(natural_blocks(keep_u, came_u, Z_FIRST))
        second = scatter_sum([block[:rows] for block in blocks])
        return jnp.concatenate([first, second], axis=1), lax.psum(sums, "dp")
    return pl.pallas_call(
        finish_heads_kernel,
        name="finish_heads",
        out_shape=(shape((rows, keep_u.shape[2] + columns), BF16), shape((4, columns), F32)),
        in_specs=[VM] * 4,
        out_specs=(VM, VM),
        compiler_params=params(8),
        cost_estimate=NO_COST,
    )(keep_u, came_u, keep, came)


def local(
    tokens,
    segment_ids,
    masked_rows,
    replacement,
    cotangent,
    w_qkv,
    w_out_attn,
    w_in_ff,
    w_out_ff,
    gain_one,
    shift_one,
    gain_two,
    shift_two,
):
    rows_dev, width = tokens.shape
    rank = lax.axis_index("sp")
    heads = HEADS // RANKS
    dim = width // HEADS
    part = heads * dim
    slopes = alibi_slopes(HEADS)

    select = jnp.arange(rows_dev, dtype=jnp.int32)[:, None] == masked_rows[None, :]
    hit = jnp.any(select, axis=1, keepdims=True)
    placed = dot(select.astype(BF16), replacement)
    start = jnp.where(hit, placed.astype(BF16), tokens)
    start_far = flip(start, "sp", 2)
    start_near = flip(start, "sp", 1)
    place = lax.axis_index("dp")
    place = place if small_mesh() else place * 0
    spot = jnp.stack([rank, place]).astype(jnp.int32)

    w_rank = jnp.concatenate(
        [
            lax.dynamic_slice_in_dim(w_qkv, third * width + rank * part, part, 1)
            for third in range(3)
        ],
        axis=1,
    )
    start_cross = flip(after(start_far, w_rank, spot), "sp", 1)
    start_blocks = [start, start_near, start_far, start_cross]
    qkv, attn, lse = attention_forward(
        spot, segment_ids, slopes, start_blocks, w_rank, heads, dim
    )
    attn_far = flip(attn, "sp", 2)
    attn_near = flip(attn, "sp", 1)
    part_units = w_out_ff.shape[0] // lax.axis_size("dp") // RANKS
    packed_in, packed_down = pack_weights(after(spot, lse), w_in_ff, w_out_ff, part_units)
    attn_cross = flip(after(attn_far, packed_in), "sp", 1)
    attn_parts = [attn, attn_near, attn_far, attn_cross]
    low, joined, unit, inverse = norm_one(
        spot, attn_parts, start, w_out_attn, gain_one, shift_one
    )
    layer_out, d_h2, d_ff, slope, act, sums2 = ffn_forward(
        low, unit, gain_one, shift_one, gain_two, shift_two,
        masked_rows, cotangent, w_in_ff, w_out_ff, 768,
    )
    d_ff_far = flip(d_ff, "sp", 2)
    d_ff_near = flip(d_ff, "sp", 1)
    d_h1, sent = ffn_backward(
        d_ff, d_h2, unit, inverse, gain_one, sums2, act, slope, w_in_ff, w_out_ff, 768
    )
    lows, others_joined = norm_others(
        after(spot, sent), attn_parts, start_blocks[1:], w_out_attn, gain_one, shift_one
    )
    d_ff_far = after(d_ff_far, lows[0])
    d_ff_cross = flip(d_ff_far, "sp", 1)
    d_ff_blocks = [d_ff, d_ff_near, d_ff_far, d_ff_cross]
    far = flip(sent, "sp", 2)
    near = flip(sent, "sp", 1)

    keep_g, send_g, keep_u, send_u, keep_d, send_d = ffn_grad(
        spot, [low, *lows], d_ff_blocks, packed_in, packed_down, 256
    )
    came_g = send_first(send_g, Z_FIRST)
    came_d = send_first(send_d, X_FIRST)
    cross = flip(after(far, keep_g), "sp", 1)
    d_proj_blocks = [sent, near, far, cross]

    d_qkv = attention_backward(
        spot, segment_ids, slopes, d_proj_blocks, w_out_attn, qkv, lse, heads, dim
    )
    parts = exchange_blocks(d_qkv)
    came_u = send_first(after(send_u, d_qkv[0]), Z_FIRST)
    keep_g, came_g = send_second(keep_g, after(came_g, d_qkv[0]), Z_FIRST)
    keep_d, came_d = send_second(keep_d, after(came_d, keep_g), X_FIRST)
    keep_q, send_q = qkv_grad(
        after(spot, keep_d), start_blocks, d_qkv, [joined, *others_joined], d_proj_blocks
    )
    keep_g, came_g = send_third(keep_g, after(came_g, keep_q), Z_FIRST)
    came_q = send_first(after(send_q, keep_g), X_FIRST)
    keep_d, came_d = send_third(keep_d, after(came_d, keep_g), X_FIRST)
    keep_u, came_u = send_second(keep_u, after(came_u, keep_d), Z_FIRST)
    keep_q, send_q = next_half(keep_q, after(came_q, keep_u, parts), True)
    early = finish_pair(keep_d, after(came_d, keep_q), X_FIRST, keep_g, came_g, Z_FIRST)
    came_q = send_on(after(send_q, early), X_FIRST[1])
    far = flip(early, "sp", 2)
    near = flip(early, "sp", 1)
    keep_u, came_u = send_third(keep_u, after(came_u, early), Z_FIRST)
    keep_q, came_q = send_third(keep_q, after(came_q, keep_u, came_u), X_FIRST, True)
    late, norm_sums = finish_heads(keep_u, came_u, keep_q, came_q)
    early_blocks = [early, near, far, flip(after(far, late), "sp", 1)]
    late_blocks = gather_blocks(late)
    grad_tokens, grad_replacement = token_grad(
        after(spot, late), parts, w_qkv, d_h1, masked_rows
    )
    grad_down, gates = join_early(after(spot, late), early_blocks)
    grad_in, grad_qkv, grad_out = join_late(spot, late_blocks, gates, part_units)

    return (
        layer_out,
        grad_tokens,
        grad_replacement,
        grad_qkv,
        grad_out,
        grad_in,
        grad_down,
        norm_sums[0],
        norm_sums[1],
        norm_sums[2],
        norm_sums[3],
    )


def solution(mesh):
    tokens = P(("dp", "sp"), None)
    rows = P("dp", None)
    return jax.shard_map(
        local,
        mesh=mesh,
        in_specs=(tokens, rows, P(("dp", "sp")), tokens, tokens) + (P(),) * 8,
        out_specs=(tokens,) * 3 + (rows,) * 4 + (P(),) * 4,
        check_vma=False,
    )
```

```python
import functools
import math

import jax
import jax.numpy as jnp
from jax import lax
from jax.experimental import pallas as pl
from jax.experimental.pallas import tpu as pltpu
from jax.sharding import PartitionSpec as P

HEADS = 12
RANKS = 4
EPSILON = 1e-05
FAR = 1e30
F32 = jnp.float32
BF16 = jnp.bfloat16
VM = pl.BlockSpec(memory_space=pltpu.VMEM)
SM = pl.BlockSpec(memory_space=pltpu.SMEM)


def shape(dims, kind):
    return jax.ShapeDtypeStruct(dims, kind)


def scratch(dims, kind):
    return pltpu.VMEM(dims, kind)


def params(mebibytes):
    return pltpu.CompilerParams(vmem_limit_bytes=mebibytes << 20)


def alibi_slopes(head_count):
    nearest = 2 ** int(math.floor(math.log2(head_count)))
    base_list = [2.0 ** (-8.0 * (index + 1) / nearest) for index in range(nearest)]
    extra_list = [
        2.0 ** (-8.0 * (2 * index + 1) / (2 * nearest)) for index in range(head_count - nearest)
    ]
    return jnp.array(base_list + extra_list, dtype=F32)


def dot(a, b):
    return jnp.dot(a, b, preferred_element_type=F32)


def dot_nt(a, b):
    return lax.dot_general(a, b, (((1,), (1,)), ((), ())), preferred_element_type=F32)


def dot_tn(a, b):
    return lax.dot_general(a, b, (((0,), (0,)), ((), ())), preferred_element_type=F32)


def exact_dot(a, b):
    return jnp.dot(a, b, precision=lax.Precision.HIGHEST, preferred_element_type=F32)


def standardize(value):
    center = value - jnp.mean(value, axis=-1, keepdims=True)
    spread = jnp.mean(center * center, axis=-1, keepdims=True)
    inverse = lax.rsqrt(spread + EPSILON)
    return center * inverse, inverse


def standardize_back(grad, unit, inverse):
    mean = jnp.mean(grad, axis=-1, keepdims=True)
    return inverse * (grad - mean - unit * jnp.mean(grad * unit, axis=-1, keepdims=True))


def gelu_pair(x):
    cdf = 0.5 * (1.0 + lax.erf(x * math.sqrt(0.5)))
    pdf = jnp.exp(-0.5 * x * x) * (1.0 / math.sqrt(2.0 * math.pi))
    return x * cdf, cdf + x * pdf


def pair_active(seg, rank, first, second, rows):
    one, two = rank ^ first, rank ^ second
    low, high = jnp.minimum(one, two), jnp.maximum(one, two)
    return jnp.logical_or(one == two, seg[0, low * rows + rows - 1] == seg[0, high * rows])


def key_sequences(seg_rows, seg_keys, rank, rows):
    for at in range(RANKS):
        first = pl.multiple_of((rank ^ at) * rows, rows)
        line = jnp.broadcast_to(seg_rows[:, pl.ds(first, rows)], (128, rows))
        seg_keys[at * rows : (at + 1) * rows, :] = jnp.transpose(line)


def pair_distance(seg_rows, seg_keys, rank, keys_at, query_at, rows):
    key_pos, query_pos = (rank ^ keys_at) * rows, (rank ^ query_at) * rows
    down = lax.broadcasted_iota(jnp.int32, (rows, rows), 0)
    across = lax.broadcasted_iota(jnp.int32, (rows, rows), 1)
    gap = jnp.abs(down - across + (key_pos - query_pos)).astype(F32)
    seg_q = seg_rows[:, pl.ds(pl.multiple_of(query_pos, rows), rows)]
    seg_k = seg_keys[pl.ds(pl.multiple_of(keys_at * rows, rows), rows), 0:1]
    return jnp.where(seg_k == seg_q, gap, FAR)


def attention_forward_kernel(
    rows, heads, dim, info, seg, slopes, x0, x1, x2, x3, w, seg_rows,
    qkv_out, out_t, lse, qs, ks, vt, dist, seg_keys, score, peak,
):
    rank = info[0]
    width = heads * dim
    key_sequences(seg_rows, seg_keys, rank, rows)
    for at, x in enumerate((x0, x1, x2, x3)):
        qkv = dot(x[...], w[...]).astype(BF16)
        here = pl.ds(at * rows, rows)
        qkv_out[here, :] = qkv
        for h in range(heads):
            qs[h, here, :] = (qkv[:, h * dim : (h + 1) * dim] * dim**-0.5).astype(BF16)
            ks[h, here, :] = qkv[:, width + h * dim : width + (h + 1) * dim]
        vt[:, here] = jnp.transpose(qkv[:, 2 * width :])

    for a in range(RANKS):
        mine = pl.ds(a * rows, rows)
        peak[...] = jnp.full_like(peak, -jnp.inf)

        def first_pass(b, carry):
            @pl.when(pair_active(seg, rank, a, b, rows))
            def _():
                theirs = pl.ds(pl.multiple_of(b * rows, rows), rows)
                gap = pair_distance(seg_rows, seg_keys, rank, b, a, rows)
                for h in range(heads):
                    slope = slopes[rank * heads + h]
                    s = dot_nt(ks[h, theirs, :], qs[h, mine, :]) - slope * gap
                    score[h, theirs, :] = s
                    peak[h : h + 1, :] = jnp.maximum(
                        peak[h : h + 1, :], jnp.max(s, axis=0, keepdims=True)
                    )

            return carry

        lax.fori_loop(0, RANKS, first_pass, 0)

        def second_pass(b, carry):
            def add(carry):
                theirs = pl.ds(pl.multiple_of(b * rows, rows), rows)
                result = []
                for h in range(heads):
                    acc, total = carry[h]
                    p = jnp.exp(score[h, theirs, :] - peak[h : h + 1, :])
                    total = total + jnp.sum(p, axis=0, keepdims=True)
                    span = slice(h * dim, (h + 1) * dim)
                    result.append((acc + dot(vt[span, theirs], p.astype(BF16)), total))
                return tuple(result)

            return lax.cond(pair_active(seg, rank, a, b, rows), add, lambda carry: carry, carry)

        empty = (jnp.zeros((dim, rows), F32), jnp.zeros((1, rows), F32))
        sums = lax.fori_loop(0, RANKS, second_pass, (empty,) * heads)
        for h in range(heads):
            acc, total = sums[h]
            span = slice(h * dim, (h + 1) * dim)
            out_t[span, mine] = (acc / total).astype(BF16)
            lse[h : h + 1, mine] = peak[h : h + 1, :] + jnp.log(total)


def attention_forward(info, seg, slopes, blocks, w, heads, dim):
    rows = blocks[0].shape[0]
    tok, lw = rows * RANKS, heads * dim
    return pl.pallas_call(
        functools.partial(attention_forward_kernel, rows, heads, dim),
        name="attention_forward",
        out_shape=(
            shape((tok, 3 * lw), BF16),
            shape((lw, tok), BF16),
            shape((heads, tok), F32),
        ),
        in_specs=[SM] * 3 + [VM] * 6,
        out_specs=(VM,) * 3,
        scratch_shapes=[
            scratch((heads, tok, dim), BF16),
            scratch((heads, tok, dim), BF16),
            scratch((lw, tok), BF16),
            scratch((rows, rows), F32),
            scratch((tok, 128), jnp.int32),
            scratch((heads, tok, rows), F32),
            scratch((heads, rows), F32),
        ],
        compiler_params=params(14),
        cost_estimate=pl.CostEstimate(
            flops=4 * 10**9, bytes_accessed=6 * 10**6, transcendentals=3 * 10**6
        ),
    )(info, seg, slopes, *blocks, w, seg)


def attention_backward_kernel(
    rows, heads, dim, info, seg, slopes, g0, g1, g2, g3, w, qkv, lse, seg_rows,
    d0, d1, d2, d3, qs, ks, kt, vs, do, seg_keys, prob, dprob, dk, dv, dqt, delta,
):
    rank = info[0]
    width = heads * dim
    scale = dim**-0.5
    key_sequences(seg_rows, seg_keys, rank, rows)
    w_rank = w[pl.ds(pl.multiple_of(rank * width, width), width), :]
    for at, g in enumerate((g0, g1, g2, g3)):
        here = pl.ds(at * rows, rows)
        grad = dot_nt(g[0:rows, :], w_rank).astype(BF16)
        value = qkv[here, :]
        kt[:, here] = jnp.transpose(value[:, width : 2 * width])
        for h in range(heads):
            do[h, here, :] = grad[:, h * dim : (h + 1) * dim]
            qs[h, here, :] = (value[:, h * dim : (h + 1) * dim] * scale).astype(BF16)
            ks[h, here, :] = value[:, width + h * dim : width + (h + 1) * dim]
            vs[h, here, :] = value[:, 2 * width + h * dim : 2 * width + (h + 1) * dim]
    dk[...] = jnp.zeros_like(dk)
    dv[...] = jnp.zeros_like(dv)

    for a in range(RANKS):
        mine = pl.ds(a * rows, rows)
        delta[...] = jnp.zeros_like(delta)
        dqt[...] = jnp.zeros_like(dqt)

        def first_pass(b, carry):
            @pl.when(pair_active(seg, rank, a, b, rows))
            def _():
                theirs = pl.ds(pl.multiple_of(b * rows, rows), rows)
                gap = pair_distance(seg_rows, seg_keys, rank, b, a, rows)
                for h in range(heads):
                    slope = slopes[rank * heads + h]
                    s = dot_nt(ks[h, theirs, :], qs[h, mine, :]) - slope * gap
                    p = jnp.exp(s - lse[h : h + 1, mine])
                    dp = dot_nt(vs[h, theirs, :], do[h, mine, :])
                    delta[h : h + 1, :] += jnp.sum(p * dp, axis=0, keepdims=True)
                    prob[h, theirs, :] = p
                    dprob[h, theirs, :] = dp

            return carry

        lax.fori_loop(0, RANKS, first_pass, 0)

        def second_pass(b, carry):
            @pl.when(pair_active(seg, rank, a, b, rows))
            def _():
                theirs = pl.ds(pl.multiple_of(b * rows, rows), rows)
                for h in range(heads):
                    p = prob[h, theirs, :]
                    ds = (p * (dprob[h, theirs, :] - delta[h : h + 1, :])).astype(BF16)
                    dv[h, theirs, :] += dot(p.astype(BF16), do[h, mine, :])
                    dk[h, theirs, :] += dot(ds, qs[h, mine, :])
                    span = slice(h * dim, (h + 1) * dim)
                    dqt[span, :] += dot(kt[span, theirs], ds)

            return carry

        lax.fori_loop(0, RANKS, second_pass, 0)
        (d0, d1, d2, d3)[a][0:width, :] = (dqt[...] * scale).astype(BF16)

    for at, d_qkv in enumerate((d0, d1, d2, d3)):
        here = pl.ds(at * rows, rows)
        for h in range(heads):
            first = width + h * dim
            d_qkv[first : first + dim, :] = jnp.transpose(dk[h, here, :]).astype(BF16)
            first = 2 * width + h * dim
            d_qkv[first : first + dim, :] = jnp.transpose(dv[h, here, :]).astype(BF16)


def attention_backward(info, seg, slopes, blocks, w, qkv, lse, heads, dim):
    tok, lw = qkv.shape[0], heads * dim
    rows = tok // RANKS
    return pl.pallas_call(
        functools.partial(attention_backward_kernel, rows, heads, dim),
        name="attention_backward",
        out_shape=(shape((3 * lw, rows), BF16),) * RANKS,
        in_specs=[SM] * 3 + [VM] * 8,
        out_specs=(VM,) * RANKS,
        scratch_shapes=[
            scratch((heads, tok, dim), BF16),
            scratch((heads, tok, dim), BF16),
            scratch((lw, tok), BF16),
            scratch((heads, tok, dim), BF16),
            scratch((heads, tok, dim), BF16),
            scratch((tok, 128), jnp.int32),
            scratch((heads, tok, rows), F32),
            scratch((heads, tok, rows), F32),
            scratch((heads, tok, dim), F32),
            scratch((heads, tok, dim), F32),
            scratch((lw, rows), F32),
            scratch((heads, rows), F32),
        ],
        compiler_params=params(20),
        cost_estimate=pl.CostEstimate(
            flops=8 * 10**9, bytes_accessed=6 * 10**6, transcendentals=3 * 10**6
        ),
    )(info, seg, slopes, *blocks, w, qkv, lse, seg)


def line(vector):
    return vector[...].reshape(1, -1)


def join_tokens(rank, arrays, tokens_of, joined):
    part = arrays[0].shape[0]
    rows = arrays[0].shape[1] // RANKS
    for step, array in enumerate(arrays):
        first = pl.multiple_of((rank ^ step) * part, part)
        block = step ^ tokens_of
        joined[pl.ds(first, part), :] = array[:, block * rows : (block + 1) * rows]


def norm_one_kernel(
    info, own, near, far, cross, start, w, gain, shift, low, joined, unit, inverse
):
    join_tokens(info[0], (own, near, far, cross), 0, joined)
    x, inv = standardize(start[...].astype(F32) + dot_tn(joined[...], w[...]))
    unit[...] = x
    inverse[...] = inv
    low[...] = (x * line(gain) + line(shift)).astype(BF16)


def norm_one(info, parts, start, w, gain, shift):
    rows, width = start.shape
    return pl.pallas_call(
        norm_one_kernel,
        name="norm_one",
        out_shape=(
            shape((rows, width), BF16),
            shape((width, rows), BF16),
            shape((rows, width), F32),
            shape((rows, 1), F32),
        ),
        in_specs=[SM] + [VM] * 8,
        out_specs=(VM,) * 4,
        compiler_params=params(12),
        cost_estimate=pl.CostEstimate(
            flops=2 * rows * width * width, bytes_accessed=4 * 10**6, transcendentals=0
        ),
    )(info, *parts, start, w, gain, shift)


def norm_others_kernel(
    info, own, near, far, cross, s1, s2, s3, w, gain, shift, l1, l2, l3, j1, j2, j3
):
    for tokens_of, (start, low, joined) in enumerate(((s1, l1, j1), (s2, l2, j2), (s3, l3, j3))):
        join_tokens(info[0], (own, near, far, cross), tokens_of + 1, joined)
        x, _ = standardize(start[...].astype(F32) + dot_tn(joined[...], w[...]))
        low[...] = (x * line(gain) + line(shift)).astype(BF16)


def norm_others(info, parts, starts, w, gain, shift):
    rows, width = starts[0].shape
    results = pl.pallas_call(
        norm_others_kernel,
        name="norm_others",
        out_shape=(shape((rows, width), BF16),) * 3 + (shape((width, rows), BF16),) * 3,
        in_specs=[SM] + [VM] * 10,
        out_specs=(VM,) * 6,
        compiler_params=params(12),
        cost_estimate=pl.CostEstimate(
            flops=6 * rows * width * width, bytes_accessed=4 * 10**6, transcendentals=0
        ),
    )(info, *parts, *starts, w, gain, shift)
    return results[:3], results[3:]


def packing(rows, columns, part, rank):
    units = lax.broadcasted_iota(jnp.int32, (rows, columns), 0)
    packed = lax.broadcasted_iota(jnp.int32, (1, columns), 1)
    places = packed + rank * part
    for index in range(1, columns // part):
        places = places + jnp.where(packed >= index * part, (RANKS - 1) * part, 0)
    return (units == places).astype(BF16)


def pack_kernel(part, info, w_in, w_down, packed_in, packed_down):
    rank = info[0]
    width, hid = w_in.shape[0], w_down.shape[0]
    run = hid // 2
    select = packing(run, run // RANKS, part, rank)
    for index in range(4):
        piece = dot(w_in[:, index * run : (index + 1) * run], select)
        packed_in[:, index * run // RANKS : (index + 1) * run // RANKS] = piece.astype(BF16)
    if part % 16:
        for index in range(2):
            piece = dot_tn(select, w_down[index * run : (index + 1) * run, :])
            packed_down[index * run // RANKS : (index + 1) * run // RANKS, :] = piece.astype(BF16)
    else:
        for index in range(hid // RANKS // part):
            rows = pl.ds(pl.multiple_of((index * RANKS + rank) * part, part), part)
            packed_down[index * part : (index + 1) * part, :] = w_down[rows, :]


def pack_weights(info, w_in, w_out, part):
    width, hid = w_in.shape[0], w_out.shape[0]
    return pl.pallas_call(
        functools.partial(pack_kernel, part),
        name="pack_weights",
        out_shape=(shape((width, 2 * hid // RANKS), BF16), shape((hid // RANKS, width), BF16)),
        in_specs=[SM, VM, VM],
        out_specs=(VM, VM),
        compiler_params=params(14),
        cost_estimate=pl.CostEstimate(
            flops=4 * 10**9, bytes_accessed=17 * 10**6, transcendentals=0
        ),
    )(info, w_in, w_out)


def ffn_forward_kernel(
    low, unit, gain1, shift1, gain2, shift2, masked, cot, w_in, w_down,
    layer_out, d_h2, d_ff, slope, act, sums, acc, gates, ups,
):
    hid = w_down.shape[0]
    size = gates.shape[2]
    count = hid // size

    def project(block, slot):
        first = pl.multiple_of(block * size, size)
        gates[slot] = dot(low[...], w_in[:, pl.ds(first, size)])
        ups[slot] = dot(low[...], w_in[:, pl.ds(pl.multiple_of(hid + first, size), size)])

    def finish(block, slot):
        here = pl.ds(pl.multiple_of(block * size, size), size)
        up = ups[slot]
        value, grad = gelu_pair(gates[slot])
        act[:, here] = value.astype(BF16)
        slope[:, here] = (up * grad).astype(BF16)
        acc[...] += dot((value * up).astype(BF16), w_down[here, :])

    acc[...] = unit[...] * line(gain1) + line(shift1)
    project(0, 0)

    def pair(index, carry):
        block = index * 2
        project(block + 1, 1)
        finish(block, 0)
        project(block + 2, 0)
        finish(block + 1, 1)
        return carry

    lax.fori_loop(0, count // 2 - 1, pair, 0)
    project(count - 1, 1)
    finish(count - 2, 0)
    finish(count - 1, 1)
    x, inv = standardize(acc[...])
    layer_out[...] = (x * line(gain2) + line(shift2)).astype(BF16)
    places = lax.broadcasted_iota(jnp.int32, (low.shape[0], masked.shape[0]), 0)
    dy = exact_dot((places == line(masked)).astype(F32), cot[...])
    sums[0:1, :] = jnp.sum(dy * x, axis=0, keepdims=True)
    sums[1:2, :] = jnp.sum(dy, axis=0, keepdims=True)
    grad_in = standardize_back(dy * line(gain2), x, inv)
    d_h2[...] = grad_in
    d_ff[...] = grad_in.astype(BF16)


def ffn_forward(low, unit, gain1, shift1, gain2, shift2, masked, cot, w_in, w_out, size):
    rows, width = low.shape
    hid = w_out.shape[0]
    return pl.pallas_call(
        ffn_forward_kernel,
        name="ffn_forward",
        out_shape=(
            shape((rows, width), BF16),
            shape((rows, width), F32),
            shape((rows, width), BF16),
            shape((rows, hid), BF16),
            shape((rows, hid), BF16),
            shape((2, width), F32),
        ),
        in_specs=[VM] * 10,
        out_specs=(VM,) * 6,
        scratch_shapes=[
            scratch((rows, width), F32),
            scratch((2, rows, size), F32),
            scratch((2, rows, size), F32),
        ],
        compiler_params=params(14),
        cost_estimate=pl.CostEstimate(
            flops=6 * rows * width * hid, bytes_accessed=18 * 10**6, transcendentals=2 * rows * hid
        ),
    )(low, unit, gain1, shift1, gain2, shift2, masked, cot, w_in, w_out)


def ffn_backward_kernel(
    d_ff, d_h2, unit, inverse, gain1, sums2, act, slope, w_in, w_down, d_h1, sent, acc, hidden
):
    hid = w_down.shape[0]
    size = hidden.shape[2]
    count = hid // size

    def project(block, slot):
        here = pl.ds(pl.multiple_of(block * size, size), size)
        hidden[slot] = dot_nt(d_ff[...], w_down[here, :])

    def finish(block, slot):
        first = pl.multiple_of(block * size, size)
        here, there = pl.ds(first, size), pl.ds(pl.multiple_of(hid + first, size), size)
        d_hidden = hidden[slot]
        d_gate = (d_hidden * slope[:, here].astype(F32)).astype(BF16)
        d_up = (d_hidden * act[:, here].astype(F32)).astype(BF16)
        acc[...] += dot_nt(d_gate, w_in[:, here]) + dot_nt(d_up, w_in[:, there])

    acc[...] = d_h2[...]
    project(0, 0)

    def pair(index, carry):
        block = index * 2
        project(block + 1, 1)
        finish(block, 0)
        project(block + 2, 0)
        finish(block + 1, 1)
        return carry

    lax.fori_loop(0, count // 2 - 1, pair, 0)
    project(count - 1, 1)
    finish(count - 2, 0)
    finish(count - 1, 1)
    total = acc[...]
    rows = total.shape[0]
    x = unit[...]
    gain_sum = jnp.sum(total * x, axis=0, keepdims=True)
    shift_sum = jnp.sum(total, axis=0, keepdims=True)
    sums = jnp.concatenate([gain_sum, shift_sum, sums2[...]], axis=0)
    high = sums.astype(BF16).astype(F32)
    tail = jnp.concatenate([high, sums - high, jnp.zeros((8, sums.shape[1]), F32)], axis=0)
    grad = standardize_back(total * line(gain1), x, inverse[...])
    d_h1[...] = grad
    sent[0:rows, :] = grad.astype(BF16)
    sent[rows : rows + 16, :] = tail.astype(BF16)


def ffn_backward(d_ff, d_h2, unit, inverse, gain1, sums2, act, slope, w_in, w_out, size):
    rows, width = d_ff.shape
    hid = w_out.shape[0]
    return pl.pallas_call(
        ffn_backward_kernel,
        name="ffn_backward",
        out_shape=(shape((rows, width), F32), shape((rows + 16, width), BF16)),
        in_specs=[VM] * 10,
        out_specs=(VM,) * 2,
        scratch_shapes=[scratch((rows, width), F32), scratch((2, rows, size), F32)],
        compiler_params=params(14),
        cost_estimate=pl.CostEstimate(
            flops=6 * rows * width * hid, bytes_accessed=20 * 10**6, transcendentals=0
        ),
    )(d_ff, d_h2, unit, inverse, gain1, sums2, act, slope, w_in, w_out)


X_FIRST = (1, 2, 4)
Z_FIRST = (2, 1, 4)


def bit_of(value, mask):
    return (value // mask) % 2


def store_blocks(blocks, keep, send, place, order, columns):
    one, two, three = order
    odd = bit_of(place, one) == 1
    for index in range(8):
        if index & one:
            continue
        spot = bit_of(place ^ index, two) * 2 + bit_of(place ^ index, three)
        low, high = blocks(index), blocks(index | one)
        keep[spot, :, columns] = jnp.where(odd, high, low).astype(BF16)
        send[spot, :, columns] = jnp.where(odd, low, high).astype(BF16)


def row_blocks(grad):
    each = grad.shape[0] // 8
    return lambda index: grad[index * each : (index + 1) * each]


def ffn_grad_kernel(
    size, info, n0, n1, n2, n3, f0, f1, f2, f3, w_in, w_down,
    keep_gate, send_gate, keep_up, send_up, keep_down, send_down,
    tok_t, gates, ups, d_hiddens, hidden_t, d_gate, d_up, d_ff, down,
):
    toks, grads = (n0, n1, n2, n3), (f0, f1, f2, f3)
    rows = n0.shape[0]
    units = w_down.shape[0]
    for at in range(RANKS):
        here = slice(at * rows, (at + 1) * rows)
        d_ff[here, :] = grads[at][...]
        tok_t[:, here] = jnp.transpose(toks[at][...])

    def unit_block(step, carry):
        here = pl.ds(pl.multiple_of(step * size, size), size)
        there = pl.ds(pl.multiple_of(units + step * size, size), size)
        w_gate, w_up, w_rows = w_in[:, here], w_in[:, there], w_down[here, :]

        def project(at):
            slot = at % 2
            gates[slot] = dot(toks[at][...], w_gate)
            ups[slot] = dot(toks[at][...], w_up)
            d_hiddens[slot] = dot_nt(grads[at][...], w_rows)

        def finish(at):
            slot = at % 2
            here = slice(at * rows, (at + 1) * rows)
            value, grad = gelu_pair(gates[slot])
            up, d_hidden = ups[slot], d_hiddens[slot]
            hidden_t[:, here] = jnp.transpose((value * up).astype(BF16))
            d_gate[here, :] = (d_hidden * up * grad).astype(BF16)
            d_up[here, :] = (d_hidden * value).astype(BF16)

        project(0)
        for at in range(RANKS):
            if at + 1 < RANKS:
                project(at + 1)
            finish(at)
        total = dot(tok_t[...], d_gate[...])
        store_blocks(row_blocks(total), keep_gate, send_gate, info[1], Z_FIRST, here)
        total = dot(tok_t[...], d_up[...])
        store_blocks(row_blocks(total), keep_up, send_up, info[1], Z_FIRST, here)
        down[here, :] = dot(hidden_t[...], d_ff[...])
        return carry

    lax.fori_loop(0, units // size, unit_block, 0)
    store_blocks(row_blocks(down), keep_down, send_down, info[1], X_FIRST, slice(None))


def ffn_grad(info, toks, grads, w_in, w_down, size):
    rows, width = toks[0].shape
    units = w_down.shape[0]
    tok = rows * RANKS
    dims = [(4, width // 8, units)] * 4 + [(4, units // 8, width)] * 2
    return pl.pallas_call(
        functools.partial(ffn_grad_kernel, size),
        name="ffn_grad",
        out_shape=[shape(each, BF16) for each in dims],
        in_specs=[SM] + [VM] * 10,
        out_specs=[VM] * 6,
        scratch_shapes=[
            scratch((width, tok), BF16),
            scratch((2, rows, size), F32),
            scratch((2, rows, size), F32),
            scratch((2, rows, size), F32),
            scratch((size, tok), BF16),
            scratch((tok, size), BF16),
            scratch((tok, size), BF16),
            scratch((tok, width), BF16),
            scratch((units, width), F32),
        ],
        compiler_params=params(18),
        cost_estimate=pl.CostEstimate(
            flops=12 * tok * width * units,
            bytes_accessed=8 * 10**6,
            transcendentals=2 * tok * units,
        ),
    )(info, *toks, *grads, w_in, w_down)


def qkv_grad_kernel(
    info, x0, x1, x2, x3, d0, d1, d2, d3, j0, j1, j2, j3, g0, g1, g2, g3, keep, send, columns, grad
):
    rows, width = x0.shape
    part = width // RANKS
    total = 0.0
    for x, d_qkv in zip((x0, x1, x2, x3), (d0, d1, d2, d3)):
        total = total + dot(d_qkv[...], x[...])
    grad[:, : 3 * part] = jnp.transpose(total)
    for value in range(RANKS):

        @pl.when(info[0] == value)
        def _():
            for at, g in enumerate((g0, g1, g2, g3)):
                columns[at] = g[0:rows, value * part : (value + 1) * part]

    total = 0.0
    sums = 0.0
    for at, (joined, g) in enumerate(zip((j0, j1, j2, j3), (g0, g1, g2, g3))):
        total = total + dot(joined[...], columns[at])
        pair = g[rows : rows + 16, :].astype(F32)
        sums = sums + pair[0:4] + pair[4:8]
    grad[:, 3 * part :] = total
    high = sums.astype(BF16).astype(F32)
    tail = jnp.concatenate([high, sums - high], axis=0)
    each = width // 8

    def blocks(index):
        return jnp.concatenate([grad[index * each : (index + 1) * each], tail], axis=0)

    store_blocks(blocks, keep, send, info[1], X_FIRST, slice(None))


def qkv_grad(info, blocks, d_qkv, joined, d_proj):
    rows, width = blocks[0].shape
    return pl.pallas_call(
        qkv_grad_kernel,
        name="qkv_grad",
        out_shape=(shape((4, width // 8 + 8, width), BF16),) * 2,
        in_specs=[SM] + [VM] * 16,
        out_specs=(VM, VM),
        scratch_shapes=[
            scratch((RANKS, rows, width // RANKS), BF16),
            scratch((width, width), F32),
        ],
        compiler_params=params(14),
        cost_estimate=pl.CostEstimate(
            flops=8 * rows * width * width, bytes_accessed=4 * 10**6, transcendentals=0
        ),
    )(info, *blocks, *d_qkv, *joined, *d_proj)


def unpack(part, packed, wide, first):
    few = packed.shape[1] // RANKS
    for run in range(few // part):
        pieces = []
        for value in range(RANKS):
            at = value * few + run * part
            pieces.append(packed[:, at : at + part])
        at = first + run * RANKS * part
        wide[:, at : at + RANKS * part] = jnp.concatenate(pieces, axis=1).astype(F32)


def join_early_kernel(info, b0, b1, b2, b3, down, packed):
    rows, columns = b0.shape
    few = columns // 2
    for step, block in enumerate((b0, b1, b2, b3)):
        there = info[0] ^ step
        packed[:, pl.ds(pl.multiple_of(there * few, few), few)] = block[:, few:]
        down[pl.ds(pl.multiple_of(there * rows, rows), rows), :] = block[:, :few].astype(F32)


def join_late_kernel(part, info, b0, b1, b2, b3, gates, wide, out, rest, ups):
    width = rest.shape[1]
    heads = width // RANKS
    few = gates.shape[1] // RANKS
    blocks = (b0, b1, b2, b3)
    for step, block in enumerate(blocks):
        there = pl.multiple_of((info[0] ^ step) * few, few)
        ups[:, pl.ds(there, few)] = block[:, :few]
    unpack(part, gates, wide, 0)
    unpack(part, ups, wide, RANKS * few)
    for value in range(RANKS):

        @pl.when(info[0] == value)
        def _():
            for step, block in enumerate(blocks):
                there = (value ^ step) * heads
                for third in range(3):
                    first = few + third * heads
                    at = third * width + there
                    out[:, at : at + heads] = block[:, first : first + heads].astype(F32)
                first = few + 3 * heads
                rest[:, there : there + heads] = block[:, first:].astype(F32)


def join_early(info, blocks):
    rows, columns = blocks[0].shape
    if rows % 8:
        stacked = jnp.stack(blocks)[info[0] ^ jnp.arange(RANKS)]
        few = columns // 2
        gates = jnp.concatenate(list(stacked[:, :, few:]), axis=1)
        return stacked[:, :, :few].reshape(-1, few).astype(F32), gates
    return pl.pallas_call(
        join_early_kernel,
        name="join_early",
        out_shape=(
            shape((rows * RANKS, columns // 2), F32),
            shape((rows, RANKS * columns // 2), BF16),
        ),
        in_specs=[SM] + [VM] * 4,
        out_specs=(VM, VM),
        compiler_params=params(8),
        cost_estimate=NO_COST,
    )(info, *blocks)


def join_late(info, blocks, gates, part):
    rows, columns = blocks[0].shape
    width = columns // 2
    if RANKS * part % 128:
        stacked = jnp.stack(blocks)[info[0] ^ jnp.arange(RANKS)].astype(F32)
        both = [gates.astype(F32), jnp.concatenate(list(stacked[:, :, :width]), axis=1)]
        wide = [each.reshape(rows, RANKS, -1, part).transpose(0, 2, 1, 3) for each in both]
        wide = jnp.concatenate([each.reshape(rows, -1) for each in wide], axis=1)
        heads = stacked[:, :, width:].reshape(RANKS, rows, RANKS, -1).transpose(1, 2, 0, 3)
        heads = heads.reshape(rows, RANKS, -1)
        return wide, heads[:, :3].reshape(rows, -1), heads[:, 3]
    return pl.pallas_call(
        functools.partial(join_late_kernel, part),
        name="join_late",
        out_shape=(
            shape((rows, 2 * RANKS * width), F32),
            shape((rows, 3 * width), F32),
            shape((rows, width), F32),
        ),
        in_specs=[SM] + [VM] * 5,
        out_specs=(VM,) * 3,
        scratch_shapes=[scratch((rows, RANKS * width), BF16)],
        compiler_params=params(14),
        cost_estimate=NO_COST,
    )(info, *blocks, gates)


def token_grad_kernel(
    info, own, near, far, cross, w, d_h1, masked, tokens, replacement, joined
):
    rows, width = d_h1.shape
    part = width // RANKS
    for step, block in enumerate((own, near, far, cross)):
        for third in range(3):
            first = pl.multiple_of(third * width + (info[0] ^ step) * part, part)
            joined[pl.ds(first, part), :] = block[third * part : (third + 1) * part, :]
    grad = d_h1[...] + jnp.transpose(dot(w[...], joined[...]))
    count = masked.shape[0]
    places = lax.broadcasted_iota(jnp.int32, (rows, count), 0)
    select = (places == line(masked)).astype(F32)
    hit = jnp.max(select, axis=1, keepdims=True)
    tokens[...] = jnp.where(hit > 0.5, 0.0, grad)
    replacement[...] = lax.dot_general(
        select, grad, (((0,), (0,)), ((), ())),
        precision=lax.Precision.HIGHEST, preferred_element_type=F32,
    )


def token_grad(info, parts, w, d_h1, masked):
    rows, width = d_h1.shape
    return pl.pallas_call(
        token_grad_kernel,
        name="token_grad",
        out_shape=(shape((rows, width), F32), shape((masked.shape[0], width), F32)),
        in_specs=[SM] + [VM] * 7,
        out_specs=(VM, VM),
        scratch_shapes=[scratch((3 * width, rows), BF16)],
        compiler_params=params(16),
        cost_estimate=pl.CostEstimate(
            flops=6 * rows * width * width, bytes_accessed=8 * 10**6, transcendentals=0
        ),
    )(info, *parts, w, d_h1, masked)


def after(value, *others):
    return lax.optimization_barrier((value,) + others)[0]


def flip(value, axis, bits):
    count = lax.axis_size(axis)
    return lax.ppermute(value, axis, [(index, index ^ bits) for index in range(count)])


def gather_blocks(value):
    far = flip(value, "sp", 2)
    near = flip(value, "sp", 1)
    cross = flip(far, "sp", 1)
    return [value, near, far, cross]


def exchange_blocks(blocks):
    via = flip(blocks[3], "sp", 1)
    near = flip(blocks[1], "sp", 1)
    far = flip(blocks[2], "sp", 2)
    cross = flip(via, "sp", 2)
    return [blocks[0], near, far, cross]


def small_mesh():
    return lax.axis_size("dp") == 8


NO_COST = pl.CostEstimate(flops=0, bytes_accessed=0, transcendentals=0)


def tidy_sums(value):
    first = value.shape[1] - 8
    sums = value[:, first : first + 4] + value[:, first + 4 :]
    high = sums.astype(BF16).astype(F32)
    return jnp.concatenate([value[:, :first], high, sums - high], axis=1)


def halve_kernel(with_sums, keep, came, kept, sent):
    half = keep.shape[0] // 2
    value = keep[...].astype(F32) + came[...].astype(F32)
    if with_sums:
        value = tidy_sums(value)
    kept[...] = value[:half]
    sent[...] = value[half:].astype(BF16)


def halve(keep, came, with_sums=False):
    dims = (keep.shape[0] // 2,) + keep.shape[1:]
    return pl.pallas_call(
        functools.partial(halve_kernel, with_sums),
        name="halve",
        out_shape=(shape(dims, F32), shape(dims, BF16)),
        in_specs=[VM] * 2,
        out_specs=(VM, VM),
        compiler_params=params(12),
        cost_estimate=NO_COST,
    )(keep, came)


def send_first(send, order):
    return flip(send, "dp", order[0]) if small_mesh() else send


def next_half(keep, came, with_sums=False):
    return halve(keep, came, with_sums) if small_mesh() else (keep, came)


def send_on(send, bits):
    return flip(send, "dp", bits) if small_mesh() else send


def send_second(keep, came, order, with_sums=False):
    keep, send = next_half(keep, came, with_sums)
    return keep, send_on(send, order[1])


def send_third(keep, came, order, with_sums=False):
    keep, send = next_half(keep, came, with_sums)
    return keep, send_on(send, order[2])


def natural_blocks(keep, send, order):
    both = jnp.concatenate([keep, send], axis=0).astype(F32)
    places = []
    for index in range(8):
        bits = [1 if index & mask else 0 for mask in order]
        places.append(both[bits[0] * 4 + bits[1] * 2 + bits[2]])
    return places


def scatter_sum(blocks):
    grad = jnp.concatenate(blocks, axis=0)
    return lax.psum_scatter(grad, "dp", scatter_dimension=0, tiled=True).astype(BF16)


def finish_pair_kernel(keep_a, came_a, keep_b, came_b, out):
    columns = keep_a.shape[2]
    out[:, :columns] = (keep_a[0] + came_a[0].astype(F32)).astype(BF16)
    out[:, columns:] = (keep_b[0] + came_b[0].astype(F32)).astype(BF16)


def finish_pair(keep_a, came_a, order_a, keep_b, came_b, order_b):
    if not small_mesh():
        first = scatter_sum(natural_blocks(keep_a, came_a, order_a))
        second = scatter_sum(natural_blocks(keep_b, came_b, order_b))
        return jnp.concatenate([first, second], axis=1)
    _, rows, columns = keep_a.shape
    return pl.pallas_call(
        finish_pair_kernel,
        name="finish_pair",
        out_shape=shape((rows, columns + keep_b.shape[2]), BF16),
        in_specs=[VM] * 4,
        out_specs=VM,
        compiler_params=params(8),
        cost_estimate=NO_COST,
    )(keep_a, came_a, keep_b, came_b)


def finish_heads_kernel(keep_u, came_u, keep, came, out, *sums):
    columns = keep_u.shape[2]
    rows = out.shape[0]
    out[:, :columns] = (keep_u[0] + came_u[0].astype(F32)).astype(BF16)
    total = keep[0] + came[0].astype(F32)
    out[:, columns:] = total[:rows].astype(BF16)
    for index, vector in enumerate(sums):
        value = total[rows + index : rows + index + 1] + total[rows + 4 + index : rows + 5 + index]
        vector[...] = value.reshape(-1)


def finish_heads(keep_u, came_u, keep, came):
    _, rows, columns = keep.shape
    rows = rows - 8
    if not small_mesh():
        blocks = natural_blocks(keep, came, X_FIRST)
        sums = blocks[0][rows : rows + 4] + blocks[0][rows + 4 :]
        first = scatter_sum(natural_blocks(keep_u, came_u, Z_FIRST))
        second = scatter_sum([block[:rows] for block in blocks])
        return jnp.concatenate([first, second], axis=1), list(lax.psum(sums, "dp"))
    out, *sums = pl.pallas_call(
        finish_heads_kernel,
        name="finish_heads",
        out_shape=(shape((rows, keep_u.shape[2] + columns), BF16),) + (shape((columns,), F32),) * 4,
        in_specs=[VM] * 4,
        out_specs=(VM,) * 5,
        compiler_params=params(8),
        cost_estimate=NO_COST,
    )(keep_u, came_u, keep, came)
    return out, sums


def local(
    tokens,
    segment_ids,
    masked_rows,
    replacement,
    cotangent,
    w_qkv,
    w_out_attn,
    w_in_ff,
    w_out_ff,
    gain_one,
    shift_one,
    gain_two,
    shift_two,
):
    rows_dev, width = tokens.shape
    rank = lax.axis_index("sp")
    heads = HEADS // RANKS
    dim = width // HEADS
    part = heads * dim
    slopes = alibi_slopes(HEADS)

    select = jnp.arange(rows_dev, dtype=jnp.int32)[:, None] == masked_rows[None, :]
    hit = jnp.any(select, axis=1, keepdims=True)
    placed = dot(select.astype(BF16), replacement)
    start = jnp.where(hit, placed.astype(BF16), tokens)
    start_far = flip(start, "sp", 2)
    start_near = flip(start, "sp", 1)
    place = lax.axis_index("dp")
    place = place if small_mesh() else place * 0
    spot = jnp.stack([rank, place]).astype(jnp.int32)

    w_rank = jnp.concatenate(
        [
            lax.dynamic_slice_in_dim(w_qkv, third * width + rank * part, part, 1)
            for third in range(3)
        ],
        axis=1,
    )
    start_cross = flip(after(start_far, w_rank, spot), "sp", 1)
    start_blocks = [start, start_near, start_far, start_cross]
    qkv, attn, lse = attention_forward(
        spot, segment_ids, slopes, start_blocks, w_rank, heads, dim
    )
    attn_far = flip(attn, "sp", 2)
    attn_near = flip(attn, "sp", 1)
    part_units = w_out_ff.shape[0] // lax.axis_size("dp") // RANKS
    packed_in, packed_down = pack_weights(after(spot, lse), w_in_ff, w_out_ff, part_units)
    attn_cross = flip(after(attn_far, packed_in), "sp", 1)
    attn_parts = [attn, attn_near, attn_far, attn_cross]
    low, joined, unit, inverse = norm_one(
        spot, attn_parts, start, w_out_attn, gain_one, shift_one
    )
    layer_out, d_h2, d_ff, slope, act, sums2 = ffn_forward(
        low, unit, gain_one, shift_one, gain_two, shift_two,
        masked_rows, cotangent, w_in_ff, w_out_ff, 768,
    )
    d_ff_far = flip(d_ff, "sp", 2)
    d_ff_near = flip(d_ff, "sp", 1)
    d_h1, sent = ffn_backward(
        d_ff, d_h2, unit, inverse, gain_one, sums2, act, slope, w_in_ff, w_out_ff, 768
    )
    lows, others_joined = norm_others(
        after(spot, sent), attn_parts, start_blocks[1:], w_out_attn, gain_one, shift_one
    )
    d_ff_far = after(d_ff_far, lows[0])
    d_ff_cross = flip(d_ff_far, "sp", 1)
    d_ff_blocks = [d_ff, d_ff_near, d_ff_far, d_ff_cross]
    far = flip(sent, "sp", 2)
    near = flip(sent, "sp", 1)

    keep_g, send_g, keep_u, send_u, keep_d, send_d = ffn_grad(
        spot, [low, *lows], d_ff_blocks, packed_in, packed_down, 256
    )
    came_g = send_first(send_g, Z_FIRST)
    came_d = send_first(send_d, X_FIRST)
    cross = flip(after(far, keep_g), "sp", 1)
    d_proj_blocks = [sent, near, far, cross]

    d_qkv = attention_backward(
        spot, segment_ids, slopes, d_proj_blocks, w_out_attn, qkv, lse, heads, dim
    )
    parts = exchange_blocks(d_qkv)
    came_u = send_first(after(send_u, d_qkv[0]), Z_FIRST)
    keep_g, came_g = send_second(keep_g, after(came_g, d_qkv[0]), Z_FIRST)
    keep_d, came_d = send_second(keep_d, after(came_d, keep_g), X_FIRST)
    keep_q, send_q = qkv_grad(
        after(spot, keep_d), start_blocks, d_qkv, [joined, *others_joined], d_proj_blocks
    )
    keep_g, came_g = send_third(keep_g, after(came_g, keep_q), Z_FIRST)
    came_q = send_first(after(send_q, keep_g), X_FIRST)
    keep_d, came_d = send_third(keep_d, after(came_d, keep_g), X_FIRST)
    keep_u, came_u = send_second(keep_u, after(came_u, keep_d), Z_FIRST)
    keep_q, send_q = next_half(keep_q, after(came_q, keep_u, parts), True)
    early = finish_pair(keep_d, after(came_d, keep_q), X_FIRST, keep_g, came_g, Z_FIRST)
    came_q = send_on(after(send_q, early), X_FIRST[1])
    far = flip(early, "sp", 2)
    near = flip(early, "sp", 1)
    keep_u, came_u = send_third(keep_u, after(came_u, early), Z_FIRST)
    keep_q, came_q = send_third(keep_q, after(came_q, keep_u, came_u, far), X_FIRST, True)
    early_blocks = [early, near, far, flip(after(far, keep_q), "sp", 1)]
    grad_tokens, grad_replacement = token_grad(
        after(spot, keep_q), parts, w_qkv, d_h1, masked_rows
    )
    grad_down, gates = join_early(after(spot, grad_tokens), early_blocks)
    late, norm_sums = finish_heads(keep_u, came_u, keep_q, after(came_q, gates))
    late_blocks = gather_blocks(late)
    grad_in, grad_qkv, grad_out = join_late(spot, late_blocks, gates, part_units)

    return (
        layer_out,
        grad_tokens,
        grad_replacement,
        grad_qkv,
        grad_out,
        grad_in,
        grad_down,
        norm_sums[0],
        norm_sums[1],
        norm_sums[2],
        norm_sums[3],
    )


def solution(mesh):
    tokens = P(("dp", "sp"), None)
    rows = P("dp", None)
    return jax.shard_map(
        local,
        mesh=mesh,
        in_specs=(tokens, rows, P(("dp", "sp")), tokens, tokens) + (P(),) * 8,
        out_specs=(tokens,) * 3 + (rows,) * 4 + (P(),) * 4,
        check_vma=False,
    )
```

```python
import functools
import math

import jax
import jax.numpy as jnp
from jax import lax
from jax.experimental import pallas as pl
from jax.experimental.pallas import tpu as pltpu
from jax.sharding import PartitionSpec as P

HEADS = 12
RANKS = 4
EPSILON = 1e-05
FAR = 1e30
F32 = jnp.float32
BF16 = jnp.bfloat16
VM = pl.BlockSpec(memory_space=pltpu.VMEM)
SM = pl.BlockSpec(memory_space=pltpu.SMEM)


def shape(dims, kind):
    return jax.ShapeDtypeStruct(dims, kind)


def scratch(dims, kind):
    return pltpu.VMEM(dims, kind)


def params(mebibytes):
    return pltpu.CompilerParams(vmem_limit_bytes=mebibytes << 20)


def alibi_slopes(head_count):
    nearest = 2 ** int(math.floor(math.log2(head_count)))
    base_list = [2.0 ** (-8.0 * (index + 1) / nearest) for index in range(nearest)]
    extra_list = [
        2.0 ** (-8.0 * (2 * index + 1) / (2 * nearest)) for index in range(head_count - nearest)
    ]
    return jnp.array(base_list + extra_list, dtype=F32)


def dot(a, b):
    return jnp.dot(a, b, preferred_element_type=F32)


def dot_nt(a, b):
    return lax.dot_general(a, b, (((1,), (1,)), ((), ())), preferred_element_type=F32)


def dot_tn(a, b):
    return lax.dot_general(a, b, (((0,), (0,)), ((), ())), preferred_element_type=F32)


def exact_dot(a, b):
    return jnp.dot(a, b, precision=lax.Precision.HIGHEST, preferred_element_type=F32)


def standardize(value):
    center = value - jnp.mean(value, axis=-1, keepdims=True)
    spread = jnp.mean(center * center, axis=-1, keepdims=True)
    inverse = lax.rsqrt(spread + EPSILON)
    return center * inverse, inverse


def standardize_back(grad, unit, inverse):
    mean = jnp.mean(grad, axis=-1, keepdims=True)
    return inverse * (grad - mean - unit * jnp.mean(grad * unit, axis=-1, keepdims=True))


def gelu_pair(x):
    cdf = 0.5 * (1.0 + lax.erf(x * math.sqrt(0.5)))
    pdf = jnp.exp(-0.5 * x * x) * (1.0 / math.sqrt(2.0 * math.pi))
    return x * cdf, cdf + x * pdf


def pair_active(seg, rank, first, second, rows):
    one, two = rank ^ first, rank ^ second
    low, high = jnp.minimum(one, two), jnp.maximum(one, two)
    return jnp.logical_or(one == two, seg[0, low * rows + rows - 1] == seg[0, high * rows])


def key_sequences(seg_rows, seg_keys, rank, rows):
    for at in range(RANKS):
        first = pl.multiple_of((rank ^ at) * rows, rows)
        line = jnp.broadcast_to(seg_rows[:, pl.ds(first, rows)], (128, rows))
        seg_keys[at * rows : (at + 1) * rows, :] = jnp.transpose(line)


def pair_distance(seg_rows, seg_keys, rank, keys_at, query_at, rows):
    key_pos, query_pos = (rank ^ keys_at) * rows, (rank ^ query_at) * rows
    down = lax.broadcasted_iota(jnp.int32, (rows, rows), 0)
    across = lax.broadcasted_iota(jnp.int32, (rows, rows), 1)
    gap = jnp.abs(down - across + (key_pos - query_pos)).astype(F32)
    seg_q = seg_rows[:, pl.ds(pl.multiple_of(query_pos, rows), rows)]
    seg_k = seg_keys[pl.ds(pl.multiple_of(keys_at * rows, rows), rows), 0:1]
    return jnp.where(seg_k == seg_q, gap, FAR)


def attention_forward_kernel(
    rows, heads, dim, info, seg, slopes, x0, x1, x2, x3, w, seg_rows,
    qkv_out, out_t, lse, qs, ks, vt, dist, seg_keys, score, peak,
):
    rank = info[0]
    width = heads * dim
    key_sequences(seg_rows, seg_keys, rank, rows)
    for at, x in enumerate((x0, x1, x2, x3)):
        qkv = dot(x[...], w[...]).astype(BF16)
        here = pl.ds(at * rows, rows)
        qkv_out[here, :] = qkv
        for h in range(heads):
            qs[h, here, :] = (qkv[:, h * dim : (h + 1) * dim] * dim**-0.5).astype(BF16)
            ks[h, here, :] = qkv[:, width + h * dim : width + (h + 1) * dim]
        vt[:, here] = jnp.transpose(qkv[:, 2 * width :])

    for a in range(RANKS):
        mine = pl.ds(a * rows, rows)
        peak[...] = jnp.full_like(peak, -jnp.inf)

        def first_pass(b, carry):
            @pl.when(pair_active(seg, rank, a, b, rows))
            def _():
                theirs = pl.ds(pl.multiple_of(b * rows, rows), rows)
                gap = pair_distance(seg_rows, seg_keys, rank, b, a, rows)
                for h in range(heads):
                    slope = slopes[rank * heads + h]
                    s = dot_nt(ks[h, theirs, :], qs[h, mine, :]) - slope * gap
                    score[h, theirs, :] = s
                    peak[h : h + 1, :] = jnp.maximum(
                        peak[h : h + 1, :], jnp.max(s, axis=0, keepdims=True)
                    )

            return carry

        lax.fori_loop(0, RANKS, first_pass, 0)

        def second_pass(b, carry):
            def add(carry):
                theirs = pl.ds(pl.multiple_of(b * rows, rows), rows)
                result = []
                for h in range(heads):
                    acc, total = carry[h]
                    p = jnp.exp(score[h, theirs, :] - peak[h : h + 1, :])
                    total = total + jnp.sum(p, axis=0, keepdims=True)
                    span = slice(h * dim, (h + 1) * dim)
                    result.append((acc + dot(vt[span, theirs], p.astype(BF16)), total))
                return tuple(result)

            return lax.cond(pair_active(seg, rank, a, b, rows), add, lambda carry: carry, carry)

        empty = (jnp.zeros((dim, rows), F32), jnp.zeros((1, rows), F32))
        sums = lax.fori_loop(0, RANKS, second_pass, (empty,) * heads)
        for h in range(heads):
            acc, total = sums[h]
            span = slice(h * dim, (h + 1) * dim)
            out_t[span, mine] = (acc / total).astype(BF16)
            lse[h : h + 1, mine] = peak[h : h + 1, :] + jnp.log(total)


def attention_forward(info, seg, slopes, blocks, w, heads, dim):
    rows = blocks[0].shape[0]
    tok, lw = rows * RANKS, heads * dim
    return pl.pallas_call(
        functools.partial(attention_forward_kernel, rows, heads, dim),
        name="attention_forward",
        out_shape=(
            shape((tok, 3 * lw), BF16),
            shape((lw, tok), BF16),
            shape((heads, tok), F32),
        ),
        in_specs=[SM] * 3 + [VM] * 6,
        out_specs=(VM,) * 3,
        scratch_shapes=[
            scratch((heads, tok, dim), BF16),
            scratch((heads, tok, dim), BF16),
            scratch((lw, tok), BF16),
            scratch((rows, rows), F32),
            scratch((tok, 128), jnp.int32),
            scratch((heads, tok, rows), F32),
            scratch((heads, rows), F32),
        ],
        compiler_params=params(14),
        cost_estimate=pl.CostEstimate(
            flops=4 * 10**9, bytes_accessed=6 * 10**6, transcendentals=3 * 10**6
        ),
    )(info, seg, slopes, *blocks, w, seg)


def attention_backward_kernel(
    rows, heads, dim, info, seg, slopes, g0, g1, g2, g3, w, qkv, lse, seg_rows,
    d0, d1, d2, d3, qs, ks, kt, vs, do, seg_keys, prob, dprob, dk, dv, dqt, delta,
):
    rank = info[0]
    width = heads * dim
    scale = dim**-0.5
    key_sequences(seg_rows, seg_keys, rank, rows)
    w_rank = w[pl.ds(pl.multiple_of(rank * width, width), width), :]
    for at, g in enumerate((g0, g1, g2, g3)):
        here = pl.ds(at * rows, rows)
        grad = dot_nt(g[0:rows, :], w_rank).astype(BF16)
        value = qkv[here, :]
        kt[:, here] = jnp.transpose(value[:, width : 2 * width])
        for h in range(heads):
            do[h, here, :] = grad[:, h * dim : (h + 1) * dim]
            qs[h, here, :] = (value[:, h * dim : (h + 1) * dim] * scale).astype(BF16)
            ks[h, here, :] = value[:, width + h * dim : width + (h + 1) * dim]
            vs[h, here, :] = value[:, 2 * width + h * dim : 2 * width + (h + 1) * dim]
    dk[...] = jnp.zeros_like(dk)
    dv[...] = jnp.zeros_like(dv)

    for a in range(RANKS):
        mine = pl.ds(a * rows, rows)
        delta[...] = jnp.zeros_like(delta)
        dqt[...] = jnp.zeros_like(dqt)

        def first_pass(b, carry):
            @pl.when(pair_active(seg, rank, a, b, rows))
            def _():
                theirs = pl.ds(pl.multiple_of(b * rows, rows), rows)
                gap = pair_distance(seg_rows, seg_keys, rank, b, a, rows)
                for h in range(heads):
                    slope = slopes[rank * heads + h]
                    s = dot_nt(ks[h, theirs, :], qs[h, mine, :]) - slope * gap
                    p = jnp.exp(s - lse[h : h + 1, mine])
                    dp = dot_nt(vs[h, theirs, :], do[h, mine, :])
                    delta[h : h + 1, :] += jnp.sum(p * dp, axis=0, keepdims=True)
                    prob[h, theirs, :] = p
                    dprob[h, theirs, :] = dp

            return carry

        lax.fori_loop(0, RANKS, first_pass, 0)

        def second_pass(b, carry):
            @pl.when(pair_active(seg, rank, a, b, rows))
            def _():
                theirs = pl.ds(pl.multiple_of(b * rows, rows), rows)
                for h in range(heads):
                    p = prob[h, theirs, :]
                    ds = (p * (dprob[h, theirs, :] - delta[h : h + 1, :])).astype(BF16)
                    dv[h, theirs, :] += dot(p.astype(BF16), do[h, mine, :])
                    dk[h, theirs, :] += dot(ds, qs[h, mine, :])
                    span = slice(h * dim, (h + 1) * dim)
                    dqt[span, :] += dot(kt[span, theirs], ds)

            return carry

        lax.fori_loop(0, RANKS, second_pass, 0)
        (d0, d1, d2, d3)[a][0:width, :] = (dqt[...] * scale).astype(BF16)

    for at, d_qkv in enumerate((d0, d1, d2, d3)):
        here = pl.ds(at * rows, rows)
        for h in range(heads):
            first = width + h * dim
            d_qkv[first : first + dim, :] = jnp.transpose(dk[h, here, :]).astype(BF16)
            first = 2 * width + h * dim
            d_qkv[first : first + dim, :] = jnp.transpose(dv[h, here, :]).astype(BF16)


def attention_backward(info, seg, slopes, blocks, w, qkv, lse, heads, dim):
    tok, lw = qkv.shape[0], heads * dim
    rows = tok // RANKS
    return pl.pallas_call(
        functools.partial(attention_backward_kernel, rows, heads, dim),
        name="attention_backward",
        out_shape=(shape((3 * lw, rows), BF16),) * RANKS,
        in_specs=[SM] * 3 + [VM] * 8,
        out_specs=(VM,) * RANKS,
        scratch_shapes=[
            scratch((heads, tok, dim), BF16),
            scratch((heads, tok, dim), BF16),
            scratch((lw, tok), BF16),
            scratch((heads, tok, dim), BF16),
            scratch((heads, tok, dim), BF16),
            scratch((tok, 128), jnp.int32),
            scratch((heads, tok, rows), F32),
            scratch((heads, tok, rows), F32),
            scratch((heads, tok, dim), F32),
            scratch((heads, tok, dim), F32),
            scratch((lw, rows), F32),
            scratch((heads, rows), F32),
        ],
        compiler_params=params(20),
        cost_estimate=pl.CostEstimate(
            flops=8 * 10**9, bytes_accessed=6 * 10**6, transcendentals=3 * 10**6
        ),
    )(info, seg, slopes, *blocks, w, qkv, lse, seg)


def line(vector):
    return vector[...].reshape(1, -1)


def join_tokens(rank, arrays, tokens_of, joined):
    part = arrays[0].shape[0]
    rows = arrays[0].shape[1] // RANKS
    for step, array in enumerate(arrays):
        first = pl.multiple_of((rank ^ step) * part, part)
        block = step ^ tokens_of
        joined[pl.ds(first, part), :] = array[:, block * rows : (block + 1) * rows]


def norm_one_kernel(
    info, own, near, far, cross, start, w, gain, shift, low, joined, unit, inverse
):
    join_tokens(info[0], (own, near, far, cross), 0, joined)
    x, inv = standardize(start[...].astype(F32) + dot_tn(joined[...], w[...]))
    unit[...] = x
    inverse[...] = inv
    low[...] = (x * line(gain) + line(shift)).astype(BF16)


def norm_one(info, parts, start, w, gain, shift):
    rows, width = start.shape
    return pl.pallas_call(
        norm_one_kernel,
        name="norm_one",
        out_shape=(
            shape((rows, width), BF16),
            shape((width, rows), BF16),
            shape((rows, width), F32),
            shape((rows, 1), F32),
        ),
        in_specs=[SM] + [VM] * 8,
        out_specs=(VM,) * 4,
        compiler_params=params(12),
        cost_estimate=pl.CostEstimate(
            flops=2 * rows * width * width, bytes_accessed=4 * 10**6, transcendentals=0
        ),
    )(info, *parts, start, w, gain, shift)


def norm_others_kernel(
    info, own, near, far, cross, s1, s2, s3, w, gain, shift, l1, l2, l3, j1, j2, j3
):
    for tokens_of, (start, low, joined) in enumerate(((s1, l1, j1), (s2, l2, j2), (s3, l3, j3))):
        join_tokens(info[0], (own, near, far, cross), tokens_of + 1, joined)
        x, _ = standardize(start[...].astype(F32) + dot_tn(joined[...], w[...]))
        low[...] = (x * line(gain) + line(shift)).astype(BF16)


def norm_others(info, parts, starts, w, gain, shift):
    rows, width = starts[0].shape
    results = pl.pallas_call(
        norm_others_kernel,
        name="norm_others",
        out_shape=(shape((rows, width), BF16),) * 3 + (shape((width, rows), BF16),) * 3,
        in_specs=[SM] + [VM] * 10,
        out_specs=(VM,) * 6,
        compiler_params=params(12),
        cost_estimate=pl.CostEstimate(
            flops=6 * rows * width * width, bytes_accessed=4 * 10**6, transcendentals=0
        ),
    )(info, *parts, *starts, w, gain, shift)
    return results[:3], results[3:]


def packing(rows, columns, part, rank):
    units = lax.broadcasted_iota(jnp.int32, (rows, columns), 0)
    packed = lax.broadcasted_iota(jnp.int32, (1, columns), 1)
    places = packed + rank * part
    for index in range(1, columns // part):
        places = places + jnp.where(packed >= index * part, (RANKS - 1) * part, 0)
    return (units == places).astype(BF16)


def pack_kernel(part, info, w_in, w_down, packed_in, packed_down):
    rank = info[0]
    width, hid = w_in.shape[0], w_down.shape[0]
    run = hid // 2
    select = packing(run, run // RANKS, part, rank)
    for index in range(4):
        piece = dot(w_in[:, index * run : (index + 1) * run], select)
        packed_in[:, index * run // RANKS : (index + 1) * run // RANKS] = piece.astype(BF16)
    if part % 16:
        for index in range(2):
            piece = dot_tn(select, w_down[index * run : (index + 1) * run, :])
            packed_down[index * run // RANKS : (index + 1) * run // RANKS, :] = piece.astype(BF16)
    else:
        for index in range(hid // RANKS // part):
            rows = pl.ds(pl.multiple_of((index * RANKS + rank) * part, part), part)
            packed_down[index * part : (index + 1) * part, :] = w_down[rows, :]


def pack_weights(info, w_in, w_out, part):
    width, hid = w_in.shape[0], w_out.shape[0]
    return pl.pallas_call(
        functools.partial(pack_kernel, part),
        name="pack_weights",
        out_shape=(shape((width, 2 * hid // RANKS), BF16), shape((hid // RANKS, width), BF16)),
        in_specs=[SM, VM, VM],
        out_specs=(VM, VM),
        compiler_params=params(14),
        cost_estimate=pl.CostEstimate(
            flops=4 * 10**9, bytes_accessed=17 * 10**6, transcendentals=0
        ),
    )(info, w_in, w_out)


def ffn_forward_kernel(
    low, unit, gain1, shift1, gain2, shift2, masked, cot, w_in, w_down,
    layer_out, d_h2, d_ff, slope, act, sums, acc, gates, ups,
):
    hid = w_down.shape[0]
    size = gates.shape[2]
    count = hid // size

    def project(block, slot):
        first = pl.multiple_of(block * size, size)
        gates[slot] = dot(low[...], w_in[:, pl.ds(first, size)])
        ups[slot] = dot(low[...], w_in[:, pl.ds(pl.multiple_of(hid + first, size), size)])

    def finish(block, slot):
        here = pl.ds(pl.multiple_of(block * size, size), size)
        up = ups[slot]
        value, grad = gelu_pair(gates[slot])
        act[:, here] = value.astype(BF16)
        slope[:, here] = (up * grad).astype(BF16)
        acc[...] += dot((value * up).astype(BF16), w_down[here, :])

    acc[...] = unit[...] * line(gain1) + line(shift1)
    project(0, 0)

    def pair(index, carry):
        block = index * 2
        project(block + 1, 1)
        finish(block, 0)
        project(block + 2, 0)
        finish(block + 1, 1)
        return carry

    lax.fori_loop(0, count // 2 - 1, pair, 0)
    project(count - 1, 1)
    finish(count - 2, 0)
    finish(count - 1, 1)
    x, inv = standardize(acc[...])
    layer_out[...] = (x * line(gain2) + line(shift2)).astype(BF16)
    places = lax.broadcasted_iota(jnp.int32, (low.shape[0], masked.shape[0]), 0)
    dy = exact_dot((places == line(masked)).astype(F32), cot[...])
    sums[0:1, :] = jnp.sum(dy * x, axis=0, keepdims=True)
    sums[1:2, :] = jnp.sum(dy, axis=0, keepdims=True)
    grad_in = standardize_back(dy * line(gain2), x, inv)
    d_h2[...] = grad_in
    d_ff[...] = grad_in.astype(BF16)


def ffn_forward(low, unit, gain1, shift1, gain2, shift2, masked, cot, w_in, w_out, size):
    rows, width = low.shape
    hid = w_out.shape[0]
    return pl.pallas_call(
        ffn_forward_kernel,
        name="ffn_forward",
        out_shape=(
            shape((rows, width), BF16),
            shape((rows, width), F32),
            shape((rows, width), BF16),
            shape((rows, hid), BF16),
            shape((rows, hid), BF16),
            shape((2, width), F32),
        ),
        in_specs=[VM] * 10,
        out_specs=(VM,) * 6,
        scratch_shapes=[
            scratch((rows, width), F32),
            scratch((2, rows, size), F32),
            scratch((2, rows, size), F32),
        ],
        compiler_params=params(14),
        cost_estimate=pl.CostEstimate(
            flops=6 * rows * width * hid, bytes_accessed=18 * 10**6, transcendentals=2 * rows * hid
        ),
    )(low, unit, gain1, shift1, gain2, shift2, masked, cot, w_in, w_out)


def ffn_backward_kernel(
    d_ff, d_h2, unit, inverse, gain1, sums2, act, slope, w_in, w_down, d_h1, sent, acc, hidden
):
    hid = w_down.shape[0]
    size = hidden.shape[2]
    count = hid // size

    def project(block, slot):
        here = pl.ds(pl.multiple_of(block * size, size), size)
        hidden[slot] = dot_nt(d_ff[...], w_down[here, :])

    def finish(block, slot):
        first = pl.multiple_of(block * size, size)
        here, there = pl.ds(first, size), pl.ds(pl.multiple_of(hid + first, size), size)
        d_hidden = hidden[slot]
        d_gate = (d_hidden * slope[:, here].astype(F32)).astype(BF16)
        d_up = (d_hidden * act[:, here].astype(F32)).astype(BF16)
        acc[...] += dot_nt(d_gate, w_in[:, here]) + dot_nt(d_up, w_in[:, there])

    acc[...] = d_h2[...]
    project(0, 0)

    def pair(index, carry):
        block = index * 2
        project(block + 1, 1)
        finish(block, 0)
        project(block + 2, 0)
        finish(block + 1, 1)
        return carry

    lax.fori_loop(0, count // 2 - 1, pair, 0)
    project(count - 1, 1)
    finish(count - 2, 0)
    finish(count - 1, 1)
    total = acc[...]
    rows = total.shape[0]
    x = unit[...]
    gain_sum = jnp.sum(total * x, axis=0, keepdims=True)
    shift_sum = jnp.sum(total, axis=0, keepdims=True)
    sums = jnp.concatenate([gain_sum, shift_sum, sums2[...]], axis=0)
    high = sums.astype(BF16).astype(F32)
    tail = jnp.concatenate([high, sums - high, jnp.zeros((8, sums.shape[1]), F32)], axis=0)
    grad = standardize_back(total * line(gain1), x, inverse[...])
    d_h1[...] = grad
    sent[0:rows, :] = grad.astype(BF16)
    sent[rows : rows + 16, :] = tail.astype(BF16)


def ffn_backward(d_ff, d_h2, unit, inverse, gain1, sums2, act, slope, w_in, w_out, size):
    rows, width = d_ff.shape
    hid = w_out.shape[0]
    return pl.pallas_call(
        ffn_backward_kernel,
        name="ffn_backward",
        out_shape=(shape((rows, width), F32), shape((rows + 16, width), BF16)),
        in_specs=[VM] * 10,
        out_specs=(VM,) * 2,
        scratch_shapes=[scratch((rows, width), F32), scratch((2, rows, size), F32)],
        compiler_params=params(14),
        cost_estimate=pl.CostEstimate(
            flops=6 * rows * width * hid, bytes_accessed=20 * 10**6, transcendentals=0
        ),
    )(d_ff, d_h2, unit, inverse, gain1, sums2, act, slope, w_in, w_out)


X_FIRST = (1, 2, 4)
Z_FIRST = (2, 1, 4)


def bit_of(value, mask):
    return (value // mask) % 2


def store_blocks(blocks, keep, send, place, order, columns):
    one, two, three = order
    odd = bit_of(place, one) == 1
    for index in range(8):
        if index & one:
            continue
        spot = bit_of(place ^ index, two) * 2 + bit_of(place ^ index, three)
        low, high = blocks(index), blocks(index | one)
        keep[spot, :, columns] = jnp.where(odd, high, low).astype(BF16)
        send[spot, :, columns] = jnp.where(odd, low, high).astype(BF16)


def row_blocks(grad):
    each = grad.shape[0] // 8
    return lambda index: grad[index * each : (index + 1) * each]


def ffn_grad_kernel(
    size, info, n0, n1, n2, n3, f0, f1, f2, f3, w_in, w_down,
    keep_gate, send_gate, keep_up, send_up, keep_down, send_down,
    tok_t, gates, ups, d_hiddens, hidden_t, d_gate, d_up, d_ff, down,
):
    toks, grads = (n0, n1, n2, n3), (f0, f1, f2, f3)
    rows = n0.shape[0]
    units = w_down.shape[0]
    for at in range(RANKS):
        here = slice(at * rows, (at + 1) * rows)
        d_ff[here, :] = grads[at][...]
        tok_t[:, here] = jnp.transpose(toks[at][...])

    def unit_block(step, carry):
        here = pl.ds(pl.multiple_of(step * size, size), size)
        there = pl.ds(pl.multiple_of(units + step * size, size), size)
        w_gate, w_up, w_rows = w_in[:, here], w_in[:, there], w_down[here, :]

        def project(at):
            slot = at % 2
            gates[slot] = dot(toks[at][...], w_gate)
            ups[slot] = dot(toks[at][...], w_up)
            d_hiddens[slot] = dot_nt(grads[at][...], w_rows)

        def finish(at):
            slot = at % 2
            here = slice(at * rows, (at + 1) * rows)
            value, grad = gelu_pair(gates[slot])
            up, d_hidden = ups[slot], d_hiddens[slot]
            hidden_t[:, here] = jnp.transpose((value * up).astype(BF16))
            d_gate[here, :] = (d_hidden * up * grad).astype(BF16)
            d_up[here, :] = (d_hidden * value).astype(BF16)

        project(0)
        for at in range(RANKS):
            if at + 1 < RANKS:
                project(at + 1)
            finish(at)
        total = dot(tok_t[...], d_gate[...])
        store_blocks(row_blocks(total), keep_gate, send_gate, info[1], Z_FIRST, here)
        total = dot(tok_t[...], d_up[...])
        store_blocks(row_blocks(total), keep_up, send_up, info[1], Z_FIRST, here)
        down[here, :] = dot(hidden_t[...], d_ff[...])
        return carry

    lax.fori_loop(0, units // size, unit_block, 0)
    store_blocks(row_blocks(down), keep_down, send_down, info[1], X_FIRST, slice(None))


def ffn_grad(info, toks, grads, w_in, w_down, size):
    rows, width = toks[0].shape
    units = w_down.shape[0]
    tok = rows * RANKS
    dims = [(4, width // 8, units)] * 4 + [(4, units // 8, width)] * 2
    return pl.pallas_call(
        functools.partial(ffn_grad_kernel, size),
        name="ffn_grad",
        out_shape=[shape(each, BF16) for each in dims],
        in_specs=[SM] + [VM] * 10,
        out_specs=[VM] * 6,
        scratch_shapes=[
            scratch((width, tok), BF16),
            scratch((2, rows, size), F32),
            scratch((2, rows, size), F32),
            scratch((2, rows, size), F32),
            scratch((size, tok), BF16),
            scratch((tok, size), BF16),
            scratch((tok, size), BF16),
            scratch((tok, width), BF16),
            scratch((units, width), F32),
        ],
        compiler_params=params(18),
        cost_estimate=pl.CostEstimate(
            flops=12 * tok * width * units,
            bytes_accessed=8 * 10**6,
            transcendentals=2 * tok * units,
        ),
    )(info, *toks, *grads, w_in, w_down)


def qkv_grad_kernel(
    info, x0, x1, x2, x3, d0, d1, d2, d3, j0, j1, j2, j3, g0, g1, g2, g3, keep, send, columns, grad
):
    rows, width = x0.shape
    part = width // RANKS
    total = 0.0
    for x, d_qkv in zip((x0, x1, x2, x3), (d0, d1, d2, d3)):
        total = total + dot(d_qkv[...], x[...])
    grad[:, : 3 * part] = jnp.transpose(total)
    for value in range(RANKS):

        @pl.when(info[0] == value)
        def _():
            for at, g in enumerate((g0, g1, g2, g3)):
                columns[at] = g[0:rows, value * part : (value + 1) * part]

    total = 0.0
    sums = 0.0
    for at, (joined, g) in enumerate(zip((j0, j1, j2, j3), (g0, g1, g2, g3))):
        total = total + dot(joined[...], columns[at])
        pair = g[rows : rows + 16, :].astype(F32)
        sums = sums + pair[0:4] + pair[4:8]
    grad[:, 3 * part :] = total
    high = sums.astype(BF16).astype(F32)
    tail = jnp.concatenate([high, sums - high], axis=0)
    each = width // 8

    def blocks(index):
        return jnp.concatenate([grad[index * each : (index + 1) * each], tail], axis=0)

    store_blocks(blocks, keep, send, info[1], X_FIRST, slice(None))


def qkv_grad(info, blocks, d_qkv, joined, d_proj):
    rows, width = blocks[0].shape
    return pl.pallas_call(
        qkv_grad_kernel,
        name="qkv_grad",
        out_shape=(shape((4, width // 8 + 8, width), BF16),) * 2,
        in_specs=[SM] + [VM] * 16,
        out_specs=(VM, VM),
        scratch_shapes=[
            scratch((RANKS, rows, width // RANKS), BF16),
            scratch((width, width), F32),
        ],
        compiler_params=params(14),
        cost_estimate=pl.CostEstimate(
            flops=8 * rows * width * width, bytes_accessed=4 * 10**6, transcendentals=0
        ),
    )(info, *blocks, *d_qkv, *joined, *d_proj)


def unpack(part, packed, wide, first):
    few = packed.shape[1] // RANKS
    for run in range(few // part):
        pieces = []
        for value in range(RANKS):
            at = value * few + run * part
            pieces.append(packed[:, at : at + part])
        at = first + run * RANKS * part
        wide[:, at : at + RANKS * part] = jnp.concatenate(pieces, axis=1).astype(F32)


def join_early_kernel(info, b0, b1, b2, b3, down, packed):
    rows, columns = b0.shape
    few = columns // 2
    for step, block in enumerate((b0, b1, b2, b3)):
        there = info[0] ^ step
        packed[:, pl.ds(pl.multiple_of(there * few, few), few)] = block[:, few:]
        down[pl.ds(pl.multiple_of(there * rows, rows), rows), :] = block[:, :few].astype(F32)


def join_wide_kernel(part, info, b0, b1, b2, b3, gates, wide, ups):
    few = b0.shape[1]
    for step, block in enumerate((b0, b1, b2, b3)):
        there = pl.multiple_of((info[0] ^ step) * few, few)
        ups[:, pl.ds(there, few)] = block[...]
    unpack(part, gates, wide, 0)
    unpack(part, ups, wide, RANKS * few)


def join_heads_kernel(info, b0, b1, b2, b3, out, rest):
    width = rest.shape[1]
    heads = width // RANKS
    for value in range(RANKS):

        @pl.when(info[0] == value)
        def _():
            for step, block in enumerate((b0, b1, b2, b3)):
                there = (value ^ step) * heads
                for third in range(3):
                    piece = block[:, third * heads : (third + 1) * heads].astype(F32)
                    out[:, third * width + there : third * width + there + heads] = piece
                rest[:, there : there + heads] = block[:, 3 * heads :].astype(F32)


def join_early(info, blocks):
    rows, columns = blocks[0].shape
    if rows % 8:
        stacked = jnp.stack(blocks)[info[0] ^ jnp.arange(RANKS)]
        few = columns // 2
        gates = jnp.concatenate(list(stacked[:, :, few:]), axis=1)
        return stacked[:, :, :few].reshape(-1, few).astype(F32), gates
    return pl.pallas_call(
        join_early_kernel,
        name="join_early",
        out_shape=(
            shape((rows * RANKS, columns // 2), F32),
            shape((rows, RANKS * columns // 2), BF16),
        ),
        in_specs=[SM] + [VM] * 4,
        out_specs=(VM, VM),
        compiler_params=params(8),
        cost_estimate=NO_COST,
    )(info, *blocks)


def join_wide(info, blocks, gates, part):
    rows, width = blocks[0].shape
    if RANKS * part % 128:
        stacked = jnp.stack(blocks)[info[0] ^ jnp.arange(RANKS)].astype(F32)
        both = [gates.astype(F32), jnp.concatenate(list(stacked), axis=1)]
        wide = [each.reshape(rows, RANKS, -1, part).transpose(0, 2, 1, 3) for each in both]
        return jnp.concatenate([each.reshape(rows, -1) for each in wide], axis=1)
    return pl.pallas_call(
        functools.partial(join_wide_kernel, part),
        name="join_wide",
        out_shape=shape((rows, 2 * RANKS * width), F32),
        in_specs=[SM] + [VM] * 5,
        out_specs=VM,
        scratch_shapes=[scratch((rows, RANKS * width), BF16)],
        compiler_params=params(14),
        cost_estimate=NO_COST,
    )(info, *blocks, gates)


def join_heads(info, blocks):
    rows, width = blocks[0].shape
    return pl.pallas_call(
        join_heads_kernel,
        name="join_heads",
        out_shape=(shape((rows, 3 * width), F32), shape((rows, width), F32)),
        in_specs=[SM] + [VM] * 4,
        out_specs=(VM, VM),
        compiler_params=params(8),
        cost_estimate=NO_COST,
    )(info, *blocks)


def token_grad_kernel(
    info, own, near, far, cross, w, d_h1, masked, tokens, replacement, joined
):
    rows, width = d_h1.shape
    part = width // RANKS
    for step, block in enumerate((own, near, far, cross)):
        for third in range(3):
            first = pl.multiple_of(third * width + (info[0] ^ step) * part, part)
            joined[pl.ds(first, part), :] = block[third * part : (third + 1) * part, :]
    grad = d_h1[...] + jnp.transpose(dot(w[...], joined[...]))
    count = masked.shape[0]
    places = lax.broadcasted_iota(jnp.int32, (rows, count), 0)
    select = (places == line(masked)).astype(F32)
    hit = jnp.max(select, axis=1, keepdims=True)
    tokens[...] = jnp.where(hit > 0.5, 0.0, grad)
    replacement[...] = lax.dot_general(
        select, grad, (((0,), (0,)), ((), ())),
        precision=lax.Precision.HIGHEST, preferred_element_type=F32,
    )


def token_grad(info, parts, w, d_h1, masked):
    rows, width = d_h1.shape
    return pl.pallas_call(
        token_grad_kernel,
        name="token_grad",
        out_shape=(shape((rows, width), F32), shape((masked.shape[0], width), F32)),
        in_specs=[SM] + [VM] * 7,
        out_specs=(VM, VM),
        scratch_shapes=[scratch((3 * width, rows), BF16)],
        compiler_params=params(16),
        cost_estimate=pl.CostEstimate(
            flops=6 * rows * width * width, bytes_accessed=8 * 10**6, transcendentals=0
        ),
    )(info, *parts, w, d_h1, masked)


def after(value, *others):
    return lax.optimization_barrier((value,) + others)[0]


def flip(value, axis, bits):
    count = lax.axis_size(axis)
    return lax.ppermute(value, axis, [(index, index ^ bits) for index in range(count)])


def gather_blocks(value):
    far = flip(value, "sp", 2)
    near = flip(value, "sp", 1)
    cross = flip(far, "sp", 1)
    return [value, near, far, cross]


def exchange_blocks(blocks):
    via = flip(blocks[3], "sp", 1)
    near = flip(blocks[1], "sp", 1)
    far = flip(blocks[2], "sp", 2)
    cross = flip(via, "sp", 2)
    return [blocks[0], near, far, cross]


def small_mesh():
    return lax.axis_size("dp") == 8


NO_COST = pl.CostEstimate(flops=0, bytes_accessed=0, transcendentals=0)


def tidy_sums(value):
    first = value.shape[1] - 8
    sums = value[:, first : first + 4] + value[:, first + 4 :]
    high = sums.astype(BF16).astype(F32)
    return jnp.concatenate([value[:, :first], high, sums - high], axis=1)


def halve_kernel(with_sums, keep, came, kept, sent):
    half = keep.shape[0] // 2
    value = keep[...].astype(F32) + came[...].astype(F32)
    if with_sums:
        value = tidy_sums(value)
    kept[...] = value[:half]
    sent[...] = value[half:].astype(BF16)


def halve(keep, came, with_sums=False):
    dims = (keep.shape[0] // 2,) + keep.shape[1:]
    return pl.pallas_call(
        functools.partial(halve_kernel, with_sums),
        name="halve",
        out_shape=(shape(dims, F32), shape(dims, BF16)),
        in_specs=[VM] * 2,
        out_specs=(VM, VM),
        compiler_params=params(12),
        cost_estimate=NO_COST,
    )(keep, came)


def send_first(send, order):
    return flip(send, "dp", order[0]) if small_mesh() else send


def next_half(keep, came, with_sums=False):
    return halve(keep, came, with_sums) if small_mesh() else (keep, came)


def send_on(send, bits):
    return flip(send, "dp", bits) if small_mesh() else send


def send_second(keep, came, order, with_sums=False):
    keep, send = next_half(keep, came, with_sums)
    return keep, send_on(send, order[1])


def send_third(keep, came, order, with_sums=False):
    keep, send = next_half(keep, came, with_sums)
    return keep, send_on(send, order[2])


def natural_blocks(keep, send, order):
    both = jnp.concatenate([keep, send], axis=0).astype(F32)
    places = []
    for index in range(8):
        bits = [1 if index & mask else 0 for mask in order]
        places.append(both[bits[0] * 4 + bits[1] * 2 + bits[2]])
    return places


def scatter_sum(blocks):
    grad = jnp.concatenate(blocks, axis=0)
    return lax.psum_scatter(grad, "dp", scatter_dimension=0, tiled=True).astype(BF16)


def finish_pair_kernel(keep_a, came_a, keep_b, came_b, out):
    columns = keep_a.shape[2]
    out[:, :columns] = (keep_a[0] + came_a[0].astype(F32)).astype(BF16)
    out[:, columns:] = (keep_b[0] + came_b[0].astype(F32)).astype(BF16)


def finish_pair(keep_a, came_a, order_a, keep_b, came_b, order_b):
    if not small_mesh():
        first = scatter_sum(natural_blocks(keep_a, came_a, order_a))
        second = scatter_sum(natural_blocks(keep_b, came_b, order_b))
        return jnp.concatenate([first, second], axis=1)
    _, rows, columns = keep_a.shape
    return pl.pallas_call(
        finish_pair_kernel,
        name="finish_pair",
        out_shape=shape((rows, columns + keep_b.shape[2]), BF16),
        in_specs=[VM] * 4,
        out_specs=VM,
        compiler_params=params(8),
        cost_estimate=NO_COST,
    )(keep_a, came_a, keep_b, came_b)


def finish_kernel(keep, came, out):
    out[...] = (keep[0] + came[0].astype(F32)).astype(BF16)


def finish_sum(keep, came, order):
    if not small_mesh():
        return scatter_sum(natural_blocks(keep, came, order))
    return pl.pallas_call(
        finish_kernel,
        name="finish_sum",
        out_shape=shape(keep.shape[1:], BF16),
        in_specs=[VM] * 2,
        out_specs=VM,
        compiler_params=params(8),
        cost_estimate=NO_COST,
    )(keep, came)


def finish_heads_kernel(keep, came, out, *sums):
    rows = out.shape[0]
    total = keep[0] + came[0].astype(F32)
    out[...] = total[:rows].astype(BF16)
    for index, vector in enumerate(sums):
        value = total[rows + index : rows + index + 1] + total[rows + 4 + index : rows + 5 + index]
        vector[...] = value.reshape(-1)


def finish_heads(keep, came):
    _, rows, columns = keep.shape
    rows = rows - 8
    if not small_mesh():
        blocks = natural_blocks(keep, came, X_FIRST)
        sums = blocks[0][rows : rows + 4] + blocks[0][rows + 4 :]
        return scatter_sum([block[:rows] for block in blocks]), list(lax.psum(sums, "dp"))
    out, *sums = pl.pallas_call(
        finish_heads_kernel,
        name="finish_heads",
        out_shape=(shape((rows, columns), BF16),) + (shape((columns,), F32),) * 4,
        in_specs=[VM] * 2,
        out_specs=(VM,) * 5,
        compiler_params=params(8),
        cost_estimate=NO_COST,
    )(keep, came)
    return out, sums


def local(
    tokens,
    segment_ids,
    masked_rows,
    replacement,
    cotangent,
    w_qkv,
    w_out_attn,
    w_in_ff,
    w_out_ff,
    gain_one,
    shift_one,
    gain_two,
    shift_two,
):
    rows_dev, width = tokens.shape
    rank = lax.axis_index("sp")
    heads = HEADS // RANKS
    dim = width // HEADS
    part = heads * dim
    slopes = alibi_slopes(HEADS)

    select = jnp.arange(rows_dev, dtype=jnp.int32)[:, None] == masked_rows[None, :]
    hit = jnp.any(select, axis=1, keepdims=True)
    placed = dot(select.astype(BF16), replacement)
    start = jnp.where(hit, placed.astype(BF16), tokens)
    start_far = flip(start, "sp", 2)
    start_near = flip(start, "sp", 1)
    place = lax.axis_index("dp")
    place = place if small_mesh() else place * 0
    spot = jnp.stack([rank, place]).astype(jnp.int32)

    w_rank = jnp.concatenate(
        [
            lax.dynamic_slice_in_dim(w_qkv, third * width + rank * part, part, 1)
            for third in range(3)
        ],
        axis=1,
    )
    start_cross = flip(after(start_far, w_rank, spot), "sp", 1)
    start_blocks = [start, start_near, start_far, start_cross]
    qkv, attn, lse = attention_forward(
        spot, segment_ids, slopes, start_blocks, w_rank, heads, dim
    )
    attn_far = flip(attn, "sp", 2)
    attn_near = flip(attn, "sp", 1)
    part_units = w_out_ff.shape[0] // lax.axis_size("dp") // RANKS
    packed_in, packed_down = pack_weights(after(spot, lse), w_in_ff, w_out_ff, part_units)
    attn_cross = flip(after(attn_far, packed_in), "sp", 1)
    attn_parts = [attn, attn_near, attn_far, attn_cross]
    low, joined, unit, inverse = norm_one(
        spot, attn_parts, start, w_out_attn, gain_one, shift_one
    )
    layer_out, d_h2, d_ff, slope, act, sums2 = ffn_forward(
        low, unit, gain_one, shift_one, gain_two, shift_two,
        masked_rows, cotangent, w_in_ff, w_out_ff, 768,
    )
    d_ff_far = flip(d_ff, "sp", 2)
    d_ff_near = flip(d_ff, "sp", 1)
    d_h1, sent = ffn_backward(
        d_ff, d_h2, unit, inverse, gain_one, sums2, act, slope, w_in_ff, w_out_ff, 768
    )
    lows, others_joined = norm_others(
        after(spot, sent), attn_parts, start_blocks[1:], w_out_attn, gain_one, shift_one
    )
    d_ff_far = after(d_ff_far, lows[0])
    d_ff_cross = flip(d_ff_far, "sp", 1)
    d_ff_blocks = [d_ff, d_ff_near, d_ff_far, d_ff_cross]
    far = flip(sent, "sp", 2)
    near = flip(sent, "sp", 1)

    keep_g, send_g, keep_u, send_u, keep_d, send_d = ffn_grad(
        spot, [low, *lows], d_ff_blocks, packed_in, packed_down, 256
    )
    came_g = send_first(send_g, Z_FIRST)
    came_d = send_first(send_d, X_FIRST)
    cross = flip(after(far, keep_g), "sp", 1)
    d_proj_blocks = [sent, near, far, cross]

    d_qkv = attention_backward(
        spot, segment_ids, slopes, d_proj_blocks, w_out_attn, qkv, lse, heads, dim
    )
    parts = exchange_blocks(d_qkv)
    came_u = send_first(after(send_u, d_qkv[0]), Z_FIRST)
    keep_g, came_g = send_second(keep_g, after(came_g, d_qkv[0]), Z_FIRST)
    keep_d, came_d = send_second(keep_d, after(came_d, keep_g), X_FIRST)
    keep_q, send_q = qkv_grad(
        after(spot, keep_d), start_blocks, d_qkv, [joined, *others_joined], d_proj_blocks
    )
    keep_g, came_g = send_third(keep_g, after(came_g, keep_q), Z_FIRST)
    came_q = send_first(after(send_q, keep_g), X_FIRST)
    keep_d, came_d = send_third(keep_d, after(came_d, keep_g), X_FIRST)
    keep_u, came_u = send_second(keep_u, after(came_u, keep_d), Z_FIRST)
    keep_q, send_q = next_half(keep_q, after(came_q, keep_u, parts), True)
    early = finish_pair(keep_d, after(came_d, keep_q), X_FIRST, keep_g, came_g, Z_FIRST)
    came_q = send_on(after(send_q, early), X_FIRST[1])
    far = flip(early, "sp", 2)
    near = flip(early, "sp", 1)
    keep_u, came_u = send_third(keep_u, after(came_u, early), Z_FIRST)
    keep_q, came_q = send_third(keep_q, after(came_q, keep_u, came_u, far), X_FIRST, True)
    early_blocks = [early, near, far, flip(after(far, keep_q), "sp", 1)]
    ups = finish_sum(keep_u, after(came_u, keep_q), Z_FIRST)
    far = flip(ups, "sp", 2)
    near = flip(ups, "sp", 1)
    grad_tokens, grad_replacement = token_grad(
        after(spot, ups), parts, w_qkv, d_h1, masked_rows
    )
    grad_down, gates = join_early(after(spot, grad_tokens), early_blocks)
    up_blocks = [ups, near, far, flip(after(far, gates), "sp", 1)]
    heads_share, norm_sums = finish_heads(keep_q, after(came_q, gates, up_blocks[2]))
    far = flip(heads_share, "sp", 2)
    near = flip(heads_share, "sp", 1)
    grad_in = join_wide(after(spot, heads_share), up_blocks, gates, part_units)
    head_blocks = [heads_share, near, far, flip(after(far, grad_in), "sp", 1)]
    grad_qkv, grad_out = join_heads(spot, head_blocks)

    return (
        layer_out,
        grad_tokens,
        grad_replacement,
        grad_qkv,
        grad_out,
        grad_in,
        grad_down,
        norm_sums[0],
        norm_sums[1],
        norm_sums[2],
        norm_sums[3],
    )


def solution(mesh):
    tokens = P(("dp", "sp"), None)
    rows = P("dp", None)
    return jax.shard_map(
        local,
        mesh=mesh,
        in_specs=(tokens, rows, P(("dp", "sp")), tokens, tokens) + (P(),) * 8,
        out_specs=(tokens,) * 3 + (rows,) * 4 + (P(),) * 4,
        check_vma=False,
    )
```

```python
import functools
import math

import jax
import jax.numpy as jnp
from jax import lax
from jax.experimental import pallas as pl
from jax.experimental.pallas import tpu as pltpu
from jax.sharding import PartitionSpec as P

HEADS = 12
RANKS = 4
EPSILON = 1e-05
FAR = 1e30
F32 = jnp.float32
BF16 = jnp.bfloat16
VM = pl.BlockSpec(memory_space=pltpu.VMEM)
SM = pl.BlockSpec(memory_space=pltpu.SMEM)


def shape(dims, kind):
    return jax.ShapeDtypeStruct(dims, kind)


def scratch(dims, kind):
    return pltpu.VMEM(dims, kind)


def params(mebibytes):
    return pltpu.CompilerParams(vmem_limit_bytes=mebibytes << 20)


def alibi_slopes(head_count):
    nearest = 2 ** int(math.floor(math.log2(head_count)))
    base_list = [2.0 ** (-8.0 * (index + 1) / nearest) for index in range(nearest)]
    extra_list = [
        2.0 ** (-8.0 * (2 * index + 1) / (2 * nearest)) for index in range(head_count - nearest)
    ]
    return jnp.array(base_list + extra_list, dtype=F32)


def dot(a, b):
    return jnp.dot(a, b, preferred_element_type=F32)


def dot_nt(a, b):
    return lax.dot_general(a, b, (((1,), (1,)), ((), ())), preferred_element_type=F32)


def dot_tn(a, b):
    return lax.dot_general(a, b, (((0,), (0,)), ((), ())), preferred_element_type=F32)


def exact_dot(a, b):
    return jnp.dot(a, b, precision=lax.Precision.HIGHEST, preferred_element_type=F32)


def standardize(value):
    center = value - jnp.mean(value, axis=-1, keepdims=True)
    spread = jnp.mean(center * center, axis=-1, keepdims=True)
    inverse = lax.rsqrt(spread + EPSILON)
    return center * inverse, inverse


def standardize_back(grad, unit, inverse):
    mean = jnp.mean(grad, axis=-1, keepdims=True)
    return inverse * (grad - mean - unit * jnp.mean(grad * unit, axis=-1, keepdims=True))


def gelu_pair(x):
    cdf = 0.5 * (1.0 + lax.erf(x * math.sqrt(0.5)))
    pdf = jnp.exp(-0.5 * x * x) * (1.0 / math.sqrt(2.0 * math.pi))
    return x * cdf, cdf + x * pdf


def pair_active(seg, rank, first, second, rows):
    one, two = rank ^ first, rank ^ second
    low, high = jnp.minimum(one, two), jnp.maximum(one, two)
    return jnp.logical_or(one == two, seg[0, low * rows + rows - 1] == seg[0, high * rows])


def key_sequences(seg_rows, seg_keys, rank, rows):
    for at in range(RANKS):
        first = pl.multiple_of((rank ^ at) * rows, rows)
        line = jnp.broadcast_to(seg_rows[:, pl.ds(first, rows)], (128, rows))
        seg_keys[at * rows : (at + 1) * rows, :] = jnp.transpose(line)


def pair_distance(seg_rows, seg_keys, rank, keys_at, query_at, rows):
    key_pos, query_pos = (rank ^ keys_at) * rows, (rank ^ query_at) * rows
    down = lax.broadcasted_iota(jnp.int32, (rows, rows), 0)
    across = lax.broadcasted_iota(jnp.int32, (rows, rows), 1)
    gap = jnp.abs(down - across + (key_pos - query_pos)).astype(F32)
    seg_q = seg_rows[:, pl.ds(pl.multiple_of(query_pos, rows), rows)]
    seg_k = seg_keys[pl.ds(pl.multiple_of(keys_at * rows, rows), rows), 0:1]
    return jnp.where(seg_k == seg_q, gap, FAR)


def attention_forward_kernel(
    rows, heads, dim, info, seg, slopes, x0, x1, x2, x3, w, seg_rows,
    qkv_out, out_t, lse, qs, ks, vt, dist, seg_keys, score, peak,
):
    rank = info[0]
    width = heads * dim
    key_sequences(seg_rows, seg_keys, rank, rows)
    for at, x in enumerate((x0, x1, x2, x3)):
        qkv = dot(x[...], w[...]).astype(BF16)
        here = pl.ds(at * rows, rows)
        qkv_out[here, :] = qkv
        for h in range(heads):
            qs[h, here, :] = (qkv[:, h * dim : (h + 1) * dim] * dim**-0.5).astype(BF16)
            ks[h, here, :] = qkv[:, width + h * dim : width + (h + 1) * dim]
        vt[:, here] = jnp.transpose(qkv[:, 2 * width :])

    for a in range(RANKS):
        mine = pl.ds(a * rows, rows)
        peak[...] = jnp.full_like(peak, -jnp.inf)

        def first_pass(b, carry):
            @pl.when(pair_active(seg, rank, a, b, rows))
            def _():
                theirs = pl.ds(pl.multiple_of(b * rows, rows), rows)
                gap = pair_distance(seg_rows, seg_keys, rank, b, a, rows)
                for h in range(heads):
                    slope = slopes[rank * heads + h]
                    s = dot_nt(ks[h, theirs, :], qs[h, mine, :]) - slope * gap
                    score[h, theirs, :] = s
                    peak[h : h + 1, :] = jnp.maximum(
                        peak[h : h + 1, :], jnp.max(s, axis=0, keepdims=True)
                    )

            return carry

        lax.fori_loop(0, RANKS, first_pass, 0)

        def second_pass(b, carry):
            def add(carry):
                theirs = pl.ds(pl.multiple_of(b * rows, rows), rows)
                result = []
                for h in range(heads):
                    acc, total = carry[h]
                    p = jnp.exp(score[h, theirs, :] - peak[h : h + 1, :])
                    total = total + jnp.sum(p, axis=0, keepdims=True)
                    span = slice(h * dim, (h + 1) * dim)
                    result.append((acc + dot(vt[span, theirs], p.astype(BF16)), total))
                return tuple(result)

            return lax.cond(pair_active(seg, rank, a, b, rows), add, lambda carry: carry, carry)

        empty = (jnp.zeros((dim, rows), F32), jnp.zeros((1, rows), F32))
        sums = lax.fori_loop(0, RANKS, second_pass, (empty,) * heads)
        for h in range(heads):
            acc, total = sums[h]
            span = slice(h * dim, (h + 1) * dim)
            out_t[span, mine] = (acc / total).astype(BF16)
            lse[h : h + 1, mine] = peak[h : h + 1, :] + jnp.log(total)


def attention_forward(info, seg, slopes, blocks, w, heads, dim):
    rows = blocks[0].shape[0]
    tok, lw = rows * RANKS, heads * dim
    return pl.pallas_call(
        functools.partial(attention_forward_kernel, rows, heads, dim),
        name="attention_forward",
        out_shape=(
            shape((tok, 3 * lw), BF16),
            shape((lw, tok), BF16),
            shape((heads, tok), F32),
        ),
        in_specs=[SM] * 3 + [VM] * 6,
        out_specs=(VM,) * 3,
        scratch_shapes=[
            scratch((heads, tok, dim), BF16),
            scratch((heads, tok, dim), BF16),
            scratch((lw, tok), BF16),
            scratch((rows, rows), F32),
            scratch((tok, 128), jnp.int32),
            scratch((heads, tok, rows), F32),
            scratch((heads, rows), F32),
        ],
        compiler_params=params(14),
        cost_estimate=pl.CostEstimate(
            flops=4 * 10**9, bytes_accessed=6 * 10**6, transcendentals=3 * 10**6
        ),
    )(info, seg, slopes, *blocks, w, seg)


def attention_backward_kernel(
    rows, heads, dim, info, seg, slopes, g0, g1, g2, g3, w, qkv, lse, seg_rows,
    d0, d2, pair, qs, ks, kt, vs, do, seg_keys, prob, dprob, dk, dv, dqt, delta,
):
    rank = info[0]
    width = heads * dim
    scale = dim**-0.5
    key_sequences(seg_rows, seg_keys, rank, rows)
    w_rank = w[pl.ds(pl.multiple_of(rank * width, width), width), :]
    for at, g in enumerate((g0, g1, g2, g3)):
        here = pl.ds(at * rows, rows)
        grad = dot_nt(g[0:rows, :], w_rank).astype(BF16)
        value = qkv[here, :]
        kt[:, here] = jnp.transpose(value[:, width : 2 * width])
        for h in range(heads):
            do[h, here, :] = grad[:, h * dim : (h + 1) * dim]
            qs[h, here, :] = (value[:, h * dim : (h + 1) * dim] * scale).astype(BF16)
            ks[h, here, :] = value[:, width + h * dim : width + (h + 1) * dim]
            vs[h, here, :] = value[:, 2 * width + h * dim : 2 * width + (h + 1) * dim]
    dk[...] = jnp.zeros_like(dk)
    dv[...] = jnp.zeros_like(dv)

    for a in range(RANKS):
        mine = pl.ds(a * rows, rows)
        delta[...] = jnp.zeros_like(delta)
        dqt[...] = jnp.zeros_like(dqt)

        def first_pass(b, carry):
            @pl.when(pair_active(seg, rank, a, b, rows))
            def _():
                theirs = pl.ds(pl.multiple_of(b * rows, rows), rows)
                gap = pair_distance(seg_rows, seg_keys, rank, b, a, rows)
                for h in range(heads):
                    slope = slopes[rank * heads + h]
                    s = dot_nt(ks[h, theirs, :], qs[h, mine, :]) - slope * gap
                    p = jnp.exp(s - lse[h : h + 1, mine])
                    dp = dot_nt(vs[h, theirs, :], do[h, mine, :])
                    delta[h : h + 1, :] += jnp.sum(p * dp, axis=0, keepdims=True)
                    prob[h, theirs, :] = p
                    dprob[h, theirs, :] = dp

            return carry

        lax.fori_loop(0, RANKS, first_pass, 0)

        def second_pass(b, carry):
            @pl.when(pair_active(seg, rank, a, b, rows))
            def _():
                theirs = pl.ds(pl.multiple_of(b * rows, rows), rows)
                for h in range(heads):
                    p = prob[h, theirs, :]
                    ds = (p * (dprob[h, theirs, :] - delta[h : h + 1, :])).astype(BF16)
                    dv[h, theirs, :] += dot(p.astype(BF16), do[h, mine, :])
                    dk[h, theirs, :] += dot(ds, qs[h, mine, :])
                    span = slice(h * dim, (h + 1) * dim)
                    dqt[span, :] += dot(kt[span, theirs], ds)

            return carry

        lax.fori_loop(0, RANKS, second_pass, 0)
        (d0, pair.at[0], d2, pair.at[1])[a][0:width, :] = (dqt[...] * scale).astype(BF16)

    for at, d_qkv in enumerate((d0, pair.at[0], d2, pair.at[1])):
        here = pl.ds(at * rows, rows)
        for h in range(heads):
            first = width + h * dim
            d_qkv[first : first + dim, :] = jnp.transpose(dk[h, here, :]).astype(BF16)
            first = 2 * width + h * dim
            d_qkv[first : first + dim, :] = jnp.transpose(dv[h, here, :]).astype(BF16)


def attention_backward(info, seg, slopes, blocks, w, qkv, lse, heads, dim):
    tok, lw = qkv.shape[0], heads * dim
    rows = tok // RANKS
    return pl.pallas_call(
        functools.partial(attention_backward_kernel, rows, heads, dim),
        name="attention_backward",
        out_shape=(shape((3 * lw, rows), BF16),) * 2 + (shape((2, 3 * lw, rows), BF16),),
        in_specs=[SM] * 3 + [VM] * 8,
        out_specs=(VM,) * 3,
        scratch_shapes=[
            scratch((heads, tok, dim), BF16),
            scratch((heads, tok, dim), BF16),
            scratch((lw, tok), BF16),
            scratch((heads, tok, dim), BF16),
            scratch((heads, tok, dim), BF16),
            scratch((tok, 128), jnp.int32),
            scratch((heads, tok, rows), F32),
            scratch((heads, tok, rows), F32),
            scratch((heads, tok, dim), F32),
            scratch((heads, tok, dim), F32),
            scratch((lw, rows), F32),
            scratch((heads, rows), F32),
        ],
        compiler_params=params(20),
        cost_estimate=pl.CostEstimate(
            flops=8 * 10**9, bytes_accessed=6 * 10**6, transcendentals=3 * 10**6
        ),
    )(info, seg, slopes, *blocks, w, qkv, lse, seg)


def line(vector):
    return vector[...].reshape(1, -1)


def join_tokens(rank, arrays, tokens_of, joined):
    part = arrays[0].shape[0]
    rows = arrays[0].shape[1] // RANKS
    for step, array in enumerate(arrays):
        first = pl.multiple_of((rank ^ step) * part, part)
        block = step ^ tokens_of
        joined[pl.ds(first, part), :] = array[:, block * rows : (block + 1) * rows]


def norm_one_kernel(
    info, own, near, far, cross, start, w, gain, shift, low, joined, unit, inverse
):
    join_tokens(info[0], (own, near, far, cross), 0, joined)
    x, inv = standardize(start[...].astype(F32) + dot_tn(joined[...], w[...]))
    unit[...] = x
    inverse[...] = inv
    low[...] = (x * line(gain) + line(shift)).astype(BF16)


def norm_one(info, parts, start, w, gain, shift):
    rows, width = start.shape
    return pl.pallas_call(
        norm_one_kernel,
        name="norm_one",
        out_shape=(
            shape((rows, width), BF16),
            shape((width, rows), BF16),
            shape((rows, width), F32),
            shape((rows, 1), F32),
        ),
        in_specs=[SM] + [VM] * 8,
        out_specs=(VM,) * 4,
        compiler_params=params(12),
        cost_estimate=pl.CostEstimate(
            flops=2 * rows * width * width, bytes_accessed=4 * 10**6, transcendentals=0
        ),
    )(info, *parts, start, w, gain, shift)


def norm_others_kernel(
    info, own, near, far, cross, s1, s2, s3, w, gain, shift, l1, l2, l3, j1, j2, j3
):
    for tokens_of, (start, low, joined) in enumerate(((s1, l1, j1), (s2, l2, j2), (s3, l3, j3))):
        join_tokens(info[0], (own, near, far, cross), tokens_of + 1, joined)
        x, _ = standardize(start[...].astype(F32) + dot_tn(joined[...], w[...]))
        low[...] = (x * line(gain) + line(shift)).astype(BF16)


def norm_others(info, parts, starts, w, gain, shift):
    rows, width = starts[0].shape
    results = pl.pallas_call(
        norm_others_kernel,
        name="norm_others",
        out_shape=(shape((rows, width), BF16),) * 3 + (shape((width, rows), BF16),) * 3,
        in_specs=[SM] + [VM] * 10,
        out_specs=(VM,) * 6,
        compiler_params=params(12),
        cost_estimate=pl.CostEstimate(
            flops=6 * rows * width * width, bytes_accessed=4 * 10**6, transcendentals=0
        ),
    )(info, *parts, *starts, w, gain, shift)
    return results[:3], results[3:]


def packing(rows, columns, part, rank):
    units = lax.broadcasted_iota(jnp.int32, (rows, columns), 0)
    packed = lax.broadcasted_iota(jnp.int32, (1, columns), 1)
    places = packed + rank * part
    for index in range(1, columns // part):
        places = places + jnp.where(packed >= index * part, (RANKS - 1) * part, 0)
    return (units == places).astype(BF16)


def pack_kernel(part, info, w_in, w_down, packed_in, packed_down):
    rank = info[0]
    width, hid = w_in.shape[0], w_down.shape[0]
    run = hid // 2
    select = packing(run, run // RANKS, part, rank)
    for index in range(4):
        piece = dot(w_in[:, index * run : (index + 1) * run], select)
        packed_in[:, index * run // RANKS : (index + 1) * run // RANKS] = piece.astype(BF16)
    if part % 16:
        for index in range(2):
            piece = dot_tn(select, w_down[index * run : (index + 1) * run, :])
            packed_down[index * run // RANKS : (index + 1) * run // RANKS, :] = piece.astype(BF16)
    else:
        for index in range(hid // RANKS // part):
            rows = pl.ds(pl.multiple_of((index * RANKS + rank) * part, part), part)
            packed_down[index * part : (index + 1) * part, :] = w_down[rows, :]


def pack_weights(info, w_in, w_out, part):
    width, hid = w_in.shape[0], w_out.shape[0]
    return pl.pallas_call(
        functools.partial(pack_kernel, part),
        name="pack_weights",
        out_shape=(shape((width, 2 * hid // RANKS), BF16), shape((hid // RANKS, width), BF16)),
        in_specs=[SM, VM, VM],
        out_specs=(VM, VM),
        compiler_params=params(14),
        cost_estimate=pl.CostEstimate(
            flops=4 * 10**9, bytes_accessed=17 * 10**6, transcendentals=0
        ),
    )(info, w_in, w_out)


def ffn_forward_kernel(
    low, unit, gain1, shift1, gain2, shift2, masked, cot, w_in, w_down,
    layer_out, d_h2, d_ff, slope, act, sums, acc, gates, ups,
):
    hid = w_down.shape[0]
    size = gates.shape[2]
    count = hid // size

    def project(block, slot):
        first = pl.multiple_of(block * size, size)
        gates[slot] = dot(low[...], w_in[:, pl.ds(first, size)])
        ups[slot] = dot(low[...], w_in[:, pl.ds(pl.multiple_of(hid + first, size), size)])

    def finish(block, slot):
        here = pl.ds(pl.multiple_of(block * size, size), size)
        up = ups[slot]
        value, grad = gelu_pair(gates[slot])
        act[:, here] = value.astype(BF16)
        slope[:, here] = (up * grad).astype(BF16)
        acc[...] += dot((value * up).astype(BF16), w_down[here, :])

    acc[...] = unit[...] * line(gain1) + line(shift1)
    project(0, 0)

    def pair(index, carry):
        block = index * 2
        project(block + 1, 1)
        finish(block, 0)
        project(block + 2, 0)
        finish(block + 1, 1)
        return carry

    lax.fori_loop(0, count // 2 - 1, pair, 0)
    project(count - 1, 1)
    finish(count - 2, 0)
    finish(count - 1, 1)
    x, inv = standardize(acc[...])
    layer_out[...] = (x * line(gain2) + line(shift2)).astype(BF16)
    places = lax.broadcasted_iota(jnp.int32, (low.shape[0], masked.shape[0]), 0)
    dy = exact_dot((places == line(masked)).astype(F32), cot[...])
    sums[0:1, :] = jnp.sum(dy * x, axis=0, keepdims=True)
    sums[1:2, :] = jnp.sum(dy, axis=0, keepdims=True)
    grad_in = standardize_back(dy * line(gain2), x, inv)
    d_h2[...] = grad_in
    d_ff[...] = grad_in.astype(BF16)


def ffn_forward(low, unit, gain1, shift1, gain2, shift2, masked, cot, w_in, w_out, size):
    rows, width = low.shape
    hid = w_out.shape[0]
    return pl.pallas_call(
        ffn_forward_kernel,
        name="ffn_forward",
        out_shape=(
            shape((rows, width), BF16),
            shape((rows, width), F32),
            shape((rows, width), BF16),
            shape((rows, hid), BF16),
            shape((rows, hid), BF16),
            shape((2, width), F32),
        ),
        in_specs=[VM] * 10,
        out_specs=(VM,) * 6,
        scratch_shapes=[
            scratch((rows, width), F32),
            scratch((2, rows, size), F32),
            scratch((2, rows, size), F32),
        ],
        compiler_params=params(14),
        cost_estimate=pl.CostEstimate(
            flops=6 * rows * width * hid, bytes_accessed=18 * 10**6, transcendentals=2 * rows * hid
        ),
    )(low, unit, gain1, shift1, gain2, shift2, masked, cot, w_in, w_out)


def ffn_backward_kernel(
    d_ff, d_h2, unit, inverse, gain1, sums2, act, slope, w_in, w_down, d_h1, sent, acc, hidden
):
    hid = w_down.shape[0]
    size = hidden.shape[2]
    count = hid // size

    def project(block, slot):
        here = pl.ds(pl.multiple_of(block * size, size), size)
        hidden[slot] = dot_nt(d_ff[...], w_down[here, :])

    def finish(block, slot):
        first = pl.multiple_of(block * size, size)
        here, there = pl.ds(first, size), pl.ds(pl.multiple_of(hid + first, size), size)
        d_hidden = hidden[slot]
        d_gate = (d_hidden * slope[:, here].astype(F32)).astype(BF16)
        d_up = (d_hidden * act[:, here].astype(F32)).astype(BF16)
        acc[...] += dot_nt(d_gate, w_in[:, here]) + dot_nt(d_up, w_in[:, there])

    acc[...] = d_h2[...]
    project(0, 0)

    def pair(index, carry):
        block = index * 2
        project(block + 1, 1)
        finish(block, 0)
        project(block + 2, 0)
        finish(block + 1, 1)
        return carry

    lax.fori_loop(0, count // 2 - 1, pair, 0)
    project(count - 1, 1)
    finish(count - 2, 0)
    finish(count - 1, 1)
    total = acc[...]
    rows = total.shape[0]
    x = unit[...]
    gain_sum = jnp.sum(total * x, axis=0, keepdims=True)
    shift_sum = jnp.sum(total, axis=0, keepdims=True)
    sums = jnp.concatenate([gain_sum, shift_sum, sums2[...]], axis=0)
    high = sums.astype(BF16).astype(F32)
    tail = jnp.concatenate([high, sums - high, jnp.zeros((8, sums.shape[1]), F32)], axis=0)
    grad = standardize_back(total * line(gain1), x, inverse[...])
    d_h1[...] = grad
    sent[0:rows, :] = grad.astype(BF16)
    sent[rows : rows + 16, :] = tail.astype(BF16)


def ffn_backward(d_ff, d_h2, unit, inverse, gain1, sums2, act, slope, w_in, w_out, size):
    rows, width = d_ff.shape
    hid = w_out.shape[0]
    return pl.pallas_call(
        ffn_backward_kernel,
        name="ffn_backward",
        out_shape=(shape((rows, width), F32), shape((rows + 16, width), BF16)),
        in_specs=[VM] * 10,
        out_specs=(VM,) * 2,
        scratch_shapes=[scratch((rows, width), F32), scratch((2, rows, size), F32)],
        compiler_params=params(14),
        cost_estimate=pl.CostEstimate(
            flops=6 * rows * width * hid, bytes_accessed=20 * 10**6, transcendentals=0
        ),
    )(d_ff, d_h2, unit, inverse, gain1, sums2, act, slope, w_in, w_out)


X_FIRST = (1, 2, 4)
Z_FIRST = (2, 1, 4)


def bit_of(value, mask):
    return (value // mask) % 2


def store_blocks(blocks, keep, send, place, order, columns):
    one, two, three = order
    odd = bit_of(place, one) == 1
    for index in range(8):
        if index & one:
            continue
        spot = bit_of(place ^ index, two) * 2 + bit_of(place ^ index, three)
        low, high = blocks(index), blocks(index | one)
        keep[spot, :, columns] = jnp.where(odd, high, low).astype(BF16)
        send[spot, :, columns] = jnp.where(odd, low, high).astype(BF16)


def row_blocks(grad):
    each = grad.shape[0] // 8
    return lambda index: grad[index * each : (index + 1) * each]


def ffn_grad_kernel(
    size, info, n0, n1, n2, n3, f0, f1, f2, f3, w_in, w_down,
    keep_gate, send_gate, keep_up, send_up, keep_down, send_down,
    tok_t, gates, ups, d_hiddens, hidden_t, d_gate, d_up, d_ff, down,
):
    toks, grads = (n0, n1, n2, n3), (f0, f1, f2, f3)
    rows = n0.shape[0]
    units = w_down.shape[0]
    for at in range(RANKS):
        here = slice(at * rows, (at + 1) * rows)
        d_ff[here, :] = grads[at][...]
        tok_t[:, here] = jnp.transpose(toks[at][...])

    def unit_block(step, carry):
        here = pl.ds(pl.multiple_of(step * size, size), size)
        there = pl.ds(pl.multiple_of(units + step * size, size), size)
        w_gate, w_up, w_rows = w_in[:, here], w_in[:, there], w_down[here, :]

        def project(at):
            slot = at % 2
            gates[slot] = dot(toks[at][...], w_gate)
            ups[slot] = dot(toks[at][...], w_up)
            d_hiddens[slot] = dot_nt(grads[at][...], w_rows)

        def finish(at):
            slot = at % 2
            here = slice(at * rows, (at + 1) * rows)
            value, grad = gelu_pair(gates[slot])
            up, d_hidden = ups[slot], d_hiddens[slot]
            hidden_t[:, here] = jnp.transpose((value * up).astype(BF16))
            d_gate[here, :] = (d_hidden * up * grad).astype(BF16)
            d_up[here, :] = (d_hidden * value).astype(BF16)

        project(0)
        for at in range(RANKS):
            if at + 1 < RANKS:
                project(at + 1)
            finish(at)
        total = dot(tok_t[...], d_gate[...])
        store_blocks(row_blocks(total), keep_gate, send_gate, info[1], Z_FIRST, here)
        total = dot(tok_t[...], d_up[...])
        store_blocks(row_blocks(total), keep_up, send_up, info[1], Z_FIRST, here)
        down[here, :] = dot(hidden_t[...], d_ff[...])
        return carry

    lax.fori_loop(0, units // size, unit_block, 0)
    store_blocks(row_blocks(down), keep_down, send_down, info[1], X_FIRST, slice(None))


def ffn_grad(info, toks, grads, w_in, w_down, size):
    rows, width = toks[0].shape
    units = w_down.shape[0]
    tok = rows * RANKS
    dims = [(4, width // 8, units)] * 4 + [(4, units // 8, width)] * 2
    return pl.pallas_call(
        functools.partial(ffn_grad_kernel, size),
        name="ffn_grad",
        out_shape=[shape(each, BF16) for each in dims],
        in_specs=[SM] + [VM] * 10,
        out_specs=[VM] * 6,
        scratch_shapes=[
            scratch((width, tok), BF16),
            scratch((2, rows, size), F32),
            scratch((2, rows, size), F32),
            scratch((2, rows, size), F32),
            scratch((size, tok), BF16),
            scratch((tok, size), BF16),
            scratch((tok, size), BF16),
            scratch((tok, width), BF16),
            scratch((units, width), F32),
        ],
        compiler_params=params(18),
        cost_estimate=pl.CostEstimate(
            flops=12 * tok * width * units,
            bytes_accessed=8 * 10**6,
            transcendentals=2 * tok * units,
        ),
    )(info, *toks, *grads, w_in, w_down)


def qkv_grad_kernel(
    info, x0, x1, x2, x3, d0, d2, pair, j0, j1, j2, j3, g0, g1, g2, g3, keep, send, columns, grad
):
    rows, width = x0.shape
    part = width // RANKS
    total = 0.0
    for x, d_qkv in zip((x0, x1, x2, x3), (d0, pair.at[0], d2, pair.at[1])):
        total = total + dot(d_qkv[...], x[...])
    grad[:, : 3 * part] = jnp.transpose(total)
    for value in range(RANKS):

        @pl.when(info[0] == value)
        def _():
            for at, g in enumerate((g0, g1, g2, g3)):
                columns[at] = g[0:rows, value * part : (value + 1) * part]

    total = 0.0
    sums = 0.0
    for at, (joined, g) in enumerate(zip((j0, j1, j2, j3), (g0, g1, g2, g3))):
        total = total + dot(joined[...], columns[at])
        pair = g[rows : rows + 16, :].astype(F32)
        sums = sums + pair[0:4] + pair[4:8]
    grad[:, 3 * part :] = total
    high = sums.astype(BF16).astype(F32)
    tail = jnp.concatenate([high, sums - high], axis=0)
    each = width // 8

    def blocks(index):
        return jnp.concatenate([grad[index * each : (index + 1) * each], tail], axis=0)

    store_blocks(blocks, keep, send, info[1], X_FIRST, slice(None))


def qkv_grad(info, blocks, d_qkv, joined, d_proj):
    rows, width = blocks[0].shape
    return pl.pallas_call(
        qkv_grad_kernel,
        name="qkv_grad",
        out_shape=(shape((4, width // 8 + 8, width), BF16),) * 2,
        in_specs=[SM] + [VM] * 15,
        out_specs=(VM, VM),
        scratch_shapes=[
            scratch((RANKS, rows, width // RANKS), BF16),
            scratch((width, width), F32),
        ],
        compiler_params=params(14),
        cost_estimate=pl.CostEstimate(
            flops=8 * rows * width * width, bytes_accessed=4 * 10**6, transcendentals=0
        ),
    )(info, *blocks, *d_qkv, *joined, *d_proj)


def unpack(part, packed, wide, first):
    few = packed.shape[1] // RANKS
    for run in range(few // part):
        pieces = []
        for value in range(RANKS):
            at = value * few + run * part
            pieces.append(packed[:, at : at + part])
        at = first + run * RANKS * part
        wide[:, at : at + RANKS * part] = jnp.concatenate(pieces, axis=1).astype(F32)


def join_early_kernel(info, b0, b1, b2, b3, down, packed):
    rows, columns = b0.shape
    few = columns // 2
    for step, block in enumerate((b0, b1, b2, b3)):
        there = info[0] ^ step
        packed[:, pl.ds(pl.multiple_of(there * few, few), few)] = block[:, few:]
        down[pl.ds(pl.multiple_of(there * rows, rows), rows), :] = block[:, :few].astype(F32)


def join_wide_kernel(part, info, b0, b1, b2, b3, gates, wide, ups):
    few = b0.shape[1]
    for step, block in enumerate((b0, b1, b2, b3)):
        there = pl.multiple_of((info[0] ^ step) * few, few)
        ups[:, pl.ds(there, few)] = block[...]
    unpack(part, gates, wide, 0)
    unpack(part, ups, wide, RANKS * few)


def join_heads_kernel(info, b0, b1, b2, b3, out, rest):
    width = rest.shape[1]
    heads = width // RANKS
    for value in range(RANKS):

        @pl.when(info[0] == value)
        def _():
            for step, block in enumerate((b0, b1, b2, b3)):
                there = (value ^ step) * heads
                for third in range(3):
                    piece = block[:, third * heads : (third + 1) * heads].astype(F32)
                    out[:, third * width + there : third * width + there + heads] = piece
                rest[:, there : there + heads] = block[:, 3 * heads :].astype(F32)


def join_early(info, blocks):
    rows, columns = blocks[0].shape
    if rows % 8:
        stacked = jnp.stack(blocks)[info[0] ^ jnp.arange(RANKS)]
        few = columns // 2
        gates = jnp.concatenate(list(stacked[:, :, few:]), axis=1)
        return stacked[:, :, :few].reshape(-1, few).astype(F32), gates
    return pl.pallas_call(
        join_early_kernel,
        name="join_early",
        out_shape=(
            shape((rows * RANKS, columns // 2), F32),
            shape((rows, RANKS * columns // 2), BF16),
        ),
        in_specs=[SM] + [VM] * 4,
        out_specs=(VM, VM),
        compiler_params=params(8),
        cost_estimate=NO_COST,
    )(info, *blocks)


def join_wide(info, blocks, gates, part):
    rows, width = blocks[0].shape
    if RANKS * part % 128:
        stacked = jnp.stack(blocks)[info[0] ^ jnp.arange(RANKS)].astype(F32)
        both = [gates.astype(F32), jnp.concatenate(list(stacked), axis=1)]
        wide = [each.reshape(rows, RANKS, -1, part).transpose(0, 2, 1, 3) for each in both]
        return jnp.concatenate([each.reshape(rows, -1) for each in wide], axis=1)
    return pl.pallas_call(
        functools.partial(join_wide_kernel, part),
        name="join_wide",
        out_shape=shape((rows, 2 * RANKS * width), F32),
        in_specs=[SM] + [VM] * 5,
        out_specs=VM,
        scratch_shapes=[scratch((rows, RANKS * width), BF16)],
        compiler_params=params(14),
        cost_estimate=NO_COST,
    )(info, *blocks, gates)


def join_heads(info, blocks):
    rows, width = blocks[0].shape
    return pl.pallas_call(
        join_heads_kernel,
        name="join_heads",
        out_shape=(shape((rows, 3 * width), F32), shape((rows, width), F32)),
        in_specs=[SM] + [VM] * 4,
        out_specs=(VM, VM),
        compiler_params=params(8),
        cost_estimate=NO_COST,
    )(info, *blocks)


def token_grad_kernel(
    info, own, pair, far, cross, w, d_h1, masked, tokens, replacement, joined
):
    rows, width = d_h1.shape
    part = width // RANKS
    for step, block in enumerate((own, pair.at[0], far, cross)):
        for third in range(3):
            first = pl.multiple_of(third * width + (info[0] ^ step) * part, part)
            joined[pl.ds(first, part), :] = block[third * part : (third + 1) * part, :]
    grad = d_h1[...] + jnp.transpose(dot(w[...], joined[...]))
    count = masked.shape[0]
    places = lax.broadcasted_iota(jnp.int32, (rows, count), 0)
    select = (places == line(masked)).astype(F32)
    hit = jnp.max(select, axis=1, keepdims=True)
    tokens[...] = jnp.where(hit > 0.5, 0.0, grad)
    replacement[...] = lax.dot_general(
        select, grad, (((0,), (0,)), ((), ())),
        precision=lax.Precision.HIGHEST, preferred_element_type=F32,
    )


def token_grad(info, parts, w, d_h1, masked):
    rows, width = d_h1.shape
    return pl.pallas_call(
        token_grad_kernel,
        name="token_grad",
        out_shape=(shape((rows, width), F32), shape((masked.shape[0], width), F32)),
        in_specs=[SM] + [VM] * 7,
        out_specs=(VM, VM),
        scratch_shapes=[scratch((3 * width, rows), BF16)],
        compiler_params=params(16),
        cost_estimate=pl.CostEstimate(
            flops=6 * rows * width * width, bytes_accessed=8 * 10**6, transcendentals=0
        ),
    )(info, *parts, w, d_h1, masked)


def after(value, *others):
    return lax.optimization_barrier((value,) + others)[0]


def flip(value, axis, bits):
    count = lax.axis_size(axis)
    return lax.ppermute(value, axis, [(index, index ^ bits) for index in range(count)])


def gather_blocks(value):
    far = flip(value, "sp", 2)
    near = flip(value, "sp", 1)
    cross = flip(far, "sp", 1)
    return [value, near, far, cross]


def exchange_blocks(own, far, pair):
    pair = flip(pair, "sp", 1)
    far = flip(far, "sp", 2)
    cross = flip(pair[1], "sp", 2)
    return own, pair, far, cross


def small_mesh():
    return lax.axis_size("dp") == 8


NO_COST = pl.CostEstimate(flops=0, bytes_accessed=0, transcendentals=0)


def tidy_sums(value):
    first = value.shape[1] - 8
    sums = value[:, first : first + 4] + value[:, first + 4 :]
    high = sums.astype(BF16).astype(F32)
    return jnp.concatenate([value[:, :first], high, sums - high], axis=1)


def halve_kernel(with_sums, keep, came, kept, sent):
    half = keep.shape[0] // 2
    value = keep[...].astype(F32) + came[...].astype(F32)
    if with_sums:
        value = tidy_sums(value)
    kept[...] = value[:half]
    sent[...] = value[half:].astype(BF16)


def halve(keep, came, with_sums=False):
    dims = (keep.shape[0] // 2,) + keep.shape[1:]
    return pl.pallas_call(
        functools.partial(halve_kernel, with_sums),
        name="halve",
        out_shape=(shape(dims, F32), shape(dims, BF16)),
        in_specs=[VM] * 2,
        out_specs=(VM, VM),
        compiler_params=params(12),
        cost_estimate=NO_COST,
    )(keep, came)


def send_first(send, order):
    return flip(send, "dp", order[0]) if small_mesh() else send


def next_half(keep, came, with_sums=False):
    return halve(keep, came, with_sums) if small_mesh() else (keep, came)


def send_on(send, bits):
    return flip(send, "dp", bits) if small_mesh() else send


def send_second(keep, came, order, with_sums=False):
    keep, send = next_half(keep, came, with_sums)
    return keep, send_on(send, order[1])


def send_third(keep, came, order, with_sums=False):
    keep, send = next_half(keep, came, with_sums)
    return keep, send_on(send, order[2])


def natural_blocks(keep, send, order):
    both = jnp.concatenate([keep, send], axis=0).astype(F32)
    places = []
    for index in range(8):
        bits = [1 if index & mask else 0 for mask in order]
        places.append(both[bits[0] * 4 + bits[1] * 2 + bits[2]])
    return places


def scatter_sum(blocks):
    grad = jnp.concatenate(blocks, axis=0)
    return lax.psum_scatter(grad, "dp", scatter_dimension=0, tiled=True).astype(BF16)


def finish_pair_kernel(keep_a, came_a, keep_b, came_b, out):
    columns = keep_a.shape[2]
    out[:, :columns] = (keep_a[0] + came_a[0].astype(F32)).astype(BF16)
    out[:, columns:] = (keep_b[0] + came_b[0].astype(F32)).astype(BF16)


def finish_pair(keep_a, came_a, order_a, keep_b, came_b, order_b):
    if not small_mesh():
        first = scatter_sum(natural_blocks(keep_a, came_a, order_a))
        second = scatter_sum(natural_blocks(keep_b, came_b, order_b))
        return jnp.concatenate([first, second], axis=1)
    _, rows, columns = keep_a.shape
    return pl.pallas_call(
        finish_pair_kernel,
        name="finish_pair",
        out_shape=shape((rows, columns + keep_b.shape[2]), BF16),
        in_specs=[VM] * 4,
        out_specs=VM,
        compiler_params=params(8),
        cost_estimate=NO_COST,
    )(keep_a, came_a, keep_b, came_b)


def finish_kernel(keep, came, out):
    out[...] = (keep[0] + came[0].astype(F32)).astype(BF16)


def finish_sum(keep, came, order):
    if not small_mesh():
        return scatter_sum(natural_blocks(keep, came, order))
    return pl.pallas_call(
        finish_kernel,
        name="finish_sum",
        out_shape=shape(keep.shape[1:], BF16),
        in_specs=[VM] * 2,
        out_specs=VM,
        compiler_params=params(8),
        cost_estimate=NO_COST,
    )(keep, came)


def finish_heads_kernel(keep, came, out, *sums):
    rows = out.shape[0]
    total = keep[0] + came[0].astype(F32)
    out[...] = total[:rows].astype(BF16)
    for index, vector in enumerate(sums):
        value = total[rows + index : rows + index + 1] + total[rows + 4 + index : rows + 5 + index]
        vector[...] = value.reshape(-1)


def finish_heads(keep, came):
    _, rows, columns = keep.shape
    rows = rows - 8
    if not small_mesh():
        blocks = natural_blocks(keep, came, X_FIRST)
        sums = blocks[0][rows : rows + 4] + blocks[0][rows + 4 :]
        return scatter_sum([block[:rows] for block in blocks]), list(lax.psum(sums, "dp"))
    out, *sums = pl.pallas_call(
        finish_heads_kernel,
        name="finish_heads",
        out_shape=(shape((rows, columns), BF16),) + (shape((columns,), F32),) * 4,
        in_specs=[VM] * 2,
        out_specs=(VM,) * 5,
        compiler_params=params(8),
        cost_estimate=NO_COST,
    )(keep, came)
    return out, sums


def local(
    tokens,
    segment_ids,
    masked_rows,
    replacement,
    cotangent,
    w_qkv,
    w_out_attn,
    w_in_ff,
    w_out_ff,
    gain_one,
    shift_one,
    gain_two,
    shift_two,
):
    rows_dev, width = tokens.shape
    rank = lax.axis_index("sp")
    heads = HEADS // RANKS
    dim = width // HEADS
    part = heads * dim
    slopes = alibi_slopes(HEADS)

    select = jnp.arange(rows_dev, dtype=jnp.int32)[:, None] == masked_rows[None, :]
    hit = jnp.any(select, axis=1, keepdims=True)
    placed = dot(select.astype(BF16), replacement)
    start = jnp.where(hit, placed.astype(BF16), tokens)
    start_far = flip(start, "sp", 2)
    start_near = flip(start, "sp", 1)
    place = lax.axis_index("dp")
    place = place if small_mesh() else place * 0
    spot = jnp.stack([rank, place]).astype(jnp.int32)

    w_rank = jnp.concatenate(
        [
            lax.dynamic_slice_in_dim(w_qkv, third * width + rank * part, part, 1)
            for third in range(3)
        ],
        axis=1,
    )
    start_cross = flip(after(start_far, w_rank, spot), "sp", 1)
    start_blocks = [start, start_near, start_far, start_cross]
    qkv, attn, lse = attention_forward(
        spot, segment_ids, slopes, start_blocks, w_rank, heads, dim
    )
    attn_far = flip(attn, "sp", 2)
    attn_near = flip(attn, "sp", 1)
    part_units = w_out_ff.shape[0] // lax.axis_size("dp") // RANKS
    packed_in, packed_down = pack_weights(after(spot, lse), w_in_ff, w_out_ff, part_units)
    attn_cross = flip(after(attn_far, packed_in), "sp", 1)
    attn_parts = [attn, attn_near, attn_far, attn_cross]
    low, joined, unit, inverse = norm_one(
        spot, attn_parts, start, w_out_attn, gain_one, shift_one
    )
    layer_out, d_h2, d_ff, slope, act, sums2 = ffn_forward(
        low, unit, gain_one, shift_one, gain_two, shift_two,
        masked_rows, cotangent, w_in_ff, w_out_ff, 768,
    )
    d_ff_far = flip(d_ff, "sp", 2)
    d_ff_near = flip(d_ff, "sp", 1)
    d_h1, sent = ffn_backward(
        d_ff, d_h2, unit, inverse, gain_one, sums2, act, slope, w_in_ff, w_out_ff, 768
    )
    lows, others_joined = norm_others(
        after(spot, sent), attn_parts, start_blocks[1:], w_out_attn, gain_one, shift_one
    )
    d_ff_far = after(d_ff_far, lows[0])
    d_ff_cross = flip(d_ff_far, "sp", 1)
    d_ff_blocks = [d_ff, d_ff_near, d_ff_far, d_ff_cross]
    far = flip(sent, "sp", 2)
    near = flip(sent, "sp", 1)

    keep_g, send_g, keep_u, send_u, keep_d, send_d = ffn_grad(
        spot, [low, *lows], d_ff_blocks, packed_in, packed_down, 256
    )
    came_g = send_first(send_g, Z_FIRST)
    came_d = send_first(send_d, X_FIRST)
    cross = flip(after(far, keep_g), "sp", 1)
    d_proj_blocks = [sent, near, far, cross]

    d_qkv = attention_backward(
        spot, segment_ids, slopes, d_proj_blocks, w_out_attn, qkv, lse, heads, dim
    )
    parts = exchange_blocks(*d_qkv)
    came_u = send_first(after(send_u, d_qkv[0]), Z_FIRST)
    keep_g, came_g = send_second(keep_g, after(came_g, d_qkv[0]), Z_FIRST)
    keep_d, came_d = send_second(keep_d, after(came_d, keep_g), X_FIRST)
    keep_q, send_q = qkv_grad(
        after(spot, keep_d), start_blocks, d_qkv, [joined, *others_joined], d_proj_blocks
    )
    keep_g, came_g = send_third(keep_g, after(came_g, keep_q), Z_FIRST)
    came_q = send_first(after(send_q, keep_g), X_FIRST)
    keep_d, came_d = send_third(keep_d, after(came_d, keep_g), X_FIRST)
    keep_u, came_u = send_second(keep_u, after(came_u, keep_d), Z_FIRST)
    keep_q, send_q = next_half(keep_q, after(came_q, keep_u, parts), True)
    came_q = send_on(send_q, X_FIRST[1])
    keep_u, came_u = send_third(keep_u, after(came_u, keep_q), Z_FIRST)
    early = finish_pair(keep_d, after(came_d, keep_u), X_FIRST, keep_g, came_g, Z_FIRST)
    far = flip(early, "sp", 2)
    near = flip(early, "sp", 1)
    keep_q, came_q = send_third(keep_q, after(came_q, early), X_FIRST, True)
    early_blocks = [early, near, far, flip(after(far, keep_q), "sp", 1)]
    ups = finish_sum(keep_u, after(came_u, keep_q), Z_FIRST)
    far = flip(ups, "sp", 2)
    near = flip(ups, "sp", 1)
    grad_tokens, grad_replacement = token_grad(
        after(spot, ups), parts, w_qkv, d_h1, masked_rows
    )
    grad_down, gates = join_early(after(spot, grad_tokens), early_blocks)
    up_blocks = [ups, near, far, flip(after(far, gates), "sp", 1)]
    heads_share, norm_sums = finish_heads(keep_q, after(came_q, gates, up_blocks[2]))
    far = flip(heads_share, "sp", 2)
    near = flip(heads_share, "sp", 1)
    grad_in = join_wide(after(spot, heads_share), up_blocks, gates, part_units)
    head_blocks = [heads_share, near, far, flip(after(far, grad_in), "sp", 1)]
    grad_qkv, grad_out = join_heads(spot, head_blocks)

    return (
        layer_out,
        grad_tokens,
        grad_replacement,
        grad_qkv,
        grad_out,
        grad_in,
        grad_down,
        norm_sums[0],
        norm_sums[1],
        norm_sums[2],
        norm_sums[3],
    )


def solution(mesh):
    tokens = P(("dp", "sp"), None)
    rows = P("dp", None)
    return jax.shard_map(
        local,
        mesh=mesh,
        in_specs=(tokens, rows, P(("dp", "sp")), tokens, tokens) + (P(),) * 8,
        out_specs=(tokens,) * 3 + (rows,) * 4 + (P(),) * 4,
        check_vma=False,
    )
```

```python
import functools
import math

import jax
import jax.numpy as jnp
from jax import lax
from jax.experimental import pallas as pl
from jax.experimental.pallas import tpu as pltpu
from jax.sharding import PartitionSpec as P

HEADS = 12
RANKS = 4
EPSILON = 1e-05
FAR = 1e30
F32 = jnp.float32
BF16 = jnp.bfloat16
VM = pl.BlockSpec(memory_space=pltpu.VMEM)
SM = pl.BlockSpec(memory_space=pltpu.SMEM)


def shape(dims, kind):
    return jax.ShapeDtypeStruct(dims, kind)


def scratch(dims, kind):
    return pltpu.VMEM(dims, kind)


def params(mebibytes):
    return pltpu.CompilerParams(vmem_limit_bytes=mebibytes << 20)


def alibi_slopes(head_count):
    nearest = 2 ** int(math.floor(math.log2(head_count)))
    base_list = [2.0 ** (-8.0 * (index + 1) / nearest) for index in range(nearest)]
    extra_list = [
        2.0 ** (-8.0 * (2 * index + 1) / (2 * nearest)) for index in range(head_count - nearest)
    ]
    return jnp.array(base_list + extra_list, dtype=F32)


def dot(a, b):
    return jnp.dot(a, b, preferred_element_type=F32)


def dot_nt(a, b):
    return lax.dot_general(a, b, (((1,), (1,)), ((), ())), preferred_element_type=F32)


def dot_tn(a, b):
    return lax.dot_general(a, b, (((0,), (0,)), ((), ())), preferred_element_type=F32)


def exact_dot(a, b):
    return jnp.dot(a, b, precision=lax.Precision.HIGHEST, preferred_element_type=F32)


def standardize(value):
    center = value - jnp.mean(value, axis=-1, keepdims=True)
    spread = jnp.mean(center * center, axis=-1, keepdims=True)
    inverse = lax.rsqrt(spread + EPSILON)
    return center * inverse, inverse


def standardize_back(grad, unit, inverse):
    mean = jnp.mean(grad, axis=-1, keepdims=True)
    return inverse * (grad - mean - unit * jnp.mean(grad * unit, axis=-1, keepdims=True))


def gelu_pair(x):
    cdf = 0.5 * (1.0 + lax.erf(x * math.sqrt(0.5)))
    pdf = jnp.exp(-0.5 * x * x) * (1.0 / math.sqrt(2.0 * math.pi))
    return x * cdf, cdf + x * pdf


def pair_active(seg, rank, first, second, rows):
    one, two = rank ^ first, rank ^ second
    low, high = jnp.minimum(one, two), jnp.maximum(one, two)
    return jnp.logical_or(one == two, seg[0, low * rows + rows - 1] == seg[0, high * rows])


def key_sequences(seg_rows, seg_keys, rank, rows):
    for at in range(RANKS):
        first = pl.multiple_of((rank ^ at) * rows, rows)
        line = jnp.broadcast_to(seg_rows[:, pl.ds(first, rows)], (128, rows))
        seg_keys[at * rows : (at + 1) * rows, :] = jnp.transpose(line)


def pair_distance(seg_rows, seg_keys, rank, keys_at, query_at, rows):
    key_pos, query_pos = (rank ^ keys_at) * rows, (rank ^ query_at) * rows
    down = lax.broadcasted_iota(jnp.int32, (rows, rows), 0)
    across = lax.broadcasted_iota(jnp.int32, (rows, rows), 1)
    gap = jnp.abs(down - across + (key_pos - query_pos)).astype(F32)
    seg_q = seg_rows[:, pl.ds(pl.multiple_of(query_pos, rows), rows)]
    seg_k = seg_keys[pl.ds(pl.multiple_of(keys_at * rows, rows), rows), 0:1]
    return jnp.where(seg_k == seg_q, gap, FAR)


def attention_forward_kernel(
    rows, heads, dim, info, seg, slopes, x0, x1, x2, x3, w, seg_rows,
    qkv_out, out_t, lse, qs, ks, vt, dist, seg_keys, score, peak,
):
    rank = info[0]
    width = heads * dim
    key_sequences(seg_rows, seg_keys, rank, rows)
    for at, x in enumerate((x0, x1, x2, x3)):
        qkv = dot(x[...], w[...]).astype(BF16)
        here = pl.ds(at * rows, rows)
        qkv_out[here, :] = qkv
        for h in range(heads):
            qs[h, here, :] = (qkv[:, h * dim : (h + 1) * dim] * dim**-0.5).astype(BF16)
            ks[h, here, :] = qkv[:, width + h * dim : width + (h + 1) * dim]
        vt[:, here] = jnp.transpose(qkv[:, 2 * width :])

    for a in range(RANKS):
        mine = pl.ds(a * rows, rows)
        peak[...] = jnp.full_like(peak, -jnp.inf)

        def first_pass(b, carry):
            @pl.when(pair_active(seg, rank, a, b, rows))
            def _():
                theirs = pl.ds(pl.multiple_of(b * rows, rows), rows)
                gap = pair_distance(seg_rows, seg_keys, rank, b, a, rows)
                for h in range(heads):
                    slope = slopes[rank * heads + h]
                    s = dot_nt(ks[h, theirs, :], qs[h, mine, :]) - slope * gap
                    score[h, theirs, :] = s
                    peak[h : h + 1, :] = jnp.maximum(
                        peak[h : h + 1, :], jnp.max(s, axis=0, keepdims=True)
                    )

            return carry

        lax.fori_loop(0, RANKS, first_pass, 0)

        def second_pass(b, carry):
            def add(carry):
                theirs = pl.ds(pl.multiple_of(b * rows, rows), rows)
                result = []
                for h in range(heads):
                    acc, total = carry[h]
                    p = jnp.exp(score[h, theirs, :] - peak[h : h + 1, :])
                    total = total + jnp.sum(p, axis=0, keepdims=True)
                    span = slice(h * dim, (h + 1) * dim)
                    result.append((acc + dot(vt[span, theirs], p.astype(BF16)), total))
                return tuple(result)

            return lax.cond(pair_active(seg, rank, a, b, rows), add, lambda carry: carry, carry)

        empty = (jnp.zeros((dim, rows), F32), jnp.zeros((1, rows), F32))
        sums = lax.fori_loop(0, RANKS, second_pass, (empty,) * heads)
        for h in range(heads):
            acc, total = sums[h]
            span = slice(h * dim, (h + 1) * dim)
            out_t[span, mine] = (acc / total).astype(BF16)
            lse[h : h + 1, mine] = peak[h : h + 1, :] + jnp.log(total)


def attention_forward(info, seg, slopes, blocks, w, heads, dim):
    rows = blocks[0].shape[0]
    tok, lw = rows * RANKS, heads * dim
    return pl.pallas_call(
        functools.partial(attention_forward_kernel, rows, heads, dim),
        name="attention_forward",
        out_shape=(
            shape((tok, 3 * lw), BF16),
            shape((lw, tok), BF16),
            shape((heads, tok), F32),
        ),
        in_specs=[SM] * 3 + [VM] * 6,
        out_specs=(VM,) * 3,
        scratch_shapes=[
            scratch((heads, tok, dim), BF16),
            scratch((heads, tok, dim), BF16),
            scratch((lw, tok), BF16),
            scratch((rows, rows), F32),
            scratch((tok, 128), jnp.int32),
            scratch((heads, tok, rows), F32),
            scratch((heads, rows), F32),
        ],
        compiler_params=params(14),
        cost_estimate=pl.CostEstimate(
            flops=4 * 10**9, bytes_accessed=6 * 10**6, transcendentals=3 * 10**6
        ),
    )(info, seg, slopes, *blocks, w, seg)


def attention_backward_kernel(
    rows, heads, dim, info, seg, slopes, g0, g1, g2, g3, w, qkv, lse, seg_rows,
    d0, d2, pair, qs, ks, kt, vs, do, seg_keys, prob, dprob, dk, dv, dqt, delta,
):
    rank = info[0]
    width = heads * dim
    scale = dim**-0.5
    key_sequences(seg_rows, seg_keys, rank, rows)
    w_rank = w[pl.ds(pl.multiple_of(rank * width, width), width), :]
    for at, g in enumerate((g0, g1, g2, g3)):
        here = pl.ds(at * rows, rows)
        grad = dot_nt(g[0:rows, :], w_rank).astype(BF16)
        value = qkv[here, :]
        kt[:, here] = jnp.transpose(value[:, width : 2 * width])
        for h in range(heads):
            do[h, here, :] = grad[:, h * dim : (h + 1) * dim]
            qs[h, here, :] = (value[:, h * dim : (h + 1) * dim] * scale).astype(BF16)
            ks[h, here, :] = value[:, width + h * dim : width + (h + 1) * dim]
            vs[h, here, :] = value[:, 2 * width + h * dim : 2 * width + (h + 1) * dim]
    dk[...] = jnp.zeros_like(dk)
    dv[...] = jnp.zeros_like(dv)

    for a in range(RANKS):
        mine = pl.ds(a * rows, rows)
        delta[...] = jnp.zeros_like(delta)
        dqt[...] = jnp.zeros_like(dqt)

        def first_pass(b, carry):
            @pl.when(pair_active(seg, rank, a, b, rows))
            def _():
                theirs = pl.ds(pl.multiple_of(b * rows, rows), rows)
                gap = pair_distance(seg_rows, seg_keys, rank, b, a, rows)
                for h in range(heads):
                    slope = slopes[rank * heads + h]
                    s = dot_nt(ks[h, theirs, :], qs[h, mine, :]) - slope * gap
                    p = jnp.exp(s - lse[h : h + 1, mine])
                    dp = dot_nt(vs[h, theirs, :], do[h, mine, :])
                    delta[h : h + 1, :] += jnp.sum(p * dp, axis=0, keepdims=True)
                    prob[h, theirs, :] = p
                    dprob[h, theirs, :] = dp

            return carry

        lax.fori_loop(0, RANKS, first_pass, 0)

        def second_pass(b, carry):
            @pl.when(pair_active(seg, rank, a, b, rows))
            def _():
                theirs = pl.ds(pl.multiple_of(b * rows, rows), rows)
                for h in range(heads):
                    p = prob[h, theirs, :]
                    ds = (p * (dprob[h, theirs, :] - delta[h : h + 1, :])).astype(BF16)
                    dv[h, theirs, :] += dot(p.astype(BF16), do[h, mine, :])
                    dk[h, theirs, :] += dot(ds, qs[h, mine, :])
                    span = slice(h * dim, (h + 1) * dim)
                    dqt[span, :] += dot(kt[span, theirs], ds)

            return carry

        lax.fori_loop(0, RANKS, second_pass, 0)
        (d0, pair.at[0], d2, pair.at[1])[a][0:width, :] = (dqt[...] * scale).astype(BF16)

    for at, d_qkv in enumerate((d0, pair.at[0], d2, pair.at[1])):
        here = pl.ds(at * rows, rows)
        for h in range(heads):
            first = width + h * dim
            d_qkv[first : first + dim, :] = jnp.transpose(dk[h, here, :]).astype(BF16)
            first = 2 * width + h * dim
            d_qkv[first : first + dim, :] = jnp.transpose(dv[h, here, :]).astype(BF16)


def attention_backward(info, seg, slopes, blocks, w, qkv, lse, heads, dim):
    tok, lw = qkv.shape[0], heads * dim
    rows = tok // RANKS
    return pl.pallas_call(
        functools.partial(attention_backward_kernel, rows, heads, dim),
        name="attention_backward",
        out_shape=(shape((3 * lw, rows), BF16),) * 2 + (shape((2, 3 * lw, rows), BF16),),
        in_specs=[SM] * 3 + [VM] * 8,
        out_specs=(VM,) * 3,
        scratch_shapes=[
            scratch((heads, tok, dim), BF16),
            scratch((heads, tok, dim), BF16),
            scratch((lw, tok), BF16),
            scratch((heads, tok, dim), BF16),
            scratch((heads, tok, dim), BF16),
            scratch((tok, 128), jnp.int32),
            scratch((heads, tok, rows), F32),
            scratch((heads, tok, rows), F32),
            scratch((heads, tok, dim), F32),
            scratch((heads, tok, dim), F32),
            scratch((lw, rows), F32),
            scratch((heads, rows), F32),
        ],
        compiler_params=params(20),
        cost_estimate=pl.CostEstimate(
            flops=8 * 10**9, bytes_accessed=6 * 10**6, transcendentals=3 * 10**6
        ),
    )(info, seg, slopes, *blocks, w, qkv, lse, seg)


def line(vector):
    return vector[...].reshape(1, -1)


def join_tokens(rank, arrays, tokens_of, joined):
    part = arrays[0].shape[0]
    rows = arrays[0].shape[1] // RANKS
    for step, array in enumerate(arrays):
        first = pl.multiple_of((rank ^ step) * part, part)
        block = step ^ tokens_of
        joined[pl.ds(first, part), :] = array[:, block * rows : (block + 1) * rows]


def norm_one_kernel(
    info, own, near, far, cross, start, w, gain, shift, low, joined, unit, inverse
):
    join_tokens(info[0], (own, near, far, cross), 0, joined)
    x, inv = standardize(start[...].astype(F32) + dot_tn(joined[...], w[...]))
    unit[...] = x
    inverse[...] = inv
    low[...] = (x * line(gain) + line(shift)).astype(BF16)


def norm_one(info, parts, start, w, gain, shift):
    rows, width = start.shape
    return pl.pallas_call(
        norm_one_kernel,
        name="norm_one",
        out_shape=(
            shape((rows, width), BF16),
            shape((width, rows), BF16),
            shape((rows, width), F32),
            shape((rows, 1), F32),
        ),
        in_specs=[SM] + [VM] * 8,
        out_specs=(VM,) * 4,
        compiler_params=params(12),
        cost_estimate=pl.CostEstimate(
            flops=2 * rows * width * width, bytes_accessed=4 * 10**6, transcendentals=0
        ),
    )(info, *parts, start, w, gain, shift)


def norm_others_kernel(
    info, own, near, far, cross, s1, s2, s3, w, gain, shift, l1, l2, l3, j1, j2, j3
):
    for tokens_of, (start, low, joined) in enumerate(((s1, l1, j1), (s2, l2, j2), (s3, l3, j3))):
        join_tokens(info[0], (own, near, far, cross), tokens_of + 1, joined)
        x, _ = standardize(start[...].astype(F32) + dot_tn(joined[...], w[...]))
        low[...] = (x * line(gain) + line(shift)).astype(BF16)


def norm_others(info, parts, starts, w, gain, shift):
    rows, width = starts[0].shape
    results = pl.pallas_call(
        norm_others_kernel,
        name="norm_others",
        out_shape=(shape((rows, width), BF16),) * 3 + (shape((width, rows), BF16),) * 3,
        in_specs=[SM] + [VM] * 10,
        out_specs=(VM,) * 6,
        compiler_params=params(12),
        cost_estimate=pl.CostEstimate(
            flops=6 * rows * width * width, bytes_accessed=4 * 10**6, transcendentals=0
        ),
    )(info, *parts, *starts, w, gain, shift)
    return results[:3], results[3:]


def packing(rows, columns, part, rank):
    units = lax.broadcasted_iota(jnp.int32, (rows, columns), 0)
    packed = lax.broadcasted_iota(jnp.int32, (1, columns), 1)
    places = packed + rank * part
    for index in range(1, columns // part):
        places = places + jnp.where(packed >= index * part, (RANKS - 1) * part, 0)
    return (units == places).astype(BF16)


def pack_kernel(part, info, w_in, w_down, packed_in, packed_down):
    rank = info[0]
    width, hid = w_in.shape[0], w_down.shape[0]
    run = hid // 2
    select = packing(run, run // RANKS, part, rank)
    for index in range(4):
        piece = dot(w_in[:, index * run : (index + 1) * run], select)
        packed_in[:, index * run // RANKS : (index + 1) * run // RANKS] = piece.astype(BF16)
    if part % 16:
        for index in range(2):
            piece = dot_tn(select, w_down[index * run : (index + 1) * run, :])
            packed_down[index * run // RANKS : (index + 1) * run // RANKS, :] = piece.astype(BF16)
    else:
        for index in range(hid // RANKS // part):
            rows = pl.ds(pl.multiple_of((index * RANKS + rank) * part, part), part)
            packed_down[index * part : (index + 1) * part, :] = w_down[rows, :]


def pack_weights(info, w_in, w_out, part):
    width, hid = w_in.shape[0], w_out.shape[0]
    return pl.pallas_call(
        functools.partial(pack_kernel, part),
        name="pack_weights",
        out_shape=(shape((width, 2 * hid // RANKS), BF16), shape((hid // RANKS, width), BF16)),
        in_specs=[SM, VM, VM],
        out_specs=(VM, VM),
        compiler_params=params(14),
        cost_estimate=pl.CostEstimate(
            flops=4 * 10**9, bytes_accessed=17 * 10**6, transcendentals=0
        ),
    )(info, w_in, w_out)


def ffn_forward_kernel(
    low, unit, gain1, shift1, gain2, shift2, masked, cot, w_in, w_down,
    layer_out, d_h2, d_ff, slope, act, sums, acc, gates, ups,
):
    hid = w_down.shape[0]
    size = gates.shape[2]
    count = hid // size

    def project(block, slot):
        first = pl.multiple_of(block * size, size)
        gates[slot] = dot(low[...], w_in[:, pl.ds(first, size)])
        ups[slot] = dot(low[...], w_in[:, pl.ds(pl.multiple_of(hid + first, size), size)])

    def finish(block, slot):
        here = pl.ds(pl.multiple_of(block * size, size), size)
        up = ups[slot]
        value, grad = gelu_pair(gates[slot])
        act[:, here] = value.astype(BF16)
        slope[:, here] = (up * grad).astype(BF16)
        acc[...] += dot((value * up).astype(BF16), w_down[here, :])

    acc[...] = unit[...] * line(gain1) + line(shift1)
    project(0, 0)

    def pair(index, carry):
        block = index * 2
        project(block + 1, 1)
        finish(block, 0)
        project(block + 2, 0)
        finish(block + 1, 1)
        return carry

    lax.fori_loop(0, count // 2 - 1, pair, 0)
    project(count - 1, 1)
    finish(count - 2, 0)
    finish(count - 1, 1)
    x, inv = standardize(acc[...])
    layer_out[...] = (x * line(gain2) + line(shift2)).astype(BF16)
    places = lax.broadcasted_iota(jnp.int32, (low.shape[0], masked.shape[0]), 0)
    dy = exact_dot((places == line(masked)).astype(F32), cot[...])
    sums[0:1, :] = jnp.sum(dy * x, axis=0, keepdims=True)
    sums[1:2, :] = jnp.sum(dy, axis=0, keepdims=True)
    grad_in = standardize_back(dy * line(gain2), x, inv)
    d_h2[...] = grad_in
    d_ff[...] = grad_in.astype(BF16)


def ffn_forward(low, unit, gain1, shift1, gain2, shift2, masked, cot, w_in, w_out, size):
    rows, width = low.shape
    hid = w_out.shape[0]
    return pl.pallas_call(
        ffn_forward_kernel,
        name="ffn_forward",
        out_shape=(
            shape((rows, width), BF16),
            shape((rows, width), F32),
            shape((rows, width), BF16),
            shape((rows, hid), BF16),
            shape((rows, hid), BF16),
            shape((2, width), F32),
        ),
        in_specs=[VM] * 10,
        out_specs=(VM,) * 6,
        scratch_shapes=[
            scratch((rows, width), F32),
            scratch((2, rows, size), F32),
            scratch((2, rows, size), F32),
        ],
        compiler_params=params(14),
        cost_estimate=pl.CostEstimate(
            flops=6 * rows * width * hid, bytes_accessed=18 * 10**6, transcendentals=2 * rows * hid
        ),
    )(low, unit, gain1, shift1, gain2, shift2, masked, cot, w_in, w_out)


def ffn_backward_kernel(
    d_ff, d_h2, unit, inverse, gain1, sums2, act, slope, w_in, w_down, d_h1, sent, acc, hidden
):
    hid = w_down.shape[0]
    size = hidden.shape[2]
    count = hid // size

    def project(block, slot):
        here = pl.ds(pl.multiple_of(block * size, size), size)
        hidden[slot] = dot_nt(d_ff[...], w_down[here, :])

    def finish(block, slot):
        first = pl.multiple_of(block * size, size)
        here, there = pl.ds(first, size), pl.ds(pl.multiple_of(hid + first, size), size)
        d_hidden = hidden[slot]
        d_gate = (d_hidden * slope[:, here].astype(F32)).astype(BF16)
        d_up = (d_hidden * act[:, here].astype(F32)).astype(BF16)
        acc[...] += dot_nt(d_gate, w_in[:, here]) + dot_nt(d_up, w_in[:, there])

    acc[...] = d_h2[...]
    project(0, 0)

    def pair(index, carry):
        block = index * 2
        project(block + 1, 1)
        finish(block, 0)
        project(block + 2, 0)
        finish(block + 1, 1)
        return carry

    lax.fori_loop(0, count // 2 - 1, pair, 0)
    project(count - 1, 1)
    finish(count - 2, 0)
    finish(count - 1, 1)
    total = acc[...]
    rows = total.shape[0]
    x = unit[...]
    gain_sum = jnp.sum(total * x, axis=0, keepdims=True)
    shift_sum = jnp.sum(total, axis=0, keepdims=True)
    sums = jnp.concatenate([gain_sum, shift_sum, sums2[...]], axis=0)
    high = sums.astype(BF16).astype(F32)
    tail = jnp.concatenate([high, sums - high, jnp.zeros((8, sums.shape[1]), F32)], axis=0)
    grad = standardize_back(total * line(gain1), x, inverse[...])
    d_h1[...] = grad
    sent[0:rows, :] = grad.astype(BF16)
    sent[rows : rows + 16, :] = tail.astype(BF16)


def ffn_backward(d_ff, d_h2, unit, inverse, gain1, sums2, act, slope, w_in, w_out, size):
    rows, width = d_ff.shape
    hid = w_out.shape[0]
    return pl.pallas_call(
        ffn_backward_kernel,
        name="ffn_backward",
        out_shape=(shape((rows, width), F32), shape((rows + 16, width), BF16)),
        in_specs=[VM] * 10,
        out_specs=(VM,) * 2,
        scratch_shapes=[scratch((rows, width), F32), scratch((2, rows, size), F32)],
        compiler_params=params(14),
        cost_estimate=pl.CostEstimate(
            flops=6 * rows * width * hid, bytes_accessed=20 * 10**6, transcendentals=0
        ),
    )(d_ff, d_h2, unit, inverse, gain1, sums2, act, slope, w_in, w_out)


X_FIRST = (1, 2, 4)
Z_FIRST = (2, 1, 4)


def bit_of(value, mask):
    return (value // mask) % 2


def store_blocks(blocks, keep, send, place, order, columns):
    one, two, three = order
    odd = bit_of(place, one) == 1
    for index in range(8):
        if index & one:
            continue
        spot = bit_of(place ^ index, two) * 2 + bit_of(place ^ index, three)
        low, high = blocks(index), blocks(index | one)
        keep[spot, :, columns] = jnp.where(odd, high, low).astype(BF16)
        send[spot, :, columns] = jnp.where(odd, low, high).astype(BF16)


def row_blocks(grad):
    each = grad.shape[0] // 8
    return lambda index: grad[index * each : (index + 1) * each]


def ffn_grad_kernel(
    size, info, n0, n1, n2, n3, f0, f1, f2, f3, w_in, w_down,
    keep_gate, send_gate, keep_up, send_up, keep_down, send_down,
    tok_t, gates, ups, d_hiddens, hidden_t, d_gate, d_up, d_ff, down,
):
    toks, grads = (n0, n1, n2, n3), (f0, f1, f2, f3)
    rows = n0.shape[0]
    units = w_down.shape[0]
    for at in range(RANKS):
        here = slice(at * rows, (at + 1) * rows)
        d_ff[here, :] = grads[at][...]
        tok_t[:, here] = jnp.transpose(toks[at][...])

    def unit_block(step, carry):
        here = pl.ds(pl.multiple_of(step * size, size), size)
        there = pl.ds(pl.multiple_of(units + step * size, size), size)
        w_gate, w_up, w_rows = w_in[:, here], w_in[:, there], w_down[here, :]

        def project(at):
            slot = at % 2
            gates[slot] = dot(toks[at][...], w_gate)
            ups[slot] = dot(toks[at][...], w_up)
            d_hiddens[slot] = dot_nt(grads[at][...], w_rows)

        def finish(at):
            slot = at % 2
            here = slice(at * rows, (at + 1) * rows)
            value, grad = gelu_pair(gates[slot])
            up, d_hidden = ups[slot], d_hiddens[slot]
            hidden_t[:, here] = jnp.transpose((value * up).astype(BF16))
            d_gate[here, :] = (d_hidden * up * grad).astype(BF16)
            d_up[here, :] = (d_hidden * value).astype(BF16)

        project(0)
        for at in range(RANKS):
            if at + 1 < RANKS:
                project(at + 1)
            finish(at)
        total = dot(tok_t[...], d_gate[...])
        store_blocks(row_blocks(total), keep_gate, send_gate, info[1], Z_FIRST, here)
        total = dot(tok_t[...], d_up[...])
        store_blocks(row_blocks(total), keep_up, send_up, info[1], Z_FIRST, here)
        down[here, :] = dot(hidden_t[...], d_ff[...])
        return carry

    lax.fori_loop(0, units // size, unit_block, 0)
    store_blocks(row_blocks(down), keep_down, send_down, info[1], X_FIRST, slice(None))


def ffn_grad(info, toks, grads, w_in, w_down, size):
    rows, width = toks[0].shape
    units = w_down.shape[0]
    tok = rows * RANKS
    dims = [(4, width // 8, units)] * 4 + [(4, units // 8, width)] * 2
    return pl.pallas_call(
        functools.partial(ffn_grad_kernel, size),
        name="ffn_grad",
        out_shape=[shape(each, BF16) for each in dims],
        in_specs=[SM] + [VM] * 10,
        out_specs=[VM] * 6,
        scratch_shapes=[
            scratch((width, tok), BF16),
            scratch((2, rows, size), F32),
            scratch((2, rows, size), F32),
            scratch((2, rows, size), F32),
            scratch((size, tok), BF16),
            scratch((tok, size), BF16),
            scratch((tok, size), BF16),
            scratch((tok, width), BF16),
            scratch((units, width), F32),
        ],
        compiler_params=params(18),
        cost_estimate=pl.CostEstimate(
            flops=12 * tok * width * units,
            bytes_accessed=8 * 10**6,
            transcendentals=2 * tok * units,
        ),
    )(info, *toks, *grads, w_in, w_down)


def qkv_grad_kernel(
    info, x0, x1, x2, x3, d0, d2, pair, j0, j1, j2, j3, g0, g1, g2, g3, keep, send, columns, grad
):
    rows, width = x0.shape
    part = width // RANKS
    total = 0.0
    for x, d_qkv in zip((x0, x1, x2, x3), (d0, pair.at[0], d2, pair.at[1])):
        total = total + dot(d_qkv[...], x[...])
    grad[:, : 3 * part] = jnp.transpose(total)
    for value in range(RANKS):

        @pl.when(info[0] == value)
        def _():
            for at, g in enumerate((g0, g1, g2, g3)):
                columns[at] = g[0:rows, value * part : (value + 1) * part]

    total = 0.0
    sums = 0.0
    for at, (joined, g) in enumerate(zip((j0, j1, j2, j3), (g0, g1, g2, g3))):
        total = total + dot(joined[...], columns[at])
        pair = g[rows : rows + 16, :].astype(F32)
        sums = sums + pair[0:4] + pair[4:8]
    grad[:, 3 * part :] = total
    high = sums.astype(BF16).astype(F32)
    tail = jnp.concatenate([high, sums - high], axis=0)
    each = width // 8

    def blocks(index):
        return jnp.concatenate([grad[index * each : (index + 1) * each], tail], axis=0)

    store_blocks(blocks, keep, send, info[1], X_FIRST, slice(None))


def qkv_grad(info, blocks, d_qkv, joined, d_proj):
    rows, width = blocks[0].shape
    return pl.pallas_call(
        qkv_grad_kernel,
        name="qkv_grad",
        out_shape=(shape((4, width // 8 + 8, width), BF16),) * 2,
        in_specs=[SM] + [VM] * 15,
        out_specs=(VM, VM),
        scratch_shapes=[
            scratch((RANKS, rows, width // RANKS), BF16),
            scratch((width, width), F32),
        ],
        compiler_params=params(14),
        cost_estimate=pl.CostEstimate(
            flops=8 * rows * width * width, bytes_accessed=4 * 10**6, transcendentals=0
        ),
    )(info, *blocks, *d_qkv, *joined, *d_proj)


def unpack(part, packed, wide, first):
    few = packed.shape[1] // RANKS
    for run in range(few // part):
        pieces = []
        for value in range(RANKS):
            at = value * few + run * part
            pieces.append(packed[:, at : at + part])
        at = first + run * RANKS * part
        wide[:, at : at + RANKS * part] = jnp.concatenate(pieces, axis=1).astype(F32)


def join_early_kernel(info, b0, b1, b2, b3, down, packed):
    rows, columns = b0.shape
    few = columns // 2
    for step, block in enumerate((b0, b1, b2, b3)):
        there = info[0] ^ step
        packed[:, pl.ds(pl.multiple_of(there * few, few), few)] = block[:, few:]
        down[pl.ds(pl.multiple_of(there * rows, rows), rows), :] = block[:, :few].astype(F32)


def join_wide_kernel(part, info, b0, b1, b2, b3, gates, wide, ups):
    few = b0.shape[1]
    for step, block in enumerate((b0, b1, b2, b3)):
        there = pl.multiple_of((info[0] ^ step) * few, few)
        ups[:, pl.ds(there, few)] = block[...]
    unpack(part, gates, wide, 0)
    unpack(part, ups, wide, RANKS * few)


def join_heads_kernel(info, b0, b1, b2, b3, out, rest):
    width = rest.shape[1]
    heads = width // RANKS
    for value in range(RANKS):

        @pl.when(info[0] == value)
        def _():
            for step, block in enumerate((b0, b1, b2, b3)):
                there = (value ^ step) * heads
                for third in range(3):
                    piece = block[:, third * heads : (third + 1) * heads].astype(F32)
                    out[:, third * width + there : third * width + there + heads] = piece
                rest[:, there : there + heads] = block[:, 3 * heads :].astype(F32)


def join_early(info, blocks):
    rows, columns = blocks[0].shape
    if rows % 8:
        stacked = jnp.stack(blocks)[info[0] ^ jnp.arange(RANKS)]
        few = columns // 2
        gates = jnp.concatenate(list(stacked[:, :, few:]), axis=1)
        return stacked[:, :, :few].reshape(-1, few).astype(F32), gates
    return pl.pallas_call(
        join_early_kernel,
        name="join_early",
        out_shape=(
            shape((rows * RANKS, columns // 2), F32),
            shape((rows, RANKS * columns // 2), BF16),
        ),
        in_specs=[SM] + [VM] * 4,
        out_specs=(VM, VM),
        compiler_params=params(8),
        cost_estimate=NO_COST,
    )(info, *blocks)


def join_wide(info, blocks, gates, part):
    rows, width = blocks[0].shape
    if RANKS * part % 128:
        stacked = jnp.stack(blocks)[info[0] ^ jnp.arange(RANKS)].astype(F32)
        both = [gates.astype(F32), jnp.concatenate(list(stacked), axis=1)]
        wide = [each.reshape(rows, RANKS, -1, part).transpose(0, 2, 1, 3) for each in both]
        return jnp.concatenate([each.reshape(rows, -1) for each in wide], axis=1)
    return pl.pallas_call(
        functools.partial(join_wide_kernel, part),
        name="join_wide",
        out_shape=shape((rows, 2 * RANKS * width), F32),
        in_specs=[SM] + [VM] * 5,
        out_specs=VM,
        scratch_shapes=[scratch((rows, RANKS * width), BF16)],
        compiler_params=params(14),
        cost_estimate=NO_COST,
    )(info, *blocks, gates)


def join_heads(info, blocks):
    rows, width = blocks[0].shape
    return pl.pallas_call(
        join_heads_kernel,
        name="join_heads",
        out_shape=(shape((rows, 3 * width), F32), shape((rows, width), F32)),
        in_specs=[SM] + [VM] * 4,
        out_specs=(VM, VM),
        compiler_params=params(8),
        cost_estimate=NO_COST,
    )(info, *blocks)


def token_grad_kernel(
    info, own, pair, far, cross, w, d_h1, masked, tokens, replacement, joined
):
    rows, width = d_h1.shape
    part = width // RANKS
    for step, block in enumerate((own, pair.at[0], far, cross)):
        for third in range(3):
            first = pl.multiple_of(third * width + (info[0] ^ step) * part, part)
            joined[pl.ds(first, part), :] = block[third * part : (third + 1) * part, :]
    grad = d_h1[...] + jnp.transpose(dot(w[...], joined[...]))
    count = masked.shape[0]
    places = lax.broadcasted_iota(jnp.int32, (rows, count), 0)
    select = (places == line(masked)).astype(F32)
    hit = jnp.max(select, axis=1, keepdims=True)
    tokens[...] = jnp.where(hit > 0.5, 0.0, grad)
    replacement[...] = lax.dot_general(
        select, grad, (((0,), (0,)), ((), ())),
        precision=lax.Precision.HIGHEST, preferred_element_type=F32,
    )


def token_grad(info, parts, w, d_h1, masked):
    rows, width = d_h1.shape
    return pl.pallas_call(
        token_grad_kernel,
        name="token_grad",
        out_shape=(shape((rows, width), F32), shape((masked.shape[0], width), F32)),
        in_specs=[SM] + [VM] * 7,
        out_specs=(VM, VM),
        scratch_shapes=[scratch((3 * width, rows), BF16)],
        compiler_params=params(16),
        cost_estimate=pl.CostEstimate(
            flops=6 * rows * width * width, bytes_accessed=8 * 10**6, transcendentals=0
        ),
    )(info, *parts, w, d_h1, masked)


def after(value, *others):
    return lax.optimization_barrier((value,) + others)[0]


def flip(value, axis, bits):
    count = lax.axis_size(axis)
    return lax.ppermute(value, axis, [(index, index ^ bits) for index in range(count)])


def gather_blocks(value):
    far = flip(value, "sp", 2)
    near = flip(value, "sp", 1)
    cross = flip(far, "sp", 1)
    return [value, near, far, cross]


def exchange_blocks(own, far, pair):
    pair = flip(pair, "sp", 1)
    far = flip(far, "sp", 2)
    cross = flip(pair[1], "sp", 2)
    return own, pair, far, cross


def small_mesh():
    return lax.axis_size("dp") == 8


NO_COST = pl.CostEstimate(flops=0, bytes_accessed=0, transcendentals=0)


def tidy_sums(value):
    first = value.shape[1] - 8
    sums = value[:, first : first + 4] + value[:, first + 4 :]
    high = sums.astype(BF16).astype(F32)
    return jnp.concatenate([value[:, :first], high, sums - high], axis=1)


def halve_kernel(with_sums, keep, came, kept, sent):
    half = keep.shape[0] // 2
    value = keep[...].astype(F32) + came[...].astype(F32)
    if with_sums:
        value = tidy_sums(value)
    kept[...] = value[:half]
    sent[...] = value[half:].astype(BF16)


def halve(keep, came, with_sums=False):
    dims = (keep.shape[0] // 2,) + keep.shape[1:]
    return pl.pallas_call(
        functools.partial(halve_kernel, with_sums),
        name="halve",
        out_shape=(shape(dims, F32), shape(dims, BF16)),
        in_specs=[VM] * 2,
        out_specs=(VM, VM),
        compiler_params=params(12),
        cost_estimate=NO_COST,
    )(keep, came)


def send_first(send, order):
    return flip(send, "dp", order[0]) if small_mesh() else send


def step_kernel(info, out):
    out[...] = jnp.full(out.shape, info[0], jnp.int32)


def step(info):
    return pl.pallas_call(
        step_kernel,
        name="step",
        out_shape=shape((8, 128), jnp.int32),
        in_specs=[SM],
        out_specs=VM,
        compiler_params=params(1),
        cost_estimate=NO_COST,
    )(info)


def next_half(keep, came, with_sums=False):
    return halve(keep, came, with_sums) if small_mesh() else (keep, came)


def send_on(send, bits):
    return flip(send, "dp", bits) if small_mesh() else send


def send_second(keep, came, order, with_sums=False):
    keep, send = next_half(keep, came, with_sums)
    return keep, send_on(send, order[1])


def send_third(keep, came, order, with_sums=False):
    keep, send = next_half(keep, came, with_sums)
    return keep, send_on(send, order[2])


def natural_blocks(keep, send, order):
    both = jnp.concatenate([keep, send], axis=0).astype(F32)
    places = []
    for index in range(8):
        bits = [1 if index & mask else 0 for mask in order]
        places.append(both[bits[0] * 4 + bits[1] * 2 + bits[2]])
    return places


def scatter_sum(blocks):
    grad = jnp.concatenate(blocks, axis=0)
    return lax.psum_scatter(grad, "dp", scatter_dimension=0, tiled=True).astype(BF16)


def finish_pair_kernel(keep_a, came_a, keep_b, came_b, out):
    columns = keep_a.shape[2]
    out[:, :columns] = (keep_a[0] + came_a[0].astype(F32)).astype(BF16)
    out[:, columns:] = (keep_b[0] + came_b[0].astype(F32)).astype(BF16)


def finish_pair(keep_a, came_a, order_a, keep_b, came_b, order_b):
    if not small_mesh():
        first = scatter_sum(natural_blocks(keep_a, came_a, order_a))
        second = scatter_sum(natural_blocks(keep_b, came_b, order_b))
        return jnp.concatenate([first, second], axis=1)
    _, rows, columns = keep_a.shape
    return pl.pallas_call(
        finish_pair_kernel,
        name="finish_pair",
        out_shape=shape((rows, columns + keep_b.shape[2]), BF16),
        in_specs=[VM] * 4,
        out_specs=VM,
        compiler_params=params(8),
        cost_estimate=NO_COST,
    )(keep_a, came_a, keep_b, came_b)


def finish_kernel(keep, came, out):
    out[...] = (keep[0] + came[0].astype(F32)).astype(BF16)


def finish_sum(keep, came, order):
    if not small_mesh():
        return scatter_sum(natural_blocks(keep, came, order))
    return pl.pallas_call(
        finish_kernel,
        name="finish_sum",
        out_shape=shape(keep.shape[1:], BF16),
        in_specs=[VM] * 2,
        out_specs=VM,
        compiler_params=params(8),
        cost_estimate=NO_COST,
    )(keep, came)


def finish_heads_kernel(keep, came, out, *sums):
    rows = out.shape[0]
    total = keep[0] + came[0].astype(F32)
    out[...] = total[:rows].astype(BF16)
    for index, vector in enumerate(sums):
        value = total[rows + index : rows + index + 1] + total[rows + 4 + index : rows + 5 + index]
        vector[...] = value.reshape(-1)


def finish_heads(keep, came):
    _, rows, columns = keep.shape
    rows = rows - 8
    if not small_mesh():
        blocks = natural_blocks(keep, came, X_FIRST)
        sums = blocks[0][rows : rows + 4] + blocks[0][rows + 4 :]
        return scatter_sum([block[:rows] for block in blocks]), list(lax.psum(sums, "dp"))
    out, *sums = pl.pallas_call(
        finish_heads_kernel,
        name="finish_heads",
        out_shape=(shape((rows, columns), BF16),) + (shape((columns,), F32),) * 4,
        in_specs=[VM] * 2,
        out_specs=(VM,) * 5,
        compiler_params=params(8),
        cost_estimate=NO_COST,
    )(keep, came)
    return out, sums


def local(
    tokens,
    segment_ids,
    masked_rows,
    replacement,
    cotangent,
    w_qkv,
    w_out_attn,
    w_in_ff,
    w_out_ff,
    gain_one,
    shift_one,
    gain_two,
    shift_two,
):
    rows_dev, width = tokens.shape
    rank = lax.axis_index("sp")
    heads = HEADS // RANKS
    dim = width // HEADS
    part = heads * dim
    slopes = alibi_slopes(HEADS)

    select = jnp.arange(rows_dev, dtype=jnp.int32)[:, None] == masked_rows[None, :]
    hit = jnp.any(select, axis=1, keepdims=True)
    placed = dot(select.astype(BF16), replacement)
    start = jnp.where(hit, placed.astype(BF16), tokens)
    start_far = flip(start, "sp", 2)
    start_near = flip(start, "sp", 1)
    place = lax.axis_index("dp")
    place = place if small_mesh() else place * 0
    spot = jnp.stack([rank, place]).astype(jnp.int32)

    w_rank = jnp.concatenate(
        [
            lax.dynamic_slice_in_dim(w_qkv, third * width + rank * part, part, 1)
            for third in range(3)
        ],
        axis=1,
    )
    start_cross = flip(after(start_far, w_rank, spot), "sp", 1)
    start_blocks = [start, start_near, start_far, start_cross]
    qkv, attn, lse = attention_forward(
        spot, segment_ids, slopes, start_blocks, w_rank, heads, dim
    )
    attn_far = flip(attn, "sp", 2)
    attn_near = flip(attn, "sp", 1)
    part_units = w_out_ff.shape[0] // lax.axis_size("dp") // RANKS
    packed_in, packed_down = pack_weights(after(spot, lse), w_in_ff, w_out_ff, part_units)
    attn_cross = flip(after(attn_far, packed_in), "sp", 1)
    attn_parts = [attn, attn_near, attn_far, attn_cross]
    low, joined, unit, inverse = norm_one(
        spot, attn_parts, start, w_out_attn, gain_one, shift_one
    )
    layer_out, d_h2, d_ff, slope, act, sums2 = ffn_forward(
        low, unit, gain_one, shift_one, gain_two, shift_two,
        masked_rows, cotangent, w_in_ff, w_out_ff, 768,
    )
    d_ff_far = flip(d_ff, "sp", 2)
    d_ff_near = flip(d_ff, "sp", 1)
    d_h1, sent = ffn_backward(
        d_ff, d_h2, unit, inverse, gain_one, sums2, act, slope, w_in_ff, w_out_ff, 768
    )
    lows, others_joined = norm_others(
        after(spot, sent), attn_parts, start_blocks[1:], w_out_attn, gain_one, shift_one
    )
    d_ff_far = after(d_ff_far, lows[0])
    d_ff_cross = flip(d_ff_far, "sp", 1)
    d_ff_blocks = [d_ff, d_ff_near, d_ff_far, d_ff_cross]
    far = flip(sent, "sp", 2)
    near = flip(sent, "sp", 1)

    keep_g, send_g, keep_u, send_u, keep_d, send_d = ffn_grad(
        spot, [low, *lows], d_ff_blocks, packed_in, packed_down, 256
    )
    came_g = send_first(send_g, Z_FIRST)
    came_d = send_first(send_d, X_FIRST)
    cross = flip(after(far, keep_g), "sp", 1)
    d_proj_blocks = [sent, near, far, cross]

    d_qkv = attention_backward(
        spot, segment_ids, slopes, d_proj_blocks, w_out_attn, qkv, lse, heads, dim
    )
    parts = exchange_blocks(*d_qkv)
    came_u = send_first(after(send_u, d_qkv[0]), Z_FIRST)
    keep_g, came_g = send_second(keep_g, after(came_g, d_qkv[0]), Z_FIRST)
    keep_d, came_d = send_second(keep_d, after(came_d, keep_g), X_FIRST)
    keep_q, send_q = qkv_grad(
        after(spot, keep_d), start_blocks, d_qkv, [joined, *others_joined], d_proj_blocks
    )
    keep_g, came_g = send_third(keep_g, after(came_g, keep_q), Z_FIRST)
    came_q = send_first(after(send_q, keep_g), X_FIRST)
    passed = step(after(spot, keep_g))
    keep_u, came_u = send_second(keep_u, after(came_u, passed), Z_FIRST)
    keep_d, came_d = send_third(keep_d, after(came_d, keep_u, came_g), X_FIRST)
    keep_q, send_q = next_half(keep_q, after(came_q, keep_d, parts), True)
    came_q = send_on(send_q, X_FIRST[1])
    keep_u, came_u = send_third(keep_u, after(came_u, keep_q), Z_FIRST)
    early = finish_pair(keep_d, after(came_d, keep_u), X_FIRST, keep_g, came_g, Z_FIRST)
    far = flip(early, "sp", 2)
    near = flip(early, "sp", 1)
    keep_q, came_q = send_third(keep_q, after(came_q, early), X_FIRST, True)
    early_blocks = [early, near, far, flip(after(far, keep_q), "sp", 1)]
    ups = finish_sum(keep_u, after(came_u, keep_q), Z_FIRST)
    far = flip(ups, "sp", 2)
    near = flip(ups, "sp", 1)
    grad_tokens, grad_replacement = token_grad(
        after(spot, ups), parts, w_qkv, d_h1, masked_rows
    )
    grad_down, gates = join_early(after(spot, grad_tokens), early_blocks)
    up_blocks = [ups, near, far, flip(after(far, gates), "sp", 1)]
    heads_share, norm_sums = finish_heads(keep_q, after(came_q, gates, up_blocks[2]))
    far = flip(heads_share, "sp", 2)
    near = flip(heads_share, "sp", 1)
    grad_in = join_wide(after(spot, heads_share), up_blocks, gates, part_units)
    head_blocks = [heads_share, near, far, flip(after(far, grad_in), "sp", 1)]
    grad_qkv, grad_out = join_heads(spot, head_blocks)

    return (
        layer_out,
        grad_tokens,
        grad_replacement,
        grad_qkv,
        grad_out,
        grad_in,
        grad_down,
        norm_sums[0],
        norm_sums[1],
        norm_sums[2],
        norm_sums[3],
    )


def solution(mesh):
    tokens = P(("dp", "sp"), None)
    rows = P("dp", None)
    return jax.shard_map(
        local,
        mesh=mesh,
        in_specs=(tokens, rows, P(("dp", "sp")), tokens, tokens) + (P(),) * 8,
        out_specs=(tokens,) * 3 + (rows,) * 4 + (P(),) * 4,
        check_vma=False,
    )
```

```python
import functools
import math

import jax
import jax.numpy as jnp
from jax import lax
from jax.experimental import pallas as pl
from jax.experimental.pallas import tpu as pltpu
from jax.sharding import PartitionSpec as P

HEADS = 12
RANKS = 4
EPSILON = 1e-05
FAR = 1e30
F32 = jnp.float32
BF16 = jnp.bfloat16
VM = pl.BlockSpec(memory_space=pltpu.VMEM)
SM = pl.BlockSpec(memory_space=pltpu.SMEM)


def shape(dims, kind):
    return jax.ShapeDtypeStruct(dims, kind)


def scratch(dims, kind):
    return pltpu.VMEM(dims, kind)


def params(mebibytes):
    return pltpu.CompilerParams(vmem_limit_bytes=mebibytes << 20)


def alibi_slopes(head_count):
    nearest = 2 ** int(math.floor(math.log2(head_count)))
    base_list = [2.0 ** (-8.0 * (index + 1) / nearest) for index in range(nearest)]
    extra_list = [
        2.0 ** (-8.0 * (2 * index + 1) / (2 * nearest)) for index in range(head_count - nearest)
    ]
    return jnp.array(base_list + extra_list, dtype=F32)


def dot(a, b):
    return jnp.dot(a, b, preferred_element_type=F32)


def dot_nt(a, b):
    return lax.dot_general(a, b, (((1,), (1,)), ((), ())), preferred_element_type=F32)


def dot_tn(a, b):
    return lax.dot_general(a, b, (((0,), (0,)), ((), ())), preferred_element_type=F32)


def exact_dot(a, b):
    return jnp.dot(a, b, precision=lax.Precision.HIGHEST, preferred_element_type=F32)


def standardize(value):
    center = value - jnp.mean(value, axis=-1, keepdims=True)
    spread = jnp.mean(center * center, axis=-1, keepdims=True)
    inverse = lax.rsqrt(spread + EPSILON)
    return center * inverse, inverse


def standardize_back(grad, unit, inverse):
    mean = jnp.mean(grad, axis=-1, keepdims=True)
    return inverse * (grad - mean - unit * jnp.mean(grad * unit, axis=-1, keepdims=True))


def gelu_pair(x):
    cdf = 0.5 * (1.0 + lax.erf(x * math.sqrt(0.5)))
    pdf = jnp.exp(-0.5 * x * x) * (1.0 / math.sqrt(2.0 * math.pi))
    return x * cdf, cdf + x * pdf


def pair_active(seg, rank, first, second, rows):
    one, two = rank ^ first, rank ^ second
    low, high = jnp.minimum(one, two), jnp.maximum(one, two)
    return jnp.logical_or(one == two, seg[0, low * rows + rows - 1] == seg[0, high * rows])


def key_sequences(seg_rows, seg_keys, rank, rows):
    for at in range(RANKS):
        first = pl.multiple_of((rank ^ at) * rows, rows)
        line = jnp.broadcast_to(seg_rows[:, pl.ds(first, rows)], (128, rows))
        seg_keys[at * rows : (at + 1) * rows, :] = jnp.transpose(line)


def pair_distance(seg_rows, seg_keys, rank, keys_at, query_at, rows):
    key_pos, query_pos = (rank ^ keys_at) * rows, (rank ^ query_at) * rows
    down = lax.broadcasted_iota(jnp.int32, (rows, rows), 0)
    across = lax.broadcasted_iota(jnp.int32, (rows, rows), 1)
    gap = jnp.abs(down - across + (key_pos - query_pos)).astype(F32)
    seg_q = seg_rows[:, pl.ds(pl.multiple_of(query_pos, rows), rows)]
    seg_k = seg_keys[pl.ds(pl.multiple_of(keys_at * rows, rows), rows), 0:1]
    return jnp.where(seg_k == seg_q, gap, FAR)


def attention_forward_kernel(
    rows, heads, dim, info, seg, slopes, x0, x1, x2, x3, w, seg_rows,
    qs, ks, vs, kt, out_t, lse, vt, seg_keys, score, peak,
):
    rank = info[0]
    width = heads * dim
    key_sequences(seg_rows, seg_keys, rank, rows)
    for at, x in enumerate((x0, x1, x2, x3)):
        qkv = dot(x[...], w[...]).astype(BF16)
        here = pl.ds(at * rows, rows)
        kt[:, here] = jnp.transpose(qkv[:, width : 2 * width])
        for h in range(heads):
            qs[h, here, :] = (qkv[:, h * dim : (h + 1) * dim] * dim**-0.5).astype(BF16)
            ks[h, here, :] = qkv[:, width + h * dim : width + (h + 1) * dim]
            vs[h, here, :] = qkv[:, 2 * width + h * dim : 2 * width + (h + 1) * dim]
        vt[:, here] = jnp.transpose(qkv[:, 2 * width :])

    for a in range(RANKS):
        mine = pl.ds(a * rows, rows)
        peak[...] = jnp.full_like(peak, -jnp.inf)

        def first_pass(b, carry):
            @pl.when(pair_active(seg, rank, a, b, rows))
            def _():
                theirs = pl.ds(pl.multiple_of(b * rows, rows), rows)
                gap = pair_distance(seg_rows, seg_keys, rank, b, a, rows)
                for h in range(heads):
                    slope = slopes[rank * heads + h]
                    s = dot_nt(ks[h, theirs, :], qs[h, mine, :]) - slope * gap
                    score[h, theirs, :] = s
                    peak[h : h + 1, :] = jnp.maximum(
                        peak[h : h + 1, :], jnp.max(s, axis=0, keepdims=True)
                    )

            return carry

        lax.fori_loop(0, RANKS, first_pass, 0)

        def second_pass(b, carry):
            def add(carry):
                theirs = pl.ds(pl.multiple_of(b * rows, rows), rows)
                result = []
                for h in range(heads):
                    acc, total = carry[h]
                    p = jnp.exp(score[h, theirs, :] - peak[h : h + 1, :])
                    total = total + jnp.sum(p, axis=0, keepdims=True)
                    span = slice(h * dim, (h + 1) * dim)
                    result.append((acc + dot(vt[span, theirs], p.astype(BF16)), total))
                return tuple(result)

            return lax.cond(pair_active(seg, rank, a, b, rows), add, lambda carry: carry, carry)

        empty = (jnp.zeros((dim, rows), F32), jnp.zeros((1, rows), F32))
        sums = lax.fori_loop(0, RANKS, second_pass, (empty,) * heads)
        for h in range(heads):
            acc, total = sums[h]
            span = slice(h * dim, (h + 1) * dim)
            out_t[span, mine] = (acc / total).astype(BF16)
            lse[h : h + 1, mine] = peak[h : h + 1, :] + jnp.log(total)


def attention_forward(info, seg, slopes, blocks, w, heads, dim):
    rows = blocks[0].shape[0]
    tok, lw = rows * RANKS, heads * dim
    return pl.pallas_call(
        functools.partial(attention_forward_kernel, rows, heads, dim),
        name="attention_forward",
        out_shape=(shape((heads, tok, dim), BF16),) * 3
        + (shape((lw, tok), BF16),) * 2
        + (shape((heads, tok), F32),),
        in_specs=[SM] * 3 + [VM] * 6,
        out_specs=(VM,) * 6,
        scratch_shapes=[
            scratch((lw, tok), BF16),
            scratch((tok, 128), jnp.int32),
            scratch((heads, tok, rows), F32),
            scratch((heads, rows), F32),
        ],
        compiler_params=params(14),
        cost_estimate=pl.CostEstimate(
            flops=4 * 10**9, bytes_accessed=6 * 10**6, transcendentals=3 * 10**6
        ),
    )(info, seg, slopes, *blocks, w, seg)


def attention_backward_kernel(
    rows, heads, dim, info, seg, slopes, g0, g1, g2, g3, w, qs, ks, vs, kt, lse, seg_rows,
    d0, d2, pair, do, seg_keys, prob, dprob, dk, dv, dqt, delta,
):
    rank = info[0]
    width = heads * dim
    scale = dim**-0.5
    key_sequences(seg_rows, seg_keys, rank, rows)
    w_rank = w[pl.ds(pl.multiple_of(rank * width, width), width), :]
    for at, g in enumerate((g0, g1, g2, g3)):
        here = pl.ds(at * rows, rows)
        grad = dot_nt(g[0:rows, :], w_rank).astype(BF16)
        for h in range(heads):
            do[h, here, :] = grad[:, h * dim : (h + 1) * dim]
    dk[...] = jnp.zeros_like(dk)
    dv[...] = jnp.zeros_like(dv)

    for a in range(RANKS):
        mine = pl.ds(a * rows, rows)
        delta[...] = jnp.zeros_like(delta)
        dqt[...] = jnp.zeros_like(dqt)

        def first_pass(b, carry):
            @pl.when(pair_active(seg, rank, a, b, rows))
            def _():
                theirs = pl.ds(pl.multiple_of(b * rows, rows), rows)
                gap = pair_distance(seg_rows, seg_keys, rank, b, a, rows)
                for h in range(heads):
                    slope = slopes[rank * heads + h]
                    s = dot_nt(ks[h, theirs, :], qs[h, mine, :]) - slope * gap
                    p = jnp.exp(s - lse[h : h + 1, mine])
                    dp = dot_nt(vs[h, theirs, :], do[h, mine, :])
                    delta[h : h + 1, :] += jnp.sum(p * dp, axis=0, keepdims=True)
                    prob[h, theirs, :] = p
                    dprob[h, theirs, :] = dp

            return carry

        lax.fori_loop(0, RANKS, first_pass, 0)

        def second_pass(b, carry):
            @pl.when(pair_active(seg, rank, a, b, rows))
            def _():
                theirs = pl.ds(pl.multiple_of(b * rows, rows), rows)
                for h in range(heads):
                    p = prob[h, theirs, :]
                    ds = (p * (dprob[h, theirs, :] - delta[h : h + 1, :])).astype(BF16)
                    dv[h, theirs, :] += dot(p.astype(BF16), do[h, mine, :])
                    dk[h, theirs, :] += dot(ds, qs[h, mine, :])
                    span = slice(h * dim, (h + 1) * dim)
                    dqt[span, :] += dot(kt[span, theirs], ds)

            return carry

        lax.fori_loop(0, RANKS, second_pass, 0)
        (d0, pair.at[0], d2, pair.at[1])[a][0:width, :] = (dqt[...] * scale).astype(BF16)

    for at, d_qkv in enumerate((d0, pair.at[0], d2, pair.at[1])):
        here = pl.ds(at * rows, rows)
        for h in range(heads):
            first = width + h * dim
            d_qkv[first : first + dim, :] = jnp.transpose(dk[h, here, :]).astype(BF16)
            first = 2 * width + h * dim
            d_qkv[first : first + dim, :] = jnp.transpose(dv[h, here, :]).astype(BF16)


def attention_backward(info, seg, slopes, blocks, w, saved, lse, heads, dim):
    tok, lw = lse.shape[1], heads * dim
    rows = tok // RANKS
    return pl.pallas_call(
        functools.partial(attention_backward_kernel, rows, heads, dim),
        name="attention_backward",
        out_shape=(shape((3 * lw, rows), BF16),) * 2 + (shape((2, 3 * lw, rows), BF16),),
        in_specs=[SM] * 3 + [VM] * 11,
        out_specs=(VM,) * 3,
        scratch_shapes=[
            scratch((heads, tok, dim), BF16),
            scratch((tok, 128), jnp.int32),
            scratch((heads, tok, rows), F32),
            scratch((heads, tok, rows), F32),
            scratch((heads, tok, dim), F32),
            scratch((heads, tok, dim), F32),
            scratch((lw, rows), F32),
            scratch((heads, rows), F32),
        ],
        compiler_params=params(20),
        cost_estimate=pl.CostEstimate(
            flops=8 * 10**9, bytes_accessed=6 * 10**6, transcendentals=3 * 10**6
        ),
    )(info, seg, slopes, *blocks, w, *saved, lse, seg)


def line(vector):
    return vector[...].reshape(1, -1)


def join_tokens(rank, arrays, tokens_of, joined):
    part = arrays[0].shape[0]
    rows = arrays[0].shape[1] // RANKS
    for step, array in enumerate(arrays):
        first = pl.multiple_of((rank ^ step) * part, part)
        block = step ^ tokens_of
        joined[pl.ds(first, part), :] = array[:, block * rows : (block + 1) * rows]


def norm_one_kernel(
    info, own, near, far, cross, start, w, gain, shift, low, joined, unit, inverse
):
    join_tokens(info[0], (own, near, far, cross), 0, joined)
    x, inv = standardize(start[...].astype(F32) + dot_tn(joined[...], w[...]))
    unit[...] = x
    inverse[...] = inv
    low[...] = (x * line(gain) + line(shift)).astype(BF16)


def norm_one(info, parts, start, w, gain, shift):
    rows, width = start.shape
    return pl.pallas_call(
        norm_one_kernel,
        name="norm_one",
        out_shape=(
            shape((rows, width), BF16),
            shape((width, rows), BF16),
            shape((rows, width), F32),
            shape((rows, 1), F32),
        ),
        in_specs=[SM] + [VM] * 8,
        out_specs=(VM,) * 4,
        compiler_params=params(12),
        cost_estimate=pl.CostEstimate(
            flops=2 * rows * width * width, bytes_accessed=4 * 10**6, transcendentals=0
        ),
    )(info, *parts, start, w, gain, shift)


def norm_others_kernel(
    info, own, near, far, cross, s1, s2, s3, w, gain, shift, l1, l2, l3, j1, j2, j3
):
    for tokens_of, (start, low, joined) in enumerate(((s1, l1, j1), (s2, l2, j2), (s3, l3, j3))):
        join_tokens(info[0], (own, near, far, cross), tokens_of + 1, joined)
        x, _ = standardize(start[...].astype(F32) + dot_tn(joined[...], w[...]))
        low[...] = (x * line(gain) + line(shift)).astype(BF16)


def norm_others(info, parts, starts, w, gain, shift):
    rows, width = starts[0].shape
    results = pl.pallas_call(
        norm_others_kernel,
        name="norm_others",
        out_shape=(shape((rows, width), BF16),) * 3 + (shape((width, rows), BF16),) * 3,
        in_specs=[SM] + [VM] * 10,
        out_specs=(VM,) * 6,
        compiler_params=params(12),
        cost_estimate=pl.CostEstimate(
            flops=6 * rows * width * width, bytes_accessed=4 * 10**6, transcendentals=0
        ),
    )(info, *parts, *starts, w, gain, shift)
    return results[:3], results[3:]


def packing(rows, columns, part, rank):
    units = lax.broadcasted_iota(jnp.int32, (rows, columns), 0)
    packed = lax.broadcasted_iota(jnp.int32, (1, columns), 1)
    places = packed + rank * part
    for index in range(1, columns // part):
        places = places + jnp.where(packed >= index * part, (RANKS - 1) * part, 0)
    return (units == places).astype(BF16)


def pack_kernel(part, info, w_in, w_down, packed_in, packed_down):
    rank = info[0]
    width, hid = w_in.shape[0], w_down.shape[0]
    run = hid // 2
    select = packing(run, run // RANKS, part, rank)
    for index in range(4):
        piece = dot(w_in[:, index * run : (index + 1) * run], select)
        packed_in[:, index * run // RANKS : (index + 1) * run // RANKS] = piece.astype(BF16)
    if part % 16:
        for index in range(2):
            piece = dot_tn(select, w_down[index * run : (index + 1) * run, :])
            packed_down[index * run // RANKS : (index + 1) * run // RANKS, :] = piece.astype(BF16)
    else:
        for index in range(hid // RANKS // part):
            rows = pl.ds(pl.multiple_of((index * RANKS + rank) * part, part), part)
            packed_down[index * part : (index + 1) * part, :] = w_down[rows, :]


def pack_weights(info, w_in, w_out, part):
    width, hid = w_in.shape[0], w_out.shape[0]
    return pl.pallas_call(
        functools.partial(pack_kernel, part),
        name="pack_weights",
        out_shape=(shape((width, 2 * hid // RANKS), BF16), shape((hid // RANKS, width), BF16)),
        in_specs=[SM, VM, VM],
        out_specs=(VM, VM),
        compiler_params=params(14),
        cost_estimate=pl.CostEstimate(
            flops=4 * 10**9, bytes_accessed=17 * 10**6, transcendentals=0
        ),
    )(info, w_in, w_out)


def ffn_forward_kernel(
    low, unit, gain1, shift1, gain2, shift2, masked, cot, w_in, w_down,
    layer_out, d_h2, d_ff, slope, act, sums, acc, gates, ups,
):
    hid = w_down.shape[0]
    size = gates.shape[2]
    count = hid // size

    def project(block, slot):
        first = pl.multiple_of(block * size, size)
        gates[slot] = dot(low[...], w_in[:, pl.ds(first, size)])
        ups[slot] = dot(low[...], w_in[:, pl.ds(pl.multiple_of(hid + first, size), size)])

    def finish(block, slot):
        here = pl.ds(pl.multiple_of(block * size, size), size)
        up = ups[slot]
        value, grad = gelu_pair(gates[slot])
        act[:, here] = value.astype(BF16)
        slope[:, here] = (up * grad).astype(BF16)
        acc[...] += dot((value * up).astype(BF16), w_down[here, :])

    acc[...] = unit[...] * line(gain1) + line(shift1)
    project(0, 0)

    def pair(index, carry):
        block = index * 2
        project(block + 1, 1)
        finish(block, 0)
        project(block + 2, 0)
        finish(block + 1, 1)
        return carry

    lax.fori_loop(0, count // 2 - 1, pair, 0)
    project(count - 1, 1)
    finish(count - 2, 0)
    finish(count - 1, 1)
    x, inv = standardize(acc[...])
    layer_out[...] = (x * line(gain2) + line(shift2)).astype(BF16)
    places = lax.broadcasted_iota(jnp.int32, (low.shape[0], masked.shape[0]), 0)
    dy = exact_dot((places == line(masked)).astype(F32), cot[...])
    sums[0:1, :] = jnp.sum(dy * x, axis=0, keepdims=True)
    sums[1:2, :] = jnp.sum(dy, axis=0, keepdims=True)
    grad_in = standardize_back(dy * line(gain2), x, inv)
    d_h2[...] = grad_in
    d_ff[...] = grad_in.astype(BF16)


def ffn_forward(low, unit, gain1, shift1, gain2, shift2, masked, cot, w_in, w_out, size):
    rows, width = low.shape
    hid = w_out.shape[0]
    return pl.pallas_call(
        ffn_forward_kernel,
        name="ffn_forward",
        out_shape=(
            shape((rows, width), BF16),
            shape((rows, width), F32),
            shape((rows, width), BF16),
            shape((rows, hid), BF16),
            shape((rows, hid), BF16),
            shape((2, width), F32),
        ),
        in_specs=[VM] * 10,
        out_specs=(VM,) * 6,
        scratch_shapes=[
            scratch((rows, width), F32),
            scratch((2, rows, size), F32),
            scratch((2, rows, size), F32),
        ],
        compiler_params=params(14),
        cost_estimate=pl.CostEstimate(
            flops=6 * rows * width * hid, bytes_accessed=18 * 10**6, transcendentals=2 * rows * hid
        ),
    )(low, unit, gain1, shift1, gain2, shift2, masked, cot, w_in, w_out)


def ffn_backward_kernel(
    d_ff, d_h2, unit, inverse, gain1, sums2, act, slope, w_in, w_down, d_h1, sent, acc, hidden
):
    hid = w_down.shape[0]
    size = hidden.shape[2]
    count = hid // size

    def project(block, slot):
        here = pl.ds(pl.multiple_of(block * size, size), size)
        hidden[slot] = dot_nt(d_ff[...], w_down[here, :])

    def finish(block, slot):
        first = pl.multiple_of(block * size, size)
        here, there = pl.ds(first, size), pl.ds(pl.multiple_of(hid + first, size), size)
        d_hidden = hidden[slot]
        d_gate = (d_hidden * slope[:, here].astype(F32)).astype(BF16)
        d_up = (d_hidden * act[:, here].astype(F32)).astype(BF16)
        acc[...] += dot_nt(d_gate, w_in[:, here]) + dot_nt(d_up, w_in[:, there])

    acc[...] = d_h2[...]
    project(0, 0)

    def pair(index, carry):
        block = index * 2
        project(block + 1, 1)
        finish(block, 0)
        project(block + 2, 0)
        finish(block + 1, 1)
        return carry

    lax.fori_loop(0, count // 2 - 1, pair, 0)
    project(count - 1, 1)
    finish(count - 2, 0)
    finish(count - 1, 1)
    total = acc[...]
    rows = total.shape[0]
    x = unit[...]
    gain_sum = jnp.sum(total * x, axis=0, keepdims=True)
    shift_sum = jnp.sum(total, axis=0, keepdims=True)
    sums = jnp.concatenate([gain_sum, shift_sum, sums2[...]], axis=0)
    high = sums.astype(BF16).astype(F32)
    tail = jnp.concatenate([high, sums - high, jnp.zeros((8, sums.shape[1]), F32)], axis=0)
    grad = standardize_back(total * line(gain1), x, inverse[...])
    d_h1[...] = grad
    sent[0:rows, :] = grad.astype(BF16)
    sent[rows : rows + 16, :] = tail.astype(BF16)


def ffn_backward(d_ff, d_h2, unit, inverse, gain1, sums2, act, slope, w_in, w_out, size):
    rows, width = d_ff.shape
    hid = w_out.shape[0]
    return pl.pallas_call(
        ffn_backward_kernel,
        name="ffn_backward",
        out_shape=(shape((rows, width), F32), shape((rows + 16, width), BF16)),
        in_specs=[VM] * 10,
        out_specs=(VM,) * 2,
        scratch_shapes=[scratch((rows, width), F32), scratch((2, rows, size), F32)],
        compiler_params=params(14),
        cost_estimate=pl.CostEstimate(
            flops=6 * rows * width * hid, bytes_accessed=20 * 10**6, transcendentals=0
        ),
    )(d_ff, d_h2, unit, inverse, gain1, sums2, act, slope, w_in, w_out)


X_FIRST = (1, 2, 4)
Z_FIRST = (2, 1, 4)


def bit_of(value, mask):
    return (value // mask) % 2


def store_blocks(blocks, keep, send, place, order, columns):
    one, two, three = order
    odd = bit_of(place, one) == 1
    for index in range(8):
        if index & one:
            continue
        spot = bit_of(place ^ index, two) * 2 + bit_of(place ^ index, three)
        low, high = blocks(index), blocks(index | one)
        keep[spot, :, columns] = jnp.where(odd, high, low).astype(BF16)
        send[spot, :, columns] = jnp.where(odd, low, high).astype(BF16)


def row_blocks(grad):
    each = grad.shape[0] // 8
    return lambda index: grad[index * each : (index + 1) * each]


def ffn_grad_kernel(
    size, info, n0, n1, n2, n3, f0, f1, f2, f3, w_in, w_down,
    keep_gate, send_gate, keep_up, send_up, keep_down, send_down,
    tok_t, gates, ups, d_hiddens, hidden_t, d_gate, d_up, d_ff, down,
):
    toks, grads = (n0, n1, n2, n3), (f0, f1, f2, f3)
    rows = n0.shape[0]
    units = w_down.shape[0]
    for at in range(RANKS):
        here = slice(at * rows, (at + 1) * rows)
        d_ff[here, :] = grads[at][...]
        tok_t[:, here] = jnp.transpose(toks[at][...])

    def unit_block(step, carry):
        here = pl.ds(pl.multiple_of(step * size, size), size)
        there = pl.ds(pl.multiple_of(units + step * size, size), size)
        w_gate, w_up, w_rows = w_in[:, here], w_in[:, there], w_down[here, :]

        def project(at):
            slot = at % 2
            gates[slot] = dot(toks[at][...], w_gate)
            ups[slot] = dot(toks[at][...], w_up)
            d_hiddens[slot] = dot_nt(grads[at][...], w_rows)

        def finish(at):
            slot = at % 2
            here = slice(at * rows, (at + 1) * rows)
            value, grad = gelu_pair(gates[slot])
            up, d_hidden = ups[slot], d_hiddens[slot]
            hidden_t[:, here] = jnp.transpose((value * up).astype(BF16))
            d_gate[here, :] = (d_hidden * up * grad).astype(BF16)
            d_up[here, :] = (d_hidden * value).astype(BF16)

        project(0)
        for at in range(RANKS):
            if at + 1 < RANKS:
                project(at + 1)
            finish(at)
        total = dot(tok_t[...], d_gate[...])
        store_blocks(row_blocks(total), keep_gate, send_gate, info[1], Z_FIRST, here)
        total = dot(tok_t[...], d_up[...])
        store_blocks(row_blocks(total), keep_up, send_up, info[1], Z_FIRST, here)
        down[here, :] = dot(hidden_t[...], d_ff[...])
        return carry

    lax.fori_loop(0, units // size, unit_block, 0)
    store_blocks(row_blocks(down), keep_down, send_down, info[1], X_FIRST, slice(None))


def ffn_grad(info, toks, grads, w_in, w_down, size):
    rows, width = toks[0].shape
    units = w_down.shape[0]
    tok = rows * RANKS
    dims = [(4, width // 8, units)] * 4 + [(4, units // 8, width)] * 2
    return pl.pallas_call(
        functools.partial(ffn_grad_kernel, size),
        name="ffn_grad",
        out_shape=[shape(each, BF16) for each in dims],
        in_specs=[SM] + [VM] * 10,
        out_specs=[VM] * 6,
        scratch_shapes=[
            scratch((width, tok), BF16),
            scratch((2, rows, size), F32),
            scratch((2, rows, size), F32),
            scratch((2, rows, size), F32),
            scratch((size, tok), BF16),
            scratch((tok, size), BF16),
            scratch((tok, size), BF16),
            scratch((tok, width), BF16),
            scratch((units, width), F32),
        ],
        compiler_params=params(18),
        cost_estimate=pl.CostEstimate(
            flops=12 * tok * width * units,
            bytes_accessed=8 * 10**6,
            transcendentals=2 * tok * units,
        ),
    )(info, *toks, *grads, w_in, w_down)


def qkv_grad_kernel(
    info, x0, x1, x2, x3, d0, d2, pair, j0, j1, j2, j3, g0, g1, g2, g3, keep, send, columns, grad
):
    rows, width = x0.shape
    part = width // RANKS
    total = 0.0
    for x, d_qkv in zip((x0, x1, x2, x3), (d0, pair.at[0], d2, pair.at[1])):
        total = total + dot(d_qkv[...], x[...])
    grad[:, : 3 * part] = jnp.transpose(total)
    for value in range(RANKS):

        @pl.when(info[0] == value)
        def _():
            for at, g in enumerate((g0, g1, g2, g3)):
                columns[at] = g[0:rows, value * part : (value + 1) * part]

    total = 0.0
    sums = 0.0
    for at, (joined, g) in enumerate(zip((j0, j1, j2, j3), (g0, g1, g2, g3))):
        total = total + dot(joined[...], columns[at])
        pair = g[rows : rows + 16, :].astype(F32)
        sums = sums + pair[0:4] + pair[4:8]
    grad[:, 3 * part :] = total
    high = sums.astype(BF16).astype(F32)
    tail = jnp.concatenate([high, sums - high], axis=0)
    each = width // 8

    def blocks(index):
        return jnp.concatenate([grad[index * each : (index + 1) * each], tail], axis=0)

    store_blocks(blocks, keep, send, info[1], X_FIRST, slice(None))


def qkv_grad(info, blocks, d_qkv, joined, d_proj):
    rows, width = blocks[0].shape
    return pl.pallas_call(
        qkv_grad_kernel,
        name="qkv_grad",
        out_shape=(shape((4, width // 8 + 8, width), BF16),) * 2,
        in_specs=[SM] + [VM] * 15,
        out_specs=(VM, VM),
        scratch_shapes=[
            scratch((RANKS, rows, width // RANKS), BF16),
            scratch((width, width), F32),
        ],
        compiler_params=params(14),
        cost_estimate=pl.CostEstimate(
            flops=8 * rows * width * width, bytes_accessed=4 * 10**6, transcendentals=0
        ),
    )(info, *blocks, *d_qkv, *joined, *d_proj)


def unpack(part, packed, wide, first):
    few = packed.shape[1] // RANKS
    for run in range(few // part):
        pieces = []
        for value in range(RANKS):
            at = value * few + run * part
            pieces.append(packed[:, at : at + part])
        at = first + run * RANKS * part
        wide[:, at : at + RANKS * part] = jnp.concatenate(pieces, axis=1).astype(F32)


def join_early_kernel(info, b0, b1, b2, b3, down, packed):
    rows, columns = b0.shape
    few = columns // 2
    for step, block in enumerate((b0, b1, b2, b3)):
        there = info[0] ^ step
        packed[:, pl.ds(pl.multiple_of(there * few, few), few)] = block[:, few:]
        down[pl.ds(pl.multiple_of(there * rows, rows), rows), :] = block[:, :few].astype(F32)


def join_wide_kernel(part, info, b0, b1, b2, b3, gates, wide, ups):
    few = b0.shape[1]
    for step, block in enumerate((b0, b1, b2, b3)):
        there = pl.multiple_of((info[0] ^ step) * few, few)
        ups[:, pl.ds(there, few)] = block[...]
    unpack(part, gates, wide, 0)
    unpack(part, ups, wide, RANKS * few)


def join_heads_kernel(info, b0, b1, b2, b3, out, rest):
    width = rest.shape[1]
    heads = width // RANKS
    for value in range(RANKS):

        @pl.when(info[0] == value)
        def _():
            for step, block in enumerate((b0, b1, b2, b3)):
                there = (value ^ step) * heads
                for third in range(3):
                    piece = block[:, third * heads : (third + 1) * heads].astype(F32)
                    out[:, third * width + there : third * width + there + heads] = piece
                rest[:, there : there + heads] = block[:, 3 * heads :].astype(F32)


def join_early(info, blocks):
    rows, columns = blocks[0].shape
    if rows % 8:
        stacked = jnp.stack(blocks)[info[0] ^ jnp.arange(RANKS)]
        few = columns // 2
        gates = jnp.concatenate(list(stacked[:, :, few:]), axis=1)
        return stacked[:, :, :few].reshape(-1, few).astype(F32), gates
    return pl.pallas_call(
        join_early_kernel,
        name="join_early",
        out_shape=(
            shape((rows * RANKS, columns // 2), F32),
            shape((rows, RANKS * columns // 2), BF16),
        ),
        in_specs=[SM] + [VM] * 4,
        out_specs=(VM, VM),
        compiler_params=params(8),
        cost_estimate=NO_COST,
    )(info, *blocks)


def join_wide(info, blocks, gates, part):
    rows, width = blocks[0].shape
    if RANKS * part % 128:
        stacked = jnp.stack(blocks)[info[0] ^ jnp.arange(RANKS)].astype(F32)
        both = [gates.astype(F32), jnp.concatenate(list(stacked), axis=1)]
        wide = [each.reshape(rows, RANKS, -1, part).transpose(0, 2, 1, 3) for each in both]
        return jnp.concatenate([each.reshape(rows, -1) for each in wide], axis=1)
    return pl.pallas_call(
        functools.partial(join_wide_kernel, part),
        name="join_wide",
        out_shape=shape((rows, 2 * RANKS * width), F32),
        in_specs=[SM] + [VM] * 5,
        out_specs=VM,
        scratch_shapes=[scratch((rows, RANKS * width), BF16)],
        compiler_params=params(14),
        cost_estimate=NO_COST,
    )(info, *blocks, gates)


def join_heads(info, blocks):
    rows, width = blocks[0].shape
    return pl.pallas_call(
        join_heads_kernel,
        name="join_heads",
        out_shape=(shape((rows, 3 * width), F32), shape((rows, width), F32)),
        in_specs=[SM] + [VM] * 4,
        out_specs=(VM, VM),
        compiler_params=params(8),
        cost_estimate=NO_COST,
    )(info, *blocks)


def token_grad_kernel(
    info, own, pair, far, cross, w, d_h1, masked, tokens, replacement, joined
):
    rows, width = d_h1.shape
    part = width // RANKS
    for step, block in enumerate((own, pair.at[0], far, cross)):
        for third in range(3):
            first = pl.multiple_of(third * width + (info[0] ^ step) * part, part)
            joined[pl.ds(first, part), :] = block[third * part : (third + 1) * part, :]
    grad = d_h1[...] + jnp.transpose(dot(w[...], joined[...]))
    count = masked.shape[0]
    places = lax.broadcasted_iota(jnp.int32, (rows, count), 0)
    select = (places == line(masked)).astype(F32)
    hit = jnp.max(select, axis=1, keepdims=True)
    tokens[...] = jnp.where(hit > 0.5, 0.0, grad)
    replacement[...] = lax.dot_general(
        select, grad, (((0,), (0,)), ((), ())),
        precision=lax.Precision.HIGHEST, preferred_element_type=F32,
    )


def token_grad(info, parts, w, d_h1, masked):
    rows, width = d_h1.shape
    return pl.pallas_call(
        token_grad_kernel,
        name="token_grad",
        out_shape=(shape((rows, width), F32), shape((masked.shape[0], width), F32)),
        in_specs=[SM] + [VM] * 7,
        out_specs=(VM, VM),
        scratch_shapes=[scratch((3 * width, rows), BF16)],
        compiler_params=params(16),
        cost_estimate=pl.CostEstimate(
            flops=6 * rows * width * width, bytes_accessed=8 * 10**6, transcendentals=0
        ),
    )(info, *parts, w, d_h1, masked)


def after(value, *others):
    return lax.optimization_barrier((value,) + others)[0]


def flip(value, axis, bits):
    count = lax.axis_size(axis)
    return lax.ppermute(value, axis, [(index, index ^ bits) for index in range(count)])


def gather_blocks(value):
    far = flip(value, "sp", 2)
    near = flip(value, "sp", 1)
    cross = flip(far, "sp", 1)
    return [value, near, far, cross]


def exchange_blocks(own, far, pair):
    pair = flip(pair, "sp", 1)
    far = flip(far, "sp", 2)
    cross = flip(pair[1], "sp", 2)
    return own, pair, far, cross


def small_mesh():
    return lax.axis_size("dp") == 8


NO_COST = pl.CostEstimate(flops=0, bytes_accessed=0, transcendentals=0)


def tidy_sums(value):
    first = value.shape[1] - 8
    sums = value[:, first : first + 4] + value[:, first + 4 :]
    high = sums.astype(BF16).astype(F32)
    return jnp.concatenate([value[:, :first], high, sums - high], axis=1)


def halve_kernel(with_sums, keep, came, kept, sent):
    half = keep.shape[0] // 2
    value = keep[...].astype(F32) + came[...].astype(F32)
    if with_sums:
        value = tidy_sums(value)
    kept[...] = value[:half]
    sent[...] = value[half:].astype(BF16)


def halve(keep, came, with_sums=False):
    dims = (keep.shape[0] // 2,) + keep.shape[1:]
    return pl.pallas_call(
        functools.partial(halve_kernel, with_sums),
        name="halve",
        out_shape=(shape(dims, F32), shape(dims, BF16)),
        in_specs=[VM] * 2,
        out_specs=(VM, VM),
        compiler_params=params(12),
        cost_estimate=NO_COST,
    )(keep, came)


def send_first(send, order):
    return flip(send, "dp", order[0]) if small_mesh() else send


def next_half(keep, came, with_sums=False):
    return halve(keep, came, with_sums) if small_mesh() else (keep, came)


def send_on(send, bits):
    return flip(send, "dp", bits) if small_mesh() else send


def send_second(keep, came, order, with_sums=False):
    keep, send = next_half(keep, came, with_sums)
    return keep, send_on(send, order[1])


def send_third(keep, came, order, with_sums=False):
    keep, send = next_half(keep, came, with_sums)
    return keep, send_on(send, order[2])


def natural_blocks(keep, send, order):
    both = jnp.concatenate([keep, send], axis=0).astype(F32)
    places = []
    for index in range(8):
        bits = [1 if index & mask else 0 for mask in order]
        places.append(both[bits[0] * 4 + bits[1] * 2 + bits[2]])
    return places


def scatter_sum(blocks):
    grad = jnp.concatenate(blocks, axis=0)
    return lax.psum_scatter(grad, "dp", scatter_dimension=0, tiled=True).astype(BF16)


def finish_pair_kernel(keep_a, came_a, keep_b, came_b, out):
    columns = keep_a.shape[2]
    out[:, :columns] = (keep_a[0] + came_a[0].astype(F32)).astype(BF16)
    out[:, columns:] = (keep_b[0] + came_b[0].astype(F32)).astype(BF16)


def finish_pair(keep_a, came_a, order_a, keep_b, came_b, order_b):
    if not small_mesh():
        first = scatter_sum(natural_blocks(keep_a, came_a, order_a))
        second = scatter_sum(natural_blocks(keep_b, came_b, order_b))
        return jnp.concatenate([first, second], axis=1)
    _, rows, columns = keep_a.shape
    return pl.pallas_call(
        finish_pair_kernel,
        name="finish_pair",
        out_shape=shape((rows, columns + keep_b.shape[2]), BF16),
        in_specs=[VM] * 4,
        out_specs=VM,
        compiler_params=params(8),
        cost_estimate=NO_COST,
    )(keep_a, came_a, keep_b, came_b)


def finish_kernel(keep, came, out):
    out[...] = (keep[0] + came[0].astype(F32)).astype(BF16)


def finish_sum(keep, came, order):
    if not small_mesh():
        return scatter_sum(natural_blocks(keep, came, order))
    return pl.pallas_call(
        finish_kernel,
        name="finish_sum",
        out_shape=shape(keep.shape[1:], BF16),
        in_specs=[VM] * 2,
        out_specs=VM,
        compiler_params=params(8),
        cost_estimate=NO_COST,
    )(keep, came)


def finish_heads_kernel(keep, came, out, *sums):
    rows = out.shape[0]
    total = keep[0] + came[0].astype(F32)
    out[...] = total[:rows].astype(BF16)
    for index, vector in enumerate(sums):
        value = total[rows + index : rows + index + 1] + total[rows + 4 + index : rows + 5 + index]
        vector[...] = value.reshape(-1)


def finish_heads(keep, came):
    _, rows, columns = keep.shape
    rows = rows - 8
    if not small_mesh():
        blocks = natural_blocks(keep, came, X_FIRST)
        sums = blocks[0][rows : rows + 4] + blocks[0][rows + 4 :]
        return scatter_sum([block[:rows] for block in blocks]), list(lax.psum(sums, "dp"))
    out, *sums = pl.pallas_call(
        finish_heads_kernel,
        name="finish_heads",
        out_shape=(shape((rows, columns), BF16),) + (shape((columns,), F32),) * 4,
        in_specs=[VM] * 2,
        out_specs=(VM,) * 5,
        compiler_params=params(8),
        cost_estimate=NO_COST,
    )(keep, came)
    return out, sums


def local(
    tokens,
    segment_ids,
    masked_rows,
    replacement,
    cotangent,
    w_qkv,
    w_out_attn,
    w_in_ff,
    w_out_ff,
    gain_one,
    shift_one,
    gain_two,
    shift_two,
):
    rows_dev, width = tokens.shape
    rank = lax.axis_index("sp")
    heads = HEADS // RANKS
    dim = width // HEADS
    part = heads * dim
    slopes = alibi_slopes(HEADS)

    select = jnp.arange(rows_dev, dtype=jnp.int32)[:, None] == masked_rows[None, :]
    hit = jnp.any(select, axis=1, keepdims=True)
    placed = dot(select.astype(BF16), replacement)
    start = jnp.where(hit, placed.astype(BF16), tokens)
    start_far = flip(start, "sp", 2)
    start_near = flip(start, "sp", 1)
    place = lax.axis_index("dp")
    place = place if small_mesh() else place * 0
    spot = jnp.stack([rank, place]).astype(jnp.int32)

    w_rank = jnp.concatenate(
        [
            lax.dynamic_slice_in_dim(w_qkv, third * width + rank * part, part, 1)
            for third in range(3)
        ],
        axis=1,
    )
    start_cross = flip(after(start_far, w_rank, spot), "sp", 1)
    start_blocks = [start, start_near, start_far, start_cross]
    *saved, attn, lse = attention_forward(
        spot, segment_ids, slopes, start_blocks, w_rank, heads, dim
    )
    attn_far = flip(attn, "sp", 2)
    attn_near = flip(attn, "sp", 1)
    part_units = w_out_ff.shape[0] // lax.axis_size("dp") // RANKS
    packed_in, packed_down = pack_weights(after(spot, lse), w_in_ff, w_out_ff, part_units)
    attn_cross = flip(after(attn_far, packed_in), "sp", 1)
    attn_parts = [attn, attn_near, attn_far, attn_cross]
    low, joined, unit, inverse = norm_one(
        spot, attn_parts, start, w_out_attn, gain_one, shift_one
    )
    layer_out, d_h2, d_ff, slope, act, sums2 = ffn_forward(
        low, unit, gain_one, shift_one, gain_two, shift_two,
        masked_rows, cotangent, w_in_ff, w_out_ff, 768,
    )
    d_ff_far = flip(d_ff, "sp", 2)
    d_ff_near = flip(d_ff, "sp", 1)
    d_h1, sent = ffn_backward(
        d_ff, d_h2, unit, inverse, gain_one, sums2, act, slope, w_in_ff, w_out_ff, 768
    )
    lows, others_joined = norm_others(
        after(spot, sent), attn_parts, start_blocks[1:], w_out_attn, gain_one, shift_one
    )
    d_ff_far = after(d_ff_far, lows[0])
    d_ff_cross = flip(d_ff_far, "sp", 1)
    d_ff_blocks = [d_ff, d_ff_near, d_ff_far, d_ff_cross]
    far = flip(sent, "sp", 2)
    near = flip(sent, "sp", 1)

    keep_g, send_g, keep_u, send_u, keep_d, send_d = ffn_grad(
        spot, [low, *lows], d_ff_blocks, packed_in, packed_down, 256
    )
    came_g = send_first(send_g, Z_FIRST)
    came_d = send_first(send_d, X_FIRST)
    cross = flip(after(far, keep_g), "sp", 1)
    d_proj_blocks = [sent, near, far, cross]

    d_qkv = attention_backward(
        spot, segment_ids, slopes, d_proj_blocks, w_out_attn, saved, lse, heads, dim
    )
    parts = exchange_blocks(*d_qkv)
    came_u = send_first(after(send_u, d_qkv[0]), Z_FIRST)
    keep_g, came_g = send_second(keep_g, after(came_g, d_qkv[0]), Z_FIRST)
    keep_d, came_d = send_second(keep_d, after(came_d, keep_g), X_FIRST)
    keep_q, send_q = qkv_grad(
        after(spot, keep_d), start_blocks, d_qkv, [joined, *others_joined], d_proj_blocks
    )
    keep_g, came_g = send_third(keep_g, after(came_g, keep_q), Z_FIRST)
    came_q = send_first(after(send_q, keep_g), X_FIRST)
    keep_u, came_u = send_second(keep_u, after(came_u, keep_g), Z_FIRST)
    keep_d, came_d = send_third(keep_d, after(came_d, keep_u, came_g), X_FIRST)
    keep_q, send_q = next_half(keep_q, after(came_q, keep_d, parts), True)
    came_q = send_on(send_q, X_FIRST[1])
    keep_u, came_u = send_third(keep_u, after(came_u, keep_q), Z_FIRST)
    early = finish_pair(keep_d, after(came_d, keep_u), X_FIRST, keep_g, came_g, Z_FIRST)
    far = flip(early, "sp", 2)
    near = flip(early, "sp", 1)
    keep_q, came_q = send_third(keep_q, after(came_q, early), X_FIRST, True)
    early_blocks = [early, near, far, flip(after(far, keep_q), "sp", 1)]
    ups = finish_sum(keep_u, after(came_u, keep_q), Z_FIRST)
    far = flip(ups, "sp", 2)
    near = flip(ups, "sp", 1)
    grad_tokens, grad_replacement = token_grad(
        after(spot, ups), parts, w_qkv, d_h1, masked_rows
    )
    grad_down, gates = join_early(after(spot, grad_tokens), early_blocks)
    up_blocks = [ups, near, far, flip(after(far, gates), "sp", 1)]
    heads_share, norm_sums = finish_heads(keep_q, after(came_q, gates, up_blocks[2]))
    far = flip(heads_share, "sp", 2)
    near = flip(heads_share, "sp", 1)
    grad_in = join_wide(after(spot, heads_share), up_blocks, gates, part_units)
    head_blocks = [heads_share, near, far, flip(after(far, grad_in), "sp", 1)]
    grad_qkv, grad_out = join_heads(spot, head_blocks)

    return (
        layer_out,
        grad_tokens,
        grad_replacement,
        grad_qkv,
        grad_out,
        grad_in,
        grad_down,
        norm_sums[0],
        norm_sums[1],
        norm_sums[2],
        norm_sums[3],
    )


def solution(mesh):
    tokens = P(("dp", "sp"), None)
    rows = P("dp", None)
    return jax.shard_map(
        local,
        mesh=mesh,
        in_specs=(tokens, rows, P(("dp", "sp")), tokens, tokens) + (P(),) * 8,
        out_specs=(tokens,) * 3 + (rows,) * 4 + (P(),) * 4,
        check_vma=False,
    )
```

```python
import functools
import math

import jax
import jax.numpy as jnp
from jax import lax
from jax.experimental import pallas as pl
from jax.experimental.pallas import tpu as pltpu
from jax.sharding import PartitionSpec as P

HEADS = 12
RANKS = 4
EPSILON = 1e-05
FAR = 1e30
F32 = jnp.float32
BF16 = jnp.bfloat16
VM = pl.BlockSpec(memory_space=pltpu.VMEM)
SM = pl.BlockSpec(memory_space=pltpu.SMEM)


def shape(dims, kind):
    return jax.ShapeDtypeStruct(dims, kind)


def scratch(dims, kind):
    return pltpu.VMEM(dims, kind)


def params(mebibytes):
    return pltpu.CompilerParams(vmem_limit_bytes=mebibytes << 20)


def alibi_slopes(head_count):
    nearest = 2 ** int(math.floor(math.log2(head_count)))
    base_list = [2.0 ** (-8.0 * (index + 1) / nearest) for index in range(nearest)]
    extra_list = [
        2.0 ** (-8.0 * (2 * index + 1) / (2 * nearest)) for index in range(head_count - nearest)
    ]
    return jnp.array(base_list + extra_list, dtype=F32)


def dot(a, b):
    return jnp.dot(a, b, preferred_element_type=F32)


def dot_nt(a, b):
    return lax.dot_general(a, b, (((1,), (1,)), ((), ())), preferred_element_type=F32)


def dot_tn(a, b):
    return lax.dot_general(a, b, (((0,), (0,)), ((), ())), preferred_element_type=F32)


def exact_dot(a, b):
    return jnp.dot(a, b, precision=lax.Precision.HIGHEST, preferred_element_type=F32)


def standardize(value):
    center = value - jnp.mean(value, axis=-1, keepdims=True)
    spread = jnp.mean(center * center, axis=-1, keepdims=True)
    inverse = lax.rsqrt(spread + EPSILON)
    return center * inverse, inverse


def standardize_back(grad, unit, inverse):
    mean = jnp.mean(grad, axis=-1, keepdims=True)
    return inverse * (grad - mean - unit * jnp.mean(grad * unit, axis=-1, keepdims=True))


def gelu_pair(x):
    cdf = 0.5 * (1.0 + lax.erf(x * math.sqrt(0.5)))
    pdf = jnp.exp(-0.5 * x * x) * (1.0 / math.sqrt(2.0 * math.pi))
    return x * cdf, cdf + x * pdf


def pair_active(seg, rank, first, second, rows):
    one, two = rank ^ first, rank ^ second
    low, high = jnp.minimum(one, two), jnp.maximum(one, two)
    return jnp.logical_or(one == two, seg[0, low * rows + rows - 1] == seg[0, high * rows])


def key_sequences(seg_rows, seg_keys, rank, rows):
    for at in range(RANKS):
        first = pl.multiple_of((rank ^ at) * rows, rows)
        line = jnp.broadcast_to(seg_rows[:, pl.ds(first, rows)], (128, rows))
        seg_keys[at * rows : (at + 1) * rows, :] = jnp.transpose(line)


def pair_distance(seg_rows, seg_keys, rank, keys_at, query_at, rows):
    key_pos, query_pos = (rank ^ keys_at) * rows, (rank ^ query_at) * rows
    down = lax.broadcasted_iota(jnp.int32, (rows, rows), 0)
    across = lax.broadcasted_iota(jnp.int32, (rows, rows), 1)
    gap = jnp.abs(down - across + (key_pos - query_pos)).astype(F32)
    seg_q = seg_rows[:, pl.ds(pl.multiple_of(query_pos, rows), rows)]
    seg_k = seg_keys[pl.ds(pl.multiple_of(keys_at * rows, rows), rows), 0:1]
    return jnp.where(seg_k == seg_q, gap, FAR)


def attention_forward_kernel(
    rows, heads, dim, info, seg, slopes, x0, x1, x2, x3, w, seg_rows,
    qs, ks, vs, kt, out_t, lse, vt, seg_keys, score, peak,
):
    rank = info[0]
    width = heads * dim
    key_sequences(seg_rows, seg_keys, rank, rows)
    for at, x in enumerate((x0, x1, x2, x3)):
        qkv = dot(x[...], w[...]).astype(BF16)
        here = pl.ds(at * rows, rows)
        kt[:, here] = jnp.transpose(qkv[:, width : 2 * width])
        for h in range(heads):
            qs[h, here, :] = (qkv[:, h * dim : (h + 1) * dim] * dim**-0.5).astype(BF16)
            ks[h, here, :] = qkv[:, width + h * dim : width + (h + 1) * dim]
            vs[h, here, :] = qkv[:, 2 * width + h * dim : 2 * width + (h + 1) * dim]
        vt[:, here] = jnp.transpose(qkv[:, 2 * width :])

    for a in range(RANKS):
        mine = pl.ds(a * rows, rows)
        peak[...] = jnp.full_like(peak, -jnp.inf)

        def first_pass(b, carry):
            @pl.when(pair_active(seg, rank, a, b, rows))
            def _():
                theirs = pl.ds(pl.multiple_of(b * rows, rows), rows)
                gap = pair_distance(seg_rows, seg_keys, rank, b, a, rows)
                for h in range(heads):
                    slope = slopes[rank * heads + h]
                    s = dot_nt(ks[h, theirs, :], qs[h, mine, :]) - slope * gap
                    score[h, theirs, :] = s
                    peak[h : h + 1, :] = jnp.maximum(
                        peak[h : h + 1, :], jnp.max(s, axis=0, keepdims=True)
                    )

            return carry

        lax.fori_loop(0, RANKS, first_pass, 0)

        def second_pass(b, carry):
            def add(carry):
                theirs = pl.ds(pl.multiple_of(b * rows, rows), rows)
                result = []
                for h in range(heads):
                    acc, total = carry[h]
                    p = jnp.exp(score[h, theirs, :] - peak[h : h + 1, :])
                    total = total + jnp.sum(p, axis=0, keepdims=True)
                    span = slice(h * dim, (h + 1) * dim)
                    result.append((acc + dot(vt[span, theirs], p.astype(BF16)), total))
                return tuple(result)

            return lax.cond(pair_active(seg, rank, a, b, rows), add, lambda carry: carry, carry)

        empty = (jnp.zeros((dim, rows), F32), jnp.zeros((1, rows), F32))
        sums = lax.fori_loop(0, RANKS, second_pass, (empty,) * heads)
        for h in range(heads):
            acc, total = sums[h]
            span = slice(h * dim, (h + 1) * dim)
            out_t[span, mine] = (acc / total).astype(BF16)
            lse[h : h + 1, mine] = peak[h : h + 1, :] + jnp.log(total)


def attention_forward(info, seg, slopes, blocks, w, heads, dim):
    rows = blocks[0].shape[0]
    tok, lw = rows * RANKS, heads * dim
    return pl.pallas_call(
        functools.partial(attention_forward_kernel, rows, heads, dim),
        name="attention_forward",
        out_shape=(shape((heads, tok, dim), BF16),) * 3
        + (shape((lw, tok), BF16),) * 2
        + (shape((heads, tok), F32),),
        in_specs=[SM] * 3 + [VM] * 6,
        out_specs=(VM,) * 6,
        scratch_shapes=[
            scratch((lw, tok), BF16),
            scratch((tok, 128), jnp.int32),
            scratch((heads, tok, rows), F32),
            scratch((heads, rows), F32),
        ],
        compiler_params=params(14),
        cost_estimate=pl.CostEstimate(
            flops=4 * 10**9, bytes_accessed=6 * 10**6, transcendentals=3 * 10**6
        ),
    )(info, seg, slopes, *blocks, w, seg)


def attention_backward_kernel(
    rows, heads, dim, info, seg, slopes, g0, g1, g2, g3, w, qs, ks, vs, kt, lse, seg_rows,
    d0, d2, pair, do, seg_keys, prob, dprob, dk, dv, dqt, delta,
):
    rank = info[0]
    width = heads * dim
    scale = dim**-0.5
    key_sequences(seg_rows, seg_keys, rank, rows)
    w_rank = w[pl.ds(pl.multiple_of(rank * width, width), width), :]
    for at, g in enumerate((g0, g1, g2, g3)):
        here = pl.ds(at * rows, rows)
        grad = dot_nt(g[0:rows, :], w_rank).astype(BF16)
        for h in range(heads):
            do[h, here, :] = grad[:, h * dim : (h + 1) * dim]
    dk[...] = jnp.zeros_like(dk)
    dv[...] = jnp.zeros_like(dv)

    for a in range(RANKS):
        mine = pl.ds(a * rows, rows)
        delta[...] = jnp.zeros_like(delta)
        dqt[...] = jnp.zeros_like(dqt)

        def first_pass(b, carry):
            @pl.when(pair_active(seg, rank, a, b, rows))
            def _():
                theirs = pl.ds(pl.multiple_of(b * rows, rows), rows)
                gap = pair_distance(seg_rows, seg_keys, rank, b, a, rows)
                for h in range(heads):
                    slope = slopes[rank * heads + h]
                    s = dot_nt(ks[h, theirs, :], qs[h, mine, :]) - slope * gap
                    p = jnp.exp(s - lse[h : h + 1, mine])
                    dp = dot_nt(vs[h, theirs, :], do[h, mine, :])
                    delta[h : h + 1, :] += jnp.sum(p * dp, axis=0, keepdims=True)
                    prob[h, theirs, :] = p
                    dprob[h, theirs, :] = dp

            return carry

        lax.fori_loop(0, RANKS, first_pass, 0)

        def second_pass(b, carry):
            @pl.when(pair_active(seg, rank, a, b, rows))
            def _():
                theirs = pl.ds(pl.multiple_of(b * rows, rows), rows)
                for h in range(heads):
                    p = prob[h, theirs, :]
                    ds = (p * (dprob[h, theirs, :] - delta[h : h + 1, :])).astype(BF16)
                    dv[h, theirs, :] += dot(p.astype(BF16), do[h, mine, :])
                    dk[h, theirs, :] += dot(ds, qs[h, mine, :])
                    span = slice(h * dim, (h + 1) * dim)
                    dqt[span, :] += dot(kt[span, theirs], ds)

            return carry

        lax.fori_loop(0, RANKS, second_pass, 0)
        (d0, pair.at[0], d2, pair.at[1])[a][0:width, :] = (dqt[...] * scale).astype(BF16)

    for at, d_qkv in enumerate((d0, pair.at[0], d2, pair.at[1])):
        here = pl.ds(at * rows, rows)
        for h in range(heads):
            first = width + h * dim
            d_qkv[first : first + dim, :] = jnp.transpose(dk[h, here, :].astype(BF16))
            first = 2 * width + h * dim
            d_qkv[first : first + dim, :] = jnp.transpose(dv[h, here, :].astype(BF16))


def attention_backward(info, seg, slopes, blocks, w, saved, lse, heads, dim):
    tok, lw = lse.shape[1], heads * dim
    rows = tok // RANKS
    return pl.pallas_call(
        functools.partial(attention_backward_kernel, rows, heads, dim),
        name="attention_backward",
        out_shape=(shape((3 * lw, rows), BF16),) * 2 + (shape((2, 3 * lw, rows), BF16),),
        in_specs=[SM] * 3 + [VM] * 11,
        out_specs=(VM,) * 3,
        scratch_shapes=[
            scratch((heads, tok, dim), BF16),
            scratch((tok, 128), jnp.int32),
            scratch((heads, tok, rows), F32),
            scratch((heads, tok, rows), F32),
            scratch((heads, tok, dim), F32),
            scratch((heads, tok, dim), F32),
            scratch((lw, rows), F32),
            scratch((heads, rows), F32),
        ],
        compiler_params=params(20),
        cost_estimate=pl.CostEstimate(
            flops=8 * 10**9, bytes_accessed=6 * 10**6, transcendentals=3 * 10**6
        ),
    )(info, seg, slopes, *blocks, w, *saved, lse, seg)


def line(vector):
    return vector[...].reshape(1, -1)


def join_tokens(rank, arrays, tokens_of, joined):
    part = arrays[0].shape[0]
    rows = arrays[0].shape[1] // RANKS
    for step, array in enumerate(arrays):
        first = pl.multiple_of((rank ^ step) * part, part)
        block = step ^ tokens_of
        joined[pl.ds(first, part), :] = array[:, block * rows : (block + 1) * rows]


def norm_one_kernel(
    info, own, near, far, cross, start, w, gain, shift, low, joined, unit, inverse
):
    join_tokens(info[0], (own, near, far, cross), 0, joined)
    x, inv = standardize(start[...].astype(F32) + dot_tn(joined[...], w[...]))
    unit[...] = x
    inverse[...] = inv
    low[...] = (x * line(gain) + line(shift)).astype(BF16)


def norm_one(info, parts, start, w, gain, shift):
    rows, width = start.shape
    return pl.pallas_call(
        norm_one_kernel,
        name="norm_one",
        out_shape=(
            shape((rows, width), BF16),
            shape((width, rows), BF16),
            shape((rows, width), F32),
            shape((rows, 1), F32),
        ),
        in_specs=[SM] + [VM] * 8,
        out_specs=(VM,) * 4,
        compiler_params=params(12),
        cost_estimate=pl.CostEstimate(
            flops=2 * rows * width * width, bytes_accessed=4 * 10**6, transcendentals=0
        ),
    )(info, *parts, start, w, gain, shift)


def norm_others_kernel(
    info, own, near, far, cross, s1, s2, s3, w, gain, shift, l1, l2, l3, j1, j2, j3
):
    for tokens_of, (start, low, joined) in enumerate(((s1, l1, j1), (s2, l2, j2), (s3, l3, j3))):
        join_tokens(info[0], (own, near, far, cross), tokens_of + 1, joined)
        x, _ = standardize(start[...].astype(F32) + dot_tn(joined[...], w[...]))
        low[...] = (x * line(gain) + line(shift)).astype(BF16)


def norm_others(info, parts, starts, w, gain, shift):
    rows, width = starts[0].shape
    results = pl.pallas_call(
        norm_others_kernel,
        name="norm_others",
        out_shape=(shape((rows, width), BF16),) * 3 + (shape((width, rows), BF16),) * 3,
        in_specs=[SM] + [VM] * 10,
        out_specs=(VM,) * 6,
        compiler_params=params(12),
        cost_estimate=pl.CostEstimate(
            flops=6 * rows * width * width, bytes_accessed=4 * 10**6, transcendentals=0
        ),
    )(info, *parts, *starts, w, gain, shift)
    return results[:3], results[3:]


def packing(rows, columns, part, rank):
    units = lax.broadcasted_iota(jnp.int32, (rows, columns), 0)
    packed = lax.broadcasted_iota(jnp.int32, (1, columns), 1)
    places = packed + rank * part
    for index in range(1, columns // part):
        places = places + jnp.where(packed >= index * part, (RANKS - 1) * part, 0)
    return (units == places).astype(BF16)


def pack_kernel(part, info, w_in, w_down, packed_in, packed_down):
    rank = info[0]
    width, hid = w_in.shape[0], w_down.shape[0]
    run = hid // 2
    select = packing(run, run // RANKS, part, rank)
    for index in range(4):
        piece = dot(w_in[:, index * run : (index + 1) * run], select)
        packed_in[:, index * run // RANKS : (index + 1) * run // RANKS] = piece.astype(BF16)
    if part % 16:
        for index in range(2):
            piece = dot_tn(select, w_down[index * run : (index + 1) * run, :])
            packed_down[index * run // RANKS : (index + 1) * run // RANKS, :] = piece.astype(BF16)
    else:
        for index in range(hid // RANKS // part):
            rows = pl.ds(pl.multiple_of((index * RANKS + rank) * part, part), part)
            packed_down[index * part : (index + 1) * part, :] = w_down[rows, :]


def pack_weights(info, w_in, w_out, part):
    width, hid = w_in.shape[0], w_out.shape[0]
    return pl.pallas_call(
        functools.partial(pack_kernel, part),
        name="pack_weights",
        out_shape=(shape((width, 2 * hid // RANKS), BF16), shape((hid // RANKS, width), BF16)),
        in_specs=[SM, VM, VM],
        out_specs=(VM, VM),
        compiler_params=params(14),
        cost_estimate=pl.CostEstimate(
            flops=4 * 10**9, bytes_accessed=17 * 10**6, transcendentals=0
        ),
    )(info, w_in, w_out)


def ffn_forward_kernel(
    low, unit, gain1, shift1, gain2, shift2, masked, cot, w_in, w_down,
    layer_out, d_h2, d_ff, slope, act, sums, acc, gates, ups,
):
    hid = w_down.shape[0]
    size = gates.shape[2]
    count = hid // size

    def project(block, slot):
        first = pl.multiple_of(block * size, size)
        gates[slot] = dot(low[...], w_in[:, pl.ds(first, size)])
        ups[slot] = dot(low[...], w_in[:, pl.ds(pl.multiple_of(hid + first, size), size)])

    def finish(block, slot):
        here = pl.ds(pl.multiple_of(block * size, size), size)
        up = ups[slot]
        value, grad = gelu_pair(gates[slot])
        act[:, here] = value.astype(BF16)
        slope[:, here] = (up * grad).astype(BF16)
        acc[...] += dot((value * up).astype(BF16), w_down[here, :])

    acc[...] = unit[...] * line(gain1) + line(shift1)
    project(0, 0)

    def pair(index, carry):
        block = index * 2
        project(block + 1, 1)
        finish(block, 0)
        project(block + 2, 0)
        finish(block + 1, 1)
        return carry

    lax.fori_loop(0, count // 2 - 1, pair, 0)
    project(count - 1, 1)
    finish(count - 2, 0)
    finish(count - 1, 1)
    x, inv = standardize(acc[...])
    layer_out[...] = (x * line(gain2) + line(shift2)).astype(BF16)
    places = lax.broadcasted_iota(jnp.int32, (low.shape[0], masked.shape[0]), 0)
    dy = exact_dot((places == line(masked)).astype(F32), cot[...])
    sums[0:1, :] = jnp.sum(dy * x, axis=0, keepdims=True)
    sums[1:2, :] = jnp.sum(dy, axis=0, keepdims=True)
    grad_in = standardize_back(dy * line(gain2), x, inv)
    d_h2[...] = grad_in
    d_ff[...] = grad_in.astype(BF16)


def ffn_forward(low, unit, gain1, shift1, gain2, shift2, masked, cot, w_in, w_out, size):
    rows, width = low.shape
    hid = w_out.shape[0]
    return pl.pallas_call(
        ffn_forward_kernel,
        name="ffn_forward",
        out_shape=(
            shape((rows, width), BF16),
            shape((rows, width), F32),
            shape((rows, width), BF16),
            shape((rows, hid), BF16),
            shape((rows, hid), BF16),
            shape((2, width), F32),
        ),
        in_specs=[VM] * 10,
        out_specs=(VM,) * 6,
        scratch_shapes=[
            scratch((rows, width), F32),
            scratch((2, rows, size), F32),
            scratch((2, rows, size), F32),
        ],
        compiler_params=params(14),
        cost_estimate=pl.CostEstimate(
            flops=6 * rows * width * hid, bytes_accessed=18 * 10**6, transcendentals=2 * rows * hid
        ),
    )(low, unit, gain1, shift1, gain2, shift2, masked, cot, w_in, w_out)


def ffn_backward_kernel(
    d_ff, d_h2, unit, inverse, gain1, sums2, act, slope, w_in, w_down, d_h1, sent, acc, hidden
):
    hid = w_down.shape[0]
    size = hidden.shape[2]
    count = hid // size

    def project(block, slot):
        here = pl.ds(pl.multiple_of(block * size, size), size)
        hidden[slot] = dot_nt(d_ff[...], w_down[here, :])

    def finish(block, slot):
        first = pl.multiple_of(block * size, size)
        here, there = pl.ds(first, size), pl.ds(pl.multiple_of(hid + first, size), size)
        d_hidden = hidden[slot]
        d_gate = (d_hidden * slope[:, here].astype(F32)).astype(BF16)
        d_up = (d_hidden * act[:, here].astype(F32)).astype(BF16)
        acc[...] += dot_nt(d_gate, w_in[:, here]) + dot_nt(d_up, w_in[:, there])

    acc[...] = d_h2[...]
    project(0, 0)

    def pair(index, carry):
        block = index * 2
        project(block + 1, 1)
        finish(block, 0)
        project(block + 2, 0)
        finish(block + 1, 1)
        return carry

    lax.fori_loop(0, count // 2 - 1, pair, 0)
    project(count - 1, 1)
    finish(count - 2, 0)
    finish(count - 1, 1)
    total = acc[...]
    rows = total.shape[0]
    x = unit[...]
    gain_sum = jnp.sum(total * x, axis=0, keepdims=True)
    shift_sum = jnp.sum(total, axis=0, keepdims=True)
    sums = jnp.concatenate([gain_sum, shift_sum, sums2[...]], axis=0)
    high = sums.astype(BF16).astype(F32)
    tail = jnp.concatenate([high, sums - high, jnp.zeros((8, sums.shape[1]), F32)], axis=0)
    grad = standardize_back(total * line(gain1), x, inverse[...])
    d_h1[...] = grad
    sent[0:rows, :] = grad.astype(BF16)
    sent[rows : rows + 16, :] = tail.astype(BF16)


def ffn_backward(d_ff, d_h2, unit, inverse, gain1, sums2, act, slope, w_in, w_out, size):
    rows, width = d_ff.shape
    hid = w_out.shape[0]
    return pl.pallas_call(
        ffn_backward_kernel,
        name="ffn_backward",
        out_shape=(shape((rows, width), F32), shape((rows + 16, width), BF16)),
        in_specs=[VM] * 10,
        out_specs=(VM,) * 2,
        scratch_shapes=[scratch((rows, width), F32), scratch((2, rows, size), F32)],
        compiler_params=params(14),
        cost_estimate=pl.CostEstimate(
            flops=6 * rows * width * hid, bytes_accessed=20 * 10**6, transcendentals=0
        ),
    )(d_ff, d_h2, unit, inverse, gain1, sums2, act, slope, w_in, w_out)


X_FIRST = (1, 2, 4)
Z_FIRST = (2, 1, 4)


def bit_of(value, mask):
    return (value // mask) % 2


def store_blocks(blocks, keep, send, place, order, columns):
    one, two, three = order
    odd = bit_of(place, one) == 1
    for index in range(8):
        if index & one:
            continue
        spot = bit_of(place ^ index, two) * 2 + bit_of(place ^ index, three)
        low, high = blocks(index), blocks(index | one)
        keep[spot, :, columns] = jnp.where(odd, high, low).astype(BF16)
        send[spot, :, columns] = jnp.where(odd, low, high).astype(BF16)


def row_blocks(grad):
    each = grad.shape[0] // 8
    return lambda index: grad[index * each : (index + 1) * each]


def ffn_grad_kernel(
    size, info, n0, n1, n2, n3, f0, f1, f2, f3, w_in, w_down,
    keep_gate, send_gate, keep_up, send_up, keep_down, send_down,
    tok_t, gates, ups, d_hiddens, hidden_t, d_gate, d_up, d_ff, down,
):
    toks, grads = (n0, n1, n2, n3), (f0, f1, f2, f3)
    rows = n0.shape[0]
    units = w_down.shape[0]
    for at in range(RANKS):
        here = slice(at * rows, (at + 1) * rows)
        d_ff[here, :] = grads[at][...]
        tok_t[:, here] = jnp.transpose(toks[at][...])

    def unit_block(step, carry):
        here = pl.ds(pl.multiple_of(step * size, size), size)
        there = pl.ds(pl.multiple_of(units + step * size, size), size)
        w_gate, w_up, w_rows = w_in[:, here], w_in[:, there], w_down[here, :]

        def project(at):
            slot = at % 2
            gates[slot] = dot(toks[at][...], w_gate)
            ups[slot] = dot(toks[at][...], w_up)
            d_hiddens[slot] = dot_nt(grads[at][...], w_rows)

        def finish(at):
            slot = at % 2
            here = slice(at * rows, (at + 1) * rows)
            value, grad = gelu_pair(gates[slot])
            up, d_hidden = ups[slot], d_hiddens[slot]
            hidden_t[:, here] = jnp.transpose((value * up).astype(BF16))
            d_gate[here, :] = (d_hidden * up * grad).astype(BF16)
            d_up[here, :] = (d_hidden * value).astype(BF16)

        project(0)
        for at in range(RANKS):
            if at + 1 < RANKS:
                project(at + 1)
            finish(at)
        total = dot(tok_t[...], d_gate[...])
        store_blocks(row_blocks(total), keep_gate, send_gate, info[1], Z_FIRST, here)
        total = dot(tok_t[...], d_up[...])
        store_blocks(row_blocks(total), keep_up, send_up, info[1], Z_FIRST, here)
        down[here, :] = dot(hidden_t[...], d_ff[...])
        return carry

    lax.fori_loop(0, units // size, unit_block, 0)
    store_blocks(row_blocks(down), keep_down, send_down, info[1], X_FIRST, slice(None))


def ffn_grad(info, toks, grads, w_in, w_down, size):
    rows, width = toks[0].shape
    units = w_down.shape[0]
    tok = rows * RANKS
    dims = [(4, width // 8, units)] * 4 + [(4, units // 8, width)] * 2
    return pl.pallas_call(
        functools.partial(ffn_grad_kernel, size),
        name="ffn_grad",
        out_shape=[shape(each, BF16) for each in dims],
        in_specs=[SM] + [VM] * 10,
        out_specs=[VM] * 6,
        scratch_shapes=[
            scratch((width, tok), BF16),
            scratch((2, rows, size), F32),
            scratch((2, rows, size), F32),
            scratch((2, rows, size), F32),
            scratch((size, tok), BF16),
            scratch((tok, size), BF16),
            scratch((tok, size), BF16),
            scratch((tok, width), BF16),
            scratch((units, width), F32),
        ],
        compiler_params=params(18),
        cost_estimate=pl.CostEstimate(
            flops=12 * tok * width * units,
            bytes_accessed=8 * 10**6,
            transcendentals=2 * tok * units,
        ),
    )(info, *toks, *grads, w_in, w_down)


def qkv_grad_kernel(
    info, x0, x1, x2, x3, d0, d2, pair, j0, j1, j2, j3, g0, g1, g2, g3, keep, send, columns, grad
):
    rows, width = x0.shape
    part = width // RANKS
    total = 0.0
    for x, d_qkv in zip((x0, x1, x2, x3), (d0, pair.at[0], d2, pair.at[1])):
        total = total + dot(d_qkv[...], x[...])
    grad[:, : 3 * part] = jnp.transpose(total.astype(BF16)).astype(F32)
    for value in range(RANKS):

        @pl.when(info[0] == value)
        def _():
            for at, g in enumerate((g0, g1, g2, g3)):
                columns[at] = g[0:rows, value * part : (value + 1) * part]

    total = 0.0
    sums = 0.0
    for at, (joined, g) in enumerate(zip((j0, j1, j2, j3), (g0, g1, g2, g3))):
        total = total + dot(joined[...], columns[at])
        pair = g[rows : rows + 16, :].astype(F32)
        sums = sums + pair[0:4] + pair[4:8]
    grad[:, 3 * part :] = total
    high = sums.astype(BF16).astype(F32)
    tail = jnp.concatenate([high, sums - high], axis=0)
    each = width // 8

    def blocks(index):
        return jnp.concatenate([grad[index * each : (index + 1) * each], tail], axis=0)

    store_blocks(blocks, keep, send, info[1], X_FIRST, slice(None))


def qkv_grad(info, blocks, d_qkv, joined, d_proj):
    rows, width = blocks[0].shape
    return pl.pallas_call(
        qkv_grad_kernel,
        name="qkv_grad",
        out_shape=(shape((4, width // 8 + 8, width), BF16),) * 2,
        in_specs=[SM] + [VM] * 15,
        out_specs=(VM, VM),
        scratch_shapes=[
            scratch((RANKS, rows, width // RANKS), BF16),
            scratch((width, width), F32),
        ],
        compiler_params=params(14),
        cost_estimate=pl.CostEstimate(
            flops=8 * rows * width * width, bytes_accessed=4 * 10**6, transcendentals=0
        ),
    )(info, *blocks, *d_qkv, *joined, *d_proj)


def unpack(part, packed, wide, first):
    few = packed.shape[1] // RANKS
    for run in range(few // part):
        pieces = []
        for value in range(RANKS):
            at = value * few + run * part
            pieces.append(packed[:, at : at + part])
        at = first + run * RANKS * part
        wide[:, at : at + RANKS * part] = jnp.concatenate(pieces, axis=1).astype(F32)


def join_early_kernel(info, b0, b1, b2, b3, down, packed):
    rows, columns = b0.shape
    few = columns // 2
    for step, block in enumerate((b0, b1, b2, b3)):
        there = info[0] ^ step
        packed[:, pl.ds(pl.multiple_of(there * few, few), few)] = block[:, few:]
        down[pl.ds(pl.multiple_of(there * rows, rows), rows), :] = block[:, :few].astype(F32)


def join_wide_kernel(part, info, b0, b1, b2, b3, gates, wide, ups):
    few = b0.shape[1]
    for step, block in enumerate((b0, b1, b2, b3)):
        there = pl.multiple_of((info[0] ^ step) * few, few)
        ups[:, pl.ds(there, few)] = block[...]
    unpack(part, gates, wide, 0)
    unpack(part, ups, wide, RANKS * few)


def join_heads_kernel(info, b0, b1, b2, b3, out, rest):
    width = rest.shape[1]
    heads = width // RANKS
    for value in range(RANKS):

        @pl.when(info[0] == value)
        def _():
            for step, block in enumerate((b0, b1, b2, b3)):
                there = (value ^ step) * heads
                for third in range(3):
                    piece = block[:, third * heads : (third + 1) * heads].astype(F32)
                    out[:, third * width + there : third * width + there + heads] = piece
                rest[:, there : there + heads] = block[:, 3 * heads :].astype(F32)


def join_early(info, blocks):
    rows, columns = blocks[0].shape
    if rows % 8:
        stacked = jnp.stack(blocks)[info[0] ^ jnp.arange(RANKS)]
        few = columns // 2
        gates = jnp.concatenate(list(stacked[:, :, few:]), axis=1)
        return stacked[:, :, :few].reshape(-1, few).astype(F32), gates
    return pl.pallas_call(
        join_early_kernel,
        name="join_early",
        out_shape=(
            shape((rows * RANKS, columns // 2), F32),
            shape((rows, RANKS * columns // 2), BF16),
        ),
        in_specs=[SM] + [VM] * 4,
        out_specs=(VM, VM),
        compiler_params=params(8),
        cost_estimate=NO_COST,
    )(info, *blocks)


def join_wide(info, blocks, gates, part):
    rows, width = blocks[0].shape
    if RANKS * part % 128:
        stacked = jnp.stack(blocks)[info[0] ^ jnp.arange(RANKS)].astype(F32)
        both = [gates.astype(F32), jnp.concatenate(list(stacked), axis=1)]
        wide = [each.reshape(rows, RANKS, -1, part).transpose(0, 2, 1, 3) for each in both]
        return jnp.concatenate([each.reshape(rows, -1) for each in wide], axis=1)
    return pl.pallas_call(
        functools.partial(join_wide_kernel, part),
        name="join_wide",
        out_shape=shape((rows, 2 * RANKS * width), F32),
        in_specs=[SM] + [VM] * 5,
        out_specs=VM,
        scratch_shapes=[scratch((rows, RANKS * width), BF16)],
        compiler_params=params(14),
        cost_estimate=NO_COST,
    )(info, *blocks, gates)


def join_heads(info, blocks):
    rows, width = blocks[0].shape
    return pl.pallas_call(
        join_heads_kernel,
        name="join_heads",
        out_shape=(shape((rows, 3 * width), F32), shape((rows, width), F32)),
        in_specs=[SM] + [VM] * 4,
        out_specs=(VM, VM),
        compiler_params=params(8),
        cost_estimate=NO_COST,
    )(info, *blocks)


def token_grad_kernel(
    info, own, pair, far, cross, w, d_h1, masked, tokens, replacement, joined
):
    rows, width = d_h1.shape
    part = width // RANKS
    for step, block in enumerate((own, pair.at[0], far, cross)):
        for third in range(3):
            first = pl.multiple_of(third * width + (info[0] ^ step) * part, part)
            joined[pl.ds(first, part), :] = block[third * part : (third + 1) * part, :]
    grad = d_h1[...] + jnp.transpose(dot(w[...], joined[...]))
    count = masked.shape[0]
    places = lax.broadcasted_iota(jnp.int32, (rows, count), 0)
    select = (places == line(masked)).astype(F32)
    hit = jnp.max(select, axis=1, keepdims=True)
    tokens[...] = jnp.where(hit > 0.5, 0.0, grad)
    replacement[...] = lax.dot_general(
        select, grad, (((0,), (0,)), ((), ())),
        precision=lax.Precision.HIGHEST, preferred_element_type=F32,
    )


def token_grad(info, parts, w, d_h1, masked):
    rows, width = d_h1.shape
    return pl.pallas_call(
        token_grad_kernel,
        name="token_grad",
        out_shape=(shape((rows, width), F32), shape((masked.shape[0], width), F32)),
        in_specs=[SM] + [VM] * 7,
        out_specs=(VM, VM),
        scratch_shapes=[scratch((3 * width, rows), BF16)],
        compiler_params=params(16),
        cost_estimate=pl.CostEstimate(
            flops=6 * rows * width * width, bytes_accessed=8 * 10**6, transcendentals=0
        ),
    )(info, *parts, w, d_h1, masked)


def after(value, *others):
    return lax.optimization_barrier((value,) + others)[0]


def flip(value, axis, bits):
    count = lax.axis_size(axis)
    return lax.ppermute(value, axis, [(index, index ^ bits) for index in range(count)])


def gather_blocks(value):
    far = flip(value, "sp", 2)
    near = flip(value, "sp", 1)
    cross = flip(far, "sp", 1)
    return [value, near, far, cross]


def exchange_blocks(own, far, pair):
    pair = flip(pair, "sp", 1)
    far = flip(far, "sp", 2)
    cross = flip(pair[1], "sp", 2)
    return own, pair, far, cross


def small_mesh():
    return lax.axis_size("dp") == 8


NO_COST = pl.CostEstimate(flops=0, bytes_accessed=0, transcendentals=0)


def tidy_sums(value):
    first = value.shape[1] - 8
    sums = value[:, first : first + 4] + value[:, first + 4 :]
    high = sums.astype(BF16).astype(F32)
    return jnp.concatenate([value[:, :first], high, sums - high], axis=1)


def halve_kernel(with_sums, keep, came, kept, sent):
    half = keep.shape[0] // 2
    value = keep[...].astype(F32) + came[...].astype(F32)
    if with_sums:
        value = tidy_sums(value)
    kept[...] = value[:half]
    sent[...] = value[half:].astype(BF16)


def halve(keep, came, with_sums=False):
    dims = (keep.shape[0] // 2,) + keep.shape[1:]
    return pl.pallas_call(
        functools.partial(halve_kernel, with_sums),
        name="halve",
        out_shape=(shape(dims, F32), shape(dims, BF16)),
        in_specs=[VM] * 2,
        out_specs=(VM, VM),
        compiler_params=params(12),
        cost_estimate=NO_COST,
    )(keep, came)


def send_first(send, order):
    return flip(send, "dp", order[0]) if small_mesh() else send


def next_half(keep, came, with_sums=False):
    return halve(keep, came, with_sums) if small_mesh() else (keep, came)


def send_on(send, bits):
    return flip(send, "dp", bits) if small_mesh() else send


def send_second(keep, came, order, with_sums=False):
    keep, send = next_half(keep, came, with_sums)
    return keep, send_on(send, order[1])


def send_third(keep, came, order, with_sums=False):
    keep, send = next_half(keep, came, with_sums)
    return keep, send_on(send, order[2])


def natural_blocks(keep, send, order):
    both = jnp.concatenate([keep, send], axis=0).astype(F32)
    places = []
    for index in range(8):
        bits = [1 if index & mask else 0 for mask in order]
        places.append(both[bits[0] * 4 + bits[1] * 2 + bits[2]])
    return places


def scatter_sum(blocks):
    grad = jnp.concatenate(blocks, axis=0)
    return lax.psum_scatter(grad, "dp", scatter_dimension=0, tiled=True).astype(BF16)


def finish_pair_kernel(keep_a, came_a, keep_b, came_b, out):
    columns = keep_a.shape[2]
    out[:, :columns] = (keep_a[0] + came_a[0].astype(F32)).astype(BF16)
    out[:, columns:] = (keep_b[0] + came_b[0].astype(F32)).astype(BF16)


def finish_pair(keep_a, came_a, order_a, keep_b, came_b, order_b):
    if not small_mesh():
        first = scatter_sum(natural_blocks(keep_a, came_a, order_a))
        second = scatter_sum(natural_blocks(keep_b, came_b, order_b))
        return jnp.concatenate([first, second], axis=1)
    _, rows, columns = keep_a.shape
    return pl.pallas_call(
        finish_pair_kernel,
        name="finish_pair",
        out_shape=shape((rows, columns + keep_b.shape[2]), BF16),
        in_specs=[VM] * 4,
        out_specs=VM,
        compiler_params=params(8),
        cost_estimate=NO_COST,
    )(keep_a, came_a, keep_b, came_b)


def finish_kernel(keep, came, out):
    out[...] = (keep[0] + came[0].astype(F32)).astype(BF16)


def finish_sum(keep, came, order):
    if not small_mesh():
        return scatter_sum(natural_blocks(keep, came, order))
    return pl.pallas_call(
        finish_kernel,
        name="finish_sum",
        out_shape=shape(keep.shape[1:], BF16),
        in_specs=[VM] * 2,
        out_specs=VM,
        compiler_params=params(8),
        cost_estimate=NO_COST,
    )(keep, came)


def finish_heads_kernel(keep, came, out, *sums):
    rows = out.shape[0]
    total = keep[0] + came[0].astype(F32)
    out[...] = total[:rows].astype(BF16)
    for index, vector in enumerate(sums):
        value = total[rows + index : rows + index + 1] + total[rows + 4 + index : rows + 5 + index]
        vector[...] = value.reshape(-1)


def finish_heads(keep, came):
    _, rows, columns = keep.shape
    rows = rows - 8
    if not small_mesh():
        blocks = natural_blocks(keep, came, X_FIRST)
        sums = blocks[0][rows : rows + 4] + blocks[0][rows + 4 :]
        return scatter_sum([block[:rows] for block in blocks]), list(lax.psum(sums, "dp"))
    out, *sums = pl.pallas_call(
        finish_heads_kernel,
        name="finish_heads",
        out_shape=(shape((rows, columns), BF16),) + (shape((columns,), F32),) * 4,
        in_specs=[VM] * 2,
        out_specs=(VM,) * 5,
        compiler_params=params(8),
        cost_estimate=NO_COST,
    )(keep, came)
    return out, sums


def local(
    tokens,
    segment_ids,
    masked_rows,
    replacement,
    cotangent,
    w_qkv,
    w_out_attn,
    w_in_ff,
    w_out_ff,
    gain_one,
    shift_one,
    gain_two,
    shift_two,
):
    rows_dev, width = tokens.shape
    rank = lax.axis_index("sp")
    heads = HEADS // RANKS
    dim = width // HEADS
    part = heads * dim
    slopes = alibi_slopes(HEADS)

    select = jnp.arange(rows_dev, dtype=jnp.int32)[:, None] == masked_rows[None, :]
    hit = jnp.any(select, axis=1, keepdims=True)
    placed = dot(select.astype(BF16), replacement)
    start = jnp.where(hit, placed.astype(BF16), tokens)
    start_far = flip(start, "sp", 2)
    start_near = flip(start, "sp", 1)
    place = lax.axis_index("dp")
    place = place if small_mesh() else place * 0
    spot = jnp.stack([rank, place]).astype(jnp.int32)

    w_rank = jnp.concatenate(
        [
            lax.dynamic_slice_in_dim(w_qkv, third * width + rank * part, part, 1)
            for third in range(3)
        ],
        axis=1,
    )
    start_cross = flip(after(start_far, w_rank, spot), "sp", 1)
    start_blocks = [start, start_near, start_far, start_cross]
    *saved, attn, lse = attention_forward(
        spot, segment_ids, slopes, start_blocks, w_rank, heads, dim
    )
    attn_far = flip(attn, "sp", 2)
    attn_near = flip(attn, "sp", 1)
    part_units = w_out_ff.shape[0] // lax.axis_size("dp") // RANKS
    packed_in, packed_down = pack_weights(after(spot, lse), w_in_ff, w_out_ff, part_units)
    attn_cross = flip(after(attn_far, packed_in), "sp", 1)
    attn_parts = [attn, attn_near, attn_far, attn_cross]
    low, joined, unit, inverse = norm_one(
        spot, attn_parts, start, w_out_attn, gain_one, shift_one
    )
    layer_out, d_h2, d_ff, slope, act, sums2 = ffn_forward(
        low, unit, gain_one, shift_one, gain_two, shift_two,
        masked_rows, cotangent, w_in_ff, w_out_ff, 768,
    )
    d_ff_far = flip(d_ff, "sp", 2)
    d_ff_near = flip(d_ff, "sp", 1)
    d_h1, sent = ffn_backward(
        d_ff, d_h2, unit, inverse, gain_one, sums2, act, slope, w_in_ff, w_out_ff, 768
    )
    lows, others_joined = norm_others(
        after(spot, sent), attn_parts, start_blocks[1:], w_out_attn, gain_one, shift_one
    )
    d_ff_far = after(d_ff_far, lows[0])
    d_ff_cross = flip(d_ff_far, "sp", 1)
    d_ff_blocks = [d_ff, d_ff_near, d_ff_far, d_ff_cross]
    far = flip(sent, "sp", 2)
    near = flip(sent, "sp", 1)

    keep_g, send_g, keep_u, send_u, keep_d, send_d = ffn_grad(
        spot, [low, *lows], d_ff_blocks, packed_in, packed_down, 256
    )
    came_g = send_first(send_g, Z_FIRST)
    came_d = send_first(send_d, X_FIRST)
    cross = flip(after(far, keep_g), "sp", 1)
    d_proj_blocks = [sent, near, far, cross]

    d_qkv = attention_backward(
        spot, segment_ids, slopes, d_proj_blocks, w_out_attn, saved, lse, heads, dim
    )
    parts = exchange_blocks(*d_qkv)
    came_u = send_first(after(send_u, d_qkv[0]), Z_FIRST)
    keep_g, came_g = send_second(keep_g, after(came_g, d_qkv[0]), Z_FIRST)
    keep_d, came_d = send_second(keep_d, after(came_d, keep_g), X_FIRST)
    keep_q, send_q = qkv_grad(
        after(spot, keep_d), start_blocks, d_qkv, [joined, *others_joined], d_proj_blocks
    )
    keep_g, came_g = send_third(keep_g, after(came_g, keep_q), Z_FIRST)
    came_q = send_first(after(send_q, keep_g), X_FIRST)
    keep_u, came_u = send_second(keep_u, after(came_u, keep_g), Z_FIRST)
    keep_d, came_d = send_third(keep_d, after(came_d, keep_u, came_g), X_FIRST)
    keep_q, send_q = next_half(keep_q, after(came_q, keep_d, parts), True)
    came_q = send_on(send_q, X_FIRST[1])
    keep_u, came_u = send_third(keep_u, after(came_u, keep_q), Z_FIRST)
    early = finish_pair(keep_d, after(came_d, keep_u), X_FIRST, keep_g, came_g, Z_FIRST)
    far = flip(early, "sp", 2)
    near = flip(early, "sp", 1)
    keep_q, came_q = send_third(keep_q, after(came_q, early), X_FIRST, True)
    early_blocks = [early, near, far, flip(after(far, keep_q), "sp", 1)]
    ups = finish_sum(keep_u, after(came_u, keep_q), Z_FIRST)
    far = flip(ups, "sp", 2)
    near = flip(ups, "sp", 1)
    grad_tokens, grad_replacement = token_grad(
        after(spot, ups), parts, w_qkv, d_h1, masked_rows
    )
    grad_down, gates = join_early(after(spot, grad_tokens), early_blocks)
    up_blocks = [ups, near, far, flip(after(far, gates), "sp", 1)]
    heads_share, norm_sums = finish_heads(keep_q, after(came_q, gates, up_blocks[2]))
    far = flip(heads_share, "sp", 2)
    near = flip(heads_share, "sp", 1)
    grad_in = join_wide(after(spot, heads_share), up_blocks, gates, part_units)
    head_blocks = [heads_share, near, far, flip(after(far, grad_in), "sp", 1)]
    grad_qkv, grad_out = join_heads(spot, head_blocks)

    return (
        layer_out,
        grad_tokens,
        grad_replacement,
        grad_qkv,
        grad_out,
        grad_in,
        grad_down,
        norm_sums[0],
        norm_sums[1],
        norm_sums[2],
        norm_sums[3],
    )


def solution(mesh):
    tokens = P(("dp", "sp"), None)
    rows = P("dp", None)
    return jax.shard_map(
        local,
        mesh=mesh,
        in_specs=(tokens, rows, P(("dp", "sp")), tokens, tokens) + (P(),) * 8,
        out_specs=(tokens,) * 3 + (rows,) * 4 + (P(),) * 4,
        check_vma=False,
    )
```
